32 devices in a mesh: dp: 8 (over y, x, core), tensor: 4 (over z).
Axes of the slice: x: 2, y: 2, z: 4, core: 2. Of those that a mesh axis runs over, the one named last changes fastest.
Arguments:
- inputs: bfloat16 [8, 2048, 768], P('dp', 'tensor'), may hold values from -6 to 6
- segment_ids: int32 [8, 2048], P('dp'), may hold values from 0 to 7, never falling along the last dimension, each value on 1 to 1024 neighbouring positions
- valid_mask: int32 [8, 2048], P('dp', 'tensor'), may hold values from 0 to 1
- teacher: bfloat16 [8, 2048, 768], P('dp', 'tensor'), may hold values from -5 to 5
- cotangent: bfloat16 [8, 2048, 768], P('dp', 'tensor'), may hold values from -6 to 6
- w_query: bfloat16 [768, 768], P('dp', 'tensor'), may hold values from -0.3125 to 0.3125
- w_key: bfloat16 [768, 768], P('dp', 'tensor'), may hold values from -0.21875 to 0.21875
- w_value: bfloat16 [768, 768], P('dp', 'tensor'), may hold values from -0.21875 to 0.21875
- w_output: bfloat16 [768, 768], P('tensor', 'dp'), may hold values from -0.875 to 0.875
- w_inner: bfloat16 [768, 3072], P('dp', 'tensor'), may hold values from -0.21875 to 0.21875
- w_outer: bfloat16 [3072, 768], P('tensor', 'dp'), may hold values from -0.15625 to 0.15625
- query_bias: bfloat16 [768], replicated, may hold values from -3 to 3
- value_bias: bfloat16 [768], replicated, may hold values from -3 to 3
- output_bias: bfloat16 [768], replicated, may hold values from -3 to 3
- inner_bias: bfloat16 [3072], replicated, may hold values from -3 to 3
- outer_bias: bfloat16 [768], replicated, may hold values from -3 to 3
- gain_attn: bfloat16 [768], replicated, may hold values from 0.5 to 1.5
- shift_attn: bfloat16 [768], replicated, may hold values from -3 to 3
- gain_ffn: bfloat16 [768], replicated, may hold values from 0.5 to 1.5
- shift_ffn: bfloat16 [768], replicated, may hold values from -3 to 3
Outputs:
- layer_out: bfloat16 [8, 2048, 768], P('dp', 'tensor')
- mse_loss: float32 [], replicated
- input_grad: float32 [8, 2048, 768], P('dp', 'tensor')
- query_weight_grad: float32 [768, 768], P('dp', 'tensor')
- key_weight_grad: float32 [768, 768], P('dp', 'tensor')
- value_weight_grad: float32 [768, 768], P('dp', 'tensor')
- output_weight_grad: float32 [768, 768], P('tensor', 'dp')
- inner_weight_grad: float32 [768, 3072], P('dp', 'tensor')
- outer_weight_grad: float32 [3072, 768], P('tensor', 'dp')
- query_bias_grad: float32 [768], replicated
- value_bias_grad: float32 [768], replicated
- output_bias_grad: float32 [768], replicated
- inner_bias_grad: float32 [3072], replicated
- outer_bias_grad: float32 [768], replicated
- gain_attn_grad: float32 [768], replicated
- shift_attn_grad: float32 [768], replicated
- gain_ffn_grad: float32 [768], replicated
- shift_ffn_grad: float32 [768], replicated
The draws below stay inside these ranges and needn't reach their ends.
All inputs are finite; a program needn't handle non-finite values.
Results may differ from the reference program's by a relative error of at most 0.017.
Values may be sent and summed in bfloat16 or wider, within the bound.
No kernel may reach another device: no remote copies, remote signals or barrier semaphores. Data moves between devices by JAX's collectives and lax.ppermute only.
A program may use at most 128 MiB of HBM per device.

```python
import math
import jax
import jax.numpy as jnp
import numpy as np
from jax import lax

D = 768
HEADS = 12
DH = 64
FF = 3072
SEQ = 2048
SEQS = 1
QBLOCK = 512
SEG_COUNT = 8
SEG_MOST = 1024
NSEQ = 8
TOKENS = 16384
N_DP = 8


def draw_valid_mask(key, part):
    picks = jax.random.randint(key, (NSEQ, SEQ), 0, 1000)
    rising = 250 + 500 * jnp.arange(NSEQ, dtype=jnp.int32) // NSEQ
    chosen = (picks < rising[:, None]).astype(jnp.int32)
    first_slot = (jnp.arange(NSEQ, dtype=jnp.int32)[:, None] == 0) & (jnp.arange(SEQ, dtype=jnp.int32)[None, :] == 0)
    return jnp.where(first_slot, 1, chosen).astype(jnp.int32)


def draw_teacher(key, part):
    base = jax.random.normal(key, (NSEQ, SEQ, D), jnp.float32)
    return jnp.clip(base, -5.0, 5.0).astype(jnp.bfloat16)


def block_scale(stream_key, extent, split, least, high):
    level = 1.0
    for dim, shards_of in split:
        draws = jax.random.uniform(jax.random.fold_in(jax.random.fold_in(stream_key, 6), dim), (shards_of,), jnp.float32, least / len(split), high / len(split))
        level = level * jnp.repeat(jnp.exp(draws), extent[dim] // shards_of).reshape((-1,) + (1,) * (len(extent) - 1 - dim))
    return level


def profile(amount, total, most, slope):
    portions = [(1 << 20) // math.isqrt(standing ** slope) + 1 for standing in range(2, amount + 1)]
    surplus, holding = total - most - (amount - 1), [1] * (amount - 1)
    while surplus > 0:
        free = [i for i in range(amount - 1) if holding[i] < most]
        mass, remaining = sum([portions[i] for i in free]), surplus
        for i in free:
            more = min(most - holding[i], max(1, remaining * portions[i] // mass), surplus)
            holding[i] = holding[i] + more
            surplus = surplus - more
    return np.array([most] + holding)


def ragged(key, amount, total, limit, slope):
    if amount == 2:
        one = jax.random.randint(key, (), max(1, total - limit), min(limit, total - 1) + 1)
        return jnp.stack([one, total - one])
    tallies = jnp.asarray(profile(amount, total, limit, slope), jnp.int32)
    twos = (amount - 1) // 2
    source_of, sink = tallies[1:1 + 2 * twos:2], tallies[2:2 + 2 * twos:2]
    slack = jnp.minimum(source_of - 1, limit - sink)
    moved = jax.random.randint(jax.random.fold_in(key, 1), (twos,), 0, 1 << 20) % (slack + 1)
    tallies = tallies.at[1:1 + 2 * twos:2].set(source_of - moved).at[2:2 + 2 * twos:2].set(sink + moved)
    return tallies[jax.random.permutation(jax.random.fold_in(key, 2), amount)]


def noise(key, dims, width, limit, cuts=(), kind=jnp.bfloat16):
    values = jax.random.normal(key, dims, jnp.float32) * width
    if len(cuts) > 0:
        values = block_scale(key, dims, cuts, -0.22, 0.18) * values
    return jnp.clip(values, min=-limit, max=limit).astype(kind)


def setup_inputs(seed: int = 0) -> dict:
    seeds = jax.random.split(jax.random.key(seed), 21)
    return {
        "inputs": noise(seeds[0], (NSEQ, SEQ, D), 1.0, 6.0, ((0, 8), (1, 4))),
        "segment_ids": jax.vmap(lambda own: jnp.searchsorted(jnp.cumsum(ragged(own, SEG_COUNT, SEQ, SEG_MOST, 2)), jnp.arange(SEQ), side="right"))(jax.random.split(seeds[1], NSEQ)).reshape((NSEQ, SEQ)).astype(jnp.int32),
        "valid_mask": draw_valid_mask(jax.random.fold_in(seeds[20], 71), 0),
        "teacher": draw_teacher(jax.random.fold_in(seeds[20], 71), 0),
        "cotangent": noise(seeds[4], (NSEQ, SEQ, D), 1.0, 6.0, ((0, 8), (1, 4))),
        "w_query": noise(seeds[5], (D, D), (D // 2) ** -0.5, 0.3125, ((0, 8), (1, 4))),
        "w_key": noise(seeds[6], (D, D), D ** -0.5, 0.21875, ((0, 8), (1, 4))),
        "w_value": noise(seeds[7], (D, D), D ** -0.5, 0.21875, ((0, 8), (1, 4))),
        "w_output": noise(seeds[8], (D, D), (D // 16) ** -0.5, 0.875, ((0, 4), (1, 8))),
        "w_inner": noise(seeds[9], (D, FF), D ** -0.5, 0.21875, ((0, 8), (1, 4))),
        "w_outer": noise(seeds[10], (FF, D), (FF // 2) ** -0.5, 0.15625, ((0, 4), (1, 8))),
        "query_bias": noise(seeds[11], (D,), 0.5, 3.0),
        "value_bias": noise(seeds[12], (D,), 0.3, 3.0),
        "output_bias": noise(seeds[13], (D,), 0.3, 3.0),
        "inner_bias": noise(seeds[14], (FF,), 0.3, 3.0),
        "outer_bias": noise(seeds[15], (D,), 0.3, 3.0),
        "gain_attn": jnp.clip(1.0 + 0.1 * jax.random.normal(seeds[16], (D,), jnp.float32), 0.5, 1.5).astype(jnp.bfloat16),
        "shift_attn": noise(seeds[17], (D,), 0.3, 3.0),
        "gain_ffn": jnp.clip(1.0 + 0.1 * jax.random.normal(seeds[18], (D,), jnp.float32), 0.5, 1.5).astype(jnp.bfloat16),
        "shift_ffn": noise(seeds[19], (D,), 0.3, 3.0),
    }


HIGHEST = lax.Precision.HIGHEST
EPSILON = 1e-12

@jax.custom_vjp
def low(v):
    return lax.optimization_barrier(v.astype(jnp.bfloat16)).astype(jnp.float32)

@jax.custom_vjp
def low_back(v):
    return v

def low_keep(v):
    return (low(v), None)

def low_pass(kept, grad):
    return (grad,)

def back_keep(v):
    return (v, None)

def back_low(kept, grad):
    return (low(grad),)
low.defvjp(low_keep, low_pass)
low_back.defvjp(back_keep, back_low)

def matmul(left_side, right_side):
    return jnp.dot(left_side, right_side, precision=HIGHEST, preferred_element_type=jnp.float32)

def layer_norm(summed, gain_vec, shift_vec):
    average = lax.optimization_barrier(jnp.mean(summed, axis=-1, keepdims=True))
    centered = summed - average
    variance = lax.optimization_barrier(jnp.mean(centered * centered, axis=-1, keepdims=True))
    return centered * lax.rsqrt(variance + EPSILON) * gain_vec + shift_vec

def group_forward(param_set, group_inputs, group_segments, group_valid, group_teacher):
    w_query, w_key, w_value, w_output, w_inner, w_outer, query_bias, value_bias, output_bias, inner_bias, outer_bias, gain_attn, shift_attn, gain_ffn, shift_ffn = param_set
    flat_in = group_inputs.reshape(SEQS * SEQ, D)
    queries = low(low_back(matmul(flat_in, w_query) + query_bias))
    keys_all = low(low_back(matmul(flat_in, w_key)))
    values_all = low(low_back(matmul(flat_in, w_value) + value_bias))
    blocks = SEQ // QBLOCK
    query_blocks = queries.reshape(SEQS * blocks, QBLOCK, HEADS, DH)
    segment_blocks = group_segments.reshape(SEQS * blocks, QBLOCK)
    owners = jnp.arange(SEQS * blocks, dtype=jnp.int32) // blocks
    key_seqs = keys_all.reshape(SEQS, SEQ, HEADS, DH)
    value_seqs = values_all.reshape(SEQS, SEQ, HEADS, DH)
    score_scale = DH ** (-0.5)

    def attend(block_item):
        query_block, segment_block, owner = block_item
        key_seq = key_seqs[owner]
        value_seq = value_seqs[owner]
        segment_row = group_segments[owner]
        scores = low_back(jnp.einsum('qhd,khd->hqk', query_block, key_seq, precision=HIGHEST) * score_scale)
        allowed = segment_block[None, :, None] == segment_row[None, None, :]
        masked = jnp.where(allowed, scores, -1e+30)
        highest = lax.optimization_barrier(jnp.max(masked, axis=-1, keepdims=True))
        raised = jnp.exp(masked - highest)
        probs = raised / lax.optimization_barrier(jnp.sum(raised, axis=-1, keepdims=True))
        context = jnp.einsum('hqk,khd->qhd', low(probs), value_seq, precision=HIGHEST)
        return low(low_back(context))
    context_all = lax.map(jax.checkpoint(attend), (query_blocks, segment_blocks, owners))
    context_rows = context_all.reshape(SEQS * SEQ, D)
    attention = low_back(matmul(context_rows, w_output) + output_bias)
    first = low(layer_norm(flat_in + attention, gain_attn, shift_attn))
    hidden = low_back(matmul(first, w_inner) + inner_bias)
    activated = low(jax.nn.gelu(hidden, approximate=False))
    branch = low_back(matmul(activated, w_outer) + outer_bias)
    layer_rows = layer_norm(first + branch, gain_ffn, shift_ffn)
    misfit = layer_rows - group_teacher.reshape(SEQS * SEQ, D)
    squared = jnp.sum(group_valid.reshape(SEQS * SEQ, 1) * misfit * misfit)
    return (layer_rows.reshape(SEQS, SEQ, D), squared)

def reference(inputs, segment_ids, valid_mask, teacher, cotangent, w_query, w_key, w_value, w_output, w_inner, w_outer, query_bias, value_bias, output_bias, inner_bias, outer_bias, gain_attn, shift_attn, gain_ffn, shift_ffn):
    params = jax.tree.map(lambda array_in: array_in.astype(jnp.float32), (w_query, w_key, w_value, w_output, w_inner, w_outer, query_bias, value_bias, output_bias, inner_bias, outer_bias, gain_attn, shift_attn, gain_ffn, shift_ffn))
    valid_rows = valid_mask.astype(jnp.float32)
    counted = jnp.sum(valid_rows)
    loss_weight = TOKENS / (2.0 * counted)
    shaped = (N_DP, SEQS, SEQ, D)
    group_items = (inputs.astype(jnp.float32).reshape(shaped), segment_ids.reshape(N_DP, SEQS, SEQ), valid_rows.reshape(N_DP, SEQS, SEQ), teacher.astype(jnp.float32).reshape(shaped), cotangent.astype(jnp.float32).reshape(shaped))

    def one_group(running, group_item):
        grads, squared_sum = running
        group_inputs, group_segments, group_valid, group_teacher, group_cotangent = group_item

        def forward(param_set, inputs_in):
            return group_forward(param_set, inputs_in, group_segments, group_valid, group_teacher)
        (layer_group, squared), pullback = jax.vjp(forward, params, group_inputs)
        param_grads, input_grads = pullback((group_cotangent, jnp.ones_like(squared) * loss_weight))
        grads = jax.tree.map(lambda earlier, later: earlier + later, grads, param_grads)
        return ((grads, squared_sum + squared), (layer_group, input_grads))
    start_grads = jax.tree.map(jnp.zeros_like, params)
    (grads, squared_sum), (layers, input_grads) = lax.scan(one_group, (start_grads, jnp.zeros((), jnp.float32)), group_items)
    layer_out = layers.reshape(NSEQ, SEQ, D).astype(jnp.bfloat16)
    input_grad = input_grads.reshape(NSEQ, SEQ, D)
    mse_loss = squared_sum / (counted * D)
    return (layer_out, mse_loss, input_grad, grads[0], grads[1], grads[2], grads[3], grads[4], grads[5], grads[6], grads[7], grads[8], grads[9], grads[10], grads[11], grads[12], grads[13], grads[14])
```

```python
import functools

import jax
import jax.numpy as jnp
from jax import lax
from jax.experimental import pallas as pl
from jax.experimental.pallas import tpu as pltpu
from jax.sharding import PartitionSpec as P

DH = 64
BLOCK = 256
SLAB = 4 * DH
EPSILON = 1e-12
ROOT_HALF = 0.7071067811865476
INV_ROOT_TAU = 0.3989422804014327
LOG2E = 1.4426950408889634
LN2 = 0.6931471805599453
SCALE = DH ** (-0.5)
MASKED = -1e30

BF16 = jnp.bfloat16
F32 = jnp.float32
NN = (((1,), (0,)), ((), ()))
NT = (((1,), (1,)), ((), ()))
TN = (((0,), (0,)), ((), ()))


def dot(left_side, right_side, dims=NN):
    return lax.dot_general(left_side, right_side, dims, preferred_element_type=F32)


def norm_forward(summed, gain_vec, shift_vec):
    average = jnp.mean(summed, axis=-1, keepdims=True)
    centered = summed - average
    variance = jnp.mean(centered * centered, axis=-1, keepdims=True)
    inverse = lax.rsqrt(variance + EPSILON)
    normed = centered * inverse
    return (normed * gain_vec + shift_vec, normed, inverse)


def norm_backward(upstream, normed, inverse, gain_vec):
    scaled = upstream * gain_vec
    first_mean = jnp.mean(scaled, axis=-1, keepdims=True)
    second_mean = jnp.mean(scaled * normed, axis=-1, keepdims=True)
    back_grad = inverse * (scaled - first_mean - normed * second_mean)
    return (back_grad, jnp.sum(upstream * normed, axis=0), jnp.sum(upstream, axis=0))


def lane_is_right(rows):
    return lax.broadcasted_iota(jnp.int32, (rows, 2 * DH), 1) >= DH


def attend_forward(low_ref, high_ref, qkv_ref, seg_col_ref, seg_row_ref, ctx_ref, lse_ref, held, outs):
    head = pl.program_id(0)
    blocks = qkv_ref.shape[0] // BLOCK
    for qb in range(blocks):
        rows = pl.ds(qb * BLOCK, BLOCK)
        query = qkv_ref[rows, : 2 * DH] * jnp.asarray(SCALE, BF16)
        seg_q = seg_col_ref[rows, :]
        low, high = low_ref[qb], high_ref[qb]

        def score(kb, peak):
            keys = pl.ds(pl.multiple_of(kb * BLOCK, BLOCK), BLOCK)
            scores = dot(query, qkv_ref[keys, 2 * DH :], NT)
            scores = jnp.where(seg_q == seg_row_ref[:, keys], scores, MASKED)
            held[kb] = scores
            return jnp.maximum(peak, jnp.maximum(scores[:, :128], scores[:, 128:]))

        peak = lax.fori_loop(low, high, score, jnp.full((BLOCK, 128), MASKED, F32))
        highest = jnp.max(peak, axis=-1, keepdims=True)

        def weigh(kb, carry):
            total, acc = carry
            keys = pl.ds(pl.multiple_of(kb * BLOCK, BLOCK), BLOCK)
            raised = jnp.exp2((held[kb] - highest) * LOG2E)
            total = total + (raised[:, :128] + raised[:, 128:])
            return (total, acc + dot(raised.astype(BF16), qkv_ref[keys, 2 * DH :]))

        zero = jnp.zeros((BLOCK, 128), F32)
        total, acc = lax.fori_loop(low, high, weigh, (zero, zero))
        summed = jnp.sum(total, axis=-1, keepdims=True)
        outs[rows, :] = (acc / summed).astype(BF16)
        lse_ref[0, :, rows] = jnp.transpose(highest + jnp.log(summed))
    value = outs[...]
    right = lane_is_right(value.shape[0])

    @pl.when(head == 0)
    def _():
        ctx_ref[:, :128] = jnp.where(right, jnp.zeros_like(value), pltpu.roll(value, DH, 1))

    @pl.when(head == 1)
    def _():
        ctx_ref[:, :128] = jnp.where(right, value, ctx_ref[:, :128])

    @pl.when(head == 2)
    def _():
        ctx_ref[:, 128:] = pltpu.roll(value, DH, 1)[:, :DH]


def attend_backward(
    low_ref, high_ref, qkv_ref, seg_col_ref, seg_row_ref, ctx_ref, grad_ref, lse_ref,
    out_ref, sums_ref, grads, dkv, deltas
):
    head = pl.program_id(0)
    seq_len = qkv_ref.shape[0]
    blocks = seq_len // BLOCK
    right = lane_is_right(seq_len)

    def place(value, both):
        moved = pltpu.roll(value, DH, 1) if both else value
        grads[...] = jnp.where(right, moved, jnp.zeros_like(moved))

    def widen(ref):
        tail = ref[:, 128:]
        return jnp.concatenate([tail, jnp.zeros_like(tail)], axis=1)

    def delta_of(low_lanes, first_tile):
        if first_tile:
            product = grad_ref[:, :128].astype(F32) * ctx_ref[:, :128].astype(F32)
            keep = jnp.logical_not(right) if low_lanes else right
            product = jnp.where(keep, product, 0.0)
        else:
            product = grad_ref[:, 128:].astype(F32) * ctx_ref[:, 128:].astype(F32)
        return jnp.sum(product, axis=-1, keepdims=True)

    @pl.when(head == 0)
    def _():
        place(grad_ref[:, :128], True)
        deltas[...] = jnp.transpose(delta_of(True, True))

    @pl.when(head == 1)
    def _():
        place(grad_ref[:, :128], False)
        deltas[...] = jnp.transpose(delta_of(False, True))

    @pl.when(head == 2)
    def _():
        place(widen(grad_ref), True)
        deltas[...] = jnp.transpose(delta_of(True, False))

    dkv[...] = jnp.zeros_like(dkv)
    right_block = lane_is_right(BLOCK)
    query_total = jnp.zeros((1, 128), F32)
    for qb in range(blocks):
        rows = pl.ds(qb * BLOCK, BLOCK)
        query = qkv_ref[rows, : 2 * DH] * jnp.asarray(SCALE, BF16)
        grad = grads[rows, :]
        paired = jnp.concatenate([query, grad], axis=0)
        seg_q = seg_row_ref[:, rows]
        lse = lse_ref[0, :, rows]
        delta = deltas[:, rows]
        low, high = low_ref[qb], high_ref[qb]

        def step(kb, acc):
            keys = pl.ds(pl.multiple_of(kb * BLOCK, BLOCK), BLOCK)
            pair = qkv_ref[keys, 2 * DH :]
            scores = dot(pair, query, NT)
            scores = jnp.where(seg_col_ref[keys, :] == seg_q, scores, MASKED)
            probs = jnp.exp2((scores - lse) * LOG2E)
            probs_grad = dot(pair, grad, NT)
            score_grad = (probs * (probs_grad - delta)).astype(BF16)
            both = jnp.concatenate([score_grad, probs.astype(BF16)], axis=1)
            dkv[keys, :] += dot(both, paired)
            return acc + dot(score_grad, pair, TN)

        acc = lax.fori_loop(low, high, step, jnp.zeros((BLOCK, 128), F32))
        query_grad = jnp.where(right_block, 0.0, acc * SCALE).astype(BF16)
        out_ref[rows, : 2 * DH] = query_grad
        query_total = query_total + jnp.sum(query_grad.astype(F32), axis=0, keepdims=True)
    pair_grad = dkv[...].astype(BF16)
    out_ref[:, 2 * DH :] = pair_grad
    sums_ref[0, :, : 2 * DH] = query_total
    sums_ref[0, :, 2 * DH :] = jnp.sum(pair_grad.astype(F32), axis=0, keepdims=True)


def document_blocks(segment_row):
    blocks = segment_row.shape[0] // BLOCK
    starts = segment_row[::BLOCK]
    stops = segment_row[BLOCK - 1 :: BLOCK]
    low = jnp.sum((segment_row[None, :] < starts[:, None]).astype(jnp.int32), axis=1)
    high = jnp.sum((segment_row[None, :] <= stops[:, None]).astype(jnp.int32), axis=1)
    return (low // BLOCK, (high + BLOCK - 1) // BLOCK)


def run_forward(bounds, qkv, seg_col, seg_row):
    seq_len, width = qkv.shape
    heads = width // SLAB
    blocks = seq_len // BLOCK
    return pl.pallas_call(
        attend_forward,
        out_shape=(
            jax.ShapeDtypeStruct((seq_len, heads * DH), BF16),
            jax.ShapeDtypeStruct((heads, 1, seq_len), F32),
        ),
        grid_spec=pltpu.PrefetchScalarGridSpec(
            num_scalar_prefetch=2,
            grid=(heads,),
            in_specs=[
                pl.BlockSpec((seq_len, SLAB), lambda h, *_: (0, h)),
                pl.BlockSpec((seq_len, 1), lambda h, *_: (0, 0)),
                pl.BlockSpec((1, seq_len), lambda h, *_: (0, 0)),
            ],
            out_specs=(
                pl.BlockSpec((seq_len, heads * DH), lambda h, *_: (0, 0)),
                pl.BlockSpec((1, 1, seq_len), lambda h, *_: (h, 0, 0)),
            ),
            scratch_shapes=[
                pltpu.VMEM((blocks, BLOCK, BLOCK), F32),
                pltpu.VMEM((seq_len, 2 * DH), BF16),
            ],
        ),
        compiler_params=pltpu.CompilerParams(
            dimension_semantics=("arbitrary",), vmem_limit_bytes=40 << 20
        ),
        cost_estimate=pl.CostEstimate(
            flops=heads * seq_len * seq_len * 256, bytes_accessed=8 << 20, transcendentals=heads * seq_len * seq_len // 3
        ),
        name="attend_forward",
    )(*bounds, qkv, seg_col, seg_row)


def run_backward(bounds, qkv, seg_col, seg_row, ctx, grad, lse):
    seq_len, width = qkv.shape
    heads = width // SLAB
    return pl.pallas_call(
        attend_backward,
        out_shape=(
            jax.ShapeDtypeStruct((seq_len, width), BF16),
            jax.ShapeDtypeStruct((heads, 1, SLAB), F32),
        ),
        grid_spec=pltpu.PrefetchScalarGridSpec(
            num_scalar_prefetch=2,
            grid=(heads,),
            in_specs=[
                pl.BlockSpec((seq_len, SLAB), lambda h, *_: (0, h)),
                pl.BlockSpec((seq_len, 1), lambda h, *_: (0, 0)),
                pl.BlockSpec((1, seq_len), lambda h, *_: (0, 0)),
                pl.BlockSpec((seq_len, heads * DH), lambda h, *_: (0, 0)),
                pl.BlockSpec((seq_len, heads * DH), lambda h, *_: (0, 0)),
                pl.BlockSpec((1, 1, seq_len), lambda h, *_: (h, 0, 0)),
            ],
            out_specs=(
                pl.BlockSpec((seq_len, SLAB), lambda h, *_: (0, h)),
                pl.BlockSpec((1, 1, SLAB), lambda h, *_: (h, 0, 0)),
            ),
            scratch_shapes=[
                pltpu.VMEM((seq_len, 2 * DH), BF16),
                pltpu.VMEM((seq_len, 2 * DH), F32),
                pltpu.VMEM((1, seq_len), F32),
            ],
        ),
        compiler_params=pltpu.CompilerParams(
            dimension_semantics=("arbitrary",), vmem_limit_bytes=40 << 20
        ),
        cost_estimate=pl.CostEstimate(
            flops=heads * seq_len * seq_len * 640, bytes_accessed=12 << 20, transcendentals=heads * seq_len * seq_len // 3
        ),
        name="attend_backward",
    )(*bounds, qkv, seg_col, seg_row, ctx, grad, lse)


def interleave(query, key, value, heads):
    rows = query.shape[0]
    parts = [part.reshape(rows, heads, 1, DH) for part in (query, jnp.zeros_like(query), key, value)]
    return jnp.concatenate(parts, axis=2).reshape(rows, heads * SLAB)


def place_slice(local_grad, full_size, offset):
    return lax.dynamic_update_slice_in_dim(jnp.zeros((full_size,), F32), local_grad, offset, 0)


def local(
    inputs, segment_ids, valid_mask, teacher, cotangent,
    w_query, w_key, w_value, w_output, w_inner, w_outer,
    query_bias, value_bias, output_bias, inner_bias, outer_bias,
    gain_attn, shift_attn, gain_ffn, shift_ffn,
):
    _, part_len, width = inputs.shape
    parts = lax.axis_size("tensor")
    copies = lax.axis_size("dp")
    rank = lax.axis_index("tensor")
    total_tokens = part_len * parts * copies
    seq_len = part_len * parts
    head_cols = w_query.shape[1]
    heads = head_cols // DH
    hidden_cols = w_inner.shape[1]
    hidden_width = hidden_cols * parts

    rows_in = inputs.reshape(part_len, width)
    tokens = lax.all_gather(rows_in, "tensor", axis=0, tiled=True)
    w_heads = lax.all_gather(interleave(w_query, w_key, w_value, heads), "dp", axis=0, tiled=True)
    mine = jnp.concatenate((w_inner, w_outer.T, w_output.T), axis=1)
    whole = lax.all_gather(mine, ("dp", "tensor"), axis=0, tiled=False)
    shard_rows = mine.shape[0]
    whole = whole.reshape(copies, parts, shard_rows, -1).transpose(0, 2, 1, 3)
    inner_full = whole[..., :hidden_cols].reshape(width, hidden_width)
    outer_full = whole[..., hidden_cols : 2 * hidden_cols].reshape(width, hidden_width)
    output_full = whole[..., 2 * hidden_cols :].reshape(width, width)

    valid_rows = valid_mask.astype(F32).reshape(part_len, 1)
    counted = lax.psum(jnp.sum(valid_rows), ("dp", "tensor"))

    mine_cols = rank * head_cols
    query_shift = lax.dynamic_slice_in_dim(query_bias, mine_cols, head_cols).astype(F32)
    value_shift = lax.dynamic_slice_in_dim(value_bias, mine_cols, head_cols).astype(F32)
    shifts = interleave(query_shift[None], jnp.zeros_like(query_shift)[None], value_shift[None], heads)
    qkv = (dot(tokens, w_heads) + shifts).astype(BF16)

    segment_row = segment_ids.reshape(seq_len)
    bounds = document_blocks(segment_row)
    seg_col = segment_row.reshape(seq_len, 1)
    seg_row = segment_row.reshape(1, seq_len)
    context, lse = run_forward(bounds, qkv, seg_col, seg_row)

    def to_tokens(by_head):
        moved = lax.all_to_all(by_head.reshape(parts, part_len, head_cols), "tensor", 0, 0)
        return moved.transpose(1, 0, 2).reshape(part_len, width)

    def to_heads(by_token):
        split = by_token.reshape(part_len, parts, head_cols).transpose(1, 0, 2)
        return lax.all_to_all(split, "tensor", 0, 0).reshape(seq_len, head_cols)

    context_rows = to_tokens(context)
    attention = dot(context_rows, output_full, NT)
    first_sum = rows_in.astype(F32) + attention + output_bias.astype(F32)
    gain_one = gain_attn.astype(F32)
    first_exact, normed_one, inverse_one = norm_forward(first_sum, gain_one, shift_attn.astype(F32))
    first = first_exact.astype(BF16)
    hidden = dot(first, inner_full) + inner_bias.astype(F32)
    bend = 0.5 * (1.0 + lax.erf(hidden * ROOT_HALF))
    activated = (hidden * bend).astype(BF16)
    slope = bend + hidden * INV_ROOT_TAU * jnp.exp(-0.5 * hidden * hidden)
    branch = dot(activated, outer_full, NT)
    second_sum = first.astype(F32) + branch + outer_bias.astype(F32)
    gain_two = gain_ffn.astype(F32)
    layer_rows, normed_two, inverse_two = norm_forward(second_sum, gain_two, shift_ffn.astype(F32))
    misfit = layer_rows - teacher.reshape(part_len, width).astype(F32)
    squared = jnp.sum(valid_rows * misfit * misfit)
    out_grad = cotangent.reshape(part_len, width).astype(F32) + valid_rows * misfit * (
        total_tokens / counted
    )
    second_grad, gain_ffn_grad, shift_ffn_grad = norm_backward(
        out_grad, normed_two, inverse_two, gain_two
    )
    branch_grad = second_grad.astype(BF16)
    outer_bias_grad = jnp.sum(branch_grad.astype(F32), axis=0)
    active_grad = dot(branch_grad, outer_full)
    hidden_grad = (active_grad * slope).astype(BF16)
    inner_bias_grad = jnp.sum(hidden_grad.astype(F32), axis=0)
    ffn_back = dot(hidden_grad, inner_full, NT)
    first_grad, gain_attn_grad, shift_attn_grad = norm_backward(
        second_grad + ffn_back, normed_one, inverse_one, gain_one
    )
    attn_grad = first_grad.astype(BF16)
    output_bias_grad = jnp.sum(attn_grad.astype(F32), axis=0)
    context_grad = dot(attn_grad, output_full).astype(BF16)
    head_grad = to_heads(context_grad)

    inner_weight = dot(first, hidden_grad, TN).astype(BF16).reshape(width, parts, hidden_cols)
    outer_weight = dot(branch_grad, activated, TN).astype(BF16).reshape(width, parts, hidden_cols)
    output_weight = dot(attn_grad, context_rows, TN).astype(BF16).reshape(width, parts, head_cols)
    packed = jnp.concatenate((inner_weight, outer_weight, output_weight), axis=2)
    packed = lax.psum_scatter(packed, "dp", scatter_dimension=0, tiled=True)
    packed = lax.psum_scatter(packed.transpose(1, 0, 2), "tensor", scatter_dimension=0, tiled=True)
    packed = packed.reshape(shard_rows, -1).astype(F32)

    joined_grad, sums = run_backward(bounds, qkv, seg_col, seg_row, context, head_grad, lse)
    attn_back = dot(joined_grad, w_heads, NT).astype(BF16)
    attn_back = lax.psum_scatter(attn_back, "tensor", scatter_dimension=0, tiled=True)
    input_grad = first_grad + attn_back.astype(F32)
    head_weights = dot(tokens, joined_grad, TN).astype(BF16)
    head_weights = lax.psum_scatter(head_weights, "dp", scatter_dimension=0, tiled=True)
    head_weights = head_weights.astype(F32).reshape(shard_rows, heads, 4, DH)

    def pick(which):
        return head_weights[:, :, which, :].reshape(shard_rows, head_cols)

    sums = sums.reshape(heads, 4, DH)
    totals = lax.psum(
        (
            squared,
            place_slice(sums[:, 0].reshape(head_cols), width, mine_cols),
            place_slice(sums[:, 3].reshape(head_cols), width, mine_cols),
            output_bias_grad,
            inner_bias_grad,
            outer_bias_grad,
            gain_attn_grad,
            shift_attn_grad,
            gain_ffn_grad,
            shift_ffn_grad,
        ),
        ("dp", "tensor"),
    )
    mse_loss = totals[0] / (counted * width)
    layer_out = layer_rows.astype(BF16).reshape(1, part_len, width)
    return (
        layer_out,
        mse_loss,
        input_grad.reshape(1, part_len, width),
        pick(0),
        pick(2),
        pick(3),
        packed[:, 2 * hidden_cols :].T,
        packed[:, :hidden_cols],
        packed[:, hidden_cols : 2 * hidden_cols].T,
    ) + tuple(totals[1:])


def solution(mesh):
    shard = P("dp", "tensor", None)
    in_specs = (
        (shard, P("dp", None), P("dp", "tensor"), shard, shard)
        + (P("dp", "tensor"),) * 3
        + (P("tensor", "dp"), P("dp", "tensor"), P("tensor", "dp"))
        + (P(),) * 9
    )
    out_specs = (
        (shard, P(), shard)
        + (P("dp", "tensor"),) * 3
        + (P("tensor", "dp"), P("dp", "tensor"), P("tensor", "dp"))
        + (P(),) * 9
    )
    return jax.shard_map(local, mesh=mesh, in_specs=in_specs, out_specs=out_specs, check_vma=False)
```

```python
import functools

import jax
import jax.numpy as jnp
from jax import lax
from jax.experimental import pallas as pl
from jax.experimental.pallas import tpu as pltpu
from jax.sharding import PartitionSpec as P

DH = 64
BLOCK = 256
SLAB = 4 * DH
EPSILON = 1e-12
ROOT_HALF = 0.7071067811865476
INV_ROOT_TAU = 0.3989422804014327
LOG2E = 1.4426950408889634
LN2 = 0.6931471805599453
SCALE = DH ** (-0.5)
MASKED = -1e30

BF16 = jnp.bfloat16
F32 = jnp.float32
NN = (((1,), (0,)), ((), ()))
NT = (((1,), (1,)), ((), ()))
TN = (((0,), (0,)), ((), ()))


def dot(left_side, right_side, dims=NN):
    return lax.dot_general(left_side, right_side, dims, preferred_element_type=F32)


def norm_forward(summed, gain_vec, shift_vec):
    average = jnp.mean(summed, axis=-1, keepdims=True)
    centered = summed - average
    variance = jnp.mean(centered * centered, axis=-1, keepdims=True)
    inverse = lax.rsqrt(variance + EPSILON)
    normed = centered * inverse
    return (normed * gain_vec + shift_vec, normed, inverse)


def norm_backward(upstream, normed, inverse, gain_vec):
    scaled = upstream * gain_vec
    first_mean = jnp.mean(scaled, axis=-1, keepdims=True)
    second_mean = jnp.mean(scaled * normed, axis=-1, keepdims=True)
    return inverse * (scaled - first_mean - normed * second_mean)


def column_sum(value):
    return jnp.sum(value, axis=0, keepdims=True)


def lane_is_right(rows):
    return lax.broadcasted_iota(jnp.int32, (rows, 2 * DH), 1) >= DH


def attend_forward(low_ref, high_ref, qkv_ref, seg_col_ref, seg_row_ref, ctx_ref, lse_ref, held):
    heads = lse_ref.shape[0]
    qb = pl.program_id(0)
    rows = pl.ds(pl.multiple_of(qb * BLOCK, BLOCK), BLOCK)
    seg_q = seg_col_ref[...]
    queries = [
        qkv_ref[rows, SLAB * h : SLAB * h + 2 * DH] * jnp.asarray(SCALE, BF16) for h in range(heads)
    ]
    low, high = low_ref[qb], high_ref[qb]

    def score(kb, peaks):
        keys = pl.ds(pl.multiple_of(kb * BLOCK, BLOCK), BLOCK)
        allowed = seg_q == seg_row_ref[:, keys]
        found = []
        for h in range(heads):
            scores = dot(queries[h], qkv_ref[keys, SLAB * h + 2 * DH : SLAB * (h + 1)], NT)
            scores = jnp.where(allowed, scores, MASKED)
            held[h, kb] = scores
            found.append(jnp.maximum(peaks[h], jnp.maximum(scores[:, :128], scores[:, 128:])))
        return tuple(found)

    start = tuple(jnp.full((BLOCK, 128), MASKED, F32) for _ in range(heads))
    peaks = lax.fori_loop(low, high, score, start)
    highest = [jnp.max(peak, axis=-1, keepdims=True) for peak in peaks]

    def weigh(kb, carry):
        keys = pl.ds(pl.multiple_of(kb * BLOCK, BLOCK), BLOCK)
        found = []
        for h in range(heads):
            total, acc = carry[h]
            raised = jnp.exp2((held[h, kb] - highest[h]) * LOG2E)
            total = total + (raised[:, :128] + raised[:, 128:])
            acc = acc + dot(raised.astype(BF16), qkv_ref[keys, SLAB * h + 2 * DH : SLAB * (h + 1)])
            found.append((total, acc))
        return tuple(found)

    zero = jnp.zeros((BLOCK, 128), F32)
    done = lax.fori_loop(low, high, weigh, tuple((zero, zero) for _ in range(heads)))
    right = lane_is_right(BLOCK)
    values = []
    for h in range(heads):
        total, acc = done[h]
        summed = jnp.sum(total, axis=-1, keepdims=True)
        values.append((acc / summed).astype(BF16))
        lse_ref[h] = jnp.transpose(highest[h] + jnp.log(summed))
    for h in range(0, heads, 2):
        moved = pltpu.roll(values[h], DH, 1)
        if h + 1 < heads:
            ctx_ref[:, DH * h : DH * (h + 2)] = jnp.where(right, values[h + 1], moved)
        else:
            ctx_ref[:, DH * h : DH * (h + 1)] = moved[:, :DH]


def attend_backward(
    low_ref, high_ref, qkv_ref, seg_col_ref, seg_row_ref, ctx_ref, grad_ref, lse_ref,
    out_ref, sums_ref, dkv
):
    heads = lse_ref.shape[0]
    qb = pl.program_id(0)

    @pl.when(qb == 0)
    def _():
        dkv[...] = jnp.zeros_like(dkv)
        sums_ref[...] = jnp.zeros_like(sums_ref)

    rows = pl.ds(pl.multiple_of(qb * BLOCK, BLOCK), BLOCK)
    right = lane_is_right(BLOCK)
    product = grad_ref[...].astype(F32) * ctx_ref[...].astype(F32)
    upper = product.astype(BF16)
    lower = (product - upper.astype(F32)).astype(BF16)
    width = heads * DH
    choose = (
        lax.broadcasted_iota(jnp.int32, (8, width), 1) // DH
        == lax.broadcasted_iota(jnp.int32, (8, width), 0)
    ).astype(BF16)
    deltas = dot(choose, upper, NT) + dot(choose, lower, NT)
    queries, grads, pairs = [], [], []
    for h in range(heads):
        queries.append(qkv_ref[rows, SLAB * h : SLAB * h + 2 * DH] * jnp.asarray(SCALE, BF16))
        tile = DH * (h - h % 2)
        if tile + 2 * DH <= width:
            grad = grad_ref[:, tile : tile + 2 * DH]
        else:
            grad = grad_ref[:, tile : tile + DH]
            grad = jnp.concatenate([grad, jnp.zeros_like(grad)], axis=1)
        if h % 2 == 0:
            grad = pltpu.roll(grad, DH, 1)
        grad = jnp.where(right, grad, jnp.zeros_like(grad))
        grads.append(grad)
        pairs.append(jnp.concatenate([queries[h], grad], axis=0))
    seg_q = seg_row_ref[...]
    lses = [lse_ref[h] for h in range(heads)]
    low, high = low_ref[qb], high_ref[qb]

    def step(kb, accs):
        keys = pl.ds(pl.multiple_of(kb * BLOCK, BLOCK), BLOCK)
        allowed = seg_col_ref[keys, :] == seg_q
        found = []
        for h in range(heads):
            pair = qkv_ref[keys, SLAB * h + 2 * DH : SLAB * (h + 1)]
            scores = jnp.where(allowed, dot(pair, queries[h], NT), MASKED)
            probs = jnp.exp2((scores - lses[h]) * LOG2E)
            score_grad = (probs * (dot(pair, grads[h], NT) - deltas[h : h + 1, :])).astype(BF16)
            both = jnp.concatenate([score_grad, probs.astype(BF16)], axis=1)
            dkv[h, keys, :] += dot(both, pairs[h])
            found.append(accs[h] + dot(score_grad, pair, TN))
        return tuple(found)

    zero = jnp.zeros((BLOCK, 128), F32)
    accs = lax.fori_loop(low, high, step, tuple(zero for _ in range(heads)))
    for h in range(heads):
        query_grad = jnp.where(right, 0.0, accs[h] * SCALE).astype(BF16)
        out_ref[rows, SLAB * h : SLAB * h + 2 * DH] = query_grad
        sums_ref[:, SLAB * h : SLAB * h + 2 * DH] += column_sum(query_grad.astype(F32))

    @pl.when(qb == pl.num_programs(0) - 1)
    def _():
        for h in range(heads):
            pair_grad = dkv[h].astype(BF16)
            out_ref[:, SLAB * h + 2 * DH : SLAB * (h + 1)] = pair_grad
            sums_ref[:, SLAB * h + 2 * DH : SLAB * (h + 1)] = column_sum(pair_grad.astype(F32))


def document_blocks(segment_row):
    starts = segment_row[::BLOCK]
    stops = segment_row[BLOCK - 1 :: BLOCK]
    low = jnp.sum((segment_row[None, :] < starts[:, None]).astype(jnp.int32), axis=1)
    high = jnp.sum((segment_row[None, :] <= stops[:, None]).astype(jnp.int32), axis=1)
    return (low // BLOCK, (high + BLOCK - 1) // BLOCK)


def run_forward(bounds, qkv, seg_col, seg_row):
    seq_len, width = qkv.shape
    heads = width // SLAB
    blocks = seq_len // BLOCK
    return pl.pallas_call(
        attend_forward,
        out_shape=(
            jax.ShapeDtypeStruct((seq_len, heads * DH), BF16),
            jax.ShapeDtypeStruct((heads, 1, seq_len), F32),
        ),
        grid_spec=pltpu.PrefetchScalarGridSpec(
            num_scalar_prefetch=2,
            grid=(blocks,),
            in_specs=[
                pl.BlockSpec((seq_len, width), lambda q, *_: (0, 0), pipeline_mode=pl.Buffered(1)),
                pl.BlockSpec((BLOCK, 1), lambda q, *_: (q, 0)),
                pl.BlockSpec((1, seq_len), lambda q, *_: (0, 0)),
            ],
            out_specs=(
                pl.BlockSpec((BLOCK, heads * DH), lambda q, *_: (q, 0)),
                pl.BlockSpec((heads, 1, BLOCK), lambda q, *_: (0, 0, q)),
            ),
            scratch_shapes=[pltpu.VMEM((heads, blocks, BLOCK, BLOCK), F32)],
        ),
        compiler_params=pltpu.CompilerParams(
            dimension_semantics=("arbitrary",), vmem_limit_bytes=40 << 20
        ),
        cost_estimate=pl.CostEstimate(
            flops=heads * seq_len * seq_len * 256,
            bytes_accessed=5 << 20,
            transcendentals=heads * seq_len * seq_len // 3,
        ),
        name="attend_forward",
    )(*bounds, qkv, seg_col, seg_row)


def run_backward(bounds, qkv, seg_col, seg_row, ctx, grad, lse):
    seq_len, width = qkv.shape
    heads = width // SLAB
    return pl.pallas_call(
        attend_backward,
        out_shape=(
            jax.ShapeDtypeStruct((seq_len, width), BF16),
            jax.ShapeDtypeStruct((1, width), F32),
        ),
        grid_spec=pltpu.PrefetchScalarGridSpec(
            num_scalar_prefetch=2,
            grid=(seq_len // BLOCK,),
            in_specs=[
                pl.BlockSpec((seq_len, width), lambda q, *_: (0, 0), pipeline_mode=pl.Buffered(1)),
                pl.BlockSpec((seq_len, 1), lambda q, *_: (0, 0)),
                pl.BlockSpec((1, BLOCK), lambda q, *_: (0, q)),
                pl.BlockSpec((BLOCK, heads * DH), lambda q, *_: (q, 0)),
                pl.BlockSpec((BLOCK, heads * DH), lambda q, *_: (q, 0)),
                pl.BlockSpec((heads, 1, BLOCK), lambda q, *_: (0, 0, q)),
            ],
            out_specs=(
                pl.BlockSpec((seq_len, width), lambda q, *_: (0, 0)),
                pl.BlockSpec((1, width), lambda q, *_: (0, 0)),
            ),
            scratch_shapes=[pltpu.VMEM((heads, seq_len, 2 * DH), F32)],
        ),
        compiler_params=pltpu.CompilerParams(
            dimension_semantics=("arbitrary",), vmem_limit_bytes=40 << 20
        ),
        cost_estimate=pl.CostEstimate(
            flops=heads * seq_len * seq_len * 640,
            bytes_accessed=10 << 20,
            transcendentals=heads * seq_len * seq_len // 3,
        ),
        name="attend_backward",
    )(*bounds, qkv, seg_col, seg_row, ctx, grad, lse)


ROWS = 256


def dense_chain(
    ratio_ref, ctx_ref, in_ref, teacher_ref, cotangent_ref, valid_ref, vec_ref, inner_bias_ref, w_ref,
    layer_ref, first_grad_ref, ctx_grad_ref, first_ref, branch_grad_ref, attn_grad_ref,
    act_ref, hidden_grad_ref, sums_ref, inner_sums_ref,
    w_out, w_in, w_up, slope, sems
):
    parts, _, head_cols = w_out.shape
    hidden_cols = w_in.shape[2]
    step = pl.program_id(0)

    def fetch(which, t):
        start, size, target = (
            (2 * hidden_cols, head_cols, w_out),
            (0, hidden_cols, w_in),
            (hidden_cols, hidden_cols, w_up),
        )[which]
        return pltpu.make_async_copy(
            w_ref.at[t, :, pl.ds(start, size)], target.at[t], sems.at[which, t]
        )

    @pl.when(step == 0)
    def _():
        for which in range(3):
            for t in range(parts):
                fetch(which, t).start()
        sums_ref[...] = jnp.zeros_like(sums_ref)
        inner_sums_ref[...] = jnp.zeros_like(inner_sums_ref)

    def arrive(which, t):
        @pl.when(step == 0)
        def _():
            fetch(which, t).wait()

    def vec(which):
        return vec_ref[which : which + 1, :]

    rows = in_ref.shape[0]
    width = in_ref.shape[1]
    zero = jnp.zeros((rows, width), F32)
    attention = zero
    for t in range(parts):
        arrive(0, t)
        attention = attention + dot(ctx_ref[t], w_out[t], NT)
    first_exact, normed_one, inverse_one = norm_forward(
        in_ref[...].astype(F32) + attention + vec(0), vec(1), vec(2)
    )
    first = first_exact.astype(BF16)
    first_ref[...] = first

    def up(t, branch):
        arrive(1, t)
        hidden = dot(first, w_in[t]) + inner_bias_ref[t]
        bend = 0.5 * (1.0 + lax.erf(hidden * ROOT_HALF))
        activated = (hidden * bend).astype(BF16)
        act_ref[t] = activated
        slope[t] = bend + hidden * INV_ROOT_TAU * jnp.exp2(hidden * hidden * (-0.5 * LOG2E))
        arrive(2, t)
        return branch + dot(activated, w_up[t], NT)

    branch = lax.fori_loop(0, parts, up, zero)
    layer_rows, normed_two, inverse_two = norm_forward(first.astype(F32) + branch + vec(3), vec(4), vec(5))
    layer_ref[...] = layer_rows.astype(BF16)
    misfit = layer_rows - teacher_ref[...].astype(F32)
    weighted = valid_ref[...] * misfit
    out_grad = cotangent_ref[...].astype(F32) + weighted * ratio_ref[0]
    second_grad = norm_backward(out_grad, normed_two, inverse_two, vec(4))
    branch_grad = second_grad.astype(BF16)
    branch_grad_ref[...] = branch_grad
    sums_ref[0:1, :] += column_sum(weighted * misfit)
    sums_ref[1:2, :] += column_sum(branch_grad.astype(F32))
    sums_ref[2:3, :] += column_sum(out_grad * normed_two)
    sums_ref[3:4, :] += column_sum(out_grad)

    def down(t, back):
        hidden_grad = (dot(branch_grad, w_up[t]) * slope[t]).astype(BF16)
        hidden_grad_ref[t] = hidden_grad
        inner_sums_ref[t] += column_sum(hidden_grad.astype(F32))
        return back + dot(hidden_grad, w_in[t], NT)

    upstream = lax.fori_loop(0, parts, down, second_grad)
    first_grad = norm_backward(upstream, normed_one, inverse_one, vec(1))
    first_grad_ref[...] = first_grad
    attn_grad = first_grad.astype(BF16)
    attn_grad_ref[...] = attn_grad
    sums_ref[4:5, :] += column_sum(attn_grad.astype(F32))
    sums_ref[5:6, :] += column_sum(upstream * normed_one)
    sums_ref[6:7, :] += column_sum(upstream)
    for t in range(parts):
        ctx_grad_ref[t] = dot(attn_grad, w_out[t]).astype(BF16)


def run_dense(ratio, ctx, rows_in, teacher, cotangent, valid, vecs, inner_bias, weights):
    parts, part_len, head_cols = ctx.shape
    width = rows_in.shape[1]
    hidden_cols = inner_bias.shape[2]

    def by_rows(columns):
        return pl.BlockSpec((ROWS, columns), lambda i: (i, 0))

    def by_part(columns):
        return pl.BlockSpec((parts, ROWS, columns), lambda i: (0, i, 0))

    def fixed(shape):
        return pl.BlockSpec(shape, lambda i: (0,) * len(shape))

    low = jax.ShapeDtypeStruct((part_len, width), BF16)
    return pl.pallas_call(
        dense_chain,
        out_shape=(
            low,
            jax.ShapeDtypeStruct((part_len, width), F32),
            jax.ShapeDtypeStruct((parts, part_len, head_cols), BF16),
            low,
            low,
            low,
            jax.ShapeDtypeStruct((parts, part_len, hidden_cols), BF16),
            jax.ShapeDtypeStruct((parts, part_len, hidden_cols), BF16),
            jax.ShapeDtypeStruct((8, width), F32),
            jax.ShapeDtypeStruct((parts, 1, hidden_cols), F32),
        ),
        grid=(part_len // ROWS,),
        in_specs=[
            pl.BlockSpec(memory_space=pltpu.SMEM),
            by_part(head_cols),
            by_rows(width),
            by_rows(width),
            by_rows(width),
            by_rows(1),
            fixed(vecs.shape),
            fixed(inner_bias.shape),
            pl.BlockSpec(memory_space=pl.ANY),
        ],
        out_specs=(
            by_rows(width),
            by_rows(width),
            by_part(head_cols),
            by_rows(width),
            by_rows(width),
            by_rows(width),
            by_part(hidden_cols),
            by_part(hidden_cols),
            fixed((8, width)),
            fixed((parts, 1, hidden_cols)),
        ),
        scratch_shapes=[
            pltpu.VMEM((parts, width, head_cols), BF16),
            pltpu.VMEM((parts, width, hidden_cols), BF16),
            pltpu.VMEM((parts, width, hidden_cols), BF16),
            pltpu.VMEM((parts, ROWS, hidden_cols), F32),
            pltpu.SemaphoreType.DMA((3, parts)),
        ],
        compiler_params=pltpu.CompilerParams(
            dimension_semantics=("arbitrary",), vmem_limit_bytes=56 << 20
        ),
        cost_estimate=pl.CostEstimate(
            flops=part_len * width * (8 * hidden_cols + 4 * head_cols) * parts,
            bytes_accessed=24 << 20,
            transcendentals=2 * part_len * hidden_cols * parts,
        ),
        name="dense_chain",
    )(ratio, ctx, rows_in, teacher, cotangent, valid, vecs, inner_bias, weights)


def dense_weights(
    first_ref, branch_grad_ref, attn_grad_ref, act_ref, hidden_grad_ref, ctx_ref, out_ref, turned
):
    @pl.when(pl.program_id(0) == 0)
    def _():
        turned[0] = jnp.transpose(first_ref[...])
        turned[1] = jnp.transpose(branch_grad_ref[...])
        turned[2] = jnp.transpose(attn_grad_ref[...])

    hidden_cols = act_ref.shape[2]
    out_ref[0, :, :hidden_cols] = dot(turned[0], hidden_grad_ref[0]).astype(BF16)
    out_ref[0, :, hidden_cols : 2 * hidden_cols] = dot(turned[1], act_ref[0]).astype(BF16)
    out_ref[0, :, 2 * hidden_cols :] = dot(turned[2], ctx_ref[0]).astype(BF16)


def run_weights(first, branch_grad, attn_grad, act, hidden_grad, ctx):
    parts, part_len, hidden_cols = act.shape
    head_cols = ctx.shape[2]
    width = first.shape[1]
    columns = 2 * hidden_cols + head_cols

    def by_part(size):
        return pl.BlockSpec((1, part_len, size), lambda t: (t, 0, 0))

    whole = pl.BlockSpec((part_len, width), lambda t: (0, 0))
    return pl.pallas_call(
        dense_weights,
        out_shape=jax.ShapeDtypeStruct((parts, width, columns), BF16),
        grid=(parts,),
        in_specs=[
            whole, whole, whole, by_part(hidden_cols), by_part(hidden_cols), by_part(head_cols)
        ],
        out_specs=pl.BlockSpec((1, width, columns), lambda t: (t, 0, 0)),
        scratch_shapes=[pltpu.VMEM((3, width, part_len), BF16)],
        compiler_params=pltpu.CompilerParams(
            dimension_semantics=("arbitrary",), vmem_limit_bytes=40 << 20
        ),
        cost_estimate=pl.CostEstimate(
            flops=2 * part_len * width * columns * parts, bytes_accessed=20 << 20, transcendentals=0
        ),
        name="dense_weights",
    )(first, branch_grad, attn_grad, act, hidden_grad, ctx)


def interleave(query, key, value, heads):
    rows = query.shape[0]
    parts = [part.reshape(rows, heads, 1, DH) for part in (query, jnp.zeros_like(query), key, value)]
    return jnp.concatenate(parts, axis=2).reshape(rows, heads * SLAB)


def place_slice(local_grad, full_size, offset):
    return lax.dynamic_update_slice_in_dim(jnp.zeros((full_size,), F32), local_grad, offset, 0)


def swap(value, axis, bit):
    size = lax.axis_size(axis)
    return lax.ppermute(value, axis, [(i, i ^ bit) for i in range(size)])


def bits_of(axis):
    bit = 1
    while bit < lax.axis_size(axis):
        yield bit
        bit *= 2


def sum_everywhere(value):
    for axis in ("dp", "tensor"):
        for bit in bits_of(axis):
            value = value + swap(value, axis, bit)
    return value


def gather_rows(shard):
    held = shard
    index = lax.axis_index("dp")
    for bit in bits_of("dp"):
        other = swap(held, "dp", bit)
        mine_first = (index & bit) == 0
        held = jnp.where(
            mine_first,
            jnp.concatenate([held, other], axis=0),
            jnp.concatenate([other, held], axis=0),
        )
    return held


def scatter_rows(value):
    copies = lax.axis_size("dp")
    index = lax.axis_index("dp")
    held = value.reshape((copies,) + (value.shape[0] // copies,) + value.shape[1:])
    for bit in bits_of("dp"):
        held = held.reshape((held.shape[0] // 2, 2) + held.shape[1:])
        own = (index & bit) // bit
        keep = lax.dynamic_index_in_dim(held, own, 1, keepdims=False)
        send = lax.dynamic_index_in_dim(held, 1 - own, 1, keepdims=False)
        came = swap(send, "dp", bit)
        held = (keep.astype(F32) + came.astype(F32)).astype(BF16)
    return held[0]


def local(
    inputs, segment_ids, valid_mask, teacher, cotangent,
    w_query, w_key, w_value, w_output, w_inner, w_outer,
    query_bias, value_bias, output_bias, inner_bias, outer_bias,
    gain_attn, shift_attn, gain_ffn, shift_ffn,
):
    _, part_len, width = inputs.shape
    parts = lax.axis_size("tensor")
    copies = lax.axis_size("dp")
    rank = lax.axis_index("tensor")
    total_tokens = part_len * parts * copies
    seq_len = part_len * parts
    head_cols = w_query.shape[1]
    heads = head_cols // DH
    hidden_cols = w_inner.shape[1]
    shard_rows = w_inner.shape[0]

    rows_in = inputs.reshape(part_len, width)
    tokens = lax.all_gather(rows_in, "tensor", axis=0, tiled=True)
    w_heads = gather_rows(interleave(w_query, w_key, w_value, heads))
    mine = jnp.concatenate((w_inner, w_outer.T, w_output.T), axis=1)
    mine, tokens_first = lax.optimization_barrier((mine, rows_in))
    weights = lax.all_gather(mine, ("tensor", "dp"), axis=0, tiled=False)
    weights = weights.reshape(parts, width, 2 * hidden_cols + head_cols)

    valid_rows = valid_mask.astype(F32).reshape(part_len, 1)
    counted = sum_everywhere(jnp.sum(valid_rows).reshape(1, 1))

    mine_cols = rank * head_cols
    query_shift = lax.dynamic_slice_in_dim(query_bias, mine_cols, head_cols).astype(F32)
    value_shift = lax.dynamic_slice_in_dim(value_bias, mine_cols, head_cols).astype(F32)
    shifts = interleave(query_shift[None], jnp.zeros_like(query_shift)[None], value_shift[None], heads)
    qkv = (dot(tokens, w_heads) + shifts).astype(BF16)

    segment_row = segment_ids.reshape(seq_len)
    bounds = document_blocks(segment_row)
    seg_col = segment_row.reshape(seq_len, 1)
    seg_row = segment_row.reshape(1, seq_len)
    context, lse = run_forward(bounds, qkv, seg_col, seg_row)
    context_parts = lax.all_to_all(context.reshape(parts, part_len, head_cols), "tensor", 0, 0)

    vecs = jnp.stack(
        (output_bias, gain_attn, shift_attn, outer_bias, gain_ffn, shift_ffn, outer_bias, outer_bias)
    ).astype(F32)
    ratio = (total_tokens / counted).reshape(1)
    (
        layer_out, first_grad, context_grad, first, branch_grad, attn_grad, activated, hidden_grad,
        dense_sums, inner_sums,
    ) = run_dense(
        ratio, context_parts, rows_in, teacher.reshape(part_len, width), cotangent.reshape(part_len, width),
        valid_rows, vecs, inner_bias.astype(F32).reshape(parts, 1, hidden_cols), weights,
    )
    head_grad = lax.all_to_all(context_grad, "tensor", 0, 0).reshape(seq_len, head_cols)
    packed = run_weights(first, branch_grad, attn_grad, activated, hidden_grad, context_parts)
    packed = lax.psum_scatter(packed, "dp", scatter_dimension=1, tiled=True)
    packed = lax.psum_scatter(packed, "tensor", scatter_dimension=0, tiled=True)
    packed = packed.reshape(shard_rows, -1).astype(F32)

    joined_grad, sums = run_backward(bounds, qkv, seg_col, seg_row, context, head_grad, lse)
    attn_back = dot(joined_grad, w_heads, NT).astype(BF16)
    attn_back = lax.psum_scatter(attn_back, "tensor", scatter_dimension=0, tiled=True)
    input_grad = first_grad + attn_back.astype(F32)
    head_weights = scatter_rows(dot(tokens, joined_grad, TN).astype(BF16))
    head_weights = head_weights.astype(F32).reshape(shard_rows, heads, 4, DH)

    def pick(which):
        return head_weights[:, :, which, :].reshape(shard_rows, head_cols)

    sums = sums.reshape(heads, 4, DH)
    totals = sum_everywhere(
        jnp.concatenate(
            (
                place_slice(sums[:, 0].reshape(head_cols), width, mine_cols),
                place_slice(sums[:, 3].reshape(head_cols), width, mine_cols),
                dense_sums.reshape(-1),
                inner_sums.reshape(-1),
            )
        ).reshape(-1, 128)
    ).reshape(-1)

    def total(which):
        return totals[which * width : (which + 1) * width]

    mse_loss = jnp.sum(total(2)) / (counted[0, 0] * width)
    return (
        layer_out.reshape(1, part_len, width),
        mse_loss,
        input_grad.reshape(1, part_len, width),
        pick(0),
        pick(2),
        pick(3),
        packed[:, 2 * hidden_cols :].T,
        packed[:, :hidden_cols],
        packed[:, hidden_cols : 2 * hidden_cols].T,
        total(0),
        total(1),
        total(6),
        totals[10 * width :],
        total(3),
        total(7),
        total(8),
        total(4),
        total(5),
    )


def solution(mesh):
    shard = P("dp", "tensor", None)
    in_specs = (
        (shard, P("dp", None), P("dp", "tensor"), shard, shard)
        + (P("dp", "tensor"),) * 3
        + (P("tensor", "dp"), P("dp", "tensor"), P("tensor", "dp"))
        + (P(),) * 9
    )
    out_specs = (
        (shard, P(), shard)
        + (P("dp", "tensor"),) * 3
        + (P("tensor", "dp"), P("dp", "tensor"), P("tensor", "dp"))
        + (P(),) * 9
    )
    return jax.shard_map(local, mesh=mesh, in_specs=in_specs, out_specs=out_specs, check_vma=False)
```

```python
import functools

import jax
import jax.numpy as jnp
from jax import lax
from jax.experimental import pallas as pl
from jax.experimental.pallas import tpu as pltpu
from jax.sharding import PartitionSpec as P

DH = 64
BLOCK = 256
SLAB = 4 * DH
EPSILON = 1e-12
ROOT_HALF = 0.7071067811865476
INV_ROOT_TAU = 0.3989422804014327
LOG2E = 1.4426950408889634
LN2 = 0.6931471805599453
SCALE = DH ** (-0.5)
MASKED = -1e30
VMEM_LIMIT = 60 << 20

BF16 = jnp.bfloat16
F32 = jnp.float32
NN = (((1,), (0,)), ((), ()))
NT = (((1,), (1,)), ((), ()))
TN = (((0,), (0,)), ((), ()))


def dot(left_side, right_side, dims=NN):
    return lax.dot_general(left_side, right_side, dims, preferred_element_type=F32)


def norm_forward(summed, gain_vec, shift_vec):
    average = jnp.mean(summed, axis=-1, keepdims=True)
    centered = summed - average
    variance = jnp.mean(centered * centered, axis=-1, keepdims=True)
    inverse = lax.rsqrt(variance + EPSILON)
    normed = centered * inverse
    return (normed * gain_vec + shift_vec, normed, inverse)


def norm_backward(upstream, normed, inverse, gain_vec):
    scaled = upstream * gain_vec
    first_mean = jnp.mean(scaled, axis=-1, keepdims=True)
    second_mean = jnp.mean(scaled * normed, axis=-1, keepdims=True)
    return inverse * (scaled - first_mean - normed * second_mean)


def column_sum(value):
    return jnp.sum(value, axis=0, keepdims=True)


def lane_is_right(rows):
    return lax.broadcasted_iota(jnp.int32, (rows, 2 * DH), 1) >= DH


def pack(first_two, third_top, third_bottom):
    return jnp.concatenate([first_two, jnp.concatenate([third_top, third_bottom], axis=1)], axis=0)


def unpack(packed):
    third = packed[BLOCK:]
    third = jnp.concatenate([third[:, :DH], third[:, DH:]], axis=0)
    return jnp.concatenate([packed[:BLOCK], third], axis=1)


def attend_forward(
    which, low_ref, high_ref, qkv_ref, seg_col_ref, seg_row_ref, ctx_ref, lse_ref, held
):
    halves, half = which
    heads = lse_ref.shape[0]
    qb = pl.program_id(0) * halves + half
    rows = pl.ds(pl.multiple_of(qb * BLOCK, BLOCK), BLOCK)
    seg_q = seg_col_ref[...]
    queries = [
        qkv_ref[rows, SLAB * h : SLAB * h + 2 * DH] * jnp.asarray(SCALE, BF16) for h in range(heads)
    ]
    low, high = low_ref[qb], high_ref[qb]

    def score(kb, peaks):
        keys = pl.ds(pl.multiple_of(kb * BLOCK, BLOCK), BLOCK)
        allowed = seg_q == seg_row_ref[:, keys]
        found = []
        for h in range(heads):
            scores = dot(queries[h], qkv_ref[keys, SLAB * h + 2 * DH : SLAB * (h + 1)], NT)
            scores = jnp.where(allowed, scores, MASKED)
            held[h, kb] = scores
            found.append(jnp.maximum(peaks[h], jnp.maximum(scores[:, :128], scores[:, 128:])))
        return tuple(found)

    start = tuple(jnp.full((BLOCK, 128), MASKED, F32) for _ in range(heads))
    peaks = lax.fori_loop(low, high, score, start)
    highest = [jnp.max(peak, axis=-1, keepdims=True) for peak in peaks]

    def weigh(kb, carry):
        keys = pl.ds(pl.multiple_of(kb * BLOCK, BLOCK), BLOCK)
        found = []
        for h in range(heads):
            total, acc = carry[h]
            raised = jnp.exp2((held[h, kb] - highest[h]) * LOG2E)
            total = total + (raised[:, :128] + raised[:, 128:])
            acc = acc + dot(raised.astype(BF16), qkv_ref[keys, SLAB * h + 2 * DH : SLAB * (h + 1)])
            found.append((total, acc))
        return tuple(found)

    zero = jnp.zeros((BLOCK, 128), F32)
    done = lax.fori_loop(low, high, weigh, tuple((zero, zero) for _ in range(heads)))
    values = []
    for h in range(heads):
        total, acc = done[h]
        summed = jnp.sum(total, axis=-1, keepdims=True)
        values.append((acc / summed).astype(BF16))
        lse_ref[h] = jnp.transpose(highest[h] + jnp.log(summed))
    middle = BLOCK // 2
    ctx_ref[0, :BLOCK, :] = jnp.where(lane_is_right(BLOCK), values[1], pltpu.roll(values[0], DH, 1))
    ctx_ref[0, BLOCK:, :] = jnp.where(
        lane_is_right(middle), values[2][middle:], pltpu.roll(values[2][:middle], DH, 1)
    )


def attend_backward(
    halves, low_ref, high_ref, qkv_ref, seg_col_ref, seg_row_ref, *refs
):
    ctx_refs, grad_refs, lse_refs = refs[:halves], refs[halves : 2 * halves], refs[2 * halves : 3 * halves]
    out_ref, sums_ref, dkv = refs[3 * halves :]
    heads = dkv.shape[0]
    qb = pl.program_id(0)
    half = qb % halves

    def choose(options):
        value = options[0][...]
        for which in range(1, halves):
            value = jnp.where(half == which, options[which][...], value)
        return value

    @pl.when(qb == 0)
    def _():
        dkv[...] = jnp.zeros_like(dkv)
        sums_ref[...] = jnp.zeros_like(sums_ref)

    rows = pl.ds(pl.multiple_of(qb * BLOCK, BLOCK), BLOCK)
    right = lane_is_right(BLOCK)
    arrived = choose(grad_refs)[0]
    product = arrived.astype(F32) * choose(ctx_refs)[0].astype(F32)
    upper = product.astype(BF16)
    lower = (product - upper.astype(F32)).astype(BF16)
    pick = (
        lax.broadcasted_iota(jnp.int32, (8, 2 * DH), 1) // DH
        == lax.broadcasted_iota(jnp.int32, (8, 2 * DH), 0)
    ).astype(BF16)
    summed = dot(pick, upper, NT) + dot(pick, lower, NT)
    deltas = [
        summed[0:1, :BLOCK],
        summed[1:2, :BLOCK],
        jnp.concatenate([summed[0:1, BLOCK:], summed[1:2, BLOCK:]], axis=1),
    ]
    two, third = arrived[:BLOCK], arrived[BLOCK:]
    placed = [
        pltpu.roll(two, DH, 1),
        two,
        jnp.concatenate([pltpu.roll(third, DH, 1), third], axis=0),
    ]
    grads = [jnp.where(right, grad, jnp.zeros_like(grad)) for grad in placed]
    queries, pairs = [], []
    for h in range(heads):
        queries.append(qkv_ref[rows, SLAB * h : SLAB * h + 2 * DH] * jnp.asarray(SCALE, BF16))
        pairs.append(jnp.concatenate([queries[h], grads[h]], axis=0))
    seg_q = seg_row_ref[...]
    lses = choose(lse_refs)
    low, high = low_ref[qb], high_ref[qb]

    def step(kb, accs):
        keys = pl.ds(pl.multiple_of(kb * BLOCK, BLOCK), BLOCK)
        allowed = seg_col_ref[keys, :] == seg_q
        found = []
        for h in range(heads):
            pair = qkv_ref[keys, SLAB * h + 2 * DH : SLAB * (h + 1)]
            scores = jnp.where(allowed, dot(pair, queries[h], NT), MASKED)
            probs = jnp.exp2((scores - lses[h]) * LOG2E)
            score_grad = (probs * (dot(pair, grads[h], NT) - deltas[h])).astype(BF16)
            both = jnp.concatenate([score_grad, probs.astype(BF16)], axis=1)
            dkv[h, keys, :] += dot(both, pairs[h])
            found.append(accs[h] + dot(score_grad, pair, TN))
        return tuple(found)

    zero = jnp.zeros((BLOCK, 128), F32)
    accs = lax.fori_loop(low, high, step, tuple(zero for _ in range(heads)))
    for h in range(heads):
        query_grad = jnp.where(right, 0.0, accs[h] * SCALE).astype(BF16)
        out_ref[rows, SLAB * h : SLAB * h + 2 * DH] = query_grad
        sums_ref[:, SLAB * h : SLAB * h + 2 * DH] += column_sum(query_grad.astype(F32))

    @pl.when(qb == pl.num_programs(0) - 1)
    def _():
        for h in range(heads):
            pair_grad = dkv[h].astype(BF16)
            out_ref[:, SLAB * h + 2 * DH : SLAB * (h + 1)] = pair_grad
            sums_ref[:, SLAB * h + 2 * DH : SLAB * (h + 1)] = column_sum(pair_grad.astype(F32))


def document_blocks(segment_row):
    starts = segment_row[::BLOCK]
    stops = segment_row[BLOCK - 1 :: BLOCK]
    low = jnp.sum((segment_row[None, :] < starts[:, None]).astype(jnp.int32), axis=1)
    high = jnp.sum((segment_row[None, :] <= stops[:, None]).astype(jnp.int32), axis=1)
    return (low // BLOCK, (high + BLOCK - 1) // BLOCK)


PACKED = BLOCK + BLOCK // 2


def run_forward(which, bounds, qkv, seg_col, seg_row):
    halves, half = which
    seq_len, width = qkv.shape
    heads = width // SLAB
    blocks = seq_len // BLOCK
    steps = blocks // halves
    return pl.pallas_call(
        functools.partial(attend_forward, which),
        out_shape=(
            jax.ShapeDtypeStruct((steps, PACKED, 2 * DH), BF16),
            jax.ShapeDtypeStruct((heads, 1, steps * BLOCK), F32),
        ),
        grid_spec=pltpu.PrefetchScalarGridSpec(
            num_scalar_prefetch=2,
            grid=(steps,),
            in_specs=[
                pl.BlockSpec((seq_len, width), lambda q, *_: (0, 0), pipeline_mode=pl.Buffered(1)),
                pl.BlockSpec((BLOCK, 1), lambda q, *_: (q * halves + half, 0)),
                pl.BlockSpec((1, seq_len), lambda q, *_: (0, 0)),
            ],
            out_specs=(
                pl.BlockSpec((1, PACKED, 2 * DH), lambda q, *_: (q, 0, 0)),
                pl.BlockSpec((heads, 1, BLOCK), lambda q, *_: (0, 0, q)),
            ),
            scratch_shapes=[pltpu.VMEM((heads, blocks, BLOCK, BLOCK), F32)],
        ),
        compiler_params=pltpu.CompilerParams(
            dimension_semantics=("arbitrary",), vmem_limit_bytes=VMEM_LIMIT
        ),
        cost_estimate=pl.CostEstimate(
            flops=heads * seq_len * seq_len * 256 // halves,
            bytes_accessed=5 << 20,
            transcendentals=heads * seq_len * seq_len // 3 // halves,
        ),
        name="attend_forward",
    )(*bounds, qkv, seg_col, seg_row)


def run_backward(bounds, qkv, seg_col, seg_row, ctxs, grads, lses):
    seq_len, width = qkv.shape
    heads = width // SLAB
    halves = len(ctxs)
    packed = pl.BlockSpec((1, PACKED, 2 * DH), lambda q, *_: (q // halves, 0, 0))
    return pl.pallas_call(
        functools.partial(attend_backward, halves),
        out_shape=(
            jax.ShapeDtypeStruct((seq_len, width), BF16),
            jax.ShapeDtypeStruct((1, width), F32),
        ),
        grid_spec=pltpu.PrefetchScalarGridSpec(
            num_scalar_prefetch=2,
            grid=(seq_len // BLOCK,),
            in_specs=[
                pl.BlockSpec((seq_len, width), lambda q, *_: (0, 0), pipeline_mode=pl.Buffered(1)),
                pl.BlockSpec((seq_len, 1), lambda q, *_: (0, 0)),
                pl.BlockSpec((1, BLOCK), lambda q, *_: (0, q)),
            ]
            + [packed] * (2 * halves)
            + [pl.BlockSpec((heads, 1, BLOCK), lambda q, *_: (0, 0, q // halves))] * halves,
            out_specs=(
                pl.BlockSpec((seq_len, width), lambda q, *_: (0, 0)),
                pl.BlockSpec((1, width), lambda q, *_: (0, 0)),
            ),
            scratch_shapes=[pltpu.VMEM((heads, seq_len, 2 * DH), F32)],
        ),
        compiler_params=pltpu.CompilerParams(
            dimension_semantics=("arbitrary",), vmem_limit_bytes=VMEM_LIMIT
        ),
        cost_estimate=pl.CostEstimate(
            flops=heads * seq_len * seq_len * 640,
            bytes_accessed=10 << 20,
            transcendentals=heads * seq_len * seq_len // 3,
        ),
        name="attend_backward",
    )(*bounds, qkv, seg_col, seg_row, *ctxs, *grads, *lses)


def dense_chain(
    marks, place_ref, ratio_ref, ctx_ref, in_ref, teacher_ref, cotangent_ref, valid_ref, vec_ref,
    inner_bias_ref, *refs
):
    pieces = refs[: len(marks)]
    (
        layer_ref, first_grad_ref, ctx_grad_ref, first_ref, branch_grad_ref, attn_grad_ref,
        act_ref, hidden_grad_ref, sums_ref, inner_sums_ref, w_out, w_in, w_up, slope, sems,
    ) = refs[len(marks) :]
    parts, _, head_cols = w_out.shape
    hidden_cols = w_in.shape[2]
    rank, index = place_ref[0], place_ref[1]
    groups = (
        (2 * hidden_cols, head_cols, w_out),
        (0, hidden_cols, w_in),
        (hidden_cols, hidden_cols, w_up),
    )
    for group, (start, size, target) in enumerate(groups):
        for piece, marked in zip(pieces, marks):
            block = piece.shape[1]
            for at, (slot, turn) in enumerate(marked):
                offset = pl.multiple_of((index ^ turn) * block, block)
                pltpu.make_async_copy(
                    piece.at[at, :, pl.ds(start, size)],
                    target.at[slot, pl.ds(offset, block), :],
                    sems.at[group, slot],
                ).start()

    def arrive(group, slot):
        whole = groups[group][2].at[slot]
        pltpu.make_async_copy(whole, whole, sems.at[group, slot]).wait()

    def vec(which):
        return vec_ref[which : which + 1, :]

    inner_sums_ref[...] = jnp.zeros_like(inner_sums_ref)
    attention = jnp.zeros(in_ref.shape, F32)
    for slot in range(parts):
        arrive(0, slot)
        attention = attention + dot(unpack(ctx_ref[rank ^ slot]), w_out[slot], NT)
    first_exact, normed_one, inverse_one = norm_forward(
        in_ref[...].astype(F32) + attention + vec(0), vec(1), vec(2)
    )
    first = first_exact.astype(BF16)
    first_ref[...] = first

    def up(slot, branch):
        t = rank ^ slot
        arrive(1, slot)
        hidden = dot(first, w_in[slot]) + inner_bias_ref[t]
        bend = 0.5 * (1.0 + lax.erf(hidden * ROOT_HALF))
        activated = (hidden * bend).astype(BF16)
        act_ref[t] = activated
        slope[slot] = bend + hidden * INV_ROOT_TAU * jnp.exp2(hidden * hidden * (-0.5 * LOG2E))
        arrive(2, slot)
        return branch + dot(activated, w_up[slot], NT)

    branch = lax.fori_loop(0, parts, up, jnp.zeros(in_ref.shape, F32))
    layer_rows, normed_two, inverse_two = norm_forward(first.astype(F32) + branch + vec(3), vec(4), vec(5))
    layer_ref[...] = layer_rows.astype(BF16)
    misfit = layer_rows - teacher_ref[...].astype(F32)
    weighted = valid_ref[...] * misfit
    out_grad = cotangent_ref[...].astype(F32) + weighted * ratio_ref[0]
    second_grad = norm_backward(out_grad, normed_two, inverse_two, vec(4))
    branch_grad = second_grad.astype(BF16)
    branch_grad_ref[...] = branch_grad
    sums_ref[0:1, :] = column_sum(weighted * misfit)
    sums_ref[1:2, :] = column_sum(branch_grad.astype(F32))
    sums_ref[2:3, :] = column_sum(out_grad * normed_two)
    sums_ref[3:4, :] = column_sum(out_grad)

    def down(slot, back):
        t = rank ^ slot
        hidden_grad = (dot(branch_grad, w_up[slot]) * slope[slot]).astype(BF16)
        hidden_grad_ref[t] = hidden_grad
        inner_sums_ref[t] = column_sum(hidden_grad.astype(F32))
        return back + dot(hidden_grad, w_in[slot], NT)

    upstream = lax.fori_loop(0, parts, down, second_grad)
    first_grad = norm_backward(upstream, normed_one, inverse_one, vec(1))
    first_grad_ref[...] = first_grad
    attn_grad = first_grad.astype(BF16)
    attn_grad_ref[...] = attn_grad
    sums_ref[4:5, :] = column_sum(attn_grad.astype(F32))
    sums_ref[5:6, :] = column_sum(upstream * normed_one)
    sums_ref[6:7, :] = column_sum(upstream)
    sums_ref[7:8, :] = jnp.zeros_like(sums_ref[7:8, :])
    middle = BLOCK // 2
    for slot in range(parts):
        back = dot(attn_grad, w_out[slot]).astype(BF16)
        ctx_grad_ref[rank ^ slot] = pack(
            back[:, : 2 * DH], back[:middle, 2 * DH :], back[middle:, 2 * DH :]
        )


def run_dense(half, marks, place, ratio, ctx, rows_in, teacher, cotangent, valid, vecs, inner_bias, pieces):
    parts = ctx.shape[0]
    width = rows_in.shape[1]
    hidden_cols = inner_bias.shape[2]
    head_cols = pieces[0].shape[2] - 2 * hidden_cols

    def mine(columns):
        return pl.BlockSpec((BLOCK, columns), lambda i: (half, 0))

    def fixed(shape):
        return pl.BlockSpec(shape, lambda i: (0,) * len(shape))

    low = jax.ShapeDtypeStruct((BLOCK, width), BF16)
    out_shape = (
        low,
        jax.ShapeDtypeStruct((BLOCK, width), F32),
        jax.ShapeDtypeStruct(ctx.shape, BF16),
        low,
        low,
        low,
        jax.ShapeDtypeStruct((parts, BLOCK, hidden_cols), BF16),
        jax.ShapeDtypeStruct((parts, BLOCK, hidden_cols), BF16),
        jax.ShapeDtypeStruct((8, width), F32),
        jax.ShapeDtypeStruct((parts, 1, hidden_cols), F32),
    )
    smem = pl.BlockSpec(memory_space=pltpu.SMEM)
    return pl.pallas_call(
        functools.partial(dense_chain, marks),
        out_shape=out_shape,
        grid=(1,),
        in_specs=[
            smem,
            smem,
            fixed(ctx.shape),
            mine(width),
            mine(width),
            mine(width),
            mine(1),
            fixed(vecs.shape),
            fixed(inner_bias.shape),
        ]
        + [pl.BlockSpec(memory_space=pl.ANY)] * len(pieces),
        out_specs=tuple(fixed(out.shape) for out in out_shape),
        scratch_shapes=[
            pltpu.VMEM((parts, width, head_cols), BF16),
            pltpu.VMEM((parts, width, hidden_cols), BF16),
            pltpu.VMEM((parts, width, hidden_cols), BF16),
            pltpu.VMEM((parts, BLOCK, hidden_cols), F32),
            pltpu.SemaphoreType.DMA((3, parts)),
        ],
        compiler_params=pltpu.CompilerParams(
            dimension_semantics=("arbitrary",), vmem_limit_bytes=VMEM_LIMIT
        ),
        cost_estimate=pl.CostEstimate(
            flops=BLOCK * width * (8 * hidden_cols + 4 * head_cols) * parts,
            bytes_accessed=18 << 20,
            transcendentals=2 * BLOCK * hidden_cols * parts,
        ),
        name="dense_chain",
    )(place, ratio, ctx, rows_in, teacher, cotangent, valid, vecs, inner_bias, *pieces)


def dense_weights(base, turns, halves, place_ref, *refs):
    firsts, branch_grads, attn_grads, acts, hidden_grads, ctxs = (
        refs[k * halves : (k + 1) * halves] for k in range(6)
    )
    outs = refs[6 * halves : 6 * halves + len(turns)]
    turned, whole, sems = refs[6 * halves + len(turns) :]
    step = pl.program_id(0)
    slots = pl.num_programs(0)

    @pl.when(step == 0)
    def _():
        for which, sources in enumerate((firsts, branch_grads, attn_grads)):
            for half, source in enumerate(sources):
                turned[which, :, half * BLOCK : (half + 1) * BLOCK] = jnp.transpose(source[...])

    def both(sources):
        return jnp.concatenate([source[0] for source in sources], axis=0)

    hidden_cols = acts[0].shape[2]
    whole[step, :, :hidden_cols] = dot(turned[0], both(hidden_grads)).astype(BF16)
    whole[step, :, hidden_cols : 2 * hidden_cols] = dot(turned[1], both(acts)).astype(BF16)
    ctx = jnp.concatenate([unpack(source[0]) for source in ctxs], axis=0)
    whole[step, :, 2 * hidden_cols :] = dot(turned[2], ctx).astype(BF16)
    for out, order in zip(outs, turns):
        block = out.shape[1]
        for at, turn in enumerate(order):
            offset = pl.multiple_of((place_ref[1] ^ turn) * block, block)
            pltpu.make_async_copy(
                whole.at[step, pl.ds(offset, block), :],
                out.at[at * slots + step],
                sems.at[step],
            ).start()

    @pl.when(step == slots - 1)
    def _():
        for slot in range(whole.shape[0]):
            pltpu.make_async_copy(whole.at[slot], whole.at[slot], sems.at[slot]).wait()


def run_weights(base, slots, turns, block, place, firsts, branch_grads, attn_grads, acts, hidden_grads, ctxs):
    parts, _, hidden_cols = acts[0].shape
    halves = len(acts)
    width = firsts[0].shape[1]
    columns = 2 * hidden_cols + 3 * DH

    def by_slot(rows, size):
        return pl.BlockSpec((1, rows, size), lambda s, place: (place[0] ^ (base + s), 0, 0))

    fixed = pl.BlockSpec((BLOCK, width), lambda s, place: (0, 0))
    return pl.pallas_call(
        functools.partial(dense_weights, base, turns, halves),
        out_shape=tuple(
            jax.ShapeDtypeStruct((len(order) * slots, block, columns), BF16) for order in turns
        ),
        grid_spec=pltpu.PrefetchScalarGridSpec(
            num_scalar_prefetch=1,
            grid=(slots,),
            in_specs=[fixed] * (3 * halves)
            + [by_slot(BLOCK, hidden_cols)] * (2 * halves)
            + [by_slot(PACKED, 2 * DH)] * halves,
            out_specs=tuple(pl.BlockSpec(memory_space=pl.ANY) for _ in turns),
            scratch_shapes=[
                pltpu.VMEM((3, width, halves * BLOCK), BF16),
                pltpu.VMEM((slots, width, columns), BF16),
                pltpu.SemaphoreType.DMA((slots,)),
            ],
        ),
        compiler_params=pltpu.CompilerParams(
            dimension_semantics=("arbitrary",), vmem_limit_bytes=VMEM_LIMIT
        ),
        cost_estimate=pl.CostEstimate(
            flops=2 * halves * BLOCK * width * columns * slots,
            bytes_accessed=5 * slots << 20,
            transcendentals=0,
        ),
        name="dense_weights",
    )(place, *firsts, *branch_grads, *attn_grads, *acts, *hidden_grads, *ctxs)


def interleave(query, key, value, heads):
    rows = query.shape[0]
    parts = [part.reshape(rows, heads, 1, DH) for part in (query, jnp.zeros_like(query), key, value)]
    return jnp.concatenate(parts, axis=2).reshape(rows, heads * SLAB)


def place_slice(local_grad, full_size, offset):
    return lax.dynamic_update_slice_in_dim(jnp.zeros((full_size,), F32), local_grad, offset, 0)


def swap(value, axis, bit):
    size = lax.axis_size(axis)
    return lax.ppermute(value, axis, [(i, i ^ bit) for i in range(size)])


def bits_of(axis):
    bit = 1
    while bit < lax.axis_size(axis):
        yield bit
        bit *= 2


def sum_everywhere(value):
    for axis in ("dp", "tensor"):
        for bit in bits_of(axis):
            value = value + swap(value, axis, bit)
    return value


def gather_rows(shard):
    held = shard
    index = lax.axis_index("dp")
    for bit in bits_of("dp"):
        other = swap(held, "dp", bit)
        mine_first = (index & bit) == 0
        held = jnp.where(
            mine_first,
            jnp.concatenate([held, other], axis=0),
            jnp.concatenate([other, held], axis=0),
        )
    return held


def scatter_rows(value):
    copies = lax.axis_size("dp")
    index = lax.axis_index("dp")
    held = value.reshape((copies,) + (value.shape[0] // copies,) + value.shape[1:])
    for bit in bits_of("dp"):
        held = held.reshape((held.shape[0] // 2, 2) + held.shape[1:])
        own = (index & bit) // bit
        keep = lax.dynamic_index_in_dim(held, own, 1, keepdims=False)
        send = lax.dynamic_index_in_dim(held, 1 - own, 1, keepdims=False)
        came = swap(send, "dp", bit)
        held = (keep.astype(F32) + came.astype(F32)).astype(BF16)
    return held[0]


def gather_pieces(shard):
    pair = jnp.concatenate([shard[None], swap(shard[None], "tensor", 1)], axis=0)
    far = swap(pair, "tensor", 2)
    bits = list(bits_of("dp"))
    pieces, marks = [], []
    for held, base in ((pair, 0), (far, 2)):
        marked = [(base, 0), (base + 1, 0)]
        for bit in bits[1:]:
            held = jnp.concatenate([held, swap(held, "dp", bit)], axis=0)
            marked = marked + [(slot, turn ^ bit) for slot, turn in marked]
        pieces += [held, swap(held, "dp", bits[0])]
        marks += [marked, [(slot, turn ^ bits[0]) for slot, turn in marked]]
    return (pieces, marks)


def add_low(left_side, right_side):
    return (left_side.astype(F32) + right_side.astype(F32)).astype(BF16)


def spread(order):
    turns = [0]
    for bit in reversed(order):
        turns = turns + [turn | bit for turn in turns]
    return turns


def add_halves(left_side, right_side):
    half = left_side.shape[0] // 2
    return (
        add_low(left_side[:half], right_side[:half]),
        add_low(left_side[half:], right_side[half:]),
    )


def local(
    inputs, segment_ids, valid_mask, teacher, cotangent,
    w_query, w_key, w_value, w_output, w_inner, w_outer,
    query_bias, value_bias, output_bias, inner_bias, outer_bias,
    gain_attn, shift_attn, gain_ffn, shift_ffn,
):
    _, part_len, width = inputs.shape
    parts = lax.axis_size("tensor")
    copies = lax.axis_size("dp")
    rank = lax.axis_index("tensor")
    total_tokens = part_len * parts * copies
    seq_len = part_len * parts
    head_cols = w_query.shape[1]
    heads = head_cols // DH
    hidden_cols = w_inner.shape[1]
    shard_rows = w_inner.shape[0]
    halves = part_len // BLOCK
    aligned = shard_rows % 16 == 0 and parts == 4 and copies >= 4

    rows_in = inputs.reshape(part_len, width)
    tokens = lax.all_gather(rows_in, "tensor", axis=0, tiled=True)
    w_heads = gather_rows(interleave(w_query, w_key, w_value, heads))
    mine = jnp.concatenate((w_inner, w_outer.T, w_output.T), axis=1)
    if aligned:
        place = jnp.stack([rank, lax.axis_index("dp")]).astype(jnp.int32)
        pieces, marks = gather_pieces(mine)
    else:
        place = jnp.zeros((2,), jnp.int32)
        weights = lax.all_gather(mine, ("tensor", "dp"), axis=0, tiled=False)
        pieces = [weights.reshape(parts, width, 2 * hidden_cols + head_cols)]
        marks = [[(t, 0) for t in range(parts)]]

    valid_rows = valid_mask.astype(F32).reshape(part_len, 1)
    counted = sum_everywhere(jnp.sum(valid_rows).reshape(1, 1))
    ratio = (total_tokens / counted).reshape(1)
    w_heads, ratio = lax.optimization_barrier((w_heads, ratio))

    mine_cols = rank * head_cols
    query_shift = lax.dynamic_slice_in_dim(query_bias, mine_cols, head_cols).astype(F32)
    value_shift = lax.dynamic_slice_in_dim(value_bias, mine_cols, head_cols).astype(F32)
    shifts = interleave(query_shift[None], jnp.zeros_like(query_shift)[None], value_shift[None], heads)
    qkv = (dot(tokens, w_heads) + shifts).astype(BF16)

    segment_row = segment_ids.reshape(seq_len)
    bounds = document_blocks(segment_row)
    seg_col = segment_row.reshape(seq_len, 1)
    seg_row = segment_row.reshape(1, seq_len)

    def exchange(blocks):
        return lax.all_to_all(blocks, "tensor", 0, 0)

    contexts, lses, arrived = [], [], []
    for half in range(halves):
        context, lse = run_forward((halves, half), bounds, qkv, seg_col, seg_row)
        contexts.append(context)
        lses.append(lse)
        arrived.append(exchange(context))

    vecs = jnp.stack(
        (output_bias, gain_attn, shift_attn, outer_bias, gain_ffn, shift_ffn, outer_bias, outer_bias)
    ).astype(F32)
    inner_rows = inner_bias.astype(F32).reshape(parts, 1, hidden_cols)
    teacher_rows = teacher.reshape(part_len, width)
    cotangent_rows = cotangent.reshape(part_len, width)
    chains = [
        run_dense(
            half, marks, place, ratio, arrived[half], rows_in, teacher_rows, cotangent_rows,
            valid_rows, vecs, inner_rows, pieces,
        )
        for half in range(halves)
    ]
    (
        layers, first_grads, context_grads, firsts, branch_grads, attn_grads, acts, hidden_grads,
        dense_sums, inner_sums,
    ) = zip(*chains)
    head_grads = [exchange(context_grad) for context_grad in context_grads]
    dense_sums = sum(dense_sums)
    inner_sums = sum(inner_sums)
    sources = (firsts, branch_grads, attn_grads, acts, hidden_grads, arrived)
    head_grads[:-1], sources = lax.optimization_barrier((head_grads[:-1], sources))
    if aligned:
        rest = list(bits_of("dp"))[1:]
        orders = (rest, rest[::-1])
        begun = []
        for which, order in enumerate(orders):
            turns = spread(order)
            keep, send = run_weights(
                2 * which, 2, (turns, [turn | 1 for turn in turns]), shard_rows, place, *sources
            )
            if which == 1:
                head_grads[-1], keep, send = lax.optimization_barrier((head_grads[-1], keep, send))
            shape = (copies // 2, 2) + keep.shape[1:]
            begun.append(add_halves(keep.reshape(shape), swap(send.reshape(shape), "dp", 1)))
        head_grads[-1], begun = lax.optimization_barrier((head_grads[-1], begun))
        moving = [(keep, swap(send, "dp", order[0])) for (keep, send), order in zip(begun, orders)]
    else:
        (packed,) = run_weights(0, parts, ([0],), width, place, *sources)
        packed = lax.psum_scatter(packed, "dp", scatter_dimension=1, tiled=True)
        packed = lax.psum_scatter(packed, "tensor", scatter_dimension=0, tiled=True)
        packed = packed.reshape(shard_rows, -1).astype(F32)

    joined_grad, sums = run_backward(bounds, qkv, seg_col, seg_row, contexts, head_grads, lses)
    if aligned:
        joined_grad, moving = lax.optimization_barrier((joined_grad, moving))
        reduced = []
        for (keep, came), order in zip(moving, orders):
            for bit in order[1:]:
                keep, send = add_halves(keep, came)
                came = swap(send, "dp", bit)
            held = add_low(keep, came)
            reduced.append(held[0])
        near = add_low(reduced[0], swap(reduced[1], "tensor", 2))
        packed = near[0].astype(F32) + swap(near[1], "tensor", 1).astype(F32)
    attn_back = dot(joined_grad, w_heads, NT).astype(BF16)
    attn_back, sums = lax.optimization_barrier((attn_back, sums))
    attn_back = lax.psum_scatter(attn_back, "tensor", scatter_dimension=0, tiled=True)
    input_grad = jnp.concatenate(first_grads, axis=0) + attn_back.astype(F32)
    head_weights = scatter_rows(dot(tokens, joined_grad, TN).astype(BF16))
    head_weights = head_weights.astype(F32).reshape(shard_rows, heads, 4, DH)

    def pick(which):
        return head_weights[:, :, which, :].reshape(shard_rows, head_cols)

    sums = sums.reshape(heads, 4, DH)
    totals = sum_everywhere(
        jnp.concatenate(
            (
                place_slice(sums[:, 0].reshape(head_cols), width, mine_cols),
                place_slice(sums[:, 3].reshape(head_cols), width, mine_cols),
                dense_sums.reshape(-1),
                inner_sums.reshape(-1),
            )
        ).reshape(-1, 128)
    ).reshape(-1)

    def total(which):
        return totals[which * width : (which + 1) * width]

    mse_loss = jnp.sum(total(2)) / (counted[0, 0] * width)
    return (
        jnp.concatenate(layers, axis=0).reshape(1, part_len, width),
        mse_loss,
        input_grad.reshape(1, part_len, width),
        pick(0),
        pick(2),
        pick(3),
        packed[:, 2 * hidden_cols :].T,
        packed[:, :hidden_cols],
        packed[:, hidden_cols : 2 * hidden_cols].T,
        total(0),
        total(1),
        total(6),
        totals[10 * width :],
        total(3),
        total(7),
        total(8),
        total(4),
        total(5),
    )


def solution(mesh):
    shard = P("dp", "tensor", None)
    in_specs = (
        (shard, P("dp", None), P("dp", "tensor"), shard, shard)
        + (P("dp", "tensor"),) * 3
        + (P("tensor", "dp"), P("dp", "tensor"), P("tensor", "dp"))
        + (P(),) * 9
    )
    out_specs = (
        (shard, P(), shard)
        + (P("dp", "tensor"),) * 3
        + (P("tensor", "dp"), P("dp", "tensor"), P("tensor", "dp"))
        + (P(),) * 9
    )
    return jax.shard_map(local, mesh=mesh, in_specs=in_specs, out_specs=out_specs, check_vma=False)
```

```python
import functools

import jax
import jax.numpy as jnp
from jax import lax
from jax.experimental import pallas as pl
from jax.experimental.pallas import tpu as pltpu
from jax.sharding import PartitionSpec as P

DH = 64
BLOCK = 256
SLAB = 4 * DH
EPSILON = 1e-12
ROOT_HALF = 0.7071067811865476
INV_ROOT_TAU = 0.3989422804014327
LOG2E = 1.4426950408889634
LN2 = 0.6931471805599453
SCALE = DH ** (-0.5)
MASKED = -1e30
VMEM_LIMIT = 60 << 20

BF16 = jnp.bfloat16
F32 = jnp.float32
NN = (((1,), (0,)), ((), ()))
NT = (((1,), (1,)), ((), ()))
TN = (((0,), (0,)), ((), ()))


def dot(left_side, right_side, dims=NN):
    return lax.dot_general(left_side, right_side, dims, preferred_element_type=F32)


def norm_forward(summed, gain_vec, shift_vec):
    average = jnp.mean(summed, axis=-1, keepdims=True)
    centered = summed - average
    variance = jnp.mean(centered * centered, axis=-1, keepdims=True)
    inverse = lax.rsqrt(variance + EPSILON)
    normed = centered * inverse
    return (normed * gain_vec + shift_vec, normed, inverse)


def norm_backward(upstream, normed, inverse, gain_vec):
    scaled = upstream * gain_vec
    first_mean = jnp.mean(scaled, axis=-1, keepdims=True)
    second_mean = jnp.mean(scaled * normed, axis=-1, keepdims=True)
    return inverse * (scaled - first_mean - normed * second_mean)


def column_sum(value):
    return jnp.sum(value, axis=0, keepdims=True)


def lane_is_right(rows):
    return lax.broadcasted_iota(jnp.int32, (rows, 2 * DH), 1) >= DH


def pack(first_two, third_top, third_bottom):
    return jnp.concatenate([first_two, jnp.concatenate([third_top, third_bottom], axis=1)], axis=0)


def unpack(packed):
    third = packed[BLOCK:]
    third = jnp.concatenate([third[:, :DH], third[:, DH:]], axis=0)
    return jnp.concatenate([packed[:BLOCK], third], axis=1)


def attend_forward(
    which, low_ref, high_ref, qkv_ref, seg_col_ref, seg_row_ref, ctx_ref, lse_ref, held
):
    halves, half = which
    heads = lse_ref.shape[0]
    qb = pl.program_id(0) * halves + half
    rows = pl.ds(pl.multiple_of(qb * BLOCK, BLOCK), BLOCK)
    seg_q = seg_col_ref[...]
    queries = [
        qkv_ref[rows, SLAB * h : SLAB * h + 2 * DH] * jnp.asarray(SCALE, BF16) for h in range(heads)
    ]
    low, high = low_ref[qb], high_ref[qb]

    def score(kb, peaks):
        keys = pl.ds(pl.multiple_of(kb * BLOCK, BLOCK), BLOCK)
        allowed = seg_q == seg_row_ref[:, keys]
        found = []
        for h in range(heads):
            scores = dot(queries[h], qkv_ref[keys, SLAB * h + 2 * DH : SLAB * (h + 1)], NT)
            scores = jnp.where(allowed, scores, MASKED)
            held[h, kb] = scores
            found.append(jnp.maximum(peaks[h], jnp.maximum(scores[:, :128], scores[:, 128:])))
        return tuple(found)

    start = tuple(jnp.full((BLOCK, 128), MASKED, F32) for _ in range(heads))
    peaks = lax.fori_loop(low, high, score, start)
    highest = [jnp.max(peak, axis=-1, keepdims=True) for peak in peaks]

    def weigh(kb, carry):
        keys = pl.ds(pl.multiple_of(kb * BLOCK, BLOCK), BLOCK)
        found = []
        for h in range(heads):
            total, acc = carry[h]
            raised = jnp.exp2((held[h, kb] - highest[h]) * LOG2E)
            total = total + (raised[:, :128] + raised[:, 128:])
            acc = acc + dot(raised.astype(BF16), qkv_ref[keys, SLAB * h + 2 * DH : SLAB * (h + 1)])
            found.append((total, acc))
        return tuple(found)

    zero = jnp.zeros((BLOCK, 128), F32)
    done = lax.fori_loop(low, high, weigh, tuple((zero, zero) for _ in range(heads)))
    values = []
    for h in range(heads):
        total, acc = done[h]
        summed = jnp.sum(total, axis=-1, keepdims=True)
        values.append((acc / summed).astype(BF16))
        lse_ref[h] = jnp.transpose(highest[h] + jnp.log(summed))
    middle = BLOCK // 2
    ctx_ref[0, :BLOCK, :] = jnp.where(lane_is_right(BLOCK), values[1], pltpu.roll(values[0], DH, 1))
    ctx_ref[0, BLOCK:, :] = jnp.where(
        lane_is_right(middle), values[2][middle:], pltpu.roll(values[2][:middle], DH, 1)
    )


def attend_backward(
    which, low_ref, high_ref, qkv_ref, seg_col_ref, seg_row_ref, ctx_ref, grad_ref, lse_ref, *refs
):
    halves, half = which
    last = half == halves - 1
    earlier, refs = refs[:half], refs[half:]
    if half > 0:
        before_ref, refs = refs[0], refs[1:]
    if last:
        out_ref, sums_ref, dkv = refs
    else:
        dkv, query_ref = refs
    heads = dkv.shape[0]
    step_index = pl.program_id(0)
    qb = step_index * halves + half

    @pl.when(step_index == 0)
    def _():
        dkv[...] = before_ref[...] if half > 0 else jnp.zeros_like(dkv)

    rows = pl.ds(pl.multiple_of(qb * BLOCK, BLOCK), BLOCK)
    right = lane_is_right(BLOCK)
    arrived = grad_ref[0]
    product = arrived.astype(F32) * ctx_ref[0].astype(F32)
    upper = product.astype(BF16)
    lower = (product - upper.astype(F32)).astype(BF16)
    pick = (
        lax.broadcasted_iota(jnp.int32, (8, 2 * DH), 1) // DH
        == lax.broadcasted_iota(jnp.int32, (8, 2 * DH), 0)
    ).astype(BF16)
    summed = dot(pick, upper, NT) + dot(pick, lower, NT)
    deltas = [
        summed[0:1, :BLOCK],
        summed[1:2, :BLOCK],
        jnp.concatenate([summed[0:1, BLOCK:], summed[1:2, BLOCK:]], axis=1),
    ]
    two, third = arrived[:BLOCK], arrived[BLOCK:]
    placed = [
        pltpu.roll(two, DH, 1),
        two,
        jnp.concatenate([pltpu.roll(third, DH, 1), third], axis=0),
    ]
    grads = [jnp.where(right, grad, jnp.zeros_like(grad)) for grad in placed]
    queries, pairs = [], []
    for h in range(heads):
        queries.append(qkv_ref[rows, SLAB * h : SLAB * h + 2 * DH] * jnp.asarray(SCALE, BF16))
        pairs.append(jnp.concatenate([queries[h], grads[h]], axis=0))
    seg_q = seg_row_ref[...]
    lses = lse_ref[...]
    low, high = low_ref[qb], high_ref[qb]

    def step(kb, accs):
        keys = pl.ds(pl.multiple_of(kb * BLOCK, BLOCK), BLOCK)
        allowed = seg_col_ref[keys, :] == seg_q
        found = []
        for h in range(heads):
            pair = qkv_ref[keys, SLAB * h + 2 * DH : SLAB * (h + 1)]
            scores = jnp.where(allowed, dot(pair, queries[h], NT), MASKED)
            probs = jnp.exp2((scores - lses[h]) * LOG2E)
            score_grad = (probs * (dot(pair, grads[h], NT) - deltas[h])).astype(BF16)
            both = jnp.concatenate([score_grad, probs.astype(BF16)], axis=1)
            dkv[h, keys, :] += dot(both, pairs[h])
            found.append(accs[h] + dot(score_grad, pair, TN))
        return tuple(found)

    zero = jnp.zeros((BLOCK, 128), F32)
    accs = lax.fori_loop(low, high, step, tuple(zero for _ in range(heads)))
    for h in range(heads):
        query_grad = jnp.where(right, 0.0, accs[h] * SCALE).astype(BF16)
        if last:
            out_ref[rows, SLAB * h : SLAB * h + 2 * DH] = query_grad
        else:
            query_ref[0, :, 2 * DH * h : 2 * DH * (h + 1)] = query_grad

    if last:

        @pl.when(step_index == pl.num_programs(0) - 1)
        def _():
            for h in range(heads):
                at = SLAB * h
                for other, ref in enumerate(earlier):
                    for block in range(ref.shape[0]):
                        start = (block * halves + other) * BLOCK
                        out_ref[start : start + BLOCK, at : at + 2 * DH] = ref[
                            block, :, 2 * DH * h : 2 * DH * (h + 1)
                        ]
                out_ref[:, at + 2 * DH : at + SLAB] = dkv[h].astype(BF16)
                sums_ref[:, at : at + SLAB] = column_sum(out_ref[:, at : at + SLAB].astype(F32))


def document_blocks(segment_row):
    starts = segment_row[::BLOCK]
    stops = segment_row[BLOCK - 1 :: BLOCK]
    low = jnp.sum((segment_row[None, :] < starts[:, None]).astype(jnp.int32), axis=1)
    high = jnp.sum((segment_row[None, :] <= stops[:, None]).astype(jnp.int32), axis=1)
    return (low // BLOCK, (high + BLOCK - 1) // BLOCK)


PACKED = BLOCK + BLOCK // 2


def run_forward(which, bounds, qkv, seg_col, seg_row):
    halves, half = which
    seq_len, width = qkv.shape
    heads = width // SLAB
    blocks = seq_len // BLOCK
    steps = blocks // halves
    return pl.pallas_call(
        functools.partial(attend_forward, which),
        out_shape=(
            jax.ShapeDtypeStruct((steps, PACKED, 2 * DH), BF16),
            jax.ShapeDtypeStruct((heads, 1, steps * BLOCK), F32),
        ),
        grid_spec=pltpu.PrefetchScalarGridSpec(
            num_scalar_prefetch=2,
            grid=(steps,),
            in_specs=[
                pl.BlockSpec((seq_len, width), lambda q, *_: (0, 0), pipeline_mode=pl.Buffered(1)),
                pl.BlockSpec((BLOCK, 1), lambda q, *_: (q * halves + half, 0)),
                pl.BlockSpec((1, seq_len), lambda q, *_: (0, 0)),
            ],
            out_specs=(
                pl.BlockSpec((1, PACKED, 2 * DH), lambda q, *_: (q, 0, 0)),
                pl.BlockSpec((heads, 1, BLOCK), lambda q, *_: (0, 0, q)),
            ),
            scratch_shapes=[pltpu.VMEM((heads, blocks, BLOCK, BLOCK), F32)],
        ),
        compiler_params=pltpu.CompilerParams(
            dimension_semantics=("arbitrary",), vmem_limit_bytes=VMEM_LIMIT
        ),
        cost_estimate=pl.CostEstimate(
            flops=heads * seq_len * seq_len * 256 // halves,
            bytes_accessed=5 << 20,
            transcendentals=heads * seq_len * seq_len // 3 // halves,
        ),
        name="attend_forward",
    )(*bounds, qkv, seg_col, seg_row)


def run_backward(which, bounds, qkv, seg_col, seg_row, ctx, grad, lse, earlier, before):
    halves, half = which
    seq_len, width = qkv.shape
    heads = width // SLAB
    steps = seq_len // BLOCK // halves
    packed = pl.BlockSpec((1, PACKED, 2 * DH), lambda q, *_: (q, 0, 0))

    def fixed(shape, **more):
        return pl.BlockSpec(shape, lambda q, *_: (0,) * len(shape), **more)

    once = {"pipeline_mode": pl.Buffered(1)}
    gathered = (heads, seq_len, 2 * DH)
    carried = [fixed(value.shape, **once) for value in earlier]
    carried += [fixed(gathered, **once)] * len(before)
    if half == halves - 1:
        out_shape = (
            jax.ShapeDtypeStruct((seq_len, width), BF16),
            jax.ShapeDtypeStruct((1, width), F32),
        )
        out_specs = (fixed((seq_len, width)), fixed((1, width)))
        scratch = [pltpu.VMEM(gathered, F32)]
    else:
        out_shape = (
            jax.ShapeDtypeStruct(gathered, F32),
            jax.ShapeDtypeStruct((steps, BLOCK, heads * 2 * DH), BF16),
        )
        out_specs = (
            fixed(gathered),
            pl.BlockSpec((1, BLOCK, heads * 2 * DH), lambda q, *_: (q, 0, 0)),
        )
        scratch = []
    return pl.pallas_call(
        functools.partial(attend_backward, which),
        out_shape=out_shape,
        grid_spec=pltpu.PrefetchScalarGridSpec(
            num_scalar_prefetch=2,
            grid=(steps,),
            in_specs=[
                fixed((seq_len, width), **once),
                fixed((seq_len, 1)),
                pl.BlockSpec((1, BLOCK), lambda q, *_: (0, q * halves + half)),
                packed,
                packed,
                pl.BlockSpec((heads, 1, BLOCK), lambda q, *_: (0, 0, q)),
            ]
            + carried,
            out_specs=out_specs,
            scratch_shapes=scratch,
        ),
        compiler_params=pltpu.CompilerParams(
            dimension_semantics=("arbitrary",), vmem_limit_bytes=VMEM_LIMIT
        ),
        cost_estimate=pl.CostEstimate(
            flops=heads * seq_len * seq_len * 640 // halves,
            bytes_accessed=10 << 20,
            transcendentals=heads * seq_len * seq_len // 3 // halves,
        ),
        name="attend_backward",
    )(*bounds, qkv, seg_col, seg_row, ctx, grad, lse, *earlier, *before)


def dense_chain(
    marks, place_ref, ratio_ref, ctx_ref, in_ref, teacher_ref, cotangent_ref, valid_ref, vec_ref,
    inner_bias_ref, *refs
):
    pieces = refs[: len(marks)]
    (
        layer_ref, first_grad_ref, ctx_grad_ref, first_ref, branch_grad_ref, attn_grad_ref,
        act_ref, hidden_grad_ref, sums_ref, inner_sums_ref, w_out, w_in, w_up, slope, sems,
    ) = refs[len(marks) :]
    parts, _, head_cols = w_out.shape
    hidden_cols = w_in.shape[2]
    index = place_ref[parts]
    groups = (
        (2 * hidden_cols, head_cols, w_out),
        (0, hidden_cols, w_in),
        (hidden_cols, hidden_cols, w_up),
    )
    for group, (start, size, target) in enumerate(groups):
        for piece, marked in zip(pieces, marks):
            block = piece.shape[1]
            for at, (slot, turn) in enumerate(marked):
                offset = pl.multiple_of((index ^ turn) * block, block)
                pltpu.make_async_copy(
                    piece.at[at, :, pl.ds(start, size)],
                    target.at[slot, pl.ds(offset, block), :],
                    sems.at[group, slot],
                ).start()

    def arrive(group, slot):
        whole = groups[group][2].at[slot]
        pltpu.make_async_copy(whole, whole, sems.at[group, slot]).wait()

    def vec(which):
        return vec_ref[which : which + 1, :]

    inner_sums_ref[...] = jnp.zeros_like(inner_sums_ref)
    attention = jnp.zeros(in_ref.shape, F32)
    for slot in range(parts):
        arrive(0, slot)
        attention = attention + dot(unpack(ctx_ref[place_ref[slot]]), w_out[slot], NT)
    first_exact, normed_one, inverse_one = norm_forward(
        in_ref[...].astype(F32) + attention + vec(0), vec(1), vec(2)
    )
    first = first_exact.astype(BF16)
    first_ref[...] = first

    def up(slot, branch):
        t = place_ref[slot]
        arrive(1, slot)
        hidden = dot(first, w_in[slot]) + inner_bias_ref[t]
        bend = 0.5 * (1.0 + lax.erf(hidden * ROOT_HALF))
        activated = (hidden * bend).astype(BF16)
        act_ref[t] = activated
        slope[slot] = bend + hidden * INV_ROOT_TAU * jnp.exp2(hidden * hidden * (-0.5 * LOG2E))
        arrive(2, slot)
        return branch + dot(activated, w_up[slot], NT)

    branch = lax.fori_loop(0, parts, up, jnp.zeros(in_ref.shape, F32))
    layer_rows, normed_two, inverse_two = norm_forward(first.astype(F32) + branch + vec(3), vec(4), vec(5))
    layer_ref[...] = layer_rows.astype(BF16)
    misfit = layer_rows - teacher_ref[...].astype(F32)
    weighted = valid_ref[...] * misfit
    out_grad = cotangent_ref[...].astype(F32) + weighted * ratio_ref[0]
    second_grad = norm_backward(out_grad, normed_two, inverse_two, vec(4))
    branch_grad = second_grad.astype(BF16)
    branch_grad_ref[...] = branch_grad
    sums_ref[0:1, :] = column_sum(weighted * misfit)
    sums_ref[1:2, :] = column_sum(branch_grad.astype(F32))
    sums_ref[2:3, :] = column_sum(out_grad * normed_two)
    sums_ref[3:4, :] = column_sum(out_grad)

    def down(slot, back):
        t = place_ref[slot]
        hidden_grad = (dot(branch_grad, w_up[slot]) * slope[slot]).astype(BF16)
        hidden_grad_ref[t] = hidden_grad
        inner_sums_ref[t] = column_sum(hidden_grad.astype(F32))
        return back + dot(hidden_grad, w_in[slot], NT)

    upstream = lax.fori_loop(0, parts, down, second_grad)
    first_grad = norm_backward(upstream, normed_one, inverse_one, vec(1))
    first_grad_ref[...] = first_grad
    attn_grad = first_grad.astype(BF16)
    attn_grad_ref[...] = attn_grad
    sums_ref[4:5, :] = column_sum(attn_grad.astype(F32))
    sums_ref[5:6, :] = column_sum(upstream * normed_one)
    sums_ref[6:7, :] = column_sum(upstream)
    sums_ref[7:8, :] = jnp.zeros_like(sums_ref[7:8, :])
    middle = BLOCK // 2
    for slot in range(parts):
        back = dot(attn_grad, w_out[slot]).astype(BF16)
        ctx_grad_ref[place_ref[slot]] = pack(
            back[:, : 2 * DH], back[:middle, 2 * DH :], back[middle:, 2 * DH :]
        )


def run_dense(half, marks, place, ratio, ctx, rows_in, teacher, cotangent, valid, vecs, inner_bias, pieces):
    parts = ctx.shape[0]
    width = rows_in.shape[1]
    hidden_cols = inner_bias.shape[2]
    head_cols = pieces[0].shape[2] - 2 * hidden_cols

    def mine(columns):
        return pl.BlockSpec((BLOCK, columns), lambda i: (half, 0))

    def fixed(shape):
        return pl.BlockSpec(shape, lambda i: (0,) * len(shape))

    low = jax.ShapeDtypeStruct((BLOCK, width), BF16)
    out_shape = (
        low,
        jax.ShapeDtypeStruct((BLOCK, width), F32),
        jax.ShapeDtypeStruct(ctx.shape, BF16),
        low,
        low,
        low,
        jax.ShapeDtypeStruct((parts, BLOCK, hidden_cols), BF16),
        jax.ShapeDtypeStruct((parts, BLOCK, hidden_cols), BF16),
        jax.ShapeDtypeStruct((8, width), F32),
        jax.ShapeDtypeStruct((parts, 1, hidden_cols), F32),
    )
    smem = pl.BlockSpec(memory_space=pltpu.SMEM)
    return pl.pallas_call(
        functools.partial(dense_chain, marks),
        out_shape=out_shape,
        grid=(1,),
        in_specs=[
            smem,
            smem,
            fixed(ctx.shape),
            mine(width),
            mine(width),
            mine(width),
            mine(1),
            fixed(vecs.shape),
            fixed(inner_bias.shape),
        ]
        + [pl.BlockSpec(memory_space=pl.ANY)] * len(pieces),
        out_specs=tuple(fixed(out.shape) for out in out_shape),
        scratch_shapes=[
            pltpu.VMEM((parts, width, head_cols), BF16),
            pltpu.VMEM((parts, width, hidden_cols), BF16),
            pltpu.VMEM((parts, width, hidden_cols), BF16),
            pltpu.VMEM((parts, BLOCK, hidden_cols), F32),
            pltpu.SemaphoreType.DMA((3, parts)),
        ],
        compiler_params=pltpu.CompilerParams(
            dimension_semantics=("arbitrary",), vmem_limit_bytes=VMEM_LIMIT
        ),
        cost_estimate=pl.CostEstimate(
            flops=BLOCK * width * (8 * hidden_cols + 4 * head_cols) * parts,
            bytes_accessed=18 << 20,
            transcendentals=2 * BLOCK * hidden_cols * parts,
        ),
        name="dense_chain",
    )(place, ratio, ctx, rows_in, teacher, cotangent, valid, vecs, inner_bias, *pieces)


def dense_weights(turns, halves, place_ref, *refs):
    firsts, branch_grads, attn_grads, acts, hidden_grads, ctxs = (
        refs[k * halves : (k + 1) * halves] for k in range(6)
    )
    outs = refs[6 * halves : -3]
    turned, whole, sems = refs[-3:]
    step = pl.program_id(0)
    slots = whole.shape[0]
    teams = len(outs) // len(turns)
    each = slots // teams

    @pl.when(step == 0)
    def _():
        for which, sources in enumerate((firsts, branch_grads, attn_grads)):
            for half, source in enumerate(sources):
                turned[which, :, half * BLOCK : (half + 1) * BLOCK] = jnp.transpose(source[...])

    def both(sources):
        return jnp.concatenate([source[0] for source in sources], axis=0)

    hidden_cols = acts[0].shape[2]
    whole[step, :, :hidden_cols] = dot(turned[0], both(hidden_grads)).astype(BF16)
    whole[step, :, hidden_cols : 2 * hidden_cols] = dot(turned[1], both(acts)).astype(BF16)
    ctx = jnp.concatenate([unpack(source[0]) for source in ctxs], axis=0)
    whole[step, :, 2 * hidden_cols :] = dot(turned[2], ctx).astype(BF16)
    for team in range(teams):

        @pl.when(step // each == team)
        def _():
            for out, orders in zip(outs[team * len(turns) : (team + 1) * len(turns)], turns):
                block = out.shape[1]
                for at, turn in enumerate(orders[team]):
                    offset = pl.multiple_of((place_ref[slots] ^ turn) * block, block)
                    pltpu.make_async_copy(
                        whole.at[step, pl.ds(offset, block), :],
                        out.at[at * each + step - team * each],
                        sems.at[step],
                    ).start()

    @pl.when(step == slots - 1)
    def _():
        for slot in range(slots):
            pltpu.make_async_copy(whole.at[slot], whole.at[slot], sems.at[slot]).wait()


def run_weights(turns, teams, block, place, firsts, branch_grads, attn_grads, acts, hidden_grads, ctxs):
    parts, _, hidden_cols = acts[0].shape
    halves = len(acts)
    width = firsts[0].shape[1]
    columns = 2 * hidden_cols + 3 * DH

    def by_slot(rows, size):
        return pl.BlockSpec((1, rows, size), lambda s, place: (place[s], 0, 0))

    fixed = pl.BlockSpec((BLOCK, width), lambda s, place: (0, 0))
    outs = tuple(
        jax.ShapeDtypeStruct((len(orders[0]) * parts // teams, block, columns), BF16) for orders in turns
    ) * teams
    return pl.pallas_call(
        functools.partial(dense_weights, turns, halves),
        out_shape=outs,
        grid_spec=pltpu.PrefetchScalarGridSpec(
            num_scalar_prefetch=1,
            grid=(parts,),
            in_specs=[fixed] * (3 * halves)
            + [by_slot(BLOCK, hidden_cols)] * (2 * halves)
            + [by_slot(PACKED, 2 * DH)] * halves,
            out_specs=tuple(pl.BlockSpec(memory_space=pl.ANY) for _ in outs),
            scratch_shapes=[
                pltpu.VMEM((3, width, halves * BLOCK), BF16),
                pltpu.VMEM((parts, width, columns), BF16),
                pltpu.SemaphoreType.DMA((parts,)),
            ],
        ),
        compiler_params=pltpu.CompilerParams(
            dimension_semantics=("arbitrary",), vmem_limit_bytes=VMEM_LIMIT
        ),
        cost_estimate=pl.CostEstimate(
            flops=2 * halves * BLOCK * width * columns * parts,
            bytes_accessed=20 << 20,
            transcendentals=0,
        ),
        name="dense_weights",
    )(place, *firsts, *branch_grads, *attn_grads, *acts, *hidden_grads, *ctxs)


def finish_dense(left_ref, right_ref, inner_ref, outer_ref, output_ref):
    hidden_cols = inner_ref.shape[1]
    summed = left_ref[...].astype(F32) + right_ref[...].astype(F32)
    inner_ref[...] = summed[:, :hidden_cols]
    outer_ref[...] = summed[:, hidden_cols : 2 * hidden_cols]
    output_ref[...] = jnp.transpose(summed[:, 2 * hidden_cols :])


def run_finish_dense(left_side, right_side, hidden_cols, head_cols):
    rows = left_side.shape[0]
    return pl.pallas_call(
        finish_dense,
        out_shape=(
            jax.ShapeDtypeStruct((rows, hidden_cols), F32),
            jax.ShapeDtypeStruct((rows, hidden_cols), F32),
            jax.ShapeDtypeStruct((head_cols, rows), F32),
        ),
        name="finish_dense",
    )(left_side, right_side)


def finish_heads(left_ref, right_ref, query_ref, key_ref, value_ref):
    summed = left_ref[...].astype(F32) + right_ref[...].astype(F32)
    heads = summed.shape[1] // SLAB
    for ref, which in ((query_ref, 0), (key_ref, 2), (value_ref, 3)):
        ref[...] = jnp.concatenate(
            [summed[:, SLAB * h + which * DH : SLAB * h + (which + 1) * DH] for h in range(heads)], axis=1
        )


def run_finish_heads(left_side, right_side):
    rows, width = left_side.shape
    out = jax.ShapeDtypeStruct((rows, width // 4), F32)
    return pl.pallas_call(finish_heads, out_shape=(out, out, out), name="finish_heads")(
        left_side, right_side
    )


def interleave(query, key, value, heads):
    rows = query.shape[0]
    parts = [part.reshape(rows, heads, 1, DH) for part in (query, jnp.zeros_like(query), key, value)]
    return jnp.concatenate(parts, axis=2).reshape(rows, heads * SLAB)


def place_slice(local_grad, full_size, offset):
    return lax.dynamic_update_slice_in_dim(jnp.zeros((full_size,), F32), local_grad, offset, 0)


def swap(value, axis, bit):
    size = lax.axis_size(axis)
    return lax.ppermute(value, axis, [(i, i ^ bit) for i in range(size)])


def bits_of(axis):
    bit = 1
    while bit < lax.axis_size(axis):
        yield bit
        bit *= 2


def sum_everywhere(value):
    for axis in ("dp", "tensor"):
        for bit in bits_of(axis):
            value = value + swap(value, axis, bit)
    return value


def after(value, *others):
    return lax.optimization_barrier((value,) + others)[0]


def merge(held, other, bit):
    mine_first = (lax.axis_index("dp") & bit) == 0
    return jnp.where(
        mine_first, jnp.concatenate([held, other], axis=0), jnp.concatenate([other, held], axis=0)
    )


def scatter_rows(value):
    copies = lax.axis_size("dp")
    index = lax.axis_index("dp")
    held = value.reshape((copies,) + (value.shape[0] // copies,) + value.shape[1:])
    came = None
    for bit in bits_of("dp"):
        if came is not None:
            held = add_low(held, came)
        held = held.reshape((held.shape[0] // 2, 2) + held.shape[1:])
        own = (index & bit) // bit
        send = lax.dynamic_index_in_dim(held, 1 - own, 1, keepdims=False)
        held = lax.dynamic_index_in_dim(held, own, 1, keepdims=False)
        came = swap(send, "dp", bit)
    return (held[0], came[0])


def add_low(left_side, right_side):
    return (left_side.astype(F32) + right_side.astype(F32)).astype(BF16)


def spread(order):
    turns = [0]
    for bit in reversed(order):
        turns = turns + [turn | bit for turn in turns]
    return turns


def add_halves(left_side, right_side):
    half = left_side.shape[0] // 2
    return (
        add_low(left_side[:half], right_side[:half]),
        add_low(left_side[half:], right_side[half:]),
    )


INNER = [(1, 2), (2, 1)]
OUTWARD = [(1, 0), (2, 3)]
INWARD = [(0, 1), (3, 2)]


def local(
    inputs, segment_ids, valid_mask, teacher, cotangent,
    w_query, w_key, w_value, w_output, w_inner, w_outer,
    query_bias, value_bias, output_bias, inner_bias, outer_bias,
    gain_attn, shift_attn, gain_ffn, shift_ffn,
):
    _, part_len, width = inputs.shape
    parts = lax.axis_size("tensor")
    copies = lax.axis_size("dp")
    rank = lax.axis_index("tensor")
    total_tokens = part_len * parts * copies
    seq_len = part_len * parts
    head_cols = w_query.shape[1]
    heads = head_cols // DH
    hidden_cols = w_inner.shape[1]
    shard_rows = w_inner.shape[0]
    halves = part_len // BLOCK
    line = shard_rows % 16 == 0 and parts == 4 and copies == 8

    rows_in = inputs.reshape(part_len, width)
    tokens = lax.all_gather(rows_in, "tensor", axis=0, tiled=True)
    mine = jnp.concatenate((w_inner, w_outer.T, w_output.T), axis=1)
    head_rows = interleave(w_query, w_key, w_value, heads)
    valid_rows = valid_mask.astype(F32).reshape(part_len, 1)
    valid_count = jnp.sum(valid_rows).reshape(1, 1)
    if line:
        place = jnp.stack(
            [
                rank,
                rank ^ 1,
                jnp.where(rank < 2, 2, 1),
                jnp.where(rank < 2, 3, 0),
                lax.axis_index("dp"),
            ]
        ).astype(jnp.int32)
        own = mine[None]
        pair = jnp.concatenate([own, swap(own, "tensor", 1)], axis=0)
        head_rows = merge(head_rows, swap(head_rows, "dp", 1), 1)
        crossed = lax.ppermute(pair, "tensor", INNER)
        near = jnp.concatenate([pair, swap(pair, "dp", 2)], axis=0)
        head_rows = merge(head_rows, swap(head_rows, "dp", 2), 2)
        crossed = after(crossed, near, head_rows)
        near = jnp.concatenate([near, swap(near, "dp", 4)], axis=0)
        outward = lax.ppermute(crossed, "tensor", OUTWARD)
        w_heads = merge(head_rows, swap(head_rows, "dp", 4), 4)
        far = jnp.where((rank == 1) | (rank == 2), crossed, outward)
        far = after(far, w_heads)
        far = jnp.concatenate([far, swap(far, "dp", 2)], axis=0)
        near = after(near, far)
        near_other = swap(near, "dp", 1)
        far_last = swap(far, "dp", 4)
        counted = sum_everywhere(after(valid_count, far))
        marks = [[(slot, 0) for slot in (0, 1)], [(slot, 0) for slot in (2, 3)]]
        for bit in (2, 4):
            marks = [marked + [(slot, turn ^ bit) for slot, turn in marked] for marked in marks]
        marks = [[(slot, turn ^ flip) for slot, turn in marked] for marked in marks for flip in (0, 1)]
    else:
        place = jnp.asarray(list(range(parts)) + [0], jnp.int32)
        weights = lax.all_gather(mine, ("tensor", "dp"), axis=0, tiled=False)
        pieces = [weights.reshape(parts, width, 2 * hidden_cols + head_cols)]
        marks = [[(t, 0) for t in range(parts)]]
        w_heads = head_rows
        for bit in bits_of("dp"):
            w_heads = merge(w_heads, swap(w_heads, "dp", bit), bit)
        counted = sum_everywhere(valid_count)
    ratio = (total_tokens / counted).reshape(1)
    w_heads, ratio = lax.optimization_barrier((w_heads, ratio))

    mine_cols = rank * head_cols
    query_shift = lax.dynamic_slice_in_dim(query_bias, mine_cols, head_cols).astype(F32)
    value_shift = lax.dynamic_slice_in_dim(value_bias, mine_cols, head_cols).astype(F32)
    shifts = interleave(query_shift[None], jnp.zeros_like(query_shift)[None], value_shift[None], heads)
    qkv = (dot(tokens, w_heads) + shifts).astype(BF16)

    segment_row = segment_ids.reshape(seq_len)
    bounds = document_blocks(segment_row)
    seg_col = segment_row.reshape(seq_len, 1)
    seg_row = segment_row.reshape(1, seq_len)

    def exchange(blocks):
        return lax.all_to_all(blocks, "tensor", 0, 0)

    contexts, lses, arrived = [], [], []
    for half in range(halves):
        if half == halves - 1 and line:
            far = jnp.concatenate([far, after(far_last, contexts[0])], axis=0)
            bounds, far = lax.optimization_barrier((bounds, far))
            pieces = [near, near_other, far, swap(far, "dp", 1)]
        context, lse = run_forward((halves, half), bounds, qkv, seg_col, seg_row)
        contexts.append(context)
        lses.append(lse)
        arrived.append(exchange(context))

    vecs = jnp.stack(
        (output_bias, gain_attn, shift_attn, outer_bias, gain_ffn, shift_ffn, outer_bias, outer_bias)
    ).astype(F32)
    inner_rows = inner_bias.astype(F32).reshape(parts, 1, hidden_cols)
    teacher_rows = teacher.reshape(part_len, width)
    cotangent_rows = cotangent.reshape(part_len, width)
    chains = [
        run_dense(
            half, marks, place, ratio, arrived[half], rows_in, teacher_rows, cotangent_rows,
            valid_rows, vecs, inner_rows, pieces,
        )
        for half in range(halves)
    ]
    (
        layers, first_grads, context_grads, firsts, branch_grads, attn_grads, acts, hidden_grads,
        dense_sums, inner_sums,
    ) = zip(*chains)
    head_grads = [exchange(context_grad) for context_grad in context_grads]
    dense_sums = sum(dense_sums)
    inner_sums = sum(inner_sums)
    sources = (firsts, branch_grads, attn_grads, acts, hidden_grads, arrived)
    head_grads[:-1], sources = lax.optimization_barrier((head_grads[:-1], sources))
    orders = ([2, 4], [4, 2])
    if line:
        kept = [spread(order) for order in orders]
        turns = (kept, [[turn | 1 for turn in turns] for turns in kept])
        outs = run_weights(turns, 2, shard_rows, place, *sources)
        outs = [out.reshape((4, 2) + out.shape[1:]) for out in outs]
        came = [swap(outs[2 * team + 1], "dp", 1) for team in range(2)]
        head_grads[0], outs = lax.optimization_barrier((head_grads[0], outs))
    else:
        (packed,) = run_weights(([[0]],), 1, width, place, *sources)

    earlier, before = [], []
    for half in range(halves):
        if half == halves - 1 and line:
            came, before = lax.optimization_barrier((came, before))
            begun = [add_halves(outs[2 * team], came[team]) for team in range(2)]
            begun, before = lax.optimization_barrier((begun, before))
            moving = [swap(send, "dp", order[0]) for (_, send), order in zip(begun, orders)]
        results = run_backward(
            (halves, half), bounds, qkv, seg_col, seg_row, contexts[half], head_grads[half], lses[half],
            earlier, before,
        )
        if half < halves - 1:
            before, earlier = [results[0]], earlier + [results[1]]
    joined_grad, sums = results
    attn_back = dot(joined_grad, w_heads, NT).astype(BF16)
    attn_back, sums, joined_grad = lax.optimization_barrier((attn_back, sums, joined_grad))
    attn_back = lax.psum_scatter(attn_back, "tensor", scatter_dimension=0, tiled=True)
    if line:
        moving, joined_grad = lax.optimization_barrier((moving, joined_grad))
        halved = [add_halves(keep, came) for (keep, _), came in zip(begun, moving)]
        halved, joined_grad, sums = lax.optimization_barrier((halved, joined_grad, sums))
        near, far = (
            add_low(keep, swap(send, "dp", order[1]))[0] for (keep, send), order in zip(halved, orders)
        )
        far = add_low(far, lax.ppermute(far, "tensor", INWARD))
        near = add_low(near, lax.ppermute(far, "tensor", INNER))
        finals = (near[0], swap(near[1], "tensor", 1))
    else:
        packed = lax.psum_scatter(packed, "dp", scatter_dimension=1, tiled=True)
        packed = lax.psum_scatter(packed, "tensor", scatter_dimension=0, tiled=True)[0]
        finals = (packed, jnp.zeros_like(packed))
    inner_grad, outer_grad, output_grad = run_finish_dense(*finals, hidden_cols, head_cols)
    input_grad = jnp.concatenate(first_grads, axis=0) + attn_back.astype(F32)
    head_finals = scatter_rows(dot(tokens, joined_grad, TN).astype(BF16))

    sums = sums.reshape(heads, 4, DH)
    totals = sum_everywhere(
        jnp.concatenate(
            (
                place_slice(sums[:, 0].reshape(head_cols), width, mine_cols),
                place_slice(sums[:, 3].reshape(head_cols), width, mine_cols),
                dense_sums.reshape(-1),
                inner_sums.reshape(-1),
            )
        ).reshape(-1, 128)
    ).reshape(-1)

    def total(which):
        return totals[which * width : (which + 1) * width]

    mse_loss = jnp.sum(total(2)) / (counted[0, 0] * width)
    return (
        (
            jnp.concatenate(layers, axis=0).reshape(1, part_len, width),
            mse_loss,
            input_grad.reshape(1, part_len, width),
        )
        + tuple(run_finish_heads(*head_finals))
        + (output_grad, inner_grad, outer_grad.T)
        + (total(0), total(1), total(6), totals[10 * width :])
        + (total(3), total(7), total(8), total(4), total(5))
    )


def solution(mesh):
    shard = P("dp", "tensor", None)
    in_specs = (
        (shard, P("dp", None), P("dp", "tensor"), shard, shard)
        + (P("dp", "tensor"),) * 3
        + (P("tensor", "dp"), P("dp", "tensor"), P("tensor", "dp"))
        + (P(),) * 9
    )
    out_specs = (
        (shard, P(), shard)
        + (P("dp", "tensor"),) * 3
        + (P("tensor", "dp"), P("dp", "tensor"), P("tensor", "dp"))
        + (P(),) * 9
    )
    return jax.shard_map(local, mesh=mesh, in_specs=in_specs, out_specs=out_specs, check_vma=False)
```

```python
import functools

import jax
import jax.numpy as jnp
from jax import lax
from jax.experimental import pallas as pl
from jax.experimental.pallas import tpu as pltpu
from jax.sharding import PartitionSpec as P

DH = 64
BLOCK = 256
SLAB = 4 * DH
EPSILON = 1e-12
ROOT_HALF = 0.7071067811865476
INV_ROOT_TAU = 0.3989422804014327
LOG2E = 1.4426950408889634
LN2 = 0.6931471805599453
SCALE = DH ** (-0.5)
MASKED = -1e30
VMEM_LIMIT = 60 << 20

BF16 = jnp.bfloat16
F32 = jnp.float32
NN = (((1,), (0,)), ((), ()))
NT = (((1,), (1,)), ((), ()))
TN = (((0,), (0,)), ((), ()))


def dot(left_side, right_side, dims=NN):
    return lax.dot_general(left_side, right_side, dims, preferred_element_type=F32)


def norm_forward(summed, gain_vec, shift_vec):
    average = jnp.mean(summed, axis=-1, keepdims=True)
    centered = summed - average
    variance = jnp.mean(centered * centered, axis=-1, keepdims=True)
    inverse = lax.rsqrt(variance + EPSILON)
    normed = centered * inverse
    return (normed * gain_vec + shift_vec, normed, inverse)


def norm_backward(upstream, normed, inverse, gain_vec):
    scaled = upstream * gain_vec
    first_mean = jnp.mean(scaled, axis=-1, keepdims=True)
    second_mean = jnp.mean(scaled * normed, axis=-1, keepdims=True)
    return inverse * (scaled - first_mean - normed * second_mean)


def column_sum(value):
    return jnp.sum(value, axis=0, keepdims=True)


def lane_is_right(rows):
    return lax.broadcasted_iota(jnp.int32, (rows, 2 * DH), 1) >= DH


def pack(first_two, third_top, third_bottom):
    return jnp.concatenate([first_two, jnp.concatenate([third_top, third_bottom], axis=1)], axis=0)


def unpack(packed):
    third = packed[BLOCK:]
    third = jnp.concatenate([third[:, :DH], third[:, DH:]], axis=0)
    return jnp.concatenate([packed[:BLOCK], third], axis=1)


CHUNKS = (0, 2, 1, 3)


def fetch_chunks(lane_ref, chunk_refs, target, sems):
    rows = chunk_refs[0].shape[0]
    copies = []
    for at, (turn, chunk) in enumerate(zip(CHUNKS, chunk_refs)):
        offset = pl.multiple_of((lane_ref[0] ^ turn) * rows, rows)
        copies.append(pltpu.make_async_copy(chunk, target.at[pl.ds(offset, rows), :], sems.at[at]))
    return copies


def attend_forward(
    which, lane_ref, low_ref, high_ref, *refs
):
    chunk_refs, (seg_col_ref, seg_row_ref, ctx_ref, lse_ref, held, qkv_ref, sems) = refs[:4], refs[4:]
    halves, half = which
    heads = lse_ref.shape[0]

    @pl.when(pl.program_id(0) == 0)
    def _():
        copies = fetch_chunks(lane_ref, chunk_refs, qkv_ref, sems)
        for copy in copies:
            copy.start()
        for copy in copies:
            copy.wait()

    qb = pl.program_id(0) * halves + half
    rows = pl.ds(pl.multiple_of(qb * BLOCK, BLOCK), BLOCK)
    seg_q = seg_col_ref[...]
    queries = [
        qkv_ref[rows, SLAB * h : SLAB * h + 2 * DH] * jnp.asarray(SCALE, BF16) for h in range(heads)
    ]
    low, high = low_ref[qb], high_ref[qb]

    def score(kb, peaks):
        keys = pl.ds(pl.multiple_of(kb * BLOCK, BLOCK), BLOCK)
        allowed = seg_q == seg_row_ref[:, keys]
        found = []
        for h in range(heads):
            scores = dot(queries[h], qkv_ref[keys, SLAB * h + 2 * DH : SLAB * (h + 1)], NT)
            scores = jnp.where(allowed, scores, MASKED)
            held[h, kb] = scores
            found.append(jnp.maximum(peaks[h], jnp.maximum(scores[:, :128], scores[:, 128:])))
        return tuple(found)

    start = tuple(jnp.full((BLOCK, 128), MASKED, F32) for _ in range(heads))
    peaks = lax.fori_loop(low, high, score, start)
    highest = [jnp.max(peak, axis=-1, keepdims=True) for peak in peaks]

    def weigh(kb, carry):
        keys = pl.ds(pl.multiple_of(kb * BLOCK, BLOCK), BLOCK)
        found = []
        for h in range(heads):
            total, acc = carry[h]
            raised = jnp.exp2((held[h, kb] - highest[h]) * LOG2E)
            total = total + (raised[:, :128] + raised[:, 128:])
            acc = acc + dot(raised.astype(BF16), qkv_ref[keys, SLAB * h + 2 * DH : SLAB * (h + 1)])
            found.append((total, acc))
        return tuple(found)

    zero = jnp.zeros((BLOCK, 128), F32)
    done = lax.fori_loop(low, high, weigh, tuple((zero, zero) for _ in range(heads)))
    values = []
    for h in range(heads):
        total, acc = done[h]
        summed = jnp.sum(total, axis=-1, keepdims=True)
        values.append((acc / summed).astype(BF16))
        lse_ref[h] = jnp.transpose(highest[h] + jnp.log(summed))
    middle = BLOCK // 2
    ctx_ref[0, :BLOCK, :] = jnp.where(lane_is_right(BLOCK), values[1], pltpu.roll(values[0], DH, 1))
    ctx_ref[0, BLOCK:, :] = jnp.where(
        lane_is_right(middle), values[2][middle:], pltpu.roll(values[2][:middle], DH, 1)
    )


def attend_backward(which, lane_ref, low_ref, high_ref, *refs):
    halves, half = which
    last = half == halves - 1
    chunk_refs, refs = refs[:4], refs[4:]
    (seg_col_ref, seg_row_ref, ctx_ref, grad_ref, lse_ref), refs = refs[:5], refs[5:]
    earlier, refs = refs[:half], refs[half:]
    if half > 0:
        before_ref, refs = refs[0], refs[1:]
    if last:
        final_ref, sums_ref, dkv, out_ref, qkv_ref, sems = refs
    else:
        dkv, query_ref, qkv_ref, sems = refs
    heads = dkv.shape[0]
    step_index = pl.program_id(0)
    qb = step_index * halves + half

    @pl.when(step_index == 0)
    def _():
        copies = fetch_chunks(lane_ref, chunk_refs, qkv_ref, sems)
        for copy in copies:
            copy.start()
        dkv[...] = before_ref[...] if half > 0 else jnp.zeros_like(dkv)
        for copy in copies:
            copy.wait()

    rows = pl.ds(pl.multiple_of(qb * BLOCK, BLOCK), BLOCK)
    right = lane_is_right(BLOCK)
    arrived = grad_ref[0]
    product = arrived.astype(F32) * ctx_ref[0].astype(F32)
    upper = product.astype(BF16)
    lower = (product - upper.astype(F32)).astype(BF16)
    pick = (
        lax.broadcasted_iota(jnp.int32, (8, 2 * DH), 1) // DH
        == lax.broadcasted_iota(jnp.int32, (8, 2 * DH), 0)
    ).astype(BF16)
    summed = dot(pick, upper, NT) + dot(pick, lower, NT)
    deltas = [
        summed[0:1, :BLOCK],
        summed[1:2, :BLOCK],
        jnp.concatenate([summed[0:1, BLOCK:], summed[1:2, BLOCK:]], axis=1),
    ]
    two, third = arrived[:BLOCK], arrived[BLOCK:]
    placed = [
        pltpu.roll(two, DH, 1),
        two,
        jnp.concatenate([pltpu.roll(third, DH, 1), third], axis=0),
    ]
    grads = [jnp.where(right, grad, jnp.zeros_like(grad)) for grad in placed]
    queries, pairs = [], []
    for h in range(heads):
        queries.append(qkv_ref[rows, SLAB * h : SLAB * h + 2 * DH] * jnp.asarray(SCALE, BF16))
        pairs.append(jnp.concatenate([queries[h], grads[h]], axis=0))
    seg_q = seg_row_ref[...]
    lses = lse_ref[...]
    low, high = low_ref[qb], high_ref[qb]

    def step(kb, accs):
        keys = pl.ds(pl.multiple_of(kb * BLOCK, BLOCK), BLOCK)
        allowed = seg_col_ref[keys, :] == seg_q
        found = []
        for h in range(heads):
            pair = qkv_ref[keys, SLAB * h + 2 * DH : SLAB * (h + 1)]
            scores = jnp.where(allowed, dot(pair, queries[h], NT), MASKED)
            probs = jnp.exp2((scores - lses[h]) * LOG2E)
            score_grad = (probs * (dot(pair, grads[h], NT) - deltas[h])).astype(BF16)
            both = jnp.concatenate([score_grad, probs.astype(BF16)], axis=1)
            dkv[h, keys, :] += dot(both, pairs[h])
            found.append(accs[h] + dot(score_grad, pair, TN))
        return tuple(found)

    zero = jnp.zeros((BLOCK, 128), F32)
    accs = lax.fori_loop(low, high, step, tuple(zero for _ in range(heads)))
    for h in range(heads):
        query_grad = jnp.where(right, 0.0, accs[h] * SCALE).astype(BF16)
        if last:
            out_ref[rows, SLAB * h : SLAB * h + 2 * DH] = query_grad
        else:
            query_ref[0, :, 2 * DH * h : 2 * DH * (h + 1)] = query_grad

    if last:

        @pl.when(step_index == pl.num_programs(0) - 1)
        def _():
            for h in range(heads):
                at = SLAB * h
                for other, ref in enumerate(earlier):
                    for block in range(ref.shape[0]):
                        start = (block * halves + other) * BLOCK
                        out_ref[start : start + BLOCK, at : at + 2 * DH] = ref[
                            block, :, 2 * DH * h : 2 * DH * (h + 1)
                        ]
                out_ref[:, at + 2 * DH : at + SLAB] = dkv[h].astype(BF16)
                sums_ref[:, at : at + SLAB] = column_sum(out_ref[:, at : at + SLAB].astype(F32))
            rows_each = final_ref.shape[1]
            copies = []
            for at, turn in enumerate(CHUNKS):
                offset = pl.multiple_of((lane_ref[0] ^ turn) * rows_each, rows_each)
                copies.append(
                    pltpu.make_async_copy(
                        out_ref.at[pl.ds(offset, rows_each), :], final_ref.at[at], sems.at[at]
                    )
                )
            for copy in copies:
                copy.start()
            for copy in copies:
                copy.wait()


def document_blocks(segment_row):
    starts = segment_row[::BLOCK]
    stops = segment_row[BLOCK - 1 :: BLOCK]
    low = jnp.sum((segment_row[None, :] < starts[:, None]).astype(jnp.int32), axis=1)
    high = jnp.sum((segment_row[None, :] <= stops[:, None]).astype(jnp.int32), axis=1)
    return (low // BLOCK, (high + BLOCK - 1) // BLOCK)


PACKED = BLOCK + BLOCK // 2


def run_forward(which, lane, bounds, qkv, seg_col, seg_row):
    halves, half = which
    seq_len, width = seg_col.shape[0], qkv[0].shape[1]
    heads = width // SLAB
    blocks = seq_len // BLOCK
    steps = blocks // halves
    return pl.pallas_call(
        functools.partial(attend_forward, which),
        out_shape=(
            jax.ShapeDtypeStruct((steps, PACKED, 2 * DH), BF16),
            jax.ShapeDtypeStruct((heads, 1, steps * BLOCK), F32),
        ),
        grid_spec=pltpu.PrefetchScalarGridSpec(
            num_scalar_prefetch=3,
            grid=(steps,),
            in_specs=[pl.BlockSpec(memory_space=pl.ANY)] * 4
            + [
                pl.BlockSpec((BLOCK, 1), lambda q, *_: (q * halves + half, 0)),
                pl.BlockSpec((1, seq_len), lambda q, *_: (0, 0)),
            ],
            out_specs=(
                pl.BlockSpec((1, PACKED, 2 * DH), lambda q, *_: (q, 0, 0)),
                pl.BlockSpec((heads, 1, BLOCK), lambda q, *_: (0, 0, q)),
            ),
            scratch_shapes=[
                pltpu.VMEM((heads, blocks, BLOCK, BLOCK), F32),
                pltpu.VMEM((seq_len, width), BF16),
                pltpu.SemaphoreType.DMA((4,)),
            ],
        ),
        compiler_params=pltpu.CompilerParams(
            dimension_semantics=("arbitrary",), vmem_limit_bytes=VMEM_LIMIT
        ),
        cost_estimate=pl.CostEstimate(
            flops=heads * seq_len * seq_len * 256 // halves,
            bytes_accessed=5 << 20,
            transcendentals=heads * seq_len * seq_len // 3 // halves,
        ),
        name="attend_forward",
    )(lane, *bounds, *qkv, seg_col, seg_row)


def run_backward(which, lane, bounds, qkv, seg_col, seg_row, ctx, grad, lse, earlier, before):
    halves, half = which
    seq_len, width = seg_col.shape[0], qkv[0].shape[1]
    heads = width // SLAB
    steps = seq_len // BLOCK // halves
    packed = pl.BlockSpec((1, PACKED, 2 * DH), lambda q, *_: (q, 0, 0))

    def fixed(shape, **more):
        return pl.BlockSpec(shape, lambda q, *_: (0,) * len(shape), **more)

    once = {"pipeline_mode": pl.Buffered(1)}
    gathered = (heads, seq_len, 2 * DH)
    carried = [fixed(value.shape, **once) for value in earlier]
    carried += [fixed(gathered, **once)] * len(before)
    scratch = [pltpu.VMEM((seq_len, width), BF16), pltpu.SemaphoreType.DMA((4,))]
    if half == halves - 1:
        out_shape = (
            jax.ShapeDtypeStruct((4, seq_len // 4, width), BF16),
            jax.ShapeDtypeStruct((1, width), F32),
        )
        out_specs = (pl.BlockSpec(memory_space=pl.ANY), fixed((1, width)))
        scratch = [pltpu.VMEM(gathered, F32), pltpu.VMEM((seq_len, width), BF16)] + scratch
    else:
        out_shape = (
            jax.ShapeDtypeStruct(gathered, F32),
            jax.ShapeDtypeStruct((steps, BLOCK, heads * 2 * DH), BF16),
        )
        out_specs = (
            fixed(gathered),
            pl.BlockSpec((1, BLOCK, heads * 2 * DH), lambda q, *_: (q, 0, 0)),
        )
    return pl.pallas_call(
        functools.partial(attend_backward, which),
        out_shape=out_shape,
        grid_spec=pltpu.PrefetchScalarGridSpec(
            num_scalar_prefetch=3,
            grid=(steps,),
            in_specs=[pl.BlockSpec(memory_space=pl.ANY)] * 4
            + [
                fixed((seq_len, 1)),
                pl.BlockSpec((1, BLOCK), lambda q, *_: (0, q * halves + half)),
                packed,
                packed,
                pl.BlockSpec((heads, 1, BLOCK), lambda q, *_: (0, 0, q)),
            ]
            + carried,
            out_specs=out_specs,
            scratch_shapes=scratch,
        ),
        compiler_params=pltpu.CompilerParams(
            dimension_semantics=("arbitrary",), vmem_limit_bytes=VMEM_LIMIT
        ),
        cost_estimate=pl.CostEstimate(
            flops=heads * seq_len * seq_len * 640 // halves,
            bytes_accessed=10 << 20,
            transcendentals=heads * seq_len * seq_len // 3 // halves,
        ),
        name="attend_backward",
    )(lane, *bounds, *qkv, seg_col, seg_row, ctx, grad, lse, *earlier, *before)


def dense_chain(
    marks, place_ref, ratio_ref, ctx_ref, in_ref, teacher_ref, cotangent_ref, valid_ref, vec_ref,
    inner_bias_ref, *refs
):
    pieces = refs[: len(marks)]
    (
        layer_ref, first_grad_ref, ctx_grad_ref, first_ref, branch_grad_ref, attn_grad_ref,
        act_ref, hidden_grad_ref, sums_ref, inner_sums_ref, w_out, w_in, w_up, slope, sems,
    ) = refs[len(marks) :]
    parts, _, head_cols = w_out.shape
    hidden_cols = w_in.shape[2]
    index = place_ref[parts]
    groups = (
        (2 * hidden_cols, head_cols, w_out),
        (0, hidden_cols, w_in),
        (hidden_cols, hidden_cols, w_up),
    )
    for group, (start, size, target) in enumerate(groups):
        for piece, marked in zip(pieces, marks):
            block = piece.shape[1]
            for at, (slot, turn) in enumerate(marked):
                offset = pl.multiple_of((index ^ turn) * block, block)
                pltpu.make_async_copy(
                    piece.at[at, :, pl.ds(start, size)],
                    target.at[slot, pl.ds(offset, block), :],
                    sems.at[group, slot],
                ).start()

    def arrive(group, slot):
        whole = groups[group][2].at[slot]
        pltpu.make_async_copy(whole, whole, sems.at[group, slot]).wait()

    def vec(which):
        return vec_ref[which : which + 1, :]

    inner_sums_ref[...] = jnp.zeros_like(inner_sums_ref)
    attention = jnp.zeros(in_ref.shape, F32)
    for slot in range(parts):
        arrive(0, slot)
        attention = attention + dot(unpack(ctx_ref[place_ref[slot]]), w_out[slot], NT)
    first_exact, normed_one, inverse_one = norm_forward(
        in_ref[...].astype(F32) + attention + vec(0), vec(1), vec(2)
    )
    first = first_exact.astype(BF16)
    first_ref[...] = first

    def up(slot, branch):
        t = place_ref[slot]
        arrive(1, slot)
        hidden = dot(first, w_in[slot]) + inner_bias_ref[t]
        bend = 0.5 * (1.0 + lax.erf(hidden * ROOT_HALF))
        activated = (hidden * bend).astype(BF16)
        act_ref[t] = activated
        slope[slot] = bend + hidden * INV_ROOT_TAU * jnp.exp2(hidden * hidden * (-0.5 * LOG2E))
        arrive(2, slot)
        return branch + dot(activated, w_up[slot], NT)

    branch = lax.fori_loop(0, parts, up, jnp.zeros(in_ref.shape, F32))
    layer_rows, normed_two, inverse_two = norm_forward(first.astype(F32) + branch + vec(3), vec(4), vec(5))
    layer_ref[...] = layer_rows.astype(BF16)
    misfit = layer_rows - teacher_ref[...].astype(F32)
    weighted = valid_ref[...] * misfit
    out_grad = cotangent_ref[...].astype(F32) + weighted * ratio_ref[0]
    second_grad = norm_backward(out_grad, normed_two, inverse_two, vec(4))
    branch_grad = second_grad.astype(BF16)
    branch_grad_ref[...] = branch_grad
    sums_ref[0:1, :] = column_sum(weighted * misfit)
    sums_ref[1:2, :] = column_sum(branch_grad.astype(F32))
    sums_ref[2:3, :] = column_sum(out_grad * normed_two)
    sums_ref[3:4, :] = column_sum(out_grad)

    def down(slot, back):
        t = place_ref[slot]
        hidden_grad = (dot(branch_grad, w_up[slot]) * slope[slot]).astype(BF16)
        hidden_grad_ref[t] = hidden_grad
        inner_sums_ref[t] = column_sum(hidden_grad.astype(F32))
        return back + dot(hidden_grad, w_in[slot], NT)

    upstream = lax.fori_loop(0, parts, down, second_grad)
    first_grad = norm_backward(upstream, normed_one, inverse_one, vec(1))
    first_grad_ref[...] = first_grad
    attn_grad = first_grad.astype(BF16)
    attn_grad_ref[...] = attn_grad
    sums_ref[4:5, :] = column_sum(attn_grad.astype(F32))
    sums_ref[5:6, :] = column_sum(upstream * normed_one)
    sums_ref[6:7, :] = column_sum(upstream)
    sums_ref[7:8, :] = jnp.zeros_like(sums_ref[7:8, :])
    middle = BLOCK // 2
    for slot in range(parts):
        back = dot(attn_grad, w_out[slot]).astype(BF16)
        ctx_grad_ref[place_ref[slot]] = pack(
            back[:, : 2 * DH], back[:middle, 2 * DH :], back[middle:, 2 * DH :]
        )


def run_dense(half, marks, place, ratio, ctx, rows_in, teacher, cotangent, valid, vecs, inner_bias, pieces):
    parts = ctx.shape[0]
    width = rows_in.shape[1]
    hidden_cols = inner_bias.shape[2]
    head_cols = pieces[0].shape[2] - 2 * hidden_cols

    def mine(columns):
        return pl.BlockSpec((BLOCK, columns), lambda i: (half, 0))

    def fixed(shape):
        return pl.BlockSpec(shape, lambda i: (0,) * len(shape))

    low = jax.ShapeDtypeStruct((BLOCK, width), BF16)
    out_shape = (
        low,
        jax.ShapeDtypeStruct((BLOCK, width), F32),
        jax.ShapeDtypeStruct(ctx.shape, BF16),
        low,
        low,
        low,
        jax.ShapeDtypeStruct((parts, BLOCK, hidden_cols), BF16),
        jax.ShapeDtypeStruct((parts, BLOCK, hidden_cols), BF16),
        jax.ShapeDtypeStruct((8, width), F32),
        jax.ShapeDtypeStruct((parts, 1, hidden_cols), F32),
    )
    smem = pl.BlockSpec(memory_space=pltpu.SMEM)
    return pl.pallas_call(
        functools.partial(dense_chain, marks),
        out_shape=out_shape,
        grid=(1,),
        in_specs=[
            smem,
            smem,
            fixed(ctx.shape),
            mine(width),
            fixed(teacher.shape),
            fixed(cotangent.shape),
            mine(1),
            fixed(vecs.shape),
            fixed(inner_bias.shape),
        ]
        + [pl.BlockSpec(memory_space=pl.ANY)] * len(pieces),
        out_specs=tuple(fixed(out.shape) for out in out_shape),
        scratch_shapes=[
            pltpu.VMEM((parts, width, head_cols), BF16),
            pltpu.VMEM((parts, width, hidden_cols), BF16),
            pltpu.VMEM((parts, width, hidden_cols), BF16),
            pltpu.VMEM((parts, BLOCK, hidden_cols), F32),
            pltpu.SemaphoreType.DMA((3, parts)),
        ],
        compiler_params=pltpu.CompilerParams(
            dimension_semantics=("arbitrary",), vmem_limit_bytes=VMEM_LIMIT
        ),
        cost_estimate=pl.CostEstimate(
            flops=BLOCK * width * (8 * hidden_cols + 4 * head_cols) * parts,
            bytes_accessed=18 << 20,
            transcendentals=2 * BLOCK * hidden_cols * parts,
        ),
        name="dense_chain",
    )(place, ratio, ctx, rows_in, teacher, cotangent, valid, vecs, inner_bias, *pieces)


def dense_weights(turns, halves, place_ref, *refs):
    firsts, branch_grads, attn_grads, acts, hidden_grads, ctxs = (
        refs[k * halves : (k + 1) * halves] for k in range(6)
    )
    outs = refs[6 * halves : -3]
    turned, whole, sems = refs[-3:]
    step = pl.program_id(0)
    slots = whole.shape[0]
    teams = len(outs) // len(turns)
    each = slots // teams

    @pl.when(step == 0)
    def _():
        for which, sources in enumerate((firsts, branch_grads, attn_grads)):
            for half, source in enumerate(sources):
                turned[which, :, half * BLOCK : (half + 1) * BLOCK] = jnp.transpose(source[...])

    def both(sources):
        return jnp.concatenate([source[0] for source in sources], axis=0)

    hidden_cols = acts[0].shape[2]
    whole[step, :, :hidden_cols] = dot(turned[0], both(hidden_grads)).astype(BF16)
    whole[step, :, hidden_cols : 2 * hidden_cols] = dot(turned[1], both(acts)).astype(BF16)
    ctx = jnp.concatenate([unpack(source[0]) for source in ctxs], axis=0)
    whole[step, :, 2 * hidden_cols :] = dot(turned[2], ctx).astype(BF16)
    for team in range(teams):

        @pl.when(step // each == team)
        def _():
            for out, orders in zip(outs[team * len(turns) : (team + 1) * len(turns)], turns):
                block = out.shape[1]
                for at, turn in enumerate(orders[team]):
                    offset = pl.multiple_of((place_ref[slots] ^ turn) * block, block)
                    pltpu.make_async_copy(
                        whole.at[step, pl.ds(offset, block), :],
                        out.at[at * each + step - team * each],
                        sems.at[step],
                    ).start()

    @pl.when(step == slots - 1)
    def _():
        for slot in range(slots):
            pltpu.make_async_copy(whole.at[slot], whole.at[slot], sems.at[slot]).wait()


def run_weights(turns, teams, block, place, firsts, branch_grads, attn_grads, acts, hidden_grads, ctxs):
    parts, _, hidden_cols = acts[0].shape
    halves = len(acts)
    width = firsts[0].shape[1]
    columns = 2 * hidden_cols + 3 * DH

    def by_slot(rows, size):
        return pl.BlockSpec((1, rows, size), lambda s, place: (place[s], 0, 0))

    fixed = pl.BlockSpec((BLOCK, width), lambda s, place: (0, 0))
    outs = tuple(
        jax.ShapeDtypeStruct((len(orders[0]) * parts // teams, block, columns), BF16) for orders in turns
    ) * teams
    return pl.pallas_call(
        functools.partial(dense_weights, turns, halves),
        out_shape=outs,
        grid_spec=pltpu.PrefetchScalarGridSpec(
            num_scalar_prefetch=1,
            grid=(parts,),
            in_specs=[fixed] * (3 * halves)
            + [by_slot(BLOCK, hidden_cols)] * (2 * halves)
            + [by_slot(PACKED, 2 * DH)] * halves,
            out_specs=tuple(pl.BlockSpec(memory_space=pl.ANY) for _ in outs),
            scratch_shapes=[
                pltpu.VMEM((3, width, halves * BLOCK), BF16),
                pltpu.VMEM((parts, width, columns), BF16),
                pltpu.SemaphoreType.DMA((parts,)),
            ],
        ),
        compiler_params=pltpu.CompilerParams(
            dimension_semantics=("arbitrary",), vmem_limit_bytes=VMEM_LIMIT
        ),
        cost_estimate=pl.CostEstimate(
            flops=2 * halves * BLOCK * width * columns * parts,
            bytes_accessed=20 << 20,
            transcendentals=0,
        ),
        name="dense_weights",
    )(place, *firsts, *branch_grads, *attn_grads, *acts, *hidden_grads, *ctxs)


def finish_dense(packed_ref, inner_ref, outer_ref, output_ref):
    hidden_cols = inner_ref.shape[1]
    summed = packed_ref[...].astype(F32)
    inner_ref[...] = summed[:, :hidden_cols]
    outer_ref[...] = summed[:, hidden_cols : 2 * hidden_cols]
    output_ref[...] = jnp.transpose(summed[:, 2 * hidden_cols :])


def run_finish_dense(packed, hidden_cols, head_cols):
    rows = packed.shape[0]
    return pl.pallas_call(
        finish_dense,
        out_shape=(
            jax.ShapeDtypeStruct((rows, hidden_cols), F32),
            jax.ShapeDtypeStruct((rows, hidden_cols), F32),
            jax.ShapeDtypeStruct((head_cols, rows), F32),
        ),
        name="finish_dense",
    )(packed)


def finish_heads(value_ref, *refs):
    summed = value_ref[...].astype(F32)
    heads = summed.shape[1] // SLAB
    for ref, which in zip(refs, (0, 2, 3)):
        ref[...] = jnp.concatenate(
            [summed[:, SLAB * h + which * DH : SLAB * h + (which + 1) * DH] for h in range(heads)], axis=1
        )


def run_finish_heads(value):
    rows, width = value.shape
    out = jax.ShapeDtypeStruct((rows, width // 4), F32)
    return pl.pallas_call(finish_heads, out_shape=(out, out, out), name="finish_heads")(value)


def interleave(query, key, value, heads):
    rows = query.shape[0]
    parts = [part.reshape(rows, heads, 1, DH) for part in (query, jnp.zeros_like(query), key, value)]
    return jnp.concatenate(parts, axis=2).reshape(rows, heads * SLAB)


def place_slice(local_grad, full_size, offset):
    return lax.dynamic_update_slice_in_dim(jnp.zeros((full_size,), F32), local_grad, offset, 0)


def swap(value, axis, bit):
    size = lax.axis_size(axis)
    return lax.ppermute(value, axis, [(i, i ^ bit) for i in range(size)])


def bits_of(axis):
    bit = 1
    while bit < lax.axis_size(axis):
        yield bit
        bit *= 2


def sum_everywhere(value):
    for axis in ("lo", "hi", "tensor"):
        for bit in bits_of(axis):
            value = value + swap(value, axis, bit)
    return value


def after(value, *others):
    return lax.optimization_barrier((value,) + others)[0]


def merge(held, other, axis, bit):
    mine_first = (lax.axis_index(axis) & bit) == 0
    return jnp.where(
        mine_first, jnp.concatenate([held, other], axis=0), jnp.concatenate([other, held], axis=0)
    )


def add_low(left_side, right_side):
    return (left_side.astype(F32) + right_side.astype(F32)).astype(BF16)


def halve(held, axis, bit):
    own = (lax.axis_index(axis) & bit) // bit
    half = held.shape[0] // 2
    keep = lax.dynamic_slice_in_dim(held, own * half, half, 0)
    send = lax.dynamic_slice_in_dim(held, (1 - own) * half, half, 0)
    return (keep, swap(send, axis, bit))


PLANE = (0, 3, 1, 2)
ORIGIN = (0, 2, 3, 1)
AWAY = [(lo * 4 + z, z * 4 + PLANE[lo]) for lo in range(4) for z in range(4)]
BACK = [(there, here) for here, there in AWAY]


def send_away(value):
    return lax.ppermute(value, ("lo", "tensor"), AWAY)


def send_back(value):
    return lax.ppermute(value, ("lo", "tensor"), BACK)


def local(
    inputs, segment_ids, valid_mask, teacher, cotangent,
    w_query, w_key, w_value, w_output, w_inner, w_outer,
    query_bias, value_bias, output_bias, inner_bias, outer_bias,
    gain_attn, shift_attn, gain_ffn, shift_ffn,
):
    _, part_len, width = inputs.shape
    parts = lax.axis_size("tensor")
    copies = lax.axis_size("hi") * lax.axis_size("lo")
    lane_index = lax.axis_index("lo")
    total_tokens = part_len * parts * copies
    seq_len = part_len * parts
    head_cols = w_query.shape[1]
    heads = head_cols // DH
    hidden_cols = w_inner.shape[1]
    shard_rows = w_inner.shape[0]
    halves = part_len // BLOCK

    rows_in = send_away(inputs.reshape(part_len, width))
    whole_row = jnp.concatenate((segment_ids.reshape(seq_len), valid_mask.reshape(part_len)))
    whole_row = send_away(whole_row.reshape(-1, 128)).reshape(-1)
    head_rows = send_away(interleave(w_query, w_key, w_value, heads))
    mine = jnp.concatenate((w_inner, w_outer.T, w_output.T), axis=1)
    weights = lax.all_gather(mine, ("tensor", "hi", "lo"), axis=0, tiled=False)
    pieces = [weights.reshape(parts, width, 2 * hidden_cols + head_cols)]
    marks = [[(t, 0) for t in range(parts)]]
    place = jnp.asarray(list(range(parts)) + [0], jnp.int32)
    valid_count = jnp.sum(valid_mask.astype(F32)).reshape(1, 1)
    counted = sum_everywhere(valid_count)
    ratio = (total_tokens / counted).reshape(1)

    head_rows = merge(head_rows, swap(head_rows, "tensor", 1), "tensor", 1)
    near_chunk = swap(rows_in, "lo", 1)
    next_chunk = swap(rows_in, "lo", 2)
    head_rows = merge(head_rows, swap(head_rows, "tensor", 2), "tensor", 2)
    blocks = head_rows.reshape(4, shard_rows, -1)
    head_rows = jnp.concatenate([blocks[plane] for plane in PLANE], axis=0)
    w_heads = head_rows
    for bit in bits_of("hi"):
        w_heads = merge(w_heads, swap(w_heads, "hi", bit), "hi", bit)
    far_chunk = swap(next_chunk, "lo", 1)
    w_heads, ratio = lax.optimization_barrier((w_heads, ratio))
    tokens = [rows_in, next_chunk, near_chunk, far_chunk]

    mine_cols = lane_index * head_cols
    query_shift = lax.dynamic_slice_in_dim(query_bias, mine_cols, head_cols).astype(F32)
    value_shift = lax.dynamic_slice_in_dim(value_bias, mine_cols, head_cols).astype(F32)
    shifts = interleave(query_shift[None], jnp.zeros_like(query_shift)[None], value_shift[None], heads)
    qkv = [(dot(chunk, w_heads) + shifts).astype(BF16) for chunk in tokens]

    def half_of(value, half):
        return value.reshape(part_len, width)[half * BLOCK : (half + 1) * BLOCK]

    sides = []
    for half in range(halves):
        sides.append([send_away(after(half_of(value, half), w_heads)) for value in (teacher, cotangent)])

    segment_row = whole_row[:seq_len]
    valid_rows = whole_row[seq_len:].astype(F32).reshape(part_len, 1)
    bounds = document_blocks(segment_row)
    seg_col = segment_row.reshape(seq_len, 1)
    seg_row = segment_row.reshape(1, seq_len)
    lane = lane_index.astype(jnp.int32).reshape(1)

    def exchange(packed_blocks):
        return lax.all_to_all(packed_blocks, "lo", 0, 0)

    contexts, lses, arrived = [], [], []
    for half in range(halves):
        context, lse = run_forward((halves, half), lane, bounds, qkv, seg_col, seg_row)
        contexts.append(context)
        lses.append(lse)
        arrived.append(exchange(context))

    vecs = jnp.stack(
        (output_bias, gain_attn, shift_attn, outer_bias, gain_ffn, shift_ffn, outer_bias, outer_bias)
    ).astype(F32)
    inner_rows = inner_bias.astype(F32).reshape(parts, 1, hidden_cols)
    chains = [
        run_dense(
            half, marks, place, ratio, arrived[half], rows_in, *sides[half],
            valid_rows, vecs, inner_rows, pieces,
        )
        for half in range(halves)
    ]
    (
        layers, first_grads, context_grads, firsts, branch_grads, attn_grads, acts, hidden_grads,
        dense_sums, inner_sums,
    ) = zip(*chains)
    head_grads = [exchange(context_grad) for context_grad in context_grads]
    dense_sums = sum(dense_sums)
    inner_sums = sum(inner_sums)
    sources = (firsts, branch_grads, attn_grads, acts, hidden_grads, arrived)
    head_grads[:-1], sources = lax.optimization_barrier((head_grads[:-1], sources))
    (packed,) = run_weights(([[0]],), 1, width, place, *sources)
    packed = lax.psum_scatter(packed, ("hi", "lo"), scatter_dimension=1, tiled=True)
    packed = lax.psum_scatter(packed, "tensor", scatter_dimension=0, tiled=True)[0]
    layer_out = send_back(jnp.concatenate(layers, axis=0))

    earlier, before = [], []
    for half in range(halves):
        if half == halves - 1:
            layer_out, before = lax.optimization_barrier((layer_out, before))
        results = run_backward(
            (halves, half), lane, bounds, qkv, seg_col, seg_row, contexts[half], head_grads[half],
            lses[half], earlier, before,
        )
        if half < halves - 1:
            before, earlier = [results[0]], earlier + [results[1]]
    joined_grad, sums = results
    joined_grad = joined_grad.reshape(seq_len, width)
    middle = seq_len // 2
    core_share = swap(dot(joined_grad[middle:], w_heads, NT).astype(BF16), "lo", 1)
    own_share = dot(joined_grad[:middle], w_heads, NT)
    own_share, sums, joined_grad = lax.optimization_barrier((own_share, sums, joined_grad))
    input_share = own_share + core_share.astype(F32)
    chip_share = swap(input_share[part_len:].astype(BF16), "lo", 2)
    head_weights = dot(jnp.concatenate(tokens, axis=0), joined_grad, TN).astype(BF16)
    chip_share, head_weights = lax.optimization_barrier((chip_share, head_weights))
    held = head_weights.reshape((copies, shard_rows) + head_weights.shape[1:])
    for bit in reversed(list(bits_of("hi"))):
        held = add_low(*halve(held, "hi", bit))
    input_grad = input_share[:part_len] + chip_share.astype(F32) + jnp.concatenate(first_grads, axis=0)
    input_grad, sums, held = lax.optimization_barrier((input_grad.astype(BF16), sums, held))
    input_grad = send_back(input_grad).astype(F32)

    held = jnp.stack([held[origin] for origin in ORIGIN])
    held = add_low(*halve(held, "tensor", 2))
    held = add_low(*halve(held, "tensor", 1))
    head_final = send_back(held[0])

    inner_grad, outer_grad, output_grad = run_finish_dense(packed, hidden_cols, head_cols)

    sums = sums.reshape(heads, 4, DH)
    totals = sum_everywhere(
        jnp.concatenate(
            (
                place_slice(sums[:, 0].reshape(head_cols), width, mine_cols),
                place_slice(sums[:, 3].reshape(head_cols), width, mine_cols),
                dense_sums.reshape(-1),
                inner_sums.reshape(-1),
            )
        ).reshape(-1, 128)
    ).reshape(-1)

    def total(which):
        return totals[which * width : (which + 1) * width]

    mse_loss = jnp.sum(total(2)) / (counted[0, 0] * width)
    return (
        (
            layer_out.reshape(1, part_len, width),
            mse_loss,
            input_grad.reshape(1, part_len, width),
        )
        + tuple(run_finish_heads(head_final))
        + (output_grad, inner_grad, outer_grad.T)
        + (total(0), total(1), total(6), totals[10 * width :])
        + (total(3), total(7), total(8), total(4), total(5))
    )


def solution(mesh):
    devices = mesh.devices
    groups = devices.shape[0] // 4
    finer = jax.sharding.Mesh(
        devices.reshape((groups, 4) + devices.shape[1:]), ("hi", "lo", "tensor")
    )
    split = ("hi", "lo")
    shard = P(split, "tensor", None)
    by_dp, by_tensor = P(split, "tensor"), P("tensor", split)
    in_specs = (
        (shard, P(split, None), by_dp, shard, shard)
        + (by_dp,) * 3
        + (by_tensor, by_dp, by_tensor)
        + (P(),) * 9
    )
    out_specs = (shard, P(), shard) + (by_dp,) * 3 + (by_tensor, by_dp, by_tensor) + (P(),) * 9
    return jax.shard_map(local, mesh=finer, in_specs=in_specs, out_specs=out_specs, check_vma=False)
```

```python
import functools

import jax
import jax.numpy as jnp
from jax import lax
from jax.experimental import pallas as pl
from jax.experimental.pallas import tpu as pltpu
from jax.sharding import PartitionSpec as P

DH = 64
BLOCK = 256
SLAB = 4 * DH
EPSILON = 1e-12
ROOT_HALF = 0.7071067811865476
INV_ROOT_TAU = 0.3989422804014327
LOG2E = 1.4426950408889634
LN2 = 0.6931471805599453
SCALE = DH ** (-0.5)
MASKED = -1e30
VMEM_LIMIT = 60 << 20

BF16 = jnp.bfloat16
F32 = jnp.float32
NN = (((1,), (0,)), ((), ()))
NT = (((1,), (1,)), ((), ()))
TN = (((0,), (0,)), ((), ()))


def dot(left_side, right_side, dims=NN):
    return lax.dot_general(left_side, right_side, dims, preferred_element_type=F32)


def norm_forward(summed, gain_vec, shift_vec):
    average = jnp.mean(summed, axis=-1, keepdims=True)
    centered = summed - average
    variance = jnp.mean(centered * centered, axis=-1, keepdims=True)
    inverse = lax.rsqrt(variance + EPSILON)
    normed = centered * inverse
    return (normed * gain_vec + shift_vec, normed, inverse)


def norm_backward(upstream, normed, inverse, gain_vec):
    scaled = upstream * gain_vec
    first_mean = jnp.mean(scaled, axis=-1, keepdims=True)
    second_mean = jnp.mean(scaled * normed, axis=-1, keepdims=True)
    return inverse * (scaled - first_mean - normed * second_mean)


def column_sum(value):
    return jnp.sum(value, axis=0, keepdims=True)


def lane_is_right(rows):
    return lax.broadcasted_iota(jnp.int32, (rows, 2 * DH), 1) >= DH


def pack(first_two, third_top, third_bottom):
    return jnp.concatenate([first_two, jnp.concatenate([third_top, third_bottom], axis=1)], axis=0)


def unpack(packed):
    third = packed[BLOCK:]
    third = jnp.concatenate([third[:, :DH], third[:, DH:]], axis=0)
    return jnp.concatenate([packed[:BLOCK], third], axis=1)


CHUNKS = (0, 2, 1, 3)


def fetch_chunks(lane_ref, chunk_refs, target, sems):
    rows = chunk_refs[0].shape[0]
    copies = []
    for at, (turn, chunk) in enumerate(zip(CHUNKS, chunk_refs)):
        offset = pl.multiple_of((lane_ref[0] ^ turn) * rows, rows)
        copies.append(pltpu.make_async_copy(chunk, target.at[pl.ds(offset, rows), :], sems.at[at]))
    return copies


def attend_forward(
    which, lane_ref, low_ref, high_ref, *refs
):
    chunk_refs, (seg_col_ref, seg_row_ref, ctx_ref, lse_ref, held, qkv_ref, sems) = refs[:4], refs[4:]
    halves, half = which
    heads = lse_ref.shape[0]

    @pl.when(pl.program_id(0) == 0)
    def _():
        copies = fetch_chunks(lane_ref, chunk_refs, qkv_ref, sems)
        for copy in copies:
            copy.start()
        for copy in copies:
            copy.wait()

    qb = pl.program_id(0) * halves + half
    rows = pl.ds(pl.multiple_of(qb * BLOCK, BLOCK), BLOCK)
    seg_q = seg_col_ref[...]
    queries = [
        qkv_ref[rows, SLAB * h : SLAB * h + 2 * DH] * jnp.asarray(SCALE, BF16) for h in range(heads)
    ]
    low, high = low_ref[qb], high_ref[qb]

    def score(kb, peaks):
        keys = pl.ds(pl.multiple_of(kb * BLOCK, BLOCK), BLOCK)
        allowed = seg_q == seg_row_ref[:, keys]
        found = []
        for h in range(heads):
            scores = dot(queries[h], qkv_ref[keys, SLAB * h + 2 * DH : SLAB * (h + 1)], NT)
            scores = jnp.where(allowed, scores, MASKED)
            held[h, kb] = scores
            found.append(jnp.maximum(peaks[h], jnp.maximum(scores[:, :128], scores[:, 128:])))
        return tuple(found)

    start = tuple(jnp.full((BLOCK, 128), MASKED, F32) for _ in range(heads))
    peaks = lax.fori_loop(low, high, score, start)
    highest = [jnp.max(peak, axis=-1, keepdims=True) for peak in peaks]

    def weigh(kb, carry):
        keys = pl.ds(pl.multiple_of(kb * BLOCK, BLOCK), BLOCK)
        found = []
        for h in range(heads):
            total, acc = carry[h]
            raised = jnp.exp2((held[h, kb] - highest[h]) * LOG2E)
            total = total + (raised[:, :128] + raised[:, 128:])
            acc = acc + dot(raised.astype(BF16), qkv_ref[keys, SLAB * h + 2 * DH : SLAB * (h + 1)])
            found.append((total, acc))
        return tuple(found)

    zero = jnp.zeros((BLOCK, 128), F32)
    done = lax.fori_loop(low, high, weigh, tuple((zero, zero) for _ in range(heads)))
    values = []
    for h in range(heads):
        total, acc = done[h]
        summed = jnp.sum(total, axis=-1, keepdims=True)
        values.append((acc / summed).astype(BF16))
        lse_ref[h] = jnp.transpose(highest[h] + jnp.log(summed))
    middle = BLOCK // 2
    ctx_ref[0, :BLOCK, :] = jnp.where(lane_is_right(BLOCK), values[1], pltpu.roll(values[0], DH, 1))
    ctx_ref[0, BLOCK:, :] = jnp.where(
        lane_is_right(middle), values[2][middle:], pltpu.roll(values[2][:middle], DH, 1)
    )


def attend_backward(which, lane_ref, low_ref, high_ref, *refs):
    halves, half = which
    last = half == halves - 1
    chunk_refs, refs = refs[:4], refs[4:]
    (seg_col_ref, seg_row_ref, ctx_ref, grad_ref, lse_ref), refs = refs[:5], refs[5:]
    earlier, refs = refs[:half], refs[half:]
    if half > 0:
        before_ref, refs = refs[0], refs[1:]
    if last:
        final_ref, sums_ref, dkv, out_ref, qkv_ref, sems = refs
    else:
        dkv, query_ref, qkv_ref, sems = refs
    heads = dkv.shape[0]
    step_index = pl.program_id(0)
    qb = step_index * halves + half

    @pl.when(step_index == 0)
    def _():
        copies = fetch_chunks(lane_ref, chunk_refs, qkv_ref, sems)
        for copy in copies:
            copy.start()
        dkv[...] = before_ref[...] if half > 0 else jnp.zeros_like(dkv)
        for copy in copies:
            copy.wait()

    rows = pl.ds(pl.multiple_of(qb * BLOCK, BLOCK), BLOCK)
    right = lane_is_right(BLOCK)
    arrived = grad_ref[0]
    product = arrived.astype(F32) * ctx_ref[0].astype(F32)
    upper = product.astype(BF16)
    lower = (product - upper.astype(F32)).astype(BF16)
    pick = (
        lax.broadcasted_iota(jnp.int32, (8, 2 * DH), 1) // DH
        == lax.broadcasted_iota(jnp.int32, (8, 2 * DH), 0)
    ).astype(BF16)
    summed = dot(pick, upper, NT) + dot(pick, lower, NT)
    deltas = [
        summed[0:1, :BLOCK],
        summed[1:2, :BLOCK],
        jnp.concatenate([summed[0:1, BLOCK:], summed[1:2, BLOCK:]], axis=1),
    ]
    two, third = arrived[:BLOCK], arrived[BLOCK:]
    placed = [
        pltpu.roll(two, DH, 1),
        two,
        jnp.concatenate([pltpu.roll(third, DH, 1), third], axis=0),
    ]
    grads = [jnp.where(right, grad, jnp.zeros_like(grad)) for grad in placed]
    queries, pairs = [], []
    for h in range(heads):
        queries.append(qkv_ref[rows, SLAB * h : SLAB * h + 2 * DH] * jnp.asarray(SCALE, BF16))
        pairs.append(jnp.concatenate([queries[h], grads[h]], axis=0))
    seg_q = seg_row_ref[...]
    lses = lse_ref[...]
    low, high = low_ref[qb], high_ref[qb]

    def step(kb, accs):
        keys = pl.ds(pl.multiple_of(kb * BLOCK, BLOCK), BLOCK)
        allowed = seg_col_ref[keys, :] == seg_q
        found = []
        for h in range(heads):
            pair = qkv_ref[keys, SLAB * h + 2 * DH : SLAB * (h + 1)]
            scores = jnp.where(allowed, dot(pair, queries[h], NT), MASKED)
            probs = jnp.exp2((scores - lses[h]) * LOG2E)
            score_grad = (probs * (dot(pair, grads[h], NT) - deltas[h])).astype(BF16)
            both = jnp.concatenate([score_grad, probs.astype(BF16)], axis=1)
            dkv[h, keys, :] += dot(both, pairs[h])
            found.append(accs[h] + dot(score_grad, pair, TN))
        return tuple(found)

    zero = jnp.zeros((BLOCK, 128), F32)
    accs = lax.fori_loop(low, high, step, tuple(zero for _ in range(heads)))
    for h in range(heads):
        query_grad = jnp.where(right, 0.0, accs[h] * SCALE).astype(BF16)
        if last:
            out_ref[rows, SLAB * h : SLAB * h + 2 * DH] = query_grad
        else:
            query_ref[0, :, 2 * DH * h : 2 * DH * (h + 1)] = query_grad

    if last:

        @pl.when(step_index == pl.num_programs(0) - 1)
        def _():
            for h in range(heads):
                at = SLAB * h
                for other, ref in enumerate(earlier):
                    for block in range(ref.shape[0]):
                        start = (block * halves + other) * BLOCK
                        out_ref[start : start + BLOCK, at : at + 2 * DH] = ref[
                            block, :, 2 * DH * h : 2 * DH * (h + 1)
                        ]
                out_ref[:, at + 2 * DH : at + SLAB] = dkv[h].astype(BF16)
                sums_ref[:, at : at + SLAB] = column_sum(out_ref[:, at : at + SLAB].astype(F32))
            rows_each = final_ref.shape[1]
            copies = []
            for at, turn in enumerate(CHUNKS):
                offset = pl.multiple_of((lane_ref[0] ^ turn) * rows_each, rows_each)
                copies.append(
                    pltpu.make_async_copy(
                        out_ref.at[pl.ds(offset, rows_each), :], final_ref.at[at], sems.at[at]
                    )
                )
            for copy in copies:
                copy.start()
            for copy in copies:
                copy.wait()


def document_blocks(segment_row):
    starts = segment_row[::BLOCK]
    stops = segment_row[BLOCK - 1 :: BLOCK]
    low = jnp.sum((segment_row[None, :] < starts[:, None]).astype(jnp.int32), axis=1)
    high = jnp.sum((segment_row[None, :] <= stops[:, None]).astype(jnp.int32), axis=1)
    return (low // BLOCK, (high + BLOCK - 1) // BLOCK)


PACKED = BLOCK + BLOCK // 2


def run_forward(which, lane, bounds, qkv, seg_col, seg_row):
    halves, half = which
    seq_len, width = seg_col.shape[0], qkv[0].shape[1]
    heads = width // SLAB
    blocks = seq_len // BLOCK
    steps = blocks // halves
    return pl.pallas_call(
        functools.partial(attend_forward, which),
        out_shape=(
            jax.ShapeDtypeStruct((steps, PACKED, 2 * DH), BF16),
            jax.ShapeDtypeStruct((heads, 1, steps * BLOCK), F32),
        ),
        grid_spec=pltpu.PrefetchScalarGridSpec(
            num_scalar_prefetch=3,
            grid=(steps,),
            in_specs=[pl.BlockSpec(memory_space=pl.ANY)] * 4
            + [
                pl.BlockSpec((BLOCK, 1), lambda q, *_: (q * halves + half, 0)),
                pl.BlockSpec((1, seq_len), lambda q, *_: (0, 0)),
            ],
            out_specs=(
                pl.BlockSpec((1, PACKED, 2 * DH), lambda q, *_: (q, 0, 0)),
                pl.BlockSpec((heads, 1, BLOCK), lambda q, *_: (0, 0, q)),
            ),
            scratch_shapes=[
                pltpu.VMEM((heads, blocks, BLOCK, BLOCK), F32),
                pltpu.VMEM((seq_len, width), BF16),
                pltpu.SemaphoreType.DMA((4,)),
            ],
        ),
        compiler_params=pltpu.CompilerParams(
            dimension_semantics=("arbitrary",), vmem_limit_bytes=VMEM_LIMIT
        ),
        cost_estimate=pl.CostEstimate(
            flops=heads * seq_len * seq_len * 256 // halves,
            bytes_accessed=5 << 20,
            transcendentals=heads * seq_len * seq_len // 3 // halves,
        ),
        name="attend_forward",
    )(lane, *bounds, *qkv, seg_col, seg_row)


def run_backward(which, lane, bounds, qkv, seg_col, seg_row, ctx, grad, lse, earlier, before):
    halves, half = which
    seq_len, width = seg_col.shape[0], qkv[0].shape[1]
    heads = width // SLAB
    steps = seq_len // BLOCK // halves
    packed = pl.BlockSpec((1, PACKED, 2 * DH), lambda q, *_: (q, 0, 0))

    def fixed(shape, **more):
        return pl.BlockSpec(shape, lambda q, *_: (0,) * len(shape), **more)

    once = {"pipeline_mode": pl.Buffered(1)}
    gathered = (heads, seq_len, 2 * DH)
    carried = [fixed(value.shape, **once) for value in earlier]
    carried += [fixed(gathered, **once)] * len(before)
    scratch = [pltpu.VMEM((seq_len, width), BF16), pltpu.SemaphoreType.DMA((4,))]
    if half == halves - 1:
        out_shape = (
            jax.ShapeDtypeStruct((4, seq_len // 4, width), BF16),
            jax.ShapeDtypeStruct((1, width), F32),
        )
        out_specs = (pl.BlockSpec(memory_space=pl.ANY), fixed((1, width)))
        scratch = [pltpu.VMEM(gathered, F32), pltpu.VMEM((seq_len, width), BF16)] + scratch
    else:
        out_shape = (
            jax.ShapeDtypeStruct(gathered, F32),
            jax.ShapeDtypeStruct((steps, BLOCK, heads * 2 * DH), BF16),
        )
        out_specs = (
            fixed(gathered),
            pl.BlockSpec((1, BLOCK, heads * 2 * DH), lambda q, *_: (q, 0, 0)),
        )
    return pl.pallas_call(
        functools.partial(attend_backward, which),
        out_shape=out_shape,
        grid_spec=pltpu.PrefetchScalarGridSpec(
            num_scalar_prefetch=3,
            grid=(steps,),
            in_specs=[pl.BlockSpec(memory_space=pl.ANY)] * 4
            + [
                fixed((seq_len, 1)),
                pl.BlockSpec((1, BLOCK), lambda q, *_: (0, q * halves + half)),
                packed,
                packed,
                pl.BlockSpec((heads, 1, BLOCK), lambda q, *_: (0, 0, q)),
            ]
            + carried,
            out_specs=out_specs,
            scratch_shapes=scratch,
        ),
        compiler_params=pltpu.CompilerParams(
            dimension_semantics=("arbitrary",), vmem_limit_bytes=VMEM_LIMIT
        ),
        cost_estimate=pl.CostEstimate(
            flops=heads * seq_len * seq_len * 640 // halves,
            bytes_accessed=10 << 20,
            transcendentals=heads * seq_len * seq_len // 3 // halves,
        ),
        name="attend_backward",
    )(lane, *bounds, *qkv, seg_col, seg_row, ctx, grad, lse, *earlier, *before)


def dense_chain(
    marks, place_ref, ratio_ref, ctx_ref, in_ref, teacher_ref, cotangent_ref, valid_ref, vec_ref,
    inner_bias_ref, *refs
):
    pieces = refs[: len(marks)]
    (
        layer_ref, first_grad_ref, ctx_grad_ref, first_ref, branch_grad_ref, attn_grad_ref,
        act_ref, hidden_grad_ref, sums_ref, inner_sums_ref, w_out, w_in, w_up, slope, sems,
    ) = refs[len(marks) :]
    parts, _, head_cols = w_out.shape
    hidden_cols = w_in.shape[2]
    index = place_ref[parts]
    groups = (
        (2 * hidden_cols, head_cols, w_out),
        (0, hidden_cols, w_in),
        (hidden_cols, hidden_cols, w_up),
    )
    for group, (start, size, target) in enumerate(groups):
        for piece, marked in zip(pieces, marks):
            block = piece.shape[1]
            for at, (slot, turn) in enumerate(marked):
                offset = pl.multiple_of((index ^ turn) * block, block)
                pltpu.make_async_copy(
                    piece.at[at, :, pl.ds(start, size)],
                    target.at[slot, pl.ds(offset, block), :],
                    sems.at[group, slot],
                ).start()

    def arrive(group, slot):
        whole = groups[group][2].at[slot]
        pltpu.make_async_copy(whole, whole, sems.at[group, slot]).wait()

    def vec(which):
        return vec_ref[which : which + 1, :]

    inner_sums_ref[...] = jnp.zeros_like(inner_sums_ref)
    attention = jnp.zeros(in_ref.shape, F32)
    for slot in range(parts):
        arrive(0, slot)
        attention = attention + dot(unpack(ctx_ref[place_ref[slot]]), w_out[slot, :, : 3 * DH], NT)
    first_exact, normed_one, inverse_one = norm_forward(
        in_ref[...].astype(F32) + attention + vec(0), vec(1), vec(2)
    )
    first = first_exact.astype(BF16)
    first_ref[...] = first

    def up(slot, branch):
        t = place_ref[slot]
        arrive(1, slot)
        hidden = dot(first, w_in[slot]) + inner_bias_ref[t]
        bend = 0.5 * (1.0 + lax.erf(hidden * ROOT_HALF))
        activated = (hidden * bend).astype(BF16)
        act_ref[t] = activated
        slope[slot] = bend + hidden * INV_ROOT_TAU * jnp.exp2(hidden * hidden * (-0.5 * LOG2E))
        arrive(2, slot)
        return branch + dot(activated, w_up[slot], NT)

    branch = lax.fori_loop(0, parts, up, jnp.zeros(in_ref.shape, F32))
    layer_rows, normed_two, inverse_two = norm_forward(first.astype(F32) + branch + vec(3), vec(4), vec(5))
    layer_ref[...] = layer_rows.astype(BF16)
    misfit = layer_rows - teacher_ref[...].astype(F32)
    weighted = valid_ref[...] * misfit
    out_grad = cotangent_ref[...].astype(F32) + weighted * ratio_ref[0]
    second_grad = norm_backward(out_grad, normed_two, inverse_two, vec(4))
    branch_grad = second_grad.astype(BF16)
    branch_grad_ref[...] = branch_grad
    sums_ref[0:1, :] = column_sum(weighted * misfit)
    sums_ref[1:2, :] = column_sum(branch_grad.astype(F32))
    sums_ref[2:3, :] = column_sum(out_grad * normed_two)
    sums_ref[3:4, :] = column_sum(out_grad)

    def down(slot, back):
        t = place_ref[slot]
        hidden_grad = (dot(branch_grad, w_up[slot]) * slope[slot]).astype(BF16)
        hidden_grad_ref[t] = hidden_grad
        inner_sums_ref[t] = column_sum(hidden_grad.astype(F32))
        return back + dot(hidden_grad, w_in[slot], NT)

    upstream = lax.fori_loop(0, parts, down, second_grad)
    first_grad = norm_backward(upstream, normed_one, inverse_one, vec(1))
    first_grad_ref[...] = first_grad
    attn_grad = first_grad.astype(BF16)
    attn_grad_ref[...] = attn_grad
    sums_ref[4:5, :] = column_sum(attn_grad.astype(F32))
    sums_ref[5:6, :] = column_sum(upstream * normed_one)
    sums_ref[6:7, :] = column_sum(upstream)
    sums_ref[7:8, :] = jnp.zeros_like(sums_ref[7:8, :])
    middle = BLOCK // 2
    for slot in range(parts):
        back = dot(attn_grad, w_out[slot, :, : 3 * DH]).astype(BF16)
        ctx_grad_ref[place_ref[slot]] = pack(
            back[:, : 2 * DH], back[:middle, 2 * DH :], back[middle:, 2 * DH :]
        )


def run_dense(half, marks, place, ratio, ctx, rows_in, teacher, cotangent, valid, vecs, inner_bias, pieces):
    parts = ctx.shape[0]
    width = rows_in.shape[1]
    hidden_cols = inner_bias.shape[2]
    out_cols = pieces[0].shape[2] - 2 * hidden_cols

    def mine(columns):
        return pl.BlockSpec((BLOCK, columns), lambda i: (half, 0))

    def fixed(shape):
        return pl.BlockSpec(shape, lambda i: (0,) * len(shape))

    low = jax.ShapeDtypeStruct((BLOCK, width), BF16)
    out_shape = (
        low,
        jax.ShapeDtypeStruct((BLOCK, width), F32),
        jax.ShapeDtypeStruct(ctx.shape, BF16),
        low,
        low,
        low,
        jax.ShapeDtypeStruct((parts, BLOCK, hidden_cols), BF16),
        jax.ShapeDtypeStruct((parts, BLOCK, hidden_cols), BF16),
        jax.ShapeDtypeStruct((8, width), F32),
        jax.ShapeDtypeStruct((parts, 1, hidden_cols), F32),
    )
    smem = pl.BlockSpec(memory_space=pltpu.SMEM)
    return pl.pallas_call(
        functools.partial(dense_chain, marks),
        out_shape=out_shape,
        grid=(1,),
        in_specs=[
            smem,
            smem,
            fixed(ctx.shape),
            mine(width),
            fixed(teacher.shape),
            fixed(cotangent.shape),
            mine(1),
            fixed(vecs.shape),
            fixed(inner_bias.shape),
        ]
        + [pl.BlockSpec(memory_space=pl.ANY)] * len(pieces),
        out_specs=tuple(fixed(out.shape) for out in out_shape),
        scratch_shapes=[
            pltpu.VMEM((parts, width, out_cols), BF16),
            pltpu.VMEM((parts, width, hidden_cols), BF16),
            pltpu.VMEM((parts, width, hidden_cols), BF16),
            pltpu.VMEM((parts, BLOCK, hidden_cols), F32),
            pltpu.SemaphoreType.DMA((3, parts)),
        ],
        compiler_params=pltpu.CompilerParams(
            dimension_semantics=("arbitrary",), vmem_limit_bytes=VMEM_LIMIT
        ),
        cost_estimate=pl.CostEstimate(
            flops=BLOCK * width * (8 * hidden_cols + 4 * out_cols) * parts,
            bytes_accessed=18 << 20,
            transcendentals=2 * BLOCK * hidden_cols * parts,
        ),
        name="dense_chain",
    )(place, ratio, ctx, rows_in, teacher, cotangent, valid, vecs, inner_bias, *pieces)


def dense_weights(turns, halves, place_ref, *refs):
    firsts, branch_grads, attn_grads, acts, hidden_grads, ctxs = (
        refs[k * halves : (k + 1) * halves] for k in range(6)
    )
    notes_ref, outs = refs[6 * halves], refs[6 * halves + 1 : -3]
    turned, whole, sems = refs[-3:]
    step = pl.program_id(0)
    slots = whole.shape[0]
    teams = len(outs) // len(turns)
    each = slots // teams

    @pl.when(step == 0)
    def _():
        for which, sources in enumerate((firsts, branch_grads, attn_grads)):
            for half, source in enumerate(sources):
                turned[which, :, half * BLOCK : (half + 1) * BLOCK] = jnp.transpose(source[...])

    def both(sources):
        return jnp.concatenate([source[0] for source in sources], axis=0)

    hidden_cols = acts[0].shape[2]
    whole[step, :, :hidden_cols] = dot(turned[0], both(hidden_grads)).astype(BF16)
    whole[step, :, hidden_cols : 2 * hidden_cols] = dot(turned[1], both(acts)).astype(BF16)
    ctx = jnp.concatenate([unpack(source[0]) for source in ctxs], axis=0)
    plain = 2 * hidden_cols + ctx.shape[1]
    whole[step, :, 2 * hidden_cols : plain] = dot(turned[2], ctx).astype(BF16)
    whole[step, :, plain : plain + notes_ref.shape[1]] = notes_ref[...]
    for team in range(teams):

        @pl.when(step // each == team)
        def _():
            for out, orders in zip(outs[team * len(turns) : (team + 1) * len(turns)], turns):
                block = out.shape[1]
                for at, turn in enumerate(orders[team]):
                    offset = pl.multiple_of((place_ref[slots] ^ turn) * block, block)
                    pltpu.make_async_copy(
                        whole.at[step, pl.ds(offset, block), :],
                        out.at[at * each + step - team * each],
                        sems.at[step],
                    ).start()

    @pl.when(step == slots - 1)
    def _():
        for slot in range(slots):
            pltpu.make_async_copy(whole.at[slot], whole.at[slot], sems.at[slot]).wait()


def run_weights(turns, teams, block, place, notes, firsts, branch_grads, attn_grads, acts, hidden_grads, ctxs):
    parts, _, hidden_cols = acts[0].shape
    halves = len(acts)
    width = firsts[0].shape[1]
    columns = 2 * hidden_cols + 3 * DH + notes.shape[1]

    def by_slot(rows, size):
        return pl.BlockSpec((1, rows, size), lambda s, place: (place[s], 0, 0))

    fixed = pl.BlockSpec((BLOCK, width), lambda s, place: (0, 0))
    outs = tuple(
        jax.ShapeDtypeStruct((len(orders[0]) * parts // teams, block, columns), BF16) for orders in turns
    ) * teams
    return pl.pallas_call(
        functools.partial(dense_weights, turns, halves),
        out_shape=outs,
        grid_spec=pltpu.PrefetchScalarGridSpec(
            num_scalar_prefetch=1,
            grid=(parts,),
            in_specs=[fixed] * (3 * halves)
            + [by_slot(BLOCK, hidden_cols)] * (2 * halves)
            + [by_slot(PACKED, 2 * DH)] * halves
            + [pl.BlockSpec(notes.shape, lambda s, place: (0, 0))],
            out_specs=tuple(pl.BlockSpec(memory_space=pl.ANY) for _ in outs),
            scratch_shapes=[
                pltpu.VMEM((3, width, halves * BLOCK), BF16),
                pltpu.VMEM((parts, width, columns), BF16),
                pltpu.SemaphoreType.DMA((parts,)),
            ],
        ),
        compiler_params=pltpu.CompilerParams(
            dimension_semantics=("arbitrary",), vmem_limit_bytes=VMEM_LIMIT
        ),
        cost_estimate=pl.CostEstimate(
            flops=2 * halves * BLOCK * width * columns * parts,
            bytes_accessed=20 << 20,
            transcendentals=0,
        ),
        name="dense_weights",
    )(place, *firsts, *branch_grads, *attn_grads, *acts, *hidden_grads, *ctxs, notes)


def finish_dense(packed_ref, inner_ref, outer_ref, output_ref, notes_ref):
    hidden_cols = inner_ref.shape[1]
    summed = packed_ref[...].astype(F32)
    inner_ref[...] = summed[:, :hidden_cols]
    outer_ref[...] = summed[:, hidden_cols : 2 * hidden_cols]
    plain = 2 * hidden_cols + output_ref.shape[0]
    output_ref[...] = jnp.transpose(summed[:, 2 * hidden_cols : plain])
    notes_ref[...] = summed[:, plain:]


def run_finish_dense(packed, hidden_cols, head_cols):
    rows = packed.shape[0]
    return pl.pallas_call(
        finish_dense,
        out_shape=(
            jax.ShapeDtypeStruct((rows, hidden_cols), F32),
            jax.ShapeDtypeStruct((rows, hidden_cols), F32),
            jax.ShapeDtypeStruct((head_cols, rows), F32),
            jax.ShapeDtypeStruct((rows, packed.shape[1] - 2 * hidden_cols - head_cols), F32),
        ),
        name="finish_dense",
    )(packed)


def finish_heads(value_ref, *refs):
    summed = value_ref[...].astype(F32)
    heads = summed.shape[1] // SLAB
    for ref, which in zip(refs, (0, 2, 3, 1)):
        columns = [summed[:, SLAB * h + which * DH : SLAB * h + (which + 1) * DH] for h in range(heads)]
        ref[...] = jnp.concatenate(columns, axis=1)[: ref.shape[0]]


def run_finish_heads(value):
    rows, width = value.shape
    out = jax.ShapeDtypeStruct((rows, width // 4), F32)
    notes = jax.ShapeDtypeStruct((8, width // 4), F32)
    return pl.pallas_call(finish_heads, out_shape=(out, out, out, notes), name="finish_heads")(value)


def interleave(query, key, value, heads):
    rows = query.shape[0]
    parts = [part.reshape(rows, heads, 1, DH) for part in (query, jnp.zeros_like(query), key, value)]
    return jnp.concatenate(parts, axis=2).reshape(rows, heads * SLAB)


def swap(value, axis, bit):
    size = lax.axis_size(axis)
    return lax.ppermute(value, axis, [(i, i ^ bit) for i in range(size)])


def bits_of(axis):
    bit = 1
    while bit < lax.axis_size(axis):
        yield bit
        bit *= 2


def after(value, *others):
    return lax.optimization_barrier((value,) + others)[0]


def merge(held, other, axis, bit):
    mine_first = (lax.axis_index(axis) & bit) == 0
    return jnp.where(
        mine_first, jnp.concatenate([held, other], axis=0), jnp.concatenate([other, held], axis=0)
    )


def add_low(left_side, right_side):
    return (left_side.astype(F32) + right_side.astype(F32)).astype(BF16)


def halve(held, axis, bit):
    own = (lax.axis_index(axis) & bit) // bit
    half = held.shape[0] // 2
    keep = lax.dynamic_slice_in_dim(held, own * half, half, 0)
    send = lax.dynamic_slice_in_dim(held, (1 - own) * half, half, 0)
    return (keep, swap(send, axis, bit))


PLANE = (0, 3, 1, 2)
ORIGIN = (0, 2, 3, 1)
AWAY = [(lo * 4 + z, z * 4 + PLANE[lo]) for lo in range(4) for z in range(4)]
BACK = [(there, here) for here, there in AWAY]


def send_away(value):
    return lax.ppermute(value, ("lo", "tensor"), AWAY)


def send_back(value):
    return lax.ppermute(value, ("lo", "tensor"), BACK)


def local(
    inputs, segment_ids, valid_mask, teacher, cotangent,
    w_query, w_key, w_value, w_output, w_inner, w_outer,
    query_bias, value_bias, output_bias, inner_bias, outer_bias,
    gain_attn, shift_attn, gain_ffn, shift_ffn,
):
    _, part_len, width = inputs.shape
    parts = lax.axis_size("tensor")
    copies = lax.axis_size("hi") * lax.axis_size("lo")
    lane_index = lax.axis_index("lo")
    total_tokens = part_len * parts * copies
    seq_len = part_len * parts
    head_cols = w_query.shape[1]
    heads = head_cols // DH
    hidden_cols = w_inner.shape[1]
    shard_rows = w_inner.shape[0]
    halves = part_len // BLOCK

    rows_in = send_away(inputs.reshape(part_len, width))
    head_rows = send_away(interleave(w_query, w_key, w_value, heads))
    whole_row = jnp.concatenate((segment_ids.reshape(seq_len), valid_mask.reshape(part_len)))
    whole_row = send_away(whole_row.reshape(-1, 128)).reshape(-1)
    valid_count = jnp.sum(valid_mask.astype(F32))
    upper = jnp.floor(valid_count / 256.0)
    count_row = jnp.zeros((shard_rows, DH), BF16)
    count_row = count_row.at[0, 0].set(upper.astype(BF16)).at[0, 1].set((valid_count - 256.0 * upper).astype(BF16))
    mine = jnp.concatenate((w_inner, w_outer.T, w_output.T, count_row), axis=1)
    weights = lax.all_gather(mine, ("tensor", "hi", "lo"), axis=0, tiled=False)
    counts = weights[:, 0, -DH : 2 - DH].astype(F32)
    counted = 256.0 * jnp.sum(counts[:, 0]) + jnp.sum(counts[:, 1])
    ratio = (total_tokens / counted).reshape(1)
    pieces = [weights.reshape(parts, width, -1)]
    marks = [[(t, 0) for t in range(parts)]]
    place = jnp.asarray(list(range(parts)) + [0], jnp.int32)

    head_rows = merge(head_rows, swap(head_rows, "tensor", 1), "tensor", 1)
    head_rows = after(head_rows, rows_in)
    near_chunk = swap(rows_in, "lo", 1)
    next_chunk = swap(rows_in, "lo", 2)
    head_rows = merge(head_rows, swap(head_rows, "tensor", 2), "tensor", 2)
    head_rows = after(head_rows, next_chunk)
    far_chunk = swap(next_chunk, "lo", 1)
    blocks = head_rows.reshape(4, shard_rows, -1)
    w_heads = jnp.concatenate([blocks[plane] for plane in PLANE], axis=0)
    for bit in bits_of("hi"):
        w_heads = merge(w_heads, swap(w_heads, "hi", bit), "hi", bit)
    tokens = [rows_in, next_chunk, near_chunk, far_chunk]

    mine_cols = lane_index * head_cols
    query_shift = lax.dynamic_slice_in_dim(query_bias, mine_cols, head_cols).astype(F32)
    value_shift = lax.dynamic_slice_in_dim(value_bias, mine_cols, head_cols).astype(F32)
    shifts = interleave(query_shift[None], jnp.zeros_like(query_shift)[None], value_shift[None], heads)
    qkv = [(dot(chunk, w_heads) + shifts).astype(BF16) for chunk in tokens]

    def half_of(value, half):
        return value.reshape(part_len, width)[half * BLOCK : (half + 1) * BLOCK]

    sides = []
    for half in range(halves):
        sides.append([send_away(after(half_of(value, half), w_heads)) for value in (teacher, cotangent)])

    segment_row = whole_row[:seq_len]
    valid_rows = whole_row[seq_len:].astype(F32).reshape(part_len, 1)
    bounds = document_blocks(segment_row)
    seg_col = segment_row.reshape(seq_len, 1)
    seg_row = segment_row.reshape(1, seq_len)
    lane = lane_index.astype(jnp.int32).reshape(1)

    def exchange(packed_blocks):
        return lax.all_to_all(packed_blocks, "lo", 0, 0)

    contexts, lses, arrived = [], [], []
    for half in range(halves):
        context, lse = run_forward((halves, half), lane, bounds, qkv, seg_col, seg_row)
        contexts.append(context)
        lses.append(lse)
        arrived.append(exchange(context))

    vecs = jnp.stack(
        (output_bias, gain_attn, shift_attn, outer_bias, gain_ffn, shift_ffn, outer_bias, outer_bias)
    ).astype(F32)
    inner_rows = inner_bias.astype(F32).reshape(parts, 1, hidden_cols)
    chains = [
        run_dense(
            half, marks, place, ratio, arrived[half], rows_in, *sides[half],
            valid_rows, vecs, inner_rows, pieces,
        )
        for half in range(halves)
    ]
    (
        layers, first_grads, context_grads, firsts, branch_grads, attn_grads, acts, hidden_grads,
        dense_sums, inner_sums,
    ) = zip(*chains)
    head_grads = [exchange(context_grad) for context_grad in context_grads]
    dense_sums = sum(dense_sums)
    inner_sums = sum(inner_sums)
    sources = (firsts, branch_grads, attn_grads, acts, hidden_grads, arrived)
    head_grads[:-1], sources = lax.optimization_barrier((head_grads[:-1], sources))
    notes = jnp.concatenate((dense_sums.reshape(-1), inner_sums.reshape(-1))).astype(BF16)
    room = -(-notes.shape[0] // (shard_rows * 128)) * 128
    notes = jnp.pad(notes, (0, shard_rows * room - notes.shape[0])).reshape(shard_rows, room)
    (packed,) = run_weights(([[0]],), 1, width, place, jnp.tile(notes, (copies, 1)), *sources)
    packed = lax.psum_scatter(packed, ("hi", "lo"), scatter_dimension=1, tiled=True)
    layer_out = send_back(jnp.concatenate(layers, axis=0))

    earlier, before = [], []
    for half in range(halves):
        if half == halves - 1:
            layer_out, before = lax.optimization_barrier((layer_out, before))
        results = run_backward(
            (halves, half), lane, bounds, qkv, seg_col, seg_row, contexts[half], head_grads[half],
            lses[half], earlier, before,
        )
        if half < halves - 1:
            before, earlier = [results[0]], earlier + [results[1]]
    joined_grad, sums = results
    joined_grad = joined_grad.reshape(seq_len, width)
    middle = seq_len // 2
    core_share = swap(dot(joined_grad[middle:], w_heads, NT).astype(BF16), "lo", 1)
    sums = sums.reshape(heads, 4, DH)
    sums = jnp.concatenate((sums[:, 0].reshape(1, head_cols), sums[:, 3].reshape(1, head_cols)), axis=1)
    core_share, sums = lax.optimization_barrier((core_share, sums))
    sums = merge(sums, swap(sums, "lo", 1), "lo", 1)
    own_share = dot(joined_grad[:middle], w_heads, NT)
    own_share, joined_grad = lax.optimization_barrier((own_share, joined_grad))
    input_share = own_share + core_share.astype(F32)
    chip_share = swap(input_share[part_len:].astype(BF16), "lo", 2)
    sums = merge(sums, swap(sums, "lo", 2), "lo", 2)
    head_weights = dot(jnp.concatenate(tokens, axis=0), joined_grad, TN)
    biases = jnp.concatenate((sums[:, :head_cols].reshape(-1), sums[:, head_cols:].reshape(-1)))
    biases = jnp.pad(
        biases.reshape(8, heads, 1, DH), ((0, shard_rows - 8), (0, 0), (1, 2), (0, 0))
    ).reshape(1, shard_rows, -1)
    head_weights = (head_weights.reshape((copies, shard_rows, -1)) + biases).astype(BF16)
    chip_share, held = lax.optimization_barrier((chip_share, head_weights))
    for bit in reversed(list(bits_of("hi"))):
        held = add_low(*halve(held, "hi", bit))
    input_grad = input_share[:part_len] + chip_share.astype(F32) + jnp.concatenate(first_grads, axis=0)
    input_grad, held = lax.optimization_barrier((input_grad.astype(BF16), held))
    packed = after(packed, input_grad)
    packed = lax.psum_scatter(packed, "tensor", scatter_dimension=0, tiled=True)[0]
    input_grad = send_back(input_grad).astype(F32)
    held = jnp.stack([held[origin] for origin in ORIGIN])
    held = add_low(*halve(held, "tensor", 2))
    held = add_low(*halve(held, "tensor", 1))
    query_grad, key_grad, value_grad, biases = run_finish_heads(send_back(held[0]))
    biases = biases.reshape(2, width)

    inner_grad, outer_grad, output_grad, notes = run_finish_dense(packed, hidden_cols, head_cols)
    notes = notes.reshape(-1)

    def total(which):
        return notes[which * width : (which + 1) * width]

    mse_loss = jnp.sum(total(0)) / (counted * width)
    return (
        layer_out.reshape(1, part_len, width),
        mse_loss,
        input_grad.reshape(1, part_len, width),
        query_grad,
        key_grad,
        value_grad,
        output_grad,
        inner_grad,
        outer_grad.T,
        biases[0],
        biases[1],
        total(4),
        notes[8 * width : 8 * width + hidden_cols * parts],
        total(1),
        total(5),
        total(6),
        total(2),
        total(3),
    )


def solution(mesh):
    devices = mesh.devices
    groups = devices.shape[0] // 4
    finer = jax.sharding.Mesh(
        devices.reshape((groups, 4) + devices.shape[1:]), ("hi", "lo", "tensor")
    )
    split = ("hi", "lo")
    shard = P(split, "tensor", None)
    by_dp, by_tensor = P(split, "tensor"), P("tensor", split)
    in_specs = (
        (shard, P(split, None), by_dp, shard, shard)
        + (by_dp,) * 3
        + (by_tensor, by_dp, by_tensor)
        + (P(),) * 9
    )
    out_specs = (shard, P(), shard) + (by_dp,) * 3 + (by_tensor, by_dp, by_tensor) + (P(),) * 9
    return jax.shard_map(local, mesh=finer, in_specs=in_specs, out_specs=out_specs, check_vma=False)
```

```python
import functools

import jax
import jax.numpy as jnp
from jax import lax
from jax.experimental import pallas as pl
from jax.experimental.pallas import tpu as pltpu
from jax.sharding import PartitionSpec as P

DH = 64
BLOCK = 256
SLAB = 4 * DH
EPSILON = 1e-12
ROOT_HALF = 0.7071067811865476
INV_ROOT_TAU = 0.3989422804014327
LOG2E = 1.4426950408889634
LN2 = 0.6931471805599453
SCALE = DH ** (-0.5)
MASKED = -1e30
VMEM_LIMIT = 60 << 20

BF16 = jnp.bfloat16
F32 = jnp.float32
NN = (((1,), (0,)), ((), ()))
NT = (((1,), (1,)), ((), ()))
TN = (((0,), (0,)), ((), ()))


def dot(left_side, right_side, dims=NN):
    return lax.dot_general(left_side, right_side, dims, preferred_element_type=F32)


def norm_forward(summed, gain_vec, shift_vec):
    average = jnp.mean(summed, axis=-1, keepdims=True)
    centered = summed - average
    variance = jnp.mean(centered * centered, axis=-1, keepdims=True)
    inverse = lax.rsqrt(variance + EPSILON)
    normed = centered * inverse
    return (normed * gain_vec + shift_vec, normed, inverse)


def norm_backward(upstream, normed, inverse, gain_vec):
    scaled = upstream * gain_vec
    first_mean = jnp.mean(scaled, axis=-1, keepdims=True)
    second_mean = jnp.mean(scaled * normed, axis=-1, keepdims=True)
    return inverse * (scaled - first_mean - normed * second_mean)


def column_sum(value):
    return jnp.sum(value, axis=0, keepdims=True)


def lane_is_right(rows):
    return lax.broadcasted_iota(jnp.int32, (rows, 2 * DH), 1) >= DH


def pack(first_two, third_top, third_bottom):
    return jnp.concatenate([first_two, jnp.concatenate([third_top, third_bottom], axis=1)], axis=0)


def unpack(packed):
    third = packed[BLOCK:]
    third = jnp.concatenate([third[:, :DH], third[:, DH:]], axis=0)
    return jnp.concatenate([packed[:BLOCK], third], axis=1)


def fetch_chunks(lane_ref, chunk_refs, target, sems):
    rows = chunk_refs[0].shape[0]
    copies = []
    for at, chunk in enumerate(chunk_refs):
        offset = pl.multiple_of(lax.rem(lane_ref[0] + at, len(chunk_refs)) * rows, rows)
        copies.append(pltpu.make_async_copy(chunk, target.at[pl.ds(offset, rows), :], sems.at[at]))
    return copies


def attend_forward(
    which, lane_ref, low_ref, high_ref, *refs
):
    chunk_refs, (seg_col_ref, seg_row_ref, ctx_ref, lse_ref, held, qkv_ref, sems) = refs[:4], refs[4:]
    halves, half = which
    heads = lse_ref.shape[0]

    @pl.when(pl.program_id(0) == 0)
    def _():
        copies = fetch_chunks(lane_ref, chunk_refs, qkv_ref, sems)
        for copy in copies:
            copy.start()
        for copy in copies:
            copy.wait()

    qb = pl.program_id(0) * halves + half
    rows = pl.ds(pl.multiple_of(qb * BLOCK, BLOCK), BLOCK)
    seg_q = seg_col_ref[...]
    queries = [
        qkv_ref[rows, SLAB * h : SLAB * h + 2 * DH] * jnp.asarray(SCALE, BF16) for h in range(heads)
    ]
    low, high = low_ref[qb], high_ref[qb]

    def score(kb, peaks):
        keys = pl.ds(pl.multiple_of(kb * BLOCK, BLOCK), BLOCK)
        allowed = seg_q == seg_row_ref[:, keys]
        found = []
        for h in range(heads):
            scores = dot(queries[h], qkv_ref[keys, SLAB * h + 2 * DH : SLAB * (h + 1)], NT)
            scores = jnp.where(allowed, scores, MASKED)
            held[h, kb] = scores
            found.append(jnp.maximum(peaks[h], jnp.maximum(scores[:, :128], scores[:, 128:])))
        return tuple(found)

    start = tuple(jnp.full((BLOCK, 128), MASKED, F32) for _ in range(heads))
    peaks = lax.fori_loop(low, high, score, start)
    highest = [jnp.max(peak, axis=-1, keepdims=True) for peak in peaks]

    def weigh(kb, carry):
        keys = pl.ds(pl.multiple_of(kb * BLOCK, BLOCK), BLOCK)
        found = []
        for h in range(heads):
            total, acc = carry[h]
            raised = jnp.exp2((held[h, kb] - highest[h]) * LOG2E)
            total = total + (raised[:, :128] + raised[:, 128:])
            acc = acc + dot(raised.astype(BF16), qkv_ref[keys, SLAB * h + 2 * DH : SLAB * (h + 1)])
            found.append((total, acc))
        return tuple(found)

    zero = jnp.zeros((BLOCK, 128), F32)
    done = lax.fori_loop(low, high, weigh, tuple((zero, zero) for _ in range(heads)))
    values = []
    for h in range(heads):
        total, acc = done[h]
        summed = jnp.sum(total, axis=-1, keepdims=True)
        values.append((acc / summed).astype(BF16))
        lse_ref[h] = jnp.transpose(highest[h] + jnp.log(summed))
    middle = BLOCK // 2
    ctx_ref[0, :BLOCK, :] = jnp.where(lane_is_right(BLOCK), values[1], pltpu.roll(values[0], DH, 1))
    ctx_ref[0, BLOCK:, :] = jnp.where(
        lane_is_right(middle), values[2][middle:], pltpu.roll(values[2][:middle], DH, 1)
    )


def attend_backward(which, lane_ref, low_ref, high_ref, *refs):
    halves, half = which
    last = half == halves - 1
    chunk_refs, refs = refs[:4], refs[4:]
    (seg_col_ref, seg_row_ref, ctx_ref, grad_ref, lse_ref), refs = refs[:5], refs[5:]
    earlier, refs = refs[:half], refs[half:]
    if half > 0:
        before_ref, refs = refs[0], refs[1:]
    if last:
        final_ref, sums_ref, dkv, out_ref, qkv_ref, sems = refs
    else:
        dkv, query_ref, qkv_ref, sems = refs
    heads = dkv.shape[0]
    step_index = pl.program_id(0)
    qb = step_index * halves + half

    @pl.when(step_index == 0)
    def _():
        copies = fetch_chunks(lane_ref, chunk_refs, qkv_ref, sems)
        for copy in copies:
            copy.start()
        dkv[...] = before_ref[...] if half > 0 else jnp.zeros_like(dkv)
        for copy in copies:
            copy.wait()

    rows = pl.ds(pl.multiple_of(qb * BLOCK, BLOCK), BLOCK)
    right = lane_is_right(BLOCK)
    arrived = grad_ref[0]
    product = arrived.astype(F32) * ctx_ref[0].astype(F32)
    upper = product.astype(BF16)
    lower = (product - upper.astype(F32)).astype(BF16)
    pick = (
        lax.broadcasted_iota(jnp.int32, (8, 2 * DH), 1) // DH
        == lax.broadcasted_iota(jnp.int32, (8, 2 * DH), 0)
    ).astype(BF16)
    summed = dot(pick, upper, NT) + dot(pick, lower, NT)
    deltas = [
        summed[0:1, :BLOCK],
        summed[1:2, :BLOCK],
        jnp.concatenate([summed[0:1, BLOCK:], summed[1:2, BLOCK:]], axis=1),
    ]
    two, third = arrived[:BLOCK], arrived[BLOCK:]
    placed = [
        pltpu.roll(two, DH, 1),
        two,
        jnp.concatenate([pltpu.roll(third, DH, 1), third], axis=0),
    ]
    grads = [jnp.where(right, grad, jnp.zeros_like(grad)) for grad in placed]
    queries, pairs = [], []
    for h in range(heads):
        queries.append(qkv_ref[rows, SLAB * h : SLAB * h + 2 * DH] * jnp.asarray(SCALE, BF16))
        pairs.append(jnp.concatenate([queries[h], grads[h]], axis=0))
    seg_q = seg_row_ref[...]
    lses = lse_ref[...]
    low, high = low_ref[qb], high_ref[qb]

    def step(kb, accs):
        keys = pl.ds(pl.multiple_of(kb * BLOCK, BLOCK), BLOCK)
        allowed = seg_col_ref[keys, :] == seg_q
        found = []
        for h in range(heads):
            pair = qkv_ref[keys, SLAB * h + 2 * DH : SLAB * (h + 1)]
            scores = jnp.where(allowed, dot(pair, queries[h], NT), MASKED)
            probs = jnp.exp2((scores - lses[h]) * LOG2E)
            score_grad = (probs * (dot(pair, grads[h], NT) - deltas[h])).astype(BF16)
            both = jnp.concatenate([score_grad, probs.astype(BF16)], axis=1)
            dkv[h, keys, :] += dot(both, pairs[h])
            found.append(accs[h] + dot(score_grad, pair, TN))
        return tuple(found)

    zero = jnp.zeros((BLOCK, 128), F32)
    accs = lax.fori_loop(low, high, step, tuple(zero for _ in range(heads)))
    for h in range(heads):
        query_grad = jnp.where(right, 0.0, accs[h] * SCALE).astype(BF16)
        if last:
            out_ref[rows, SLAB * h : SLAB * h + 2 * DH] = query_grad
        else:
            query_ref[0, :, 2 * DH * h : 2 * DH * (h + 1)] = query_grad

    if last:

        @pl.when(step_index == pl.num_programs(0) - 1)
        def _():
            for h in range(heads):
                at = SLAB * h
                for other, ref in enumerate(earlier):
                    for block in range(ref.shape[0]):
                        start = (block * halves + other) * BLOCK
                        out_ref[start : start + BLOCK, at : at + 2 * DH] = ref[
                            block, :, 2 * DH * h : 2 * DH * (h + 1)
                        ]
                out_ref[:, at + 2 * DH : at + SLAB] = dkv[h].astype(BF16)
                sums_ref[:, at : at + SLAB] = column_sum(out_ref[:, at : at + SLAB].astype(F32))
            rows_each = final_ref.shape[1]
            copies = []
            for at in range(final_ref.shape[0]):
                offset = pl.multiple_of(lax.rem(lane_ref[0] + at, final_ref.shape[0]) * rows_each, rows_each)
                copies.append(
                    pltpu.make_async_copy(
                        out_ref.at[pl.ds(offset, rows_each), :], final_ref.at[at], sems.at[at]
                    )
                )
            for copy in copies:
                copy.start()
            for copy in copies:
                copy.wait()


def document_blocks(segment_row):
    starts = segment_row[::BLOCK]
    stops = segment_row[BLOCK - 1 :: BLOCK]
    low = jnp.sum((segment_row[None, :] < starts[:, None]).astype(jnp.int32), axis=1)
    high = jnp.sum((segment_row[None, :] <= stops[:, None]).astype(jnp.int32), axis=1)
    return (low // BLOCK, (high + BLOCK - 1) // BLOCK)


PACKED = BLOCK + BLOCK // 2


def run_forward(which, lane, bounds, qkv, seg_col, seg_row):
    halves, half = which
    seq_len, width = seg_col.shape[0], qkv[0].shape[1]
    heads = width // SLAB
    blocks = seq_len // BLOCK
    steps = blocks // halves
    return pl.pallas_call(
        functools.partial(attend_forward, which),
        out_shape=(
            jax.ShapeDtypeStruct((steps, PACKED, 2 * DH), BF16),
            jax.ShapeDtypeStruct((heads, 1, steps * BLOCK), F32),
        ),
        grid_spec=pltpu.PrefetchScalarGridSpec(
            num_scalar_prefetch=3,
            grid=(steps,),
            in_specs=[pl.BlockSpec(memory_space=pl.ANY)] * 4
            + [
                pl.BlockSpec((BLOCK, 1), lambda q, *_: (q * halves + half, 0)),
                pl.BlockSpec((1, seq_len), lambda q, *_: (0, 0)),
            ],
            out_specs=(
                pl.BlockSpec((1, PACKED, 2 * DH), lambda q, *_: (q, 0, 0)),
                pl.BlockSpec((heads, 1, BLOCK), lambda q, *_: (0, 0, q)),
            ),
            scratch_shapes=[
                pltpu.VMEM((heads, blocks, BLOCK, BLOCK), F32),
                pltpu.VMEM((seq_len, width), BF16),
                pltpu.SemaphoreType.DMA((4,)),
            ],
        ),
        compiler_params=pltpu.CompilerParams(
            dimension_semantics=("arbitrary",), vmem_limit_bytes=VMEM_LIMIT
        ),
        cost_estimate=pl.CostEstimate(
            flops=heads * seq_len * seq_len * 256 // halves,
            bytes_accessed=5 << 20,
            transcendentals=heads * seq_len * seq_len // 3 // halves,
        ),
        name="attend_forward",
    )(lane, *bounds, *qkv, seg_col, seg_row)


def run_backward(which, lane, bounds, qkv, seg_col, seg_row, ctx, grad, lse, earlier, before):
    halves, half = which
    seq_len, width = seg_col.shape[0], qkv[0].shape[1]
    heads = width // SLAB
    steps = seq_len // BLOCK // halves
    packed = pl.BlockSpec((1, PACKED, 2 * DH), lambda q, *_: (q, 0, 0))

    def fixed(shape, **more):
        return pl.BlockSpec(shape, lambda q, *_: (0,) * len(shape), **more)

    once = {"pipeline_mode": pl.Buffered(1)}
    gathered = (heads, seq_len, 2 * DH)
    carried = [fixed(value.shape, **once) for value in earlier]
    carried += [fixed(gathered, **once)] * len(before)
    scratch = [pltpu.VMEM((seq_len, width), BF16), pltpu.SemaphoreType.DMA((4,))]
    if half == halves - 1:
        out_shape = (
            jax.ShapeDtypeStruct((4, seq_len // 4, width), BF16),
            jax.ShapeDtypeStruct((1, width), F32),
        )
        out_specs = (pl.BlockSpec(memory_space=pl.ANY), fixed((1, width)))
        scratch = [pltpu.VMEM(gathered, F32), pltpu.VMEM((seq_len, width), BF16)] + scratch
    else:
        out_shape = (
            jax.ShapeDtypeStruct(gathered, F32),
            jax.ShapeDtypeStruct((steps, BLOCK, heads * 2 * DH), BF16),
        )
        out_specs = (
            fixed(gathered),
            pl.BlockSpec((1, BLOCK, heads * 2 * DH), lambda q, *_: (q, 0, 0)),
        )
    return pl.pallas_call(
        functools.partial(attend_backward, which),
        out_shape=out_shape,
        grid_spec=pltpu.PrefetchScalarGridSpec(
            num_scalar_prefetch=3,
            grid=(steps,),
            in_specs=[pl.BlockSpec(memory_space=pl.ANY)] * 4
            + [
                fixed((seq_len, 1)),
                pl.BlockSpec((1, BLOCK), lambda q, *_: (0, q * halves + half)),
                packed,
                packed,
                pl.BlockSpec((heads, 1, BLOCK), lambda q, *_: (0, 0, q)),
            ]
            + carried,
            out_specs=out_specs,
            scratch_shapes=scratch,
        ),
        compiler_params=pltpu.CompilerParams(
            dimension_semantics=("arbitrary",), vmem_limit_bytes=VMEM_LIMIT
        ),
        cost_estimate=pl.CostEstimate(
            flops=heads * seq_len * seq_len * 640 // halves,
            bytes_accessed=10 << 20,
            transcendentals=heads * seq_len * seq_len // 3 // halves,
        ),
        name="attend_backward",
    )(lane, *bounds, *qkv, seg_col, seg_row, ctx, grad, lse, *earlier, *before)


def dense_chain(
    marks, place_ref, ratio_ref, ctx_ref, in_ref, teacher_ref, cotangent_ref, valid_ref, vec_ref,
    inner_bias_ref, *refs
):
    pieces = refs[: len(marks)]
    (
        layer_ref, first_grad_ref, ctx_grad_ref, first_ref, branch_grad_ref, attn_grad_ref,
        act_ref, hidden_grad_ref, sums_ref, inner_sums_ref, w_out, w_in, w_up, slope, sems,
    ) = refs[len(marks) :]
    parts, _, head_cols = w_out.shape
    hidden_cols = w_in.shape[2]
    index = place_ref[parts]
    groups = (
        (2 * hidden_cols, head_cols, w_out),
        (0, hidden_cols, w_in),
        (hidden_cols, hidden_cols, w_up),
    )
    for group, (start, size, target) in enumerate(groups):
        for piece, marked in zip(pieces, marks):
            block = piece.shape[1]
            for at, (slot, turn) in enumerate(marked):
                offset = pl.multiple_of((index ^ turn) * block, block)
                pltpu.make_async_copy(
                    piece.at[at, :, pl.ds(start, size)],
                    target.at[slot, pl.ds(offset, block), :],
                    sems.at[group, slot],
                ).start()

    def arrive(group, slot):
        whole = groups[group][2].at[slot]
        pltpu.make_async_copy(whole, whole, sems.at[group, slot]).wait()

    def vec(which):
        return vec_ref[which : which + 1, :]

    inner_sums_ref[...] = jnp.zeros_like(inner_sums_ref)
    attention = jnp.zeros(in_ref.shape, F32)
    for slot in range(parts):
        arrive(0, slot)
        attention = attention + dot(unpack(ctx_ref[place_ref[slot]]), w_out[slot, :, : 3 * DH], NT)
    first_exact, normed_one, inverse_one = norm_forward(
        in_ref[...].astype(F32) + attention + vec(0), vec(1), vec(2)
    )
    first = first_exact.astype(BF16)
    first_ref[...] = first

    def up(slot, branch):
        t = place_ref[slot]
        arrive(1, slot)
        hidden = dot(first, w_in[slot]) + inner_bias_ref[t]
        bend = 0.5 * (1.0 + lax.erf(hidden * ROOT_HALF))
        activated = (hidden * bend).astype(BF16)
        act_ref[t] = activated
        slope[slot] = bend + hidden * INV_ROOT_TAU * jnp.exp2(hidden * hidden * (-0.5 * LOG2E))
        arrive(2, slot)
        return branch + dot(activated, w_up[slot], NT)

    branch = lax.fori_loop(0, parts, up, jnp.zeros(in_ref.shape, F32))
    layer_rows, normed_two, inverse_two = norm_forward(first.astype(F32) + branch + vec(3), vec(4), vec(5))
    layer_ref[...] = layer_rows.astype(BF16)
    misfit = layer_rows - teacher_ref[...].astype(F32)
    weighted = valid_ref[...] * misfit
    out_grad = cotangent_ref[...].astype(F32) + weighted * ratio_ref[0]
    second_grad = norm_backward(out_grad, normed_two, inverse_two, vec(4))
    branch_grad = second_grad.astype(BF16)
    branch_grad_ref[...] = branch_grad
    sums_ref[0:1, :] = column_sum(weighted * misfit)
    sums_ref[1:2, :] = column_sum(branch_grad.astype(F32))
    sums_ref[2:3, :] = column_sum(out_grad * normed_two)
    sums_ref[3:4, :] = column_sum(out_grad)

    def down(slot, back):
        t = place_ref[slot]
        hidden_grad = (dot(branch_grad, w_up[slot]) * slope[slot]).astype(BF16)
        hidden_grad_ref[t] = hidden_grad
        inner_sums_ref[t] = column_sum(hidden_grad.astype(F32))
        return back + dot(hidden_grad, w_in[slot], NT)

    upstream = lax.fori_loop(0, parts, down, second_grad)
    first_grad = norm_backward(upstream, normed_one, inverse_one, vec(1))
    first_grad_ref[...] = first_grad
    attn_grad = first_grad.astype(BF16)
    attn_grad_ref[...] = attn_grad
    sums_ref[4:5, :] = column_sum(attn_grad.astype(F32))
    sums_ref[5:6, :] = column_sum(upstream * normed_one)
    sums_ref[6:7, :] = column_sum(upstream)
    sums_ref[7:8, :] = jnp.zeros_like(sums_ref[7:8, :])
    middle = BLOCK // 2
    for slot in range(parts):
        back = dot(attn_grad, w_out[slot, :, : 3 * DH]).astype(BF16)
        ctx_grad_ref[place_ref[slot]] = pack(
            back[:, : 2 * DH], back[:middle, 2 * DH :], back[middle:, 2 * DH :]
        )


def run_dense(half, marks, place, ratio, ctx, rows_in, teacher, cotangent, valid, vecs, inner_bias, pieces):
    parts = ctx.shape[0]
    width = rows_in.shape[1]
    hidden_cols = inner_bias.shape[2]
    out_cols = pieces[0].shape[2] - 2 * hidden_cols

    def mine(columns):
        return pl.BlockSpec((BLOCK, columns), lambda i: (half, 0))

    def fixed(shape):
        return pl.BlockSpec(shape, lambda i: (0,) * len(shape))

    low = jax.ShapeDtypeStruct((BLOCK, width), BF16)
    out_shape = (
        low,
        jax.ShapeDtypeStruct((BLOCK, width), F32),
        jax.ShapeDtypeStruct(ctx.shape, BF16),
        low,
        low,
        low,
        jax.ShapeDtypeStruct((parts, BLOCK, hidden_cols), BF16),
        jax.ShapeDtypeStruct((parts, BLOCK, hidden_cols), BF16),
        jax.ShapeDtypeStruct((8, width), F32),
        jax.ShapeDtypeStruct((parts, 1, hidden_cols), F32),
    )
    smem = pl.BlockSpec(memory_space=pltpu.SMEM)
    return pl.pallas_call(
        functools.partial(dense_chain, marks),
        out_shape=out_shape,
        grid=(1,),
        in_specs=[
            smem,
            smem,
            fixed(ctx.shape),
            mine(width),
            mine(width),
            mine(width),
            mine(1),
            fixed(vecs.shape),
            fixed(inner_bias.shape),
        ]
        + [pl.BlockSpec(memory_space=pl.ANY)] * len(pieces),
        out_specs=tuple(fixed(out.shape) for out in out_shape),
        scratch_shapes=[
            pltpu.VMEM((parts, width, out_cols), BF16),
            pltpu.VMEM((parts, width, hidden_cols), BF16),
            pltpu.VMEM((parts, width, hidden_cols), BF16),
            pltpu.VMEM((parts, BLOCK, hidden_cols), F32),
            pltpu.SemaphoreType.DMA((3, parts)),
        ],
        compiler_params=pltpu.CompilerParams(
            dimension_semantics=("arbitrary",), vmem_limit_bytes=VMEM_LIMIT
        ),
        cost_estimate=pl.CostEstimate(
            flops=BLOCK * width * (8 * hidden_cols + 4 * out_cols) * parts,
            bytes_accessed=18 << 20,
            transcendentals=2 * BLOCK * hidden_cols * parts,
        ),
        name="dense_chain",
    )(place, ratio, ctx, rows_in, teacher, cotangent, valid, vecs, inner_bias, *pieces)


def dense_weights(turns, halves, place_ref, *refs):
    firsts, branch_grads, attn_grads, acts, hidden_grads, ctxs = (
        refs[k * halves : (k + 1) * halves] for k in range(6)
    )
    notes_ref, outs = refs[6 * halves], refs[6 * halves + 1 : -3]
    turned, whole, sems = refs[-3:]
    step = pl.program_id(0)
    slots = whole.shape[0]
    teams = len(outs) // len(turns)
    each = slots // teams

    @pl.when(step == 0)
    def _():
        for which, sources in enumerate((firsts, branch_grads, attn_grads)):
            for half, source in enumerate(sources):
                turned[which, :, half * BLOCK : (half + 1) * BLOCK] = jnp.transpose(source[...])

    def both(sources):
        return jnp.concatenate([source[0] for source in sources], axis=0)

    hidden_cols = acts[0].shape[2]
    whole[step, :, :hidden_cols] = dot(turned[0], both(hidden_grads)).astype(BF16)
    whole[step, :, hidden_cols : 2 * hidden_cols] = dot(turned[1], both(acts)).astype(BF16)
    ctx = jnp.concatenate([unpack(source[0]) for source in ctxs], axis=0)
    plain = 2 * hidden_cols + ctx.shape[1]
    whole[step, :, 2 * hidden_cols : plain] = dot(turned[2], ctx).astype(BF16)
    whole[step, :, plain : plain + notes_ref.shape[1]] = notes_ref[...]
    for team in range(teams):

        @pl.when(step // each == team)
        def _():
            for out, orders in zip(outs[team * len(turns) : (team + 1) * len(turns)], turns):
                block = out.shape[1]
                for at, turn in enumerate(orders[team]):
                    offset = pl.multiple_of((place_ref[slots] ^ turn) * block, block)
                    pltpu.make_async_copy(
                        whole.at[step, pl.ds(offset, block), :],
                        out.at[at * each + step - team * each],
                        sems.at[step],
                    ).start()

    @pl.when(step == slots - 1)
    def _():
        for slot in range(slots):
            pltpu.make_async_copy(whole.at[slot], whole.at[slot], sems.at[slot]).wait()


def run_weights(turns, teams, block, place, notes, firsts, branch_grads, attn_grads, acts, hidden_grads, ctxs):
    parts, _, hidden_cols = acts[0].shape
    halves = len(acts)
    width = firsts[0].shape[1]
    columns = 2 * hidden_cols + 3 * DH + notes.shape[1]

    def by_slot(rows, size):
        return pl.BlockSpec((1, rows, size), lambda s, place: (place[s], 0, 0))

    fixed = pl.BlockSpec((BLOCK, width), lambda s, place: (0, 0))
    outs = tuple(
        jax.ShapeDtypeStruct((len(orders[0]) * parts // teams, block, columns), BF16) for orders in turns
    ) * teams
    return pl.pallas_call(
        functools.partial(dense_weights, turns, halves),
        out_shape=outs,
        grid_spec=pltpu.PrefetchScalarGridSpec(
            num_scalar_prefetch=1,
            grid=(parts,),
            in_specs=[fixed] * (3 * halves)
            + [by_slot(BLOCK, hidden_cols)] * (2 * halves)
            + [by_slot(PACKED, 2 * DH)] * halves
            + [pl.BlockSpec(notes.shape, lambda s, place: (0, 0))],
            out_specs=tuple(pl.BlockSpec(memory_space=pl.ANY) for _ in outs),
            scratch_shapes=[
                pltpu.VMEM((3, width, halves * BLOCK), BF16),
                pltpu.VMEM((parts, width, columns), BF16),
                pltpu.SemaphoreType.DMA((parts,)),
            ],
        ),
        compiler_params=pltpu.CompilerParams(
            dimension_semantics=("arbitrary",), vmem_limit_bytes=VMEM_LIMIT
        ),
        cost_estimate=pl.CostEstimate(
            flops=2 * halves * BLOCK * width * columns * parts,
            bytes_accessed=20 << 20,
            transcendentals=0,
        ),
        name="dense_weights",
    )(place, *firsts, *branch_grads, *attn_grads, *acts, *hidden_grads, *ctxs, notes)


def finish_dense(packed_ref, inner_ref, outer_ref, output_ref, notes_ref):
    hidden_cols = inner_ref.shape[1]
    summed = packed_ref[...].astype(F32)
    inner_ref[...] = summed[:, :hidden_cols]
    outer_ref[...] = summed[:, hidden_cols : 2 * hidden_cols]
    plain = 2 * hidden_cols + output_ref.shape[0]
    output_ref[...] = jnp.transpose(summed[:, 2 * hidden_cols : plain])
    notes_ref[...] = summed[:, plain:]


def run_finish_dense(packed, hidden_cols, head_cols):
    rows = packed.shape[0]
    return pl.pallas_call(
        finish_dense,
        out_shape=(
            jax.ShapeDtypeStruct((rows, hidden_cols), F32),
            jax.ShapeDtypeStruct((rows, hidden_cols), F32),
            jax.ShapeDtypeStruct((head_cols, rows), F32),
            jax.ShapeDtypeStruct((rows, packed.shape[1] - 2 * hidden_cols - head_cols), F32),
        ),
        name="finish_dense",
    )(packed)


def finish_heads(value_ref, *refs):
    summed = value_ref[...].astype(F32)
    heads = summed.shape[1] // SLAB
    for ref, which in zip(refs, (0, 2, 3, 1)):
        columns = [summed[:, SLAB * h + which * DH : SLAB * h + (which + 1) * DH] for h in range(heads)]
        ref[...] = jnp.concatenate(columns, axis=1)[: ref.shape[0]]


def run_finish_heads(value):
    rows, width = value.shape
    out = jax.ShapeDtypeStruct((rows, width // 4), F32)
    notes = jax.ShapeDtypeStruct((8, width // 4), F32)
    return pl.pallas_call(finish_heads, out_shape=(out, out, out, notes), name="finish_heads")(value)


def interleave(query, key, value, heads):
    rows = query.shape[0]
    parts = [part.reshape(rows, heads, 1, DH) for part in (query, jnp.zeros_like(query), key, value)]
    return jnp.concatenate(parts, axis=2).reshape(rows, heads * SLAB)


def swap(value, axis, bit):
    size = lax.axis_size(axis)
    return lax.ppermute(value, axis, [(i, i ^ bit) for i in range(size)])


def bits_of(axis):
    bit = 1
    while bit < lax.axis_size(axis):
        yield bit
        bit *= 2


def after(value, *others):
    return lax.optimization_barrier((value,) + others)[0]


def merge(held, other, axis, bit):
    mine_first = (lax.axis_index(axis) & bit) == 0
    return jnp.where(
        mine_first, jnp.concatenate([held, other], axis=0), jnp.concatenate([other, held], axis=0)
    )


def add_low(left_side, right_side):
    return (left_side.astype(F32) + right_side.astype(F32)).astype(BF16)


def scatter_rows(held):
    index = lax.axis_index("dp")
    for bit in bits_of("dp"):
        held = held.reshape((held.shape[0] // 2, 2) + held.shape[1:])
        own = (index & bit) // bit
        send = lax.dynamic_index_in_dim(held, 1 - own, 1, keepdims=False)
        keep = lax.dynamic_index_in_dim(held, own, 1, keepdims=False)
        held = add_low(keep, swap(send, "dp", bit))
    return held[0]


def local(
    inputs, segment_ids, valid_mask, teacher, cotangent,
    w_query, w_key, w_value, w_output, w_inner, w_outer,
    query_bias, value_bias, output_bias, inner_bias, outer_bias,
    gain_attn, shift_attn, gain_ffn, shift_ffn,
):
    _, part_len, width = inputs.shape
    parts = lax.axis_size("tensor")
    copies = lax.axis_size("dp")
    rank = lax.axis_index("tensor")
    total_tokens = part_len * parts * copies
    seq_len = part_len * parts
    head_cols = w_query.shape[1]
    heads = head_cols // DH
    hidden_cols = w_inner.shape[1]
    shard_rows = w_inner.shape[0]
    halves = part_len // BLOCK

    def shift(value, by):
        return lax.ppermute(value, "tensor", [(i, i + by) for i in range(parts) if 0 <= i + by < parts])

    def turn(value, by):
        return lax.ppermute(value, "tensor", [(i, (i + by) % parts) for i in range(parts)])

    valid_rows = valid_mask.astype(F32).reshape(part_len, 1)
    valid_count = jnp.sum(valid_mask.astype(F32))
    upper = jnp.floor(valid_count / 256.0)
    spot = lax.broadcasted_iota(jnp.int32, (shard_rows, DH), 0) * DH + lax.broadcasted_iota(
        jnp.int32, (shard_rows, DH), 1
    )
    count_row = jnp.where(spot == 0, upper, jnp.where(spot == 1, valid_count - 256.0 * upper, 0.0))
    mine = jnp.concatenate((w_inner, w_outer.T, w_output.T, count_row.astype(BF16)), axis=1)
    weights = lax.all_gather(mine, ("tensor", "dp"), axis=0, tiled=False)
    counts = weights[:, 0, -DH : 2 - DH].astype(F32)
    counted = 256.0 * jnp.sum(counts[:, 0]) + jnp.sum(counts[:, 1])
    ratio = (total_tokens / counted).reshape(1)
    pieces = [weights.reshape(parts, width, -1)]
    marks = [[(t, 0) for t in range(parts)]]
    place = jnp.asarray(list(range(parts)) + [0], jnp.int32)

    rows_in = inputs.reshape(part_len, width)
    ahead, behind = [], []
    up, down = rows_in, rows_in
    w_heads = interleave(w_query, w_key, w_value, heads)
    steps = list(bits_of("dp"))
    for step in range(parts - 1):
        up, down = shift(up, 1), shift(down, -1)
        behind.append(up)
        ahead.append(down)
        if step < len(steps):
            w_heads = merge(w_heads, swap(w_heads, "dp", steps[step]), "dp", steps[step])
        if step < parts - 2:
            up, down, w_heads = lax.optimization_barrier((up, down, w_heads))
    for bit in steps[parts - 1 :]:
        w_heads = merge(w_heads, swap(w_heads, "dp", bit), "dp", bit)
    tokens = [rows_in] + [
        jnp.where(rank + by < parts, ahead[by - 1], behind[parts - by - 1]) for by in range(1, parts)
    ]

    mine_cols = rank * head_cols
    query_shift = lax.dynamic_slice_in_dim(query_bias, mine_cols, head_cols).astype(F32)
    value_shift = lax.dynamic_slice_in_dim(value_bias, mine_cols, head_cols).astype(F32)
    shifts = interleave(query_shift[None], jnp.zeros_like(query_shift)[None], value_shift[None], heads)
    qkv = [(dot(chunk, w_heads) + shifts).astype(BF16) for chunk in tokens]

    segment_row = segment_ids.reshape(seq_len)
    bounds = document_blocks(segment_row)
    seg_col = segment_row.reshape(seq_len, 1)
    seg_row = segment_row.reshape(1, seq_len)
    lane = rank.astype(jnp.int32).reshape(1)

    def exchange(packed_blocks):
        return lax.all_to_all(packed_blocks, "tensor", 0, 0)

    contexts, lses, arrived = [], [], []
    for half in range(halves):
        context, lse = run_forward((halves, half), lane, bounds, qkv, seg_col, seg_row)
        contexts.append(context)
        lses.append(lse)
        arrived.append(exchange(context))

    vecs = jnp.stack(
        (output_bias, gain_attn, shift_attn, outer_bias, gain_ffn, shift_ffn, outer_bias, outer_bias)
    ).astype(F32)
    inner_rows = inner_bias.astype(F32).reshape(parts, 1, hidden_cols)
    teacher_rows = teacher.reshape(part_len, width)
    cotangent_rows = cotangent.reshape(part_len, width)
    chains = [
        run_dense(
            half, marks, place, ratio, arrived[half], rows_in, teacher_rows, cotangent_rows,
            valid_rows, vecs, inner_rows, pieces,
        )
        for half in range(halves)
    ]
    (
        layers, first_grads, context_grads, firsts, branch_grads, attn_grads, acts, hidden_grads,
        dense_sums, inner_sums,
    ) = zip(*chains)
    head_grads = [exchange(context_grad) for context_grad in context_grads]
    dense_sums = sum(dense_sums)
    inner_sums = sum(inner_sums)
    sources = (firsts, branch_grads, attn_grads, acts, hidden_grads, arrived)
    head_grads[:-1], sources = lax.optimization_barrier((head_grads[:-1], sources))
    notes = jnp.concatenate((dense_sums.reshape(-1), inner_sums.reshape(-1))).astype(BF16)
    room = -(-notes.shape[0] // (shard_rows * 128)) * 128
    notes = jnp.pad(notes, (0, shard_rows * room - notes.shape[0])).reshape(shard_rows, room)
    (packed,) = run_weights(([[0]],), 1, width, place, jnp.tile(notes, (copies, 1)), *sources)
    packed = lax.psum_scatter(packed, "dp", scatter_dimension=1, tiled=True)

    earlier, before = [], []
    for half in range(halves):
        results = run_backward(
            (halves, half), lane, bounds, qkv, seg_col, seg_row, contexts[half], head_grads[half],
            lses[half], earlier, before,
        )
        if half < halves - 1:
            before, earlier = [results[0]], earlier + [results[1]]
    joined_grad, sums = results
    away = [dot(joined_grad[by], w_heads, NT).astype(BF16) for by in (2, 1, 3)]
    own_share = dot(joined_grad[0], w_heads, NT)
    away, own_share, sums, joined_grad = lax.optimization_barrier((away, own_share, sums, joined_grad))
    came = [turn(share, by) for share, by in zip(away, (2, 1, 3))]
    sums = sums.reshape(heads, 4, DH)
    sums = jnp.concatenate((sums[:, 0].reshape(1, head_cols), sums[:, 3].reshape(1, head_cols)), axis=1)
    for bit in bits_of("tensor"):
        sums = merge(sums, swap(sums, "tensor", bit), "tensor", bit)
    head_weights = dot(
        jnp.concatenate(tokens, axis=0), joined_grad.reshape(seq_len, -1), TN
    ).reshape((copies, shard_rows, -1))
    head_weights, packed = lax.optimization_barrier((head_weights, packed))
    packed = lax.psum_scatter(packed, "tensor", scatter_dimension=0, tiled=True)[0]
    biases = jnp.concatenate((sums[:, :head_cols].reshape(-1), sums[:, head_cols:].reshape(-1)))
    biases = jnp.pad(
        biases.reshape(8, heads, 1, DH), ((0, shard_rows - 8), (0, 0), (1, 2), (0, 0))
    ).reshape(1, shard_rows, -1)
    query_grad, key_grad, value_grad, biases = run_finish_heads(
        scatter_rows((head_weights + biases).astype(BF16))
    )
    biases = biases.reshape(2, width)
    input_grad = own_share + jnp.concatenate(first_grads, axis=0)
    for share in came:
        input_grad = input_grad + share.astype(F32)

    inner_grad, outer_grad, output_grad, notes = run_finish_dense(packed, hidden_cols, head_cols)
    notes = notes.reshape(-1)

    def total(which):
        return notes[which * width : (which + 1) * width]

    mse_loss = jnp.sum(total(0)) / (counted * width)
    return (
        jnp.concatenate(layers, axis=0).reshape(1, part_len, width),
        mse_loss,
        input_grad.reshape(1, part_len, width),
        query_grad,
        key_grad,
        value_grad,
        output_grad,
        inner_grad,
        outer_grad.T,
        biases[0],
        biases[1],
        total(4),
        notes[8 * width : 8 * width + hidden_cols * parts],
        total(1),
        total(5),
        total(6),
        total(2),
        total(3),
    )


def solution(mesh):
    shard = P("dp", "tensor", None)
    by_dp, by_tensor = P("dp", "tensor"), P("tensor", "dp")
    in_specs = (
        (shard, P("dp", None), by_dp, shard, shard)
        + (by_dp,) * 3
        + (by_tensor, by_dp, by_tensor)
        + (P(),) * 9
    )
    out_specs = (shard, P(), shard) + (by_dp,) * 3 + (by_tensor, by_dp, by_tensor) + (P(),) * 9
    return jax.shard_map(local, mesh=mesh, in_specs=in_specs, out_specs=out_specs, check_vma=False)
```

```python
import functools

import jax
import jax.numpy as jnp
from jax import lax
from jax.experimental import pallas as pl
from jax.experimental.pallas import tpu as pltpu
from jax.sharding import PartitionSpec as P

DH = 64
BLOCK = 256
SLAB = 4 * DH
EPSILON = 1e-12
ROOT_HALF = 0.7071067811865476
INV_ROOT_TAU = 0.3989422804014327
LOG2E = 1.4426950408889634
LN2 = 0.6931471805599453
SCALE = DH ** (-0.5)
MASKED = -1e30
VMEM_LIMIT = 60 << 20

BF16 = jnp.bfloat16
F32 = jnp.float32
NN = (((1,), (0,)), ((), ()))
NT = (((1,), (1,)), ((), ()))
TN = (((0,), (0,)), ((), ()))


def dot(left_side, right_side, dims=NN):
    return lax.dot_general(left_side, right_side, dims, preferred_element_type=F32)


def norm_forward(summed, gain_vec, shift_vec):
    average = jnp.mean(summed, axis=-1, keepdims=True)
    centered = summed - average
    variance = jnp.mean(centered * centered, axis=-1, keepdims=True)
    inverse = lax.rsqrt(variance + EPSILON)
    normed = centered * inverse
    return (normed * gain_vec + shift_vec, normed, inverse)


def norm_backward(upstream, normed, inverse, gain_vec):
    scaled = upstream * gain_vec
    first_mean = jnp.mean(scaled, axis=-1, keepdims=True)
    second_mean = jnp.mean(scaled * normed, axis=-1, keepdims=True)
    return inverse * (scaled - first_mean - normed * second_mean)


def column_sum(value):
    return jnp.sum(value, axis=0, keepdims=True)


def lane_is_right(rows):
    return lax.broadcasted_iota(jnp.int32, (rows, 2 * DH), 1) >= DH


def pack(first_two, third_top, third_bottom):
    return jnp.concatenate([first_two, jnp.concatenate([third_top, third_bottom], axis=1)], axis=0)


def unpack(packed):
    third = packed[BLOCK:]
    third = jnp.concatenate([third[:, :DH], third[:, DH:]], axis=0)
    return jnp.concatenate([packed[:BLOCK], third], axis=1)


def fetch_chunks(lane_ref, chunk_refs, target, sems):
    rows = chunk_refs[0].shape[0]
    copies = []
    for at, chunk in enumerate(chunk_refs):
        offset = pl.multiple_of(lax.rem(lane_ref[0] + at, len(chunk_refs)) * rows, rows)
        copies.append(pltpu.make_async_copy(chunk, target.at[pl.ds(offset, rows), :], sems.at[at]))
    return copies


def attend_forward(
    which, lane_ref, low_ref, high_ref, *refs
):
    chunk_refs, (seg_col_ref, seg_row_ref, ctx_ref, lse_ref, held, qkv_ref, sems) = refs[:-7], refs[-7:]
    halves, half = which
    heads = lse_ref.shape[0]

    @pl.when(pl.program_id(0) == 0)
    def _():
        copies = fetch_chunks(lane_ref, chunk_refs, qkv_ref, sems)
        for copy in copies:
            copy.start()
        for copy in copies:
            copy.wait()

    qb = pl.program_id(0) * halves + half
    rows = pl.ds(pl.multiple_of(qb * BLOCK, BLOCK), BLOCK)
    seg_q = seg_col_ref[...]
    queries = [
        qkv_ref[rows, SLAB * h : SLAB * h + 2 * DH] * jnp.asarray(SCALE, BF16) for h in range(heads)
    ]
    low, high = low_ref[qb], high_ref[qb]

    def score(kb, peaks):
        keys = pl.ds(pl.multiple_of(kb * BLOCK, BLOCK), BLOCK)
        allowed = seg_q == seg_row_ref[:, keys]
        found = []
        for h in range(heads):
            scores = dot(queries[h], qkv_ref[keys, SLAB * h + 2 * DH : SLAB * (h + 1)], NT)
            scores = jnp.where(allowed, scores, MASKED)
            held[h, kb] = scores
            found.append(jnp.maximum(peaks[h], jnp.maximum(scores[:, :128], scores[:, 128:])))
        return tuple(found)

    start = tuple(jnp.full((BLOCK, 128), MASKED, F32) for _ in range(heads))
    peaks = lax.fori_loop(low, high, score, start)
    highest = [jnp.max(peak, axis=-1, keepdims=True) for peak in peaks]

    def weigh(kb, carry):
        keys = pl.ds(pl.multiple_of(kb * BLOCK, BLOCK), BLOCK)
        found = []
        for h in range(heads):
            total, acc = carry[h]
            raised = jnp.exp2((held[h, kb] - highest[h]) * LOG2E)
            total = total + (raised[:, :128] + raised[:, 128:])
            acc = acc + dot(raised.astype(BF16), qkv_ref[keys, SLAB * h + 2 * DH : SLAB * (h + 1)])
            found.append((total, acc))
        return tuple(found)

    zero = jnp.zeros((BLOCK, 128), F32)
    done = lax.fori_loop(low, high, weigh, tuple((zero, zero) for _ in range(heads)))
    values = []
    for h in range(heads):
        total, acc = done[h]
        summed = jnp.sum(total, axis=-1, keepdims=True)
        values.append((acc / summed).astype(BF16))
        lse_ref[h] = jnp.transpose(highest[h] + jnp.log(summed))
    middle = BLOCK // 2
    ctx_ref[0, :BLOCK, :] = jnp.where(lane_is_right(BLOCK), values[1], pltpu.roll(values[0], DH, 1))
    ctx_ref[0, BLOCK:, :] = jnp.where(
        lane_is_right(middle), values[2][middle:], pltpu.roll(values[2][:middle], DH, 1)
    )


def attend_backward(which, chunks, lane_ref, low_ref, high_ref, *refs):
    halves, half = which
    last = half == halves - 1
    chunk_refs, refs = refs[:chunks], refs[chunks:]
    (seg_col_ref, seg_row_ref, ctx_ref, grad_ref, lse_ref), refs = refs[:5], refs[5:]
    earlier, refs = refs[:half], refs[half:]
    if half > 0:
        before_ref, refs = refs[0], refs[1:]
    if last:
        final_ref, sums_ref, dkv, out_ref, qkv_ref, sems = refs
    else:
        dkv, query_ref, qkv_ref, sems = refs
    heads = dkv.shape[0]
    step_index = pl.program_id(0)
    qb = step_index * halves + half

    @pl.when(step_index == 0)
    def _():
        copies = fetch_chunks(lane_ref, chunk_refs, qkv_ref, sems)
        for copy in copies:
            copy.start()
        dkv[...] = before_ref[...] if half > 0 else jnp.zeros_like(dkv)
        for copy in copies:
            copy.wait()

    rows = pl.ds(pl.multiple_of(qb * BLOCK, BLOCK), BLOCK)
    right = lane_is_right(BLOCK)
    arrived = grad_ref[0]
    product = arrived.astype(F32) * ctx_ref[0].astype(F32)
    upper = product.astype(BF16)
    lower = (product - upper.astype(F32)).astype(BF16)
    pick = (
        lax.broadcasted_iota(jnp.int32, (8, 2 * DH), 1) // DH
        == lax.broadcasted_iota(jnp.int32, (8, 2 * DH), 0)
    ).astype(BF16)
    summed = dot(pick, upper, NT) + dot(pick, lower, NT)
    deltas = [
        summed[0:1, :BLOCK],
        summed[1:2, :BLOCK],
        jnp.concatenate([summed[0:1, BLOCK:], summed[1:2, BLOCK:]], axis=1),
    ]
    two, third = arrived[:BLOCK], arrived[BLOCK:]
    placed = [
        pltpu.roll(two, DH, 1),
        two,
        jnp.concatenate([pltpu.roll(third, DH, 1), third], axis=0),
    ]
    grads = [jnp.where(right, grad, jnp.zeros_like(grad)) for grad in placed]
    queries, pairs = [], []
    for h in range(heads):
        queries.append(qkv_ref[rows, SLAB * h : SLAB * h + 2 * DH] * jnp.asarray(SCALE, BF16))
        pairs.append(jnp.concatenate([queries[h], grads[h]], axis=0))
    seg_q = seg_row_ref[...]
    lses = lse_ref[...]
    low, high = low_ref[qb], high_ref[qb]

    def step(kb, accs):
        keys = pl.ds(pl.multiple_of(kb * BLOCK, BLOCK), BLOCK)
        allowed = seg_col_ref[keys, :] == seg_q
        found = []
        for h in range(heads):
            pair = qkv_ref[keys, SLAB * h + 2 * DH : SLAB * (h + 1)]
            scores = jnp.where(allowed, dot(pair, queries[h], NT), MASKED)
            probs = jnp.exp2((scores - lses[h]) * LOG2E)
            score_grad = (probs * (dot(pair, grads[h], NT) - deltas[h])).astype(BF16)
            both = jnp.concatenate([score_grad, probs.astype(BF16)], axis=1)
            dkv[h, keys, :] += dot(both, pairs[h])
            found.append(accs[h] + dot(score_grad, pair, TN))
        return tuple(found)

    zero = jnp.zeros((BLOCK, 128), F32)
    accs = lax.fori_loop(low, high, step, tuple(zero for _ in range(heads)))
    for h in range(heads):
        query_grad = jnp.where(right, 0.0, accs[h] * SCALE).astype(BF16)
        if last:
            out_ref[rows, SLAB * h : SLAB * h + 2 * DH] = query_grad
        else:
            query_ref[0, :, 2 * DH * h : 2 * DH * (h + 1)] = query_grad

    if last:

        @pl.when(step_index == pl.num_programs(0) - 1)
        def _():
            for h in range(heads):
                at = SLAB * h
                for other, ref in enumerate(earlier):
                    for block in range(ref.shape[0]):
                        start = (block * halves + other) * BLOCK
                        out_ref[start : start + BLOCK, at : at + 2 * DH] = ref[
                            block, :, 2 * DH * h : 2 * DH * (h + 1)
                        ]
                out_ref[:, at + 2 * DH : at + SLAB] = dkv[h].astype(BF16)
                sums_ref[:, at : at + SLAB] = column_sum(out_ref[:, at : at + SLAB].astype(F32))
            rows_each = final_ref.shape[1]
            copies = []
            for at in range(final_ref.shape[0]):
                offset = pl.multiple_of(lax.rem(lane_ref[0] + at, final_ref.shape[0]) * rows_each, rows_each)
                copies.append(
                    pltpu.make_async_copy(
                        out_ref.at[pl.ds(offset, rows_each), :], final_ref.at[at], sems.at[at]
                    )
                )
            for copy in copies:
                copy.start()
            for copy in copies:
                copy.wait()


def document_blocks(segment_row):
    starts = segment_row[::BLOCK]
    stops = segment_row[BLOCK - 1 :: BLOCK]
    low = jnp.sum((segment_row[None, :] < starts[:, None]).astype(jnp.int32), axis=1)
    high = jnp.sum((segment_row[None, :] <= stops[:, None]).astype(jnp.int32), axis=1)
    return (low // BLOCK, (high + BLOCK - 1) // BLOCK)


PACKED = BLOCK + BLOCK // 2


def run_forward(which, lane, bounds, qkv, seg_col, seg_row):
    halves, half = which
    seq_len, width = seg_col.shape[0], qkv[0].shape[1]
    heads = width // SLAB
    blocks = seq_len // BLOCK
    steps = blocks // halves
    return pl.pallas_call(
        functools.partial(attend_forward, which),
        out_shape=(
            jax.ShapeDtypeStruct((steps, PACKED, 2 * DH), BF16),
            jax.ShapeDtypeStruct((heads, 1, steps * BLOCK), F32),
        ),
        grid_spec=pltpu.PrefetchScalarGridSpec(
            num_scalar_prefetch=3,
            grid=(steps,),
            in_specs=[pl.BlockSpec(memory_space=pl.ANY)] * len(qkv)
            + [
                pl.BlockSpec((BLOCK, 1), lambda q, *_: (q * halves + half, 0)),
                pl.BlockSpec((1, seq_len), lambda q, *_: (0, 0)),
            ],
            out_specs=(
                pl.BlockSpec((1, PACKED, 2 * DH), lambda q, *_: (q, 0, 0)),
                pl.BlockSpec((heads, 1, BLOCK), lambda q, *_: (0, 0, q)),
            ),
            scratch_shapes=[
                pltpu.VMEM((heads, blocks, BLOCK, BLOCK), F32),
                pltpu.VMEM((seq_len, width), BF16),
                pltpu.SemaphoreType.DMA((len(qkv),)),
            ],
        ),
        compiler_params=pltpu.CompilerParams(
            dimension_semantics=("arbitrary",), vmem_limit_bytes=VMEM_LIMIT
        ),
        cost_estimate=pl.CostEstimate(
            flops=heads * seq_len * seq_len * 256 // halves,
            bytes_accessed=5 << 20,
            transcendentals=heads * seq_len * seq_len // 3 // halves,
        ),
        name="attend_forward",
    )(lane, *bounds, *qkv, seg_col, seg_row)


def run_backward(which, lane, bounds, qkv, seg_col, seg_row, ctx, grad, lse, earlier, before):
    halves, half = which
    seq_len, width = seg_col.shape[0], qkv[0].shape[1]
    heads = width // SLAB
    steps = seq_len // BLOCK // halves
    packed = pl.BlockSpec((1, PACKED, 2 * DH), lambda q, *_: (q, 0, 0))

    def fixed(shape, **more):
        return pl.BlockSpec(shape, lambda q, *_: (0,) * len(shape), **more)

    once = {"pipeline_mode": pl.Buffered(1)}
    gathered = (heads, seq_len, 2 * DH)
    carried = [fixed(value.shape, **once) for value in earlier]
    carried += [fixed(gathered, **once)] * len(before)
    scratch = [pltpu.VMEM((seq_len, width), BF16), pltpu.SemaphoreType.DMA((len(qkv),))]
    if half == halves - 1:
        out_shape = (
            jax.ShapeDtypeStruct((len(qkv), seq_len // len(qkv), width), BF16),
            jax.ShapeDtypeStruct((1, width), F32),
        )
        out_specs = (pl.BlockSpec(memory_space=pl.ANY), fixed((1, width)))
        scratch = [pltpu.VMEM(gathered, F32), pltpu.VMEM((seq_len, width), BF16)] + scratch
    else:
        out_shape = (
            jax.ShapeDtypeStruct(gathered, F32),
            jax.ShapeDtypeStruct((steps, BLOCK, heads * 2 * DH), BF16),
        )
        out_specs = (
            fixed(gathered),
            pl.BlockSpec((1, BLOCK, heads * 2 * DH), lambda q, *_: (q, 0, 0)),
        )
    return pl.pallas_call(
        functools.partial(attend_backward, which, len(qkv)),
        out_shape=out_shape,
        grid_spec=pltpu.PrefetchScalarGridSpec(
            num_scalar_prefetch=3,
            grid=(steps,),
            in_specs=[pl.BlockSpec(memory_space=pl.ANY)] * len(qkv)
            + [
                fixed((seq_len, 1)),
                pl.BlockSpec((1, BLOCK), lambda q, *_: (0, q * halves + half)),
                packed,
                packed,
                pl.BlockSpec((heads, 1, BLOCK), lambda q, *_: (0, 0, q)),
            ]
            + carried,
            out_specs=out_specs,
            scratch_shapes=scratch,
        ),
        compiler_params=pltpu.CompilerParams(
            dimension_semantics=("arbitrary",), vmem_limit_bytes=VMEM_LIMIT
        ),
        cost_estimate=pl.CostEstimate(
            flops=heads * seq_len * seq_len * 640 // halves,
            bytes_accessed=10 << 20,
            transcendentals=heads * seq_len * seq_len // 3 // halves,
        ),
        name="attend_backward",
    )(lane, *bounds, *qkv, seg_col, seg_row, ctx, grad, lse, *earlier, *before)


def dense_chain(
    marks, place_ref, ratio_ref, ctx_ref, in_ref, teacher_ref, cotangent_ref, valid_ref, vec_ref,
    inner_bias_ref, *refs
):
    pieces = refs[: len(marks)]
    (
        layer_ref, first_grad_ref, ctx_grad_ref, first_ref, branch_grad_ref, attn_grad_ref,
        act_ref, hidden_grad_ref, sums_ref, inner_sums_ref, w_out, w_in, w_up, slope, sems,
    ) = refs[len(marks) :]
    parts, _, head_cols = w_out.shape
    hidden_cols = w_in.shape[2]
    index = place_ref[parts]
    groups = (
        (2 * hidden_cols, head_cols, w_out),
        (0, hidden_cols, w_in),
        (hidden_cols, hidden_cols, w_up),
    )
    for group, (start, size, target) in enumerate(groups):
        for piece, marked in zip(pieces, marks):
            block = piece.shape[1]
            for at, (slot, turn, relative) in enumerate(marked):
                offset = pl.multiple_of((index ^ turn) * block, block) if relative else turn * block
                pltpu.make_async_copy(
                    piece.at[at, :, pl.ds(start, size)],
                    target.at[slot, pl.ds(offset, block), :],
                    sems.at[group, slot],
                ).start()

    def arrive(group, slot):
        whole = groups[group][2].at[slot]
        pltpu.make_async_copy(whole, whole, sems.at[group, slot]).wait()

    def vec(which):
        return vec_ref[which : which + 1, :]

    inner_sums_ref[...] = jnp.zeros_like(inner_sums_ref)
    attention = jnp.zeros(in_ref.shape, F32)
    for slot in range(parts):
        arrive(0, slot)
        attention = attention + dot(unpack(ctx_ref[place_ref[slot]]), w_out[slot, :, : 3 * DH], NT)
    first_exact, normed_one, inverse_one = norm_forward(
        in_ref[...].astype(F32) + attention + vec(0), vec(1), vec(2)
    )
    first = first_exact.astype(BF16)
    first_ref[...] = first

    def up(slot, branch):
        t = place_ref[slot]
        arrive(1, slot)
        hidden = dot(first, w_in[slot]) + inner_bias_ref[t]
        bend = 0.5 * (1.0 + lax.erf(hidden * ROOT_HALF))
        activated = (hidden * bend).astype(BF16)
        act_ref[t] = activated
        slope[slot] = bend + hidden * INV_ROOT_TAU * jnp.exp2(hidden * hidden * (-0.5 * LOG2E))
        arrive(2, slot)
        return branch + dot(activated, w_up[slot], NT)

    branch = lax.fori_loop(0, parts, up, jnp.zeros(in_ref.shape, F32))
    layer_rows, normed_two, inverse_two = norm_forward(first.astype(F32) + branch + vec(3), vec(4), vec(5))
    layer_ref[...] = layer_rows.astype(BF16)
    misfit = layer_rows - teacher_ref[...].astype(F32)
    weighted = valid_ref[...] * misfit
    out_grad = cotangent_ref[...].astype(F32) + weighted * ratio_ref[0]
    second_grad = norm_backward(out_grad, normed_two, inverse_two, vec(4))
    branch_grad = second_grad.astype(BF16)
    branch_grad_ref[...] = branch_grad
    sums_ref[0:1, :] = column_sum(weighted * misfit)
    sums_ref[1:2, :] = column_sum(branch_grad.astype(F32))
    sums_ref[2:3, :] = column_sum(out_grad * normed_two)
    sums_ref[3:4, :] = column_sum(out_grad)

    def down(slot, back):
        t = place_ref[slot]
        hidden_grad = (dot(branch_grad, w_up[slot]) * slope[slot]).astype(BF16)
        hidden_grad_ref[t] = hidden_grad
        inner_sums_ref[t] = column_sum(hidden_grad.astype(F32))
        return back + dot(hidden_grad, w_in[slot], NT)

    upstream = lax.fori_loop(0, parts, down, second_grad)
    first_grad = norm_backward(upstream, normed_one, inverse_one, vec(1))
    first_grad_ref[...] = first_grad
    attn_grad = first_grad.astype(BF16)
    attn_grad_ref[...] = attn_grad
    sums_ref[4:5, :] = column_sum(attn_grad.astype(F32))
    sums_ref[5:6, :] = column_sum(upstream * normed_one)
    sums_ref[6:7, :] = column_sum(upstream)
    sums_ref[7:8, :] = jnp.zeros_like(sums_ref[7:8, :])
    middle = BLOCK // 2
    for slot in range(parts):
        back = dot(attn_grad, w_out[slot, :, : 3 * DH]).astype(BF16)
        ctx_grad_ref[place_ref[slot]] = pack(
            back[:, : 2 * DH], back[:middle, 2 * DH :], back[middle:, 2 * DH :]
        )


def run_dense(half, marks, place, ratio, ctx, rows_in, teacher, cotangent, valid, vecs, inner_bias, pieces):
    parts = ctx.shape[0]
    width = rows_in.shape[1]
    hidden_cols = inner_bias.shape[2]
    out_cols = pieces[0].shape[2] - 2 * hidden_cols

    def mine(columns):
        return pl.BlockSpec((BLOCK, columns), lambda i: (half, 0))

    def fixed(shape):
        return pl.BlockSpec(shape, lambda i: (0,) * len(shape))

    low = jax.ShapeDtypeStruct((BLOCK, width), BF16)
    out_shape = (
        low,
        jax.ShapeDtypeStruct((BLOCK, width), F32),
        jax.ShapeDtypeStruct(ctx.shape, BF16),
        low,
        low,
        low,
        jax.ShapeDtypeStruct((parts, BLOCK, hidden_cols), BF16),
        jax.ShapeDtypeStruct((parts, BLOCK, hidden_cols), BF16),
        jax.ShapeDtypeStruct((8, width), F32),
        jax.ShapeDtypeStruct((parts, 1, hidden_cols), F32),
    )
    smem = pl.BlockSpec(memory_space=pltpu.SMEM)
    return pl.pallas_call(
        functools.partial(dense_chain, marks),
        out_shape=out_shape,
        grid=(1,),
        in_specs=[
            smem,
            smem,
            fixed(ctx.shape),
            mine(width),
            mine(width),
            mine(width),
            mine(1),
            fixed(vecs.shape),
            fixed(inner_bias.shape),
        ]
        + [pl.BlockSpec(memory_space=pl.ANY)] * len(pieces),
        out_specs=tuple(fixed(out.shape) for out in out_shape),
        scratch_shapes=[
            pltpu.VMEM((parts, width, out_cols), BF16),
            pltpu.VMEM((parts, width, hidden_cols), BF16),
            pltpu.VMEM((parts, width, hidden_cols), BF16),
            pltpu.VMEM((parts, BLOCK, hidden_cols), F32),
            pltpu.SemaphoreType.DMA((3, parts)),
        ],
        compiler_params=pltpu.CompilerParams(
            dimension_semantics=("arbitrary",), vmem_limit_bytes=VMEM_LIMIT
        ),
        cost_estimate=pl.CostEstimate(
            flops=BLOCK * width * (8 * hidden_cols + 4 * out_cols) * parts,
            bytes_accessed=18 << 20,
            transcendentals=2 * BLOCK * hidden_cols * parts,
        ),
        name="dense_chain",
    )(place, ratio, ctx, rows_in, teacher, cotangent, valid, vecs, inner_bias, *pieces)


def dense_weights(plans, halves, place_ref, *refs):
    firsts, branch_grads, attn_grads, acts, hidden_grads, ctxs = (
        refs[k * halves : (k + 1) * halves] for k in range(6)
    )
    notes_ref, outs = refs[6 * halves], refs[6 * halves + 1 : -3]
    turned, whole, sems = refs[-3:]
    step = pl.program_id(0)
    slots = whole.shape[0]

    @pl.when(step == 0)
    def _():
        for which, sources in enumerate((firsts, branch_grads, attn_grads)):
            for half, source in enumerate(sources):
                turned[which, :, half * BLOCK : (half + 1) * BLOCK] = jnp.transpose(source[...])

    def both(sources):
        return jnp.concatenate([source[0] for source in sources], axis=0)

    hidden_cols = acts[0].shape[2]
    whole[step, :, :hidden_cols] = dot(turned[0], both(hidden_grads)).astype(BF16)
    whole[step, :, hidden_cols : 2 * hidden_cols] = dot(turned[1], both(acts)).astype(BF16)
    ctx = jnp.concatenate([unpack(source[0]) for source in ctxs], axis=0)
    plain = 2 * hidden_cols + ctx.shape[1]
    whole[step, :, 2 * hidden_cols : plain] = dot(turned[2], ctx).astype(BF16)
    whole[step, :, plain : plain + notes_ref.shape[1]] = notes_ref[...]
    for out, (start, stop, turns) in zip(outs, plans):

        @pl.when((step >= start) & (step < stop))
        def _():
            block = out.shape[1]
            for at, turn in enumerate(turns):
                offset = 0
                if block < whole.shape[1]:
                    offset = pl.multiple_of((place_ref[slots] ^ turn) * block, block)
                pltpu.make_async_copy(
                    whole.at[step, pl.ds(offset, block), :],
                    out.at[at * (stop - start) + step - start],
                    sems.at[step],
                ).start()

    @pl.when(step == slots - 1)
    def _():
        for slot in range(slots):
            pltpu.make_async_copy(whole.at[slot], whole.at[slot], sems.at[slot]).wait()


def run_weights(plans, place, notes, firsts, branch_grads, attn_grads, acts, hidden_grads, ctxs):
    parts, _, hidden_cols = acts[0].shape
    halves = len(acts)
    width = firsts[0].shape[1]
    columns = 2 * hidden_cols + 3 * DH + notes.shape[1]

    def by_slot(rows, size):
        return pl.BlockSpec((1, rows, size), lambda s, place: (place[s], 0, 0))

    fixed = pl.BlockSpec((BLOCK, width), lambda s, place: (0, 0))
    outs = tuple(
        jax.ShapeDtypeStruct((len(turns) * (stop - start), block, columns), BF16)
        for start, stop, block, turns in plans
    )
    inner = tuple((start, stop, turns) for start, stop, _, turns in plans)
    return pl.pallas_call(
        functools.partial(dense_weights, inner, halves),
        out_shape=outs,
        grid_spec=pltpu.PrefetchScalarGridSpec(
            num_scalar_prefetch=1,
            grid=(parts,),
            in_specs=[fixed] * (3 * halves)
            + [by_slot(BLOCK, hidden_cols)] * (2 * halves)
            + [by_slot(PACKED, 2 * DH)] * halves
            + [pl.BlockSpec(notes.shape, lambda s, place: (0, 0))],
            out_specs=tuple(pl.BlockSpec(memory_space=pl.ANY) for _ in outs),
            scratch_shapes=[
                pltpu.VMEM((3, width, halves * BLOCK), BF16),
                pltpu.VMEM((parts, width, columns), BF16),
                pltpu.SemaphoreType.DMA((parts,)),
            ],
        ),
        compiler_params=pltpu.CompilerParams(
            dimension_semantics=("arbitrary",), vmem_limit_bytes=VMEM_LIMIT
        ),
        cost_estimate=pl.CostEstimate(
            flops=2 * halves * BLOCK * width * columns * parts,
            bytes_accessed=20 << 20,
            transcendentals=0,
        ),
        name="dense_weights",
    )(place, *firsts, *branch_grads, *attn_grads, *acts, *hidden_grads, *ctxs, notes)


def finish_dense(packed_ref, inner_ref, outer_ref, output_ref, notes_ref):
    hidden_cols = inner_ref.shape[1]
    summed = packed_ref[...].astype(F32)
    inner_ref[...] = summed[:, :hidden_cols]
    outer_ref[...] = summed[:, hidden_cols : 2 * hidden_cols]
    plain = 2 * hidden_cols + output_ref.shape[0]
    output_ref[...] = jnp.transpose(summed[:, 2 * hidden_cols : plain])
    notes_ref[...] = summed[:, plain:]


def run_finish_dense(packed, hidden_cols, head_cols):
    rows = packed.shape[0]
    return pl.pallas_call(
        finish_dense,
        out_shape=(
            jax.ShapeDtypeStruct((rows, hidden_cols), F32),
            jax.ShapeDtypeStruct((rows, hidden_cols), F32),
            jax.ShapeDtypeStruct((head_cols, rows), F32),
            jax.ShapeDtypeStruct((rows, packed.shape[1] - 2 * hidden_cols - head_cols), F32),
        ),
        name="finish_dense",
    )(packed)


def finish_heads(value_ref, *refs):
    summed = value_ref[...].astype(F32)
    heads = summed.shape[1] // SLAB
    for ref, which in zip(refs, (0, 2, 3, 1)):
        columns = [summed[:, SLAB * h + which * DH : SLAB * h + (which + 1) * DH] for h in range(heads)]
        ref[...] = jnp.concatenate(columns, axis=1)[: ref.shape[0]]


def run_finish_heads(value):
    rows, width = value.shape
    out = jax.ShapeDtypeStruct((rows, width // 4), F32)
    notes = jax.ShapeDtypeStruct((8, width // 4), F32)
    return pl.pallas_call(finish_heads, out_shape=(out, out, out, notes), name="finish_heads")(value)


def interleave(query, key, value, heads):
    rows = query.shape[0]
    parts = [part.reshape(rows, heads, 1, DH) for part in (query, jnp.zeros_like(query), key, value)]
    return jnp.concatenate(parts, axis=2).reshape(rows, heads * SLAB)


def swap(value, axis, bit):
    size = lax.axis_size(axis)
    return lax.ppermute(value, axis, [(i, i ^ bit) for i in range(size)])


def bits_of(axis):
    bit = 1
    while bit < lax.axis_size(axis):
        yield bit
        bit *= 2


def after(value, *others):
    return lax.optimization_barrier((value,) + others)[0]


def merge(held, other, axis, bit):
    mine_first = (lax.axis_index(axis) & bit) == 0
    return jnp.where(
        mine_first, jnp.concatenate([held, other], axis=0), jnp.concatenate([other, held], axis=0)
    )


def add_low(left_side, right_side):
    return (left_side.astype(F32) + right_side.astype(F32)).astype(BF16)


def add_halves(left_side, right_side):
    half = left_side.shape[0] // 2
    return (
        add_low(left_side[:half], right_side[:half]),
        add_low(left_side[half:], right_side[half:]),
    )


def scatter_rows(held):
    index = lax.axis_index("dp")
    for bit in bits_of("dp"):
        held = held.reshape((held.shape[0] // 2, 2) + held.shape[1:])
        own = (index & bit) // bit
        send = lax.dynamic_index_in_dim(held, 1 - own, 1, keepdims=False)
        keep = lax.dynamic_index_in_dim(held, own, 1, keepdims=False)
        held = add_low(keep, swap(send, "dp", bit))
    return held[0]


def local(
    inputs, segment_ids, valid_mask, teacher, cotangent,
    w_query, w_key, w_value, w_output, w_inner, w_outer,
    query_bias, value_bias, output_bias, inner_bias, outer_bias,
    gain_attn, shift_attn, gain_ffn, shift_ffn,
):
    _, part_len, width = inputs.shape
    parts = lax.axis_size("tensor")
    copies = lax.axis_size("dp")
    rank = lax.axis_index("tensor")
    total_tokens = part_len * parts * copies
    seq_len = part_len * parts
    head_cols = w_query.shape[1]
    heads = head_cols // DH
    hidden_cols = w_inner.shape[1]
    shard_rows = w_inner.shape[0]
    halves = part_len // BLOCK

    rows_in = inputs.reshape(part_len, width)
    tokens = lax.all_gather(rows_in, "tensor", axis=0, tiled=True)
    w_heads = interleave(w_query, w_key, w_value, heads)
    paired = shard_rows % 16 == 0 and parts == 4 and copies == 8

    valid_rows = valid_mask.astype(F32).reshape(part_len, 1)
    valid_count = jnp.sum(valid_mask.astype(F32))
    upper = jnp.floor(valid_count / 256.0)
    spot = lax.broadcasted_iota(jnp.int32, (shard_rows, DH), 0) * DH + lax.broadcasted_iota(
        jnp.int32, (shard_rows, DH), 1
    )
    count_row = jnp.where(spot == 0, upper, jnp.where(spot == 1, valid_count - 256.0 * upper, 0.0))
    mine = jnp.concatenate((w_inner, w_outer.T, w_output.T, count_row.astype(BF16)), axis=1)
    if paired:
        place = jnp.stack([rank, rank ^ 1, rank ^ 2, rank ^ 3, lax.axis_index("dp")]).astype(jnp.int32)
        pair = jnp.concatenate([mine[None], swap(mine[None], "tensor", 1)], axis=0)
        near = pair
        w_heads = merge(w_heads, swap(w_heads, "dp", 1), "dp", 1)
        turns = [0]
        for bit in (2, 4):
            turns = turns + [turn ^ bit for turn in turns]
            near = jnp.concatenate([near, swap(near, "dp", bit)], axis=0)
            w_heads = merge(w_heads, swap(w_heads, "dp", bit), "dp", bit)
            near, w_heads = lax.optimization_barrier((near, w_heads))
        near_other = swap(near, "dp", 1)
        tokens, pair = lax.optimization_barrier((tokens, pair))
        far = swap(pair, "tensor", 2)
    else:
        place = jnp.asarray(list(range(parts)) + [0], jnp.int32)
        weights = lax.all_gather(mine, ("tensor", "dp"), axis=0, tiled=False)
        for bit in bits_of("dp"):
            w_heads = merge(w_heads, swap(w_heads, "dp", bit), "dp", bit)

    mine_cols = rank * head_cols
    query_shift = lax.dynamic_slice_in_dim(query_bias, mine_cols, head_cols).astype(F32)
    value_shift = lax.dynamic_slice_in_dim(value_bias, mine_cols, head_cols).astype(F32)
    shifts = interleave(query_shift[None], jnp.zeros_like(query_shift)[None], value_shift[None], heads)
    qkv = [(dot(tokens, w_heads) + shifts).astype(BF16)]

    segment_row = segment_ids.reshape(seq_len)
    bounds = document_blocks(segment_row)
    seg_col = segment_row.reshape(seq_len, 1)
    seg_row = segment_row.reshape(1, seq_len)
    lane = rank.astype(jnp.int32).reshape(1)

    def exchange(packed_blocks):
        return lax.all_to_all(packed_blocks, "tensor", 0, 0)

    contexts, lses, arrived = [], [], []
    for half in range(halves):
        if paired and half == halves - 1:
            bounds, far = lax.optimization_barrier((bounds, after(far, contexts[0])))
            weights = lax.all_gather(far, "dp", axis=0, tiled=False)
        context, lse = run_forward((halves, half), lane, bounds, qkv, seg_col, seg_row)
        if paired and half == halves - 1:
            context, near_other = lax.optimization_barrier((context, near_other))
        contexts.append(context)
        lses.append(lse)
        arrived.append(exchange(context))
    if paired:
        weights = weights.reshape((copies * 2,) + mine.shape)
        pieces = [near, near_other, weights]
        marks = [[(slot, turn ^ flip, True) for turn in turns for slot in (0, 1)] for flip in (0, 1)]
        marks.append([(2 + at % 2, at // 2, False) for at in range(2 * copies)])
    else:
        pieces = [weights.reshape(parts, width, -1)]
        marks = [[(t, 0, False) for t in range(parts)]]
    counts = [piece.reshape((-1,) + mine.shape)[:, 0, -DH : 2 - DH].astype(F32) for piece in pieces + [weights]]
    counts = jnp.concatenate(counts[:-1] if paired else counts[-1:], axis=0)
    counted = 256.0 * jnp.sum(counts[:, 0]) + jnp.sum(counts[:, 1])
    ratio = (total_tokens / counted).reshape(1)

    vecs = jnp.stack(
        (output_bias, gain_attn, shift_attn, outer_bias, gain_ffn, shift_ffn, outer_bias, outer_bias)
    ).astype(F32)
    inner_rows = inner_bias.astype(F32).reshape(parts, 1, hidden_cols)
    teacher_rows = teacher.reshape(part_len, width)
    cotangent_rows = cotangent.reshape(part_len, width)
    chains = [
        run_dense(
            half, marks, place, ratio, arrived[half], rows_in, teacher_rows, cotangent_rows,
            valid_rows, vecs, inner_rows, pieces,
        )
        for half in range(halves)
    ]
    (
        layers, first_grads, context_grads, firsts, branch_grads, attn_grads, acts, hidden_grads,
        dense_sums, inner_sums,
    ) = zip(*chains)
    head_grads = [exchange(context_grad) for context_grad in context_grads]
    dense_sums = sum(dense_sums)
    inner_sums = sum(inner_sums)
    sources = (firsts, branch_grads, attn_grads, acts, hidden_grads, arrived)
    head_grads[:-1], sources = lax.optimization_barrier((head_grads[:-1], sources))
    notes = jnp.concatenate((dense_sums.reshape(-1), inner_sums.reshape(-1))).astype(BF16)
    room = -(-notes.shape[0] // (shard_rows * 128)) * 128
    notes = jnp.pad(notes, (0, shard_rows * room - notes.shape[0])).reshape(shard_rows, room)
    notes = jnp.tile(notes, (copies, 1))
    if paired:
        keep_turns = (0, 4, 2, 6)
        plans = (
            (0, 2, shard_rows, keep_turns),
            (0, 2, shard_rows, tuple(turn | 1 for turn in keep_turns)),
            (2, 4, width, (0,)),
        )
        keep, send, distant = run_weights(plans, place, notes, *sources)
        keep, send = (value.reshape((4, 2) + value.shape[1:]) for value in (keep, send))
        distant = lax.psum_scatter(distant, "dp", scatter_dimension=1, tiled=True)
        came = swap(send, "dp", 1)
    else:
        (packed,) = run_weights(((0, parts, width, (0,)),), place, notes, *sources)
        packed = lax.psum_scatter(packed, "dp", scatter_dimension=1, tiled=True)

    earlier, before = [], []
    for half in range(halves):
        if paired and half == halves - 1:
            came, before, head_grads[-1] = lax.optimization_barrier((came, before, head_grads[-1]))
            keep, send = add_halves(keep, came)
            keep, send, before = lax.optimization_barrier((keep, send, before))
            came = swap(send, "dp", 2)
        results = run_backward(
            (halves, half), lane, bounds, qkv, seg_col, seg_row, contexts[half], head_grads[half],
            lses[half], earlier, before,
        )
        if half < halves - 1:
            before, earlier = [results[0]], earlier + [results[1]]
    joined_grad, sums = results
    joined_grad = joined_grad.reshape(seq_len, -1)
    if paired:
        came, joined_grad = lax.optimization_barrier((came, joined_grad))
    attn_back = dot(joined_grad, w_heads, NT).astype(BF16)
    attn_back, sums, joined_grad = lax.optimization_barrier((attn_back, sums, joined_grad))
    attn_back = lax.psum_scatter(attn_back, "tensor", scatter_dimension=0, tiled=True)
    if paired:
        keep, send = add_halves(keep, came)
        keep, send, joined_grad = lax.optimization_barrier((keep, send, joined_grad))
        came = swap(send, "dp", 4)
    sums = sums.reshape(heads, 4, DH)
    sums = jnp.concatenate((sums[:, 0].reshape(1, head_cols), sums[:, 3].reshape(1, head_cols)), axis=1)
    for bit in bits_of("tensor"):
        sums = merge(sums, swap(sums, "tensor", bit), "tensor", bit)
    head_weights = dot(tokens, joined_grad, TN).reshape((copies, shard_rows, -1))
    if paired:
        came, head_weights = lax.optimization_barrier((came, head_weights))
        slots = jnp.concatenate([add_low(keep, came)[0], distant], axis=0)
        packed = jnp.stack(
            [lax.dynamic_index_in_dim(slots, rank ^ t, 0, keepdims=False) for t in range(parts)]
        )
    packed = lax.psum_scatter(packed, "tensor", scatter_dimension=0, tiled=True)[0]
    biases = jnp.concatenate((sums[:, :head_cols].reshape(-1), sums[:, head_cols:].reshape(-1)))
    biases = jnp.pad(
        biases.reshape(8, heads, 1, DH), ((0, shard_rows - 8), (0, 0), (1, 2), (0, 0))
    ).reshape(1, shard_rows, -1)
    query_grad, key_grad, value_grad, biases = run_finish_heads(
        scatter_rows((head_weights + biases).astype(BF16))
    )
    biases = biases.reshape(2, width)
    input_grad = jnp.concatenate(first_grads, axis=0) + attn_back.astype(F32)

    inner_grad, outer_grad, output_grad, notes = run_finish_dense(packed, hidden_cols, head_cols)
    notes = notes.reshape(-1)

    def total(which):
        return notes[which * width : (which + 1) * width]

    mse_loss = jnp.sum(total(0)) / (counted * width)
    return (
        jnp.concatenate(layers, axis=0).reshape(1, part_len, width),
        mse_loss,
        input_grad.reshape(1, part_len, width),
        query_grad,
        key_grad,
        value_grad,
        output_grad,
        inner_grad,
        outer_grad.T,
        biases[0],
        biases[1],
        total(4),
        notes[8 * width : 8 * width + hidden_cols * parts],
        total(1),
        total(5),
        total(6),
        total(2),
        total(3),
    )


def solution(mesh):
    shard = P("dp", "tensor", None)
    by_dp, by_tensor = P("dp", "tensor"), P("tensor", "dp")
    in_specs = (
        (shard, P("dp", None), by_dp, shard, shard)
        + (by_dp,) * 3
        + (by_tensor, by_dp, by_tensor)
        + (P(),) * 9
    )
    out_specs = (shard, P(), shard) + (by_dp,) * 3 + (by_tensor, by_dp, by_tensor) + (P(),) * 9
    return jax.shard_map(local, mesh=mesh, in_specs=in_specs, out_specs=out_specs, check_vma=False)
```

```python
import functools

import jax
import jax.numpy as jnp
from jax import lax
from jax.experimental import pallas as pl
from jax.experimental.pallas import tpu as pltpu
from jax.sharding import PartitionSpec as P

DH = 64
BLOCK = 256
SLAB = 4 * DH
EPSILON = 1e-12
ROOT_HALF = 0.7071067811865476
INV_ROOT_TAU = 0.3989422804014327
LOG2E = 1.4426950408889634
LN2 = 0.6931471805599453
SCALE = DH ** (-0.5)
MASKED = -1e30
VMEM_LIMIT = 60 << 20

BF16 = jnp.bfloat16
F32 = jnp.float32
NN = (((1,), (0,)), ((), ()))
NT = (((1,), (1,)), ((), ()))
TN = (((0,), (0,)), ((), ()))


def dot(left_side, right_side, dims=NN):
    return lax.dot_general(left_side, right_side, dims, preferred_element_type=F32)


def norm_forward(summed, gain_vec, shift_vec):
    average = jnp.mean(summed, axis=-1, keepdims=True)
    centered = summed - average
    variance = jnp.mean(centered * centered, axis=-1, keepdims=True)
    inverse = lax.rsqrt(variance + EPSILON)
    normed = centered * inverse
    return (normed * gain_vec + shift_vec, normed, inverse)


def norm_backward(upstream, normed, inverse, gain_vec):
    scaled = upstream * gain_vec
    first_mean = jnp.mean(scaled, axis=-1, keepdims=True)
    second_mean = jnp.mean(scaled * normed, axis=-1, keepdims=True)
    return inverse * (scaled - first_mean - normed * second_mean)


def column_sum(value):
    return jnp.sum(value, axis=0, keepdims=True)


def lane_is_right(rows):
    return lax.broadcasted_iota(jnp.int32, (rows, 2 * DH), 1) >= DH


def pack(first_two, third_top, third_bottom):
    return jnp.concatenate([first_two, jnp.concatenate([third_top, third_bottom], axis=1)], axis=0)


def unpack(packed):
    third = packed[BLOCK:]
    third = jnp.concatenate([third[:, :DH], third[:, DH:]], axis=0)
    return jnp.concatenate([packed[:BLOCK], third], axis=1)


def fetch_chunks(lane_ref, chunk_refs, target, sems):
    rows = chunk_refs[0].shape[0]
    copies = []
    for at, chunk in enumerate(chunk_refs):
        offset = pl.multiple_of(lax.rem(lane_ref[0] + at, len(chunk_refs)) * rows, rows)
        copies.append(pltpu.make_async_copy(chunk, target.at[pl.ds(offset, rows), :], sems.at[at]))
    return copies


def attend_forward(
    which, lane_ref, low_ref, high_ref, *refs
):
    chunk_refs, (seg_col_ref, seg_row_ref, ctx_ref, lse_ref, held, qkv_ref, sems) = refs[:-7], refs[-7:]
    halves, half = which
    heads = lse_ref.shape[0]

    @pl.when(pl.program_id(0) == 0)
    def _():
        copies = fetch_chunks(lane_ref, chunk_refs, qkv_ref, sems)
        for copy in copies:
            copy.start()
        for copy in copies:
            copy.wait()

    qb = pl.program_id(0) * halves + half
    rows = pl.ds(pl.multiple_of(qb * BLOCK, BLOCK), BLOCK)
    seg_q = seg_col_ref[...]
    queries = [
        qkv_ref[rows, SLAB * h : SLAB * h + 2 * DH] * jnp.asarray(SCALE, BF16) for h in range(heads)
    ]
    low, high = low_ref[qb], high_ref[qb]

    def score(kb, peaks):
        keys = pl.ds(pl.multiple_of(kb * BLOCK, BLOCK), BLOCK)
        allowed = seg_q == seg_row_ref[:, keys]
        found = []
        for h in range(heads):
            scores = dot(queries[h], qkv_ref[keys, SLAB * h + 2 * DH : SLAB * (h + 1)], NT)
            scores = jnp.where(allowed, scores, MASKED)
            held[h, kb] = scores
            found.append(jnp.maximum(peaks[h], jnp.maximum(scores[:, :128], scores[:, 128:])))
        return tuple(found)

    start = tuple(jnp.full((BLOCK, 128), MASKED, F32) for _ in range(heads))
    peaks = lax.fori_loop(low, high, score, start)
    highest = [jnp.max(peak, axis=-1, keepdims=True) for peak in peaks]

    def weigh(kb, carry):
        keys = pl.ds(pl.multiple_of(kb * BLOCK, BLOCK), BLOCK)
        found = []
        for h in range(heads):
            total, acc = carry[h]
            raised = jnp.exp2((held[h, kb] - highest[h]) * LOG2E)
            total = total + (raised[:, :128] + raised[:, 128:])
            acc = acc + dot(raised.astype(BF16), qkv_ref[keys, SLAB * h + 2 * DH : SLAB * (h + 1)])
            found.append((total, acc))
        return tuple(found)

    zero = jnp.zeros((BLOCK, 128), F32)
    done = lax.fori_loop(low, high, weigh, tuple((zero, zero) for _ in range(heads)))
    values = []
    for h in range(heads):
        total, acc = done[h]
        summed = jnp.sum(total, axis=-1, keepdims=True)
        values.append((acc / summed).astype(BF16))
        lse_ref[h] = jnp.transpose(highest[h] + jnp.log(summed))
    middle = BLOCK // 2
    ctx_ref[0, :BLOCK, :] = jnp.where(lane_is_right(BLOCK), values[1], pltpu.roll(values[0], DH, 1))
    ctx_ref[0, BLOCK:, :] = jnp.where(
        lane_is_right(middle), values[2][middle:], pltpu.roll(values[2][:middle], DH, 1)
    )


def attend_backward(which, chunks, lane_ref, low_ref, high_ref, *refs):
    halves, half = which
    last = half == halves - 1
    chunk_refs, refs = refs[:chunks], refs[chunks:]
    (seg_col_ref, seg_row_ref, ctx_ref, grad_ref, lse_ref), refs = refs[:5], refs[5:]
    earlier, refs = refs[:half], refs[half:]
    if half > 0:
        before_ref, refs = refs[0], refs[1:]
    if last:
        final_ref, sums_ref, dkv, out_ref, qkv_ref, sems = refs
    else:
        dkv, query_ref, qkv_ref, sems = refs
    heads = dkv.shape[0]
    step_index = pl.program_id(0)
    qb = step_index * halves + half

    @pl.when(step_index == 0)
    def _():
        copies = fetch_chunks(lane_ref, chunk_refs, qkv_ref, sems)
        for copy in copies:
            copy.start()
        dkv[...] = before_ref[...] if half > 0 else jnp.zeros_like(dkv)
        for copy in copies:
            copy.wait()

    rows = pl.ds(pl.multiple_of(qb * BLOCK, BLOCK), BLOCK)
    right = lane_is_right(BLOCK)
    arrived = grad_ref[0]
    product = arrived.astype(F32) * ctx_ref[0].astype(F32)
    upper = product.astype(BF16)
    lower = (product - upper.astype(F32)).astype(BF16)
    pick = (
        lax.broadcasted_iota(jnp.int32, (8, 2 * DH), 1) // DH
        == lax.broadcasted_iota(jnp.int32, (8, 2 * DH), 0)
    ).astype(BF16)
    summed = dot(pick, upper, NT) + dot(pick, lower, NT)
    deltas = [
        summed[0:1, :BLOCK],
        summed[1:2, :BLOCK],
        jnp.concatenate([summed[0:1, BLOCK:], summed[1:2, BLOCK:]], axis=1),
    ]
    two, third = arrived[:BLOCK], arrived[BLOCK:]
    placed = [
        pltpu.roll(two, DH, 1),
        two,
        jnp.concatenate([pltpu.roll(third, DH, 1), third], axis=0),
    ]
    grads = [jnp.where(right, grad, jnp.zeros_like(grad)) for grad in placed]
    queries, pairs = [], []
    for h in range(heads):
        queries.append(qkv_ref[rows, SLAB * h : SLAB * h + 2 * DH] * jnp.asarray(SCALE, BF16))
        pairs.append(jnp.concatenate([queries[h], grads[h]], axis=0))
    seg_q = seg_row_ref[...]
    lses = lse_ref[...]
    low, high = low_ref[qb], high_ref[qb]

    def step(kb, accs):
        keys = pl.ds(pl.multiple_of(kb * BLOCK, BLOCK), BLOCK)
        allowed = seg_col_ref[keys, :] == seg_q
        found = []
        for h in range(heads):
            pair = qkv_ref[keys, SLAB * h + 2 * DH : SLAB * (h + 1)]
            scores = jnp.where(allowed, dot(pair, queries[h], NT), MASKED)
            probs = jnp.exp2((scores - lses[h]) * LOG2E)
            score_grad = (probs * (dot(pair, grads[h], NT) - deltas[h])).astype(BF16)
            both = jnp.concatenate([score_grad, probs.astype(BF16)], axis=1)
            dkv[h, keys, :] += dot(both, pairs[h])
            found.append(accs[h] + dot(score_grad, pair, TN))
        return tuple(found)

    zero = jnp.zeros((BLOCK, 128), F32)
    accs = lax.fori_loop(low, high, step, tuple(zero for _ in range(heads)))
    for h in range(heads):
        query_grad = jnp.where(right, 0.0, accs[h] * SCALE).astype(BF16)
        if last:
            out_ref[rows, SLAB * h : SLAB * h + 2 * DH] = query_grad
        else:
            query_ref[0, :, 2 * DH * h : 2 * DH * (h + 1)] = query_grad

    if last:

        @pl.when(step_index == pl.num_programs(0) - 1)
        def _():
            for h in range(heads):
                at = SLAB * h
                for other, ref in enumerate(earlier):
                    for block in range(ref.shape[0]):
                        start = (block * halves + other) * BLOCK
                        out_ref[start : start + BLOCK, at : at + 2 * DH] = ref[
                            block, :, 2 * DH * h : 2 * DH * (h + 1)
                        ]
                out_ref[:, at + 2 * DH : at + SLAB] = dkv[h].astype(BF16)
                sums_ref[:, at : at + SLAB] = column_sum(out_ref[:, at : at + SLAB].astype(F32))
            rows_each = final_ref.shape[1]
            copies = []
            for at in range(final_ref.shape[0]):
                offset = pl.multiple_of(lax.rem(lane_ref[0] + at, final_ref.shape[0]) * rows_each, rows_each)
                copies.append(
                    pltpu.make_async_copy(
                        out_ref.at[pl.ds(offset, rows_each), :], final_ref.at[at], sems.at[at]
                    )
                )
            for copy in copies:
                copy.start()
            for copy in copies:
                copy.wait()


def document_blocks(segment_row):
    starts = segment_row[::BLOCK]
    stops = segment_row[BLOCK - 1 :: BLOCK]
    low = jnp.sum((segment_row[None, :] < starts[:, None]).astype(jnp.int32), axis=1)
    high = jnp.sum((segment_row[None, :] <= stops[:, None]).astype(jnp.int32), axis=1)
    return (low // BLOCK, (high + BLOCK - 1) // BLOCK)


PACKED = BLOCK + BLOCK // 2


def run_forward(which, lane, bounds, qkv, seg_col, seg_row):
    halves, half = which
    seq_len, width = seg_col.shape[0], qkv[0].shape[1]
    heads = width // SLAB
    blocks = seq_len // BLOCK
    steps = blocks // halves
    return pl.pallas_call(
        functools.partial(attend_forward, which),
        out_shape=(
            jax.ShapeDtypeStruct((steps, PACKED, 2 * DH), BF16),
            jax.ShapeDtypeStruct((heads, 1, steps * BLOCK), F32),
        ),
        grid_spec=pltpu.PrefetchScalarGridSpec(
            num_scalar_prefetch=3,
            grid=(steps,),
            in_specs=[pl.BlockSpec(memory_space=pl.ANY)] * len(qkv)
            + [
                pl.BlockSpec((BLOCK, 1), lambda q, *_: (q * halves + half, 0)),
                pl.BlockSpec((1, seq_len), lambda q, *_: (0, 0)),
            ],
            out_specs=(
                pl.BlockSpec((1, PACKED, 2 * DH), lambda q, *_: (q, 0, 0)),
                pl.BlockSpec((heads, 1, BLOCK), lambda q, *_: (0, 0, q)),
            ),
            scratch_shapes=[
                pltpu.VMEM((heads, blocks, BLOCK, BLOCK), F32),
                pltpu.VMEM((seq_len, width), BF16),
                pltpu.SemaphoreType.DMA((len(qkv),)),
            ],
        ),
        compiler_params=pltpu.CompilerParams(
            dimension_semantics=("arbitrary",), vmem_limit_bytes=VMEM_LIMIT
        ),
        cost_estimate=pl.CostEstimate(
            flops=heads * seq_len * seq_len * 256 // halves,
            bytes_accessed=5 << 20,
            transcendentals=heads * seq_len * seq_len // 3 // halves,
        ),
        name="attend_forward",
    )(lane, *bounds, *qkv, seg_col, seg_row)


def run_backward(which, lane, bounds, qkv, seg_col, seg_row, ctx, grad, lse, earlier, before):
    halves, half = which
    seq_len, width = seg_col.shape[0], qkv[0].shape[1]
    heads = width // SLAB
    steps = seq_len // BLOCK // halves
    packed = pl.BlockSpec((1, PACKED, 2 * DH), lambda q, *_: (q, 0, 0))

    def fixed(shape, **more):
        return pl.BlockSpec(shape, lambda q, *_: (0,) * len(shape), **more)

    once = {"pipeline_mode": pl.Buffered(1)}
    gathered = (heads, seq_len, 2 * DH)
    carried = [fixed(value.shape, **once) for value in earlier]
    carried += [fixed(gathered, **once)] * len(before)
    scratch = [pltpu.VMEM((seq_len, width), BF16), pltpu.SemaphoreType.DMA((len(qkv),))]
    if half == halves - 1:
        out_shape = (
            jax.ShapeDtypeStruct((len(qkv), seq_len // len(qkv), width), BF16),
            jax.ShapeDtypeStruct((1, width), F32),
        )
        out_specs = (pl.BlockSpec(memory_space=pl.ANY), fixed((1, width)))
        scratch = [pltpu.VMEM(gathered, F32), pltpu.VMEM((seq_len, width), BF16)] + scratch
    else:
        out_shape = (
            jax.ShapeDtypeStruct(gathered, F32),
            jax.ShapeDtypeStruct((steps, BLOCK, heads * 2 * DH), BF16),
        )
        out_specs = (
            fixed(gathered),
            pl.BlockSpec((1, BLOCK, heads * 2 * DH), lambda q, *_: (q, 0, 0)),
        )
    return pl.pallas_call(
        functools.partial(attend_backward, which, len(qkv)),
        out_shape=out_shape,
        grid_spec=pltpu.PrefetchScalarGridSpec(
            num_scalar_prefetch=3,
            grid=(steps,),
            in_specs=[pl.BlockSpec(memory_space=pl.ANY)] * len(qkv)
            + [
                fixed((seq_len, 1)),
                pl.BlockSpec((1, BLOCK), lambda q, *_: (0, q * halves + half)),
                packed,
                packed,
                pl.BlockSpec((heads, 1, BLOCK), lambda q, *_: (0, 0, q)),
            ]
            + carried,
            out_specs=out_specs,
            scratch_shapes=scratch,
        ),
        compiler_params=pltpu.CompilerParams(
            dimension_semantics=("arbitrary",), vmem_limit_bytes=VMEM_LIMIT
        ),
        cost_estimate=pl.CostEstimate(
            flops=heads * seq_len * seq_len * 640 // halves,
            bytes_accessed=10 << 20,
            transcendentals=heads * seq_len * seq_len // 3 // halves,
        ),
        name="attend_backward",
    )(lane, *bounds, *qkv, seg_col, seg_row, ctx, grad, lse, *earlier, *before)


def dense_chain(
    marks, place_ref, ratio_ref, ctx_ref, in_ref, teacher_ref, cotangent_ref, valid_ref, vec_ref,
    inner_bias_ref, *refs
):
    pieces = refs[: len(marks)]
    (
        layer_ref, first_grad_ref, ctx_grad_ref, first_ref, branch_grad_ref, attn_grad_ref,
        act_ref, hidden_grad_ref, sums_ref, inner_sums_ref, w_out, w_in, w_up, slope, sems,
    ) = refs[len(marks) :]
    parts, _, head_cols = w_out.shape
    hidden_cols = w_in.shape[2]
    index = place_ref[parts]
    groups = (
        (2 * hidden_cols, head_cols, w_out),
        (0, hidden_cols, w_in),
        (hidden_cols, hidden_cols, w_up),
    )
    for group, (start, size, target) in enumerate(groups):
        for piece, marked in zip(pieces, marks):
            block = piece.shape[1]
            for at, (slot, turn, relative) in enumerate(marked):
                offset = pl.multiple_of((index ^ turn) * block, block) if relative else turn * block
                pltpu.make_async_copy(
                    piece.at[at, :, pl.ds(start, size)],
                    target.at[slot, pl.ds(offset, block), :],
                    sems.at[group, slot],
                ).start()

    def arrive(group, slot):
        whole = groups[group][2].at[slot]
        pltpu.make_async_copy(whole, whole, sems.at[group, slot]).wait()

    def vec(which):
        return vec_ref[which : which + 1, :]

    inner_sums_ref[...] = jnp.zeros_like(inner_sums_ref)
    attention = jnp.zeros(in_ref.shape, F32)
    for slot in range(parts):
        arrive(0, slot)
        attention = attention + dot(unpack(ctx_ref[place_ref[slot]]), w_out[slot, :, : 3 * DH], NT)
    first_exact, normed_one, inverse_one = norm_forward(
        in_ref[...].astype(F32) + attention + vec(0), vec(1), vec(2)
    )
    first = first_exact.astype(BF16)
    first_ref[...] = first

    def up(slot, branch):
        t = place_ref[slot]
        arrive(1, slot)
        hidden = dot(first, w_in[slot]) + inner_bias_ref[t]
        bend = 0.5 * (1.0 + lax.erf(hidden * ROOT_HALF))
        activated = (hidden * bend).astype(BF16)
        act_ref[t] = activated
        slope[slot] = bend + hidden * INV_ROOT_TAU * jnp.exp2(hidden * hidden * (-0.5 * LOG2E))
        arrive(2, slot)
        return branch + dot(activated, w_up[slot], NT)

    branch = lax.fori_loop(0, parts, up, jnp.zeros(in_ref.shape, F32))
    layer_rows, normed_two, inverse_two = norm_forward(first.astype(F32) + branch + vec(3), vec(4), vec(5))
    layer_ref[...] = layer_rows.astype(BF16)
    misfit = layer_rows - teacher_ref[...].astype(F32)
    weighted = valid_ref[...] * misfit
    out_grad = cotangent_ref[...].astype(F32) + weighted * ratio_ref[0]
    second_grad = norm_backward(out_grad, normed_two, inverse_two, vec(4))
    branch_grad = second_grad.astype(BF16)
    branch_grad_ref[...] = branch_grad
    sums_ref[0:1, :] = column_sum(weighted * misfit)
    sums_ref[1:2, :] = column_sum(branch_grad.astype(F32))
    sums_ref[2:3, :] = column_sum(out_grad * normed_two)
    sums_ref[3:4, :] = column_sum(out_grad)

    def down(slot, back):
        t = place_ref[slot]
        hidden_grad = (dot(branch_grad, w_up[slot]) * slope[slot]).astype(BF16)
        hidden_grad_ref[t] = hidden_grad
        inner_sums_ref[t] = column_sum(hidden_grad.astype(F32))
        return back + dot(hidden_grad, w_in[slot], NT)

    upstream = lax.fori_loop(0, parts, down, second_grad)
    first_grad = norm_backward(upstream, normed_one, inverse_one, vec(1))
    first_grad_ref[...] = first_grad
    attn_grad = first_grad.astype(BF16)
    attn_grad_ref[...] = attn_grad
    sums_ref[4:5, :] = column_sum(attn_grad.astype(F32))
    sums_ref[5:6, :] = column_sum(upstream * normed_one)
    sums_ref[6:7, :] = column_sum(upstream)
    sums_ref[7:8, :] = jnp.zeros_like(sums_ref[7:8, :])
    middle = BLOCK // 2
    for slot in range(parts):
        back = dot(attn_grad, w_out[slot, :, : 3 * DH]).astype(BF16)
        ctx_grad_ref[place_ref[slot]] = pack(
            back[:, : 2 * DH], back[:middle, 2 * DH :], back[middle:, 2 * DH :]
        )


def run_dense(half, marks, place, ratio, ctx, rows_in, teacher, cotangent, valid, vecs, inner_bias, pieces):
    parts = ctx.shape[0]
    width = rows_in.shape[1]
    hidden_cols = inner_bias.shape[2]
    out_cols = pieces[0].shape[2] - 2 * hidden_cols

    def mine(columns):
        return pl.BlockSpec((BLOCK, columns), lambda i: (half, 0))

    def fixed(shape):
        return pl.BlockSpec(shape, lambda i: (0,) * len(shape))

    low = jax.ShapeDtypeStruct((BLOCK, width), BF16)
    out_shape = (
        low,
        jax.ShapeDtypeStruct((BLOCK, width), F32),
        jax.ShapeDtypeStruct(ctx.shape, BF16),
        low,
        low,
        low,
        jax.ShapeDtypeStruct((parts, BLOCK, hidden_cols), BF16),
        jax.ShapeDtypeStruct((parts, BLOCK, hidden_cols), BF16),
        jax.ShapeDtypeStruct((8, width), F32),
        jax.ShapeDtypeStruct((parts, 1, hidden_cols), F32),
    )
    smem = pl.BlockSpec(memory_space=pltpu.SMEM)
    return pl.pallas_call(
        functools.partial(dense_chain, marks),
        out_shape=out_shape,
        grid=(1,),
        in_specs=[
            smem,
            smem,
            fixed(ctx.shape),
            mine(width),
            mine(width),
            mine(width),
            mine(1),
            fixed(vecs.shape),
            fixed(inner_bias.shape),
        ]
        + [pl.BlockSpec(memory_space=pl.ANY)] * len(pieces),
        out_specs=tuple(fixed(out.shape) for out in out_shape),
        scratch_shapes=[
            pltpu.VMEM((parts, width, out_cols), BF16),
            pltpu.VMEM((parts, width, hidden_cols), BF16),
            pltpu.VMEM((parts, width, hidden_cols), BF16),
            pltpu.VMEM((parts, BLOCK, hidden_cols), F32),
            pltpu.SemaphoreType.DMA((3, parts)),
        ],
        compiler_params=pltpu.CompilerParams(
            dimension_semantics=("arbitrary",), vmem_limit_bytes=VMEM_LIMIT
        ),
        cost_estimate=pl.CostEstimate(
            flops=BLOCK * width * (8 * hidden_cols + 4 * out_cols) * parts,
            bytes_accessed=18 << 20,
            transcendentals=2 * BLOCK * hidden_cols * parts,
        ),
        name="dense_chain",
    )(place, ratio, ctx, rows_in, teacher, cotangent, valid, vecs, inner_bias, *pieces)


def dense_weights(plans, halves, place_ref, *refs):
    firsts, branch_grads, attn_grads, acts, hidden_grads, ctxs = (
        refs[k * halves : (k + 1) * halves] for k in range(6)
    )
    notes_ref, outs = refs[6 * halves], refs[6 * halves + 1 : -3]
    turned, whole, sems = refs[-3:]
    step = pl.program_id(0)
    slots = whole.shape[0]

    @pl.when(step == 0)
    def _():
        for which, sources in enumerate((firsts, branch_grads, attn_grads)):
            for half, source in enumerate(sources):
                turned[which, :, half * BLOCK : (half + 1) * BLOCK] = jnp.transpose(source[...])

    def both(sources):
        return jnp.concatenate([source[0] for source in sources], axis=0)

    hidden_cols = acts[0].shape[2]
    whole[step, :, :hidden_cols] = dot(turned[0], both(hidden_grads)).astype(BF16)
    whole[step, :, hidden_cols : 2 * hidden_cols] = dot(turned[1], both(acts)).astype(BF16)
    ctx = jnp.concatenate([unpack(source[0]) for source in ctxs], axis=0)
    plain = 2 * hidden_cols + ctx.shape[1]
    whole[step, :, 2 * hidden_cols : plain] = dot(turned[2], ctx).astype(BF16)
    whole[step, :, plain : plain + notes_ref.shape[1]] = notes_ref[...]
    for out, (start, stop, turns) in zip(outs, plans):

        @pl.when((step >= start) & (step < stop))
        def _():
            block = out.shape[1]
            for at, turn in enumerate(turns):
                offset = 0
                if block < whole.shape[1]:
                    offset = pl.multiple_of((place_ref[slots] ^ turn) * block, block)
                pltpu.make_async_copy(
                    whole.at[step, pl.ds(offset, block), :],
                    out.at[at * (stop - start) + step - start],
                    sems.at[step],
                ).start()

    @pl.when(step == slots - 1)
    def _():
        for slot in range(slots):
            pltpu.make_async_copy(whole.at[slot], whole.at[slot], sems.at[slot]).wait()


def run_weights(plans, place, notes, firsts, branch_grads, attn_grads, acts, hidden_grads, ctxs):
    parts, _, hidden_cols = acts[0].shape
    halves = len(acts)
    width = firsts[0].shape[1]
    columns = 2 * hidden_cols + 3 * DH + notes.shape[1]

    def by_slot(rows, size):
        return pl.BlockSpec((1, rows, size), lambda s, place: (place[s], 0, 0))

    fixed = pl.BlockSpec((BLOCK, width), lambda s, place: (0, 0))
    outs = tuple(
        jax.ShapeDtypeStruct((len(turns) * (stop - start), block, columns), BF16)
        for start, stop, block, turns in plans
    )
    inner = tuple((start, stop, turns) for start, stop, _, turns in plans)
    return pl.pallas_call(
        functools.partial(dense_weights, inner, halves),
        out_shape=outs,
        grid_spec=pltpu.PrefetchScalarGridSpec(
            num_scalar_prefetch=1,
            grid=(parts,),
            in_specs=[fixed] * (3 * halves)
            + [by_slot(BLOCK, hidden_cols)] * (2 * halves)
            + [by_slot(PACKED, 2 * DH)] * halves
            + [pl.BlockSpec(notes.shape, lambda s, place: (0, 0))],
            out_specs=tuple(pl.BlockSpec(memory_space=pl.ANY) for _ in outs),
            scratch_shapes=[
                pltpu.VMEM((3, width, halves * BLOCK), BF16),
                pltpu.VMEM((parts, width, columns), BF16),
                pltpu.SemaphoreType.DMA((parts,)),
            ],
        ),
        compiler_params=pltpu.CompilerParams(
            dimension_semantics=("arbitrary",), vmem_limit_bytes=VMEM_LIMIT
        ),
        cost_estimate=pl.CostEstimate(
            flops=2 * halves * BLOCK * width * columns * parts,
            bytes_accessed=20 << 20,
            transcendentals=0,
        ),
        name="dense_weights",
    )(place, *firsts, *branch_grads, *attn_grads, *acts, *hidden_grads, *ctxs, notes)


def finish_dense(packed_ref, inner_ref, outer_ref, output_ref, notes_ref):
    hidden_cols = inner_ref.shape[1]
    summed = packed_ref[...].astype(F32)
    inner_ref[...] = summed[:, :hidden_cols]
    outer_ref[...] = summed[:, hidden_cols : 2 * hidden_cols]
    plain = 2 * hidden_cols + output_ref.shape[0]
    output_ref[...] = jnp.transpose(summed[:, 2 * hidden_cols : plain])
    notes_ref[...] = summed[:, plain:]


def run_finish_dense(packed, hidden_cols, head_cols):
    rows = packed.shape[0]
    return pl.pallas_call(
        finish_dense,
        out_shape=(
            jax.ShapeDtypeStruct((rows, hidden_cols), F32),
            jax.ShapeDtypeStruct((rows, hidden_cols), F32),
            jax.ShapeDtypeStruct((head_cols, rows), F32),
            jax.ShapeDtypeStruct((rows, packed.shape[1] - 2 * hidden_cols - head_cols), F32),
        ),
        name="finish_dense",
    )(packed)


def finish_heads(value_ref, *refs):
    summed = value_ref[...].astype(F32)
    heads = summed.shape[1] // SLAB
    for ref, which in zip(refs, (0, 2, 3, 1)):
        columns = [summed[:, SLAB * h + which * DH : SLAB * h + (which + 1) * DH] for h in range(heads)]
        ref[...] = jnp.concatenate(columns, axis=1)[: ref.shape[0]]


def run_finish_heads(value):
    rows, width = value.shape
    out = jax.ShapeDtypeStruct((rows, width // 4), F32)
    notes = jax.ShapeDtypeStruct((8, width // 4), F32)
    return pl.pallas_call(finish_heads, out_shape=(out, out, out, notes), name="finish_heads")(value)


def interleave(query, key, value, heads):
    rows = query.shape[0]
    parts = [part.reshape(rows, heads, 1, DH) for part in (query, jnp.zeros_like(query), key, value)]
    return jnp.concatenate(parts, axis=2).reshape(rows, heads * SLAB)


def swap(value, axis, bit):
    size = lax.axis_size(axis)
    return lax.ppermute(value, axis, [(i, i ^ bit) for i in range(size)])


def bits_of(axis):
    bit = 1
    while bit < lax.axis_size(axis):
        yield bit
        bit *= 2


def after(value, *others):
    return lax.optimization_barrier((value,) + others)[0]


def merge(held, other, axis, bit):
    mine_first = (lax.axis_index(axis) & bit) == 0
    return jnp.where(
        mine_first, jnp.concatenate([held, other], axis=0), jnp.concatenate([other, held], axis=0)
    )


def add_low(left_side, right_side):
    return (left_side.astype(F32) + right_side.astype(F32)).astype(BF16)


def add_halves(left_side, right_side):
    half = left_side.shape[0] // 2
    return (
        add_low(left_side[:half], right_side[:half]),
        add_low(left_side[half:], right_side[half:]),
    )


def scatter_rows(held):
    index = lax.axis_index("dp")
    for bit in bits_of("dp"):
        held = held.reshape((held.shape[0] // 2, 2) + held.shape[1:])
        own = (index & bit) // bit
        send = lax.dynamic_index_in_dim(held, 1 - own, 1, keepdims=False)
        keep = lax.dynamic_index_in_dim(held, own, 1, keepdims=False)
        held = add_low(keep, swap(send, "dp", bit))
    return held[0]


def local(
    inputs, segment_ids, valid_mask, teacher, cotangent,
    w_query, w_key, w_value, w_output, w_inner, w_outer,
    query_bias, value_bias, output_bias, inner_bias, outer_bias,
    gain_attn, shift_attn, gain_ffn, shift_ffn,
):
    _, part_len, width = inputs.shape
    parts = lax.axis_size("tensor")
    copies = lax.axis_size("dp")
    rank = lax.axis_index("tensor")
    total_tokens = part_len * parts * copies
    seq_len = part_len * parts
    head_cols = w_query.shape[1]
    heads = head_cols // DH
    hidden_cols = w_inner.shape[1]
    shard_rows = w_inner.shape[0]
    halves = part_len // BLOCK

    rows_in = inputs.reshape(part_len, width)
    tokens = lax.all_gather(rows_in, "tensor", axis=0, tiled=True)
    w_heads = interleave(w_query, w_key, w_value, heads)
    paired = shard_rows % 16 == 0 and parts == 4 and copies == 8

    valid_rows = valid_mask.astype(F32).reshape(part_len, 1)
    valid_count = jnp.sum(valid_mask.astype(F32))
    upper = jnp.floor(valid_count / 256.0)
    spot = lax.broadcasted_iota(jnp.int32, (shard_rows, DH), 0) * DH + lax.broadcasted_iota(
        jnp.int32, (shard_rows, DH), 1
    )
    count_row = jnp.where(spot == 0, upper, jnp.where(spot == 1, valid_count - 256.0 * upper, 0.0))
    mine = jnp.concatenate((w_inner, w_outer.T, w_output.T, count_row.astype(BF16)), axis=1)
    if paired:
        place = jnp.stack([rank, rank ^ 1, rank ^ 2, rank ^ 3, lax.axis_index("dp")]).astype(jnp.int32)
        pair = jnp.concatenate([mine[None], swap(mine[None], "tensor", 1)], axis=0)
        far = [swap(pair[slot : slot + 1], "tensor", 2) for slot in range(2)]
        near = jnp.concatenate([pair, swap(pair, "dp", 2)], axis=0)
        turns = [0, 2, 4, 6]
        for bit in (1, 2, 4):
            w_heads = merge(w_heads, swap(w_heads, "dp", bit), "dp", bit)
        near, w_heads, far[0] = lax.optimization_barrier((near, w_heads, far[0]))
        near = jnp.concatenate([near, swap(near, "dp", 4)], axis=0)
        tokens, far, near = lax.optimization_barrier((tokens, far, near))
        near_other = swap(near, "dp", 1)
        far = jnp.concatenate(far, axis=0)
        weights = lax.all_gather(far, "dp", axis=0, tiled=False)
    else:
        place = jnp.asarray(list(range(parts)) + [0], jnp.int32)
        weights = lax.all_gather(mine, ("tensor", "dp"), axis=0, tiled=False)
        for bit in bits_of("dp"):
            w_heads = merge(w_heads, swap(w_heads, "dp", bit), "dp", bit)

    mine_cols = rank * head_cols
    query_shift = lax.dynamic_slice_in_dim(query_bias, mine_cols, head_cols).astype(F32)
    value_shift = lax.dynamic_slice_in_dim(value_bias, mine_cols, head_cols).astype(F32)
    shifts = interleave(query_shift[None], jnp.zeros_like(query_shift)[None], value_shift[None], heads)
    qkv = [(dot(tokens, w_heads) + shifts).astype(BF16)]

    segment_row = segment_ids.reshape(seq_len)
    bounds = document_blocks(segment_row)
    seg_col = segment_row.reshape(seq_len, 1)
    seg_row = segment_row.reshape(1, seq_len)
    lane = rank.astype(jnp.int32).reshape(1)

    def exchange(packed_blocks):
        return lax.all_to_all(packed_blocks, "tensor", 0, 0)

    contexts, lses, arrived = [], [], []
    for half in range(halves):
        context, lse = run_forward((halves, half), lane, bounds, qkv, seg_col, seg_row)
        if paired and half == 0:
            context, near_other = lax.optimization_barrier((context, near_other))
        contexts.append(context)
        lses.append(lse)
        arrived.append(exchange(context))
    if paired:
        weights = weights.reshape((copies * 2,) + mine.shape)
        pieces = [near, near_other, weights]
        marks = [[(slot, turn ^ flip, True) for turn in turns for slot in (0, 1)] for flip in (0, 1)]
        marks.append([(2 + at % 2, at // 2, False) for at in range(2 * copies)])
    else:
        pieces = [weights.reshape(parts, width, -1)]
        marks = [[(t, 0, False) for t in range(parts)]]
    counts = [piece.reshape((-1,) + mine.shape)[:, 0, -DH : 2 - DH].astype(F32) for piece in pieces + [weights]]
    counts = jnp.concatenate(counts[:-1] if paired else counts[-1:], axis=0)
    counted = 256.0 * jnp.sum(counts[:, 0]) + jnp.sum(counts[:, 1])
    ratio = (total_tokens / counted).reshape(1)

    vecs = jnp.stack(
        (output_bias, gain_attn, shift_attn, outer_bias, gain_ffn, shift_ffn, outer_bias, outer_bias)
    ).astype(F32)
    inner_rows = inner_bias.astype(F32).reshape(parts, 1, hidden_cols)
    teacher_rows = teacher.reshape(part_len, width)
    cotangent_rows = cotangent.reshape(part_len, width)
    chains = [
        run_dense(
            half, marks, place, ratio, arrived[half], rows_in, teacher_rows, cotangent_rows,
            valid_rows, vecs, inner_rows, pieces,
        )
        for half in range(halves)
    ]
    (
        layers, first_grads, context_grads, firsts, branch_grads, attn_grads, acts, hidden_grads,
        dense_sums, inner_sums,
    ) = zip(*chains)
    head_grads = [exchange(context_grad) for context_grad in context_grads]
    dense_sums = sum(dense_sums)
    inner_sums = sum(inner_sums)
    sources = (firsts, branch_grads, attn_grads, acts, hidden_grads, arrived)
    head_grads[:-1], sources = lax.optimization_barrier((head_grads[:-1], sources))
    notes = jnp.concatenate((dense_sums.reshape(-1), inner_sums.reshape(-1))).astype(BF16)
    room = -(-notes.shape[0] // (shard_rows * 128)) * 128
    notes = jnp.pad(notes, (0, shard_rows * room - notes.shape[0])).reshape(shard_rows, room)
    notes = jnp.tile(notes, (copies, 1))
    if paired:
        keep_turns = (0, 4, 2, 6)
        plans = (
            (0, 2, shard_rows, keep_turns),
            (0, 2, shard_rows, tuple(turn | 1 for turn in keep_turns)),
            (2, 4, width, (0,)),
        )
        keep, send, distant = run_weights(plans, place, notes, *sources)
        keep, send = (value.reshape((4, 2) + value.shape[1:]) for value in (keep, send))
        distant = lax.psum_scatter(distant, "dp", scatter_dimension=1, tiled=True)
        came = swap(send, "dp", 1)
    else:
        (packed,) = run_weights(((0, parts, width, (0,)),), place, notes, *sources)
        packed = lax.psum_scatter(packed, "dp", scatter_dimension=1, tiled=True)

    earlier, before = [], []
    for half in range(halves):
        if paired and half == halves - 1:
            before, head_grads[-1] = lax.optimization_barrier((before, head_grads[-1]))
        results = run_backward(
            (halves, half), lane, bounds, qkv, seg_col, seg_row, contexts[half], head_grads[half],
            lses[half], earlier, before,
        )
        if half < halves - 1:
            before, earlier = [results[0]], earlier + [results[1]]
    joined_grad, sums = results
    joined_grad = joined_grad.reshape(seq_len, -1)
    attn_back = dot(joined_grad, w_heads, NT).astype(BF16)
    if paired:
        came = after(came, attn_back)
    attn_back, sums, joined_grad = lax.optimization_barrier((attn_back, sums, joined_grad))
    attn_back = lax.psum_scatter(attn_back, "tensor", scatter_dimension=0, tiled=True)
    if paired:
        keep, send = add_halves(keep, came)
        keep, send, joined_grad = lax.optimization_barrier((keep, send, joined_grad))
        came = swap(send, "dp", 2)
    head_weights = dot(tokens, joined_grad, TN).reshape((copies, shard_rows, -1))
    if paired:
        came, head_weights = lax.optimization_barrier((came, head_weights))
        keep, send = add_halves(keep, came)
        keep, send, head_weights = lax.optimization_barrier((keep, send, head_weights))
        came = swap(send, "dp", 4)
    sums = sums.reshape(heads, 4, DH)
    sums = jnp.concatenate((sums[:, 0].reshape(1, head_cols), sums[:, 3].reshape(1, head_cols)), axis=1)
    for bit in bits_of("tensor"):
        sums = merge(sums, swap(sums, "tensor", bit), "tensor", bit)
    if paired:
        came, head_weights = lax.optimization_barrier((came, head_weights))
        slots = jnp.concatenate([add_low(keep, came)[0], distant], axis=0)
        packed = jnp.stack(
            [lax.dynamic_index_in_dim(slots, rank ^ t, 0, keepdims=False) for t in range(parts)]
        )
    packed = lax.psum_scatter(packed, "tensor", scatter_dimension=0, tiled=True)[0]
    biases = jnp.concatenate((sums[:, :head_cols].reshape(-1), sums[:, head_cols:].reshape(-1)))
    biases = jnp.pad(
        biases.reshape(8, heads, 1, DH), ((0, shard_rows - 8), (0, 0), (1, 2), (0, 0))
    ).reshape(1, shard_rows, -1)
    query_grad, key_grad, value_grad, biases = run_finish_heads(
        scatter_rows((head_weights + biases).astype(BF16))
    )
    biases = biases.reshape(2, width)
    input_grad = jnp.concatenate(first_grads, axis=0) + attn_back.astype(F32)

    inner_grad, outer_grad, output_grad, notes = run_finish_dense(packed, hidden_cols, head_cols)
    notes = notes.reshape(-1)

    def total(which):
        return notes[which * width : (which + 1) * width]

    mse_loss = jnp.sum(total(0)) / (counted * width)
    return (
        jnp.concatenate(layers, axis=0).reshape(1, part_len, width),
        mse_loss,
        input_grad.reshape(1, part_len, width),
        query_grad,
        key_grad,
        value_grad,
        output_grad,
        inner_grad,
        outer_grad.T,
        biases[0],
        biases[1],
        total(4),
        notes[8 * width : 8 * width + hidden_cols * parts],
        total(1),
        total(5),
        total(6),
        total(2),
        total(3),
    )


def solution(mesh):
    shard = P("dp", "tensor", None)
    by_dp, by_tensor = P("dp", "tensor"), P("tensor", "dp")
    in_specs = (
        (shard, P("dp", None), by_dp, shard, shard)
        + (by_dp,) * 3
        + (by_tensor, by_dp, by_tensor)
        + (P(),) * 9
    )
    out_specs = (shard, P(), shard) + (by_dp,) * 3 + (by_tensor, by_dp, by_tensor) + (P(),) * 9
    return jax.shard_map(local, mesh=mesh, in_specs=in_specs, out_specs=out_specs, check_vma=False)
```

```python
import functools

import jax
import jax.numpy as jnp
from jax import lax
from jax.experimental import pallas as pl
from jax.experimental.pallas import tpu as pltpu
from jax.sharding import PartitionSpec as P

DH = 64
BLOCK = 256
SLAB = 4 * DH
EPSILON = 1e-12
ROOT_HALF = 0.7071067811865476
INV_ROOT_TAU = 0.3989422804014327
LOG2E = 1.4426950408889634
LN2 = 0.6931471805599453
SCALE = DH ** (-0.5)
MASKED = -1e30
VMEM_LIMIT = 60 << 20

BF16 = jnp.bfloat16
F32 = jnp.float32
NN = (((1,), (0,)), ((), ()))
NT = (((1,), (1,)), ((), ()))
TN = (((0,), (0,)), ((), ()))


def dot(left_side, right_side, dims=NN):
    return lax.dot_general(left_side, right_side, dims, preferred_element_type=F32)


def norm_forward(summed, gain_vec, shift_vec):
    average = jnp.mean(summed, axis=-1, keepdims=True)
    centered = summed - average
    variance = jnp.mean(centered * centered, axis=-1, keepdims=True)
    inverse = lax.rsqrt(variance + EPSILON)
    normed = centered * inverse
    return (normed * gain_vec + shift_vec, normed, inverse)


def norm_backward(upstream, normed, inverse, gain_vec):
    scaled = upstream * gain_vec
    first_mean = jnp.mean(scaled, axis=-1, keepdims=True)
    second_mean = jnp.mean(scaled * normed, axis=-1, keepdims=True)
    return inverse * (scaled - first_mean - normed * second_mean)


def column_sum(value):
    return jnp.sum(value, axis=0, keepdims=True)


def lane_is_right(rows):
    return lax.broadcasted_iota(jnp.int32, (rows, 2 * DH), 1) >= DH


def pack(first_two, third_top, third_bottom):
    return jnp.concatenate([first_two, jnp.concatenate([third_top, third_bottom], axis=1)], axis=0)


def unpack(packed):
    third = packed[BLOCK:]
    third = jnp.concatenate([third[:, :DH], third[:, DH:]], axis=0)
    return jnp.concatenate([packed[:BLOCK], third], axis=1)


def fetch_chunks(lane_ref, chunk_refs, target, sems):
    rows = chunk_refs[0].shape[0]
    copies = []
    for at, chunk in enumerate(chunk_refs):
        offset = pl.multiple_of(lax.rem(lane_ref[0] + at, len(chunk_refs)) * rows, rows)
        copies.append(pltpu.make_async_copy(chunk, target.at[pl.ds(offset, rows), :], sems.at[at]))
    return copies


def attend_forward(
    which, lane_ref, low_ref, high_ref, *refs
):
    chunk_refs, (seg_col_ref, seg_row_ref, ctx_ref, lse_ref, held, qkv_ref, sems) = refs[:-7], refs[-7:]
    halves, half = which
    heads = lse_ref.shape[0]

    @pl.when(pl.program_id(0) == 0)
    def _():
        copies = fetch_chunks(lane_ref, chunk_refs, qkv_ref, sems)
        for copy in copies:
            copy.start()
        for copy in copies:
            copy.wait()

    qb = pl.program_id(0) * halves + half
    rows = pl.ds(pl.multiple_of(qb * BLOCK, BLOCK), BLOCK)
    seg_q = seg_col_ref[...]
    queries = [
        qkv_ref[rows, SLAB * h : SLAB * h + 2 * DH] * jnp.asarray(SCALE, BF16) for h in range(heads)
    ]
    low, high = low_ref[qb], high_ref[qb]

    def score(kb, peaks):
        keys = pl.ds(pl.multiple_of(kb * BLOCK, BLOCK), BLOCK)
        allowed = seg_q == seg_row_ref[:, keys]
        found = []
        for h in range(heads):
            scores = dot(queries[h], qkv_ref[keys, SLAB * h + 2 * DH : SLAB * (h + 1)], NT)
            scores = jnp.where(allowed, scores, MASKED)
            held[h, kb] = scores
            found.append(jnp.maximum(peaks[h], jnp.maximum(scores[:, :128], scores[:, 128:])))
        return tuple(found)

    start = tuple(jnp.full((BLOCK, 128), MASKED, F32) for _ in range(heads))
    peaks = lax.fori_loop(low, high, score, start)
    highest = [jnp.max(peak, axis=-1, keepdims=True) for peak in peaks]

    def weigh(kb, carry):
        keys = pl.ds(pl.multiple_of(kb * BLOCK, BLOCK), BLOCK)
        found = []
        for h in range(heads):
            total, acc = carry[h]
            raised = jnp.exp2((held[h, kb] - highest[h]) * LOG2E)
            total = total + (raised[:, :128] + raised[:, 128:])
            acc = acc + dot(raised.astype(BF16), qkv_ref[keys, SLAB * h + 2 * DH : SLAB * (h + 1)])
            found.append((total, acc))
        return tuple(found)

    zero = jnp.zeros((BLOCK, 128), F32)
    done = lax.fori_loop(low, high, weigh, tuple((zero, zero) for _ in range(heads)))
    values = []
    for h in range(heads):
        total, acc = done[h]
        summed = jnp.sum(total, axis=-1, keepdims=True)
        values.append((acc / summed).astype(BF16))
        lse_ref[h] = jnp.transpose(highest[h] + jnp.log(summed))
    middle = BLOCK // 2
    ctx_ref[0, :BLOCK, :] = jnp.where(lane_is_right(BLOCK), values[1], pltpu.roll(values[0], DH, 1))
    ctx_ref[0, BLOCK:, :] = jnp.where(
        lane_is_right(middle), values[2][middle:], pltpu.roll(values[2][:middle], DH, 1)
    )


def attend_backward(which, chunks, lane_ref, low_ref, high_ref, *refs):
    halves, half = which
    last = half == halves - 1
    chunk_refs, refs = refs[:chunks], refs[chunks:]
    (seg_col_ref, seg_row_ref, ctx_ref, grad_ref, lse_ref), refs = refs[:5], refs[5:]
    earlier, refs = refs[:half], refs[half:]
    if half > 0:
        before_ref, refs = refs[0], refs[1:]
    if last:
        final_ref, sums_ref, dkv, out_ref, qkv_ref, sems = refs
    else:
        dkv, query_ref, qkv_ref, sems = refs
    heads = dkv.shape[0]
    step_index = pl.program_id(0)
    qb = step_index * halves + half

    @pl.when(step_index == 0)
    def _():
        copies = fetch_chunks(lane_ref, chunk_refs, qkv_ref, sems)
        for copy in copies:
            copy.start()
        dkv[...] = before_ref[...] if half > 0 else jnp.zeros_like(dkv)
        for copy in copies:
            copy.wait()

    rows = pl.ds(pl.multiple_of(qb * BLOCK, BLOCK), BLOCK)
    right = lane_is_right(BLOCK)
    arrived = grad_ref[0]
    product = arrived.astype(F32) * ctx_ref[0].astype(F32)
    upper = product.astype(BF16)
    lower = (product - upper.astype(F32)).astype(BF16)
    pick = (
        lax.broadcasted_iota(jnp.int32, (8, 2 * DH), 1) // DH
        == lax.broadcasted_iota(jnp.int32, (8, 2 * DH), 0)
    ).astype(BF16)
    summed = dot(pick, upper, NT) + dot(pick, lower, NT)
    deltas = [
        summed[0:1, :BLOCK],
        summed[1:2, :BLOCK],
        jnp.concatenate([summed[0:1, BLOCK:], summed[1:2, BLOCK:]], axis=1),
    ]
    two, third = arrived[:BLOCK], arrived[BLOCK:]
    placed = [
        pltpu.roll(two, DH, 1),
        two,
        jnp.concatenate([pltpu.roll(third, DH, 1), third], axis=0),
    ]
    grads = [jnp.where(right, grad, jnp.zeros_like(grad)) for grad in placed]
    queries, pairs = [], []
    for h in range(heads):
        queries.append(qkv_ref[rows, SLAB * h : SLAB * h + 2 * DH] * jnp.asarray(SCALE, BF16))
        pairs.append(jnp.concatenate([queries[h], grads[h]], axis=0))
    seg_q = seg_row_ref[...]
    lses = lse_ref[...]
    low, high = low_ref[qb], high_ref[qb]

    def step(kb, accs):
        keys = pl.ds(pl.multiple_of(kb * BLOCK, BLOCK), BLOCK)
        allowed = seg_col_ref[keys, :] == seg_q
        found = []
        for h in range(heads):
            pair = qkv_ref[keys, SLAB * h + 2 * DH : SLAB * (h + 1)]
            scores = jnp.where(allowed, dot(pair, queries[h], NT), MASKED)
            probs = jnp.exp2((scores - lses[h]) * LOG2E)
            score_grad = (probs * (dot(pair, grads[h], NT) - deltas[h])).astype(BF16)
            both = jnp.concatenate([score_grad, probs.astype(BF16)], axis=1)
            dkv[h, keys, :] += dot(both, pairs[h])
            found.append(accs[h] + dot(score_grad, pair, TN))
        return tuple(found)

    zero = jnp.zeros((BLOCK, 128), F32)
    accs = lax.fori_loop(low, high, step, tuple(zero for _ in range(heads)))
    for h in range(heads):
        query_grad = jnp.where(right, 0.0, accs[h] * SCALE).astype(BF16)
        if last:
            out_ref[rows, SLAB * h : SLAB * h + 2 * DH] = query_grad
        else:
            query_ref[0, :, 2 * DH * h : 2 * DH * (h + 1)] = query_grad

    if last:

        @pl.when(step_index == pl.num_programs(0) - 1)
        def _():
            for h in range(heads):
                at = SLAB * h
                for other, ref in enumerate(earlier):
                    for block in range(ref.shape[0]):
                        start = (block * halves + other) * BLOCK
                        out_ref[start : start + BLOCK, at : at + 2 * DH] = ref[
                            block, :, 2 * DH * h : 2 * DH * (h + 1)
                        ]
                out_ref[:, at + 2 * DH : at + SLAB] = dkv[h].astype(BF16)
                sums_ref[:, at : at + SLAB] = column_sum(out_ref[:, at : at + SLAB].astype(F32))
            rows_each = final_ref.shape[1]
            copies = []
            for at in range(final_ref.shape[0]):
                offset = pl.multiple_of(lax.rem(lane_ref[0] + at, final_ref.shape[0]) * rows_each, rows_each)
                copies.append(
                    pltpu.make_async_copy(
                        out_ref.at[pl.ds(offset, rows_each), :], final_ref.at[at], sems.at[at]
                    )
                )
            for copy in copies:
                copy.start()
            for copy in copies:
                copy.wait()


def document_blocks(segment_row):
    starts = segment_row[::BLOCK]
    stops = segment_row[BLOCK - 1 :: BLOCK]
    low = jnp.sum((segment_row[None, :] < starts[:, None]).astype(jnp.int32), axis=1)
    high = jnp.sum((segment_row[None, :] <= stops[:, None]).astype(jnp.int32), axis=1)
    return (low // BLOCK, (high + BLOCK - 1) // BLOCK)


PACKED = BLOCK + BLOCK // 2


def run_forward(which, lane, bounds, qkv, seg_col, seg_row):
    halves, half = which
    seq_len, width = seg_col.shape[0], qkv[0].shape[1]
    heads = width // SLAB
    blocks = seq_len // BLOCK
    steps = blocks // halves
    return pl.pallas_call(
        functools.partial(attend_forward, which),
        out_shape=(
            jax.ShapeDtypeStruct((steps, PACKED, 2 * DH), BF16),
            jax.ShapeDtypeStruct((heads, 1, steps * BLOCK), F32),
        ),
        grid_spec=pltpu.PrefetchScalarGridSpec(
            num_scalar_prefetch=3,
            grid=(steps,),
            in_specs=[pl.BlockSpec(memory_space=pl.ANY)] * len(qkv)
            + [
                pl.BlockSpec((BLOCK, 1), lambda q, *_: (q * halves + half, 0)),
                pl.BlockSpec((1, seq_len), lambda q, *_: (0, 0)),
            ],
            out_specs=(
                pl.BlockSpec((1, PACKED, 2 * DH), lambda q, *_: (q, 0, 0)),
                pl.BlockSpec((heads, 1, BLOCK), lambda q, *_: (0, 0, q)),
            ),
            scratch_shapes=[
                pltpu.VMEM((heads, blocks, BLOCK, BLOCK), F32),
                pltpu.VMEM((seq_len, width), BF16),
                pltpu.SemaphoreType.DMA((len(qkv),)),
            ],
        ),
        compiler_params=pltpu.CompilerParams(
            dimension_semantics=("arbitrary",), vmem_limit_bytes=VMEM_LIMIT
        ),
        cost_estimate=pl.CostEstimate(
            flops=heads * seq_len * seq_len * 256 // halves,
            bytes_accessed=5 << 20,
            transcendentals=heads * seq_len * seq_len // 3 // halves,
        ),
        name="attend_forward",
    )(lane, *bounds, *qkv, seg_col, seg_row)


def run_backward(which, lane, bounds, qkv, seg_col, seg_row, ctx, grad, lse, earlier, before):
    halves, half = which
    seq_len, width = seg_col.shape[0], qkv[0].shape[1]
    heads = width // SLAB
    steps = seq_len // BLOCK // halves
    packed = pl.BlockSpec((1, PACKED, 2 * DH), lambda q, *_: (q, 0, 0))

    def fixed(shape, **more):
        return pl.BlockSpec(shape, lambda q, *_: (0,) * len(shape), **more)

    once = {"pipeline_mode": pl.Buffered(1)}
    gathered = (heads, seq_len, 2 * DH)
    carried = [fixed(value.shape, **once) for value in earlier]
    carried += [fixed(gathered, **once)] * len(before)
    scratch = [pltpu.VMEM((seq_len, width), BF16), pltpu.SemaphoreType.DMA((len(qkv),))]
    if half == halves - 1:
        out_shape = (
            jax.ShapeDtypeStruct((len(qkv), seq_len // len(qkv), width), BF16),
            jax.ShapeDtypeStruct((1, width), F32),
        )
        out_specs = (pl.BlockSpec(memory_space=pl.ANY), fixed((1, width)))
        scratch = [pltpu.VMEM(gathered, F32), pltpu.VMEM((seq_len, width), BF16)] + scratch
    else:
        out_shape = (
            jax.ShapeDtypeStruct(gathered, F32),
            jax.ShapeDtypeStruct((steps, BLOCK, heads * 2 * DH), BF16),
        )
        out_specs = (
            fixed(gathered),
            pl.BlockSpec((1, BLOCK, heads * 2 * DH), lambda q, *_: (q, 0, 0)),
        )
    return pl.pallas_call(
        functools.partial(attend_backward, which, len(qkv)),
        out_shape=out_shape,
        grid_spec=pltpu.PrefetchScalarGridSpec(
            num_scalar_prefetch=3,
            grid=(steps,),
            in_specs=[pl.BlockSpec(memory_space=pl.ANY)] * len(qkv)
            + [
                fixed((seq_len, 1)),
                pl.BlockSpec((1, BLOCK), lambda q, *_: (0, q * halves + half)),
                packed,
                packed,
                pl.BlockSpec((heads, 1, BLOCK), lambda q, *_: (0, 0, q)),
            ]
            + carried,
            out_specs=out_specs,
            scratch_shapes=scratch,
        ),
        compiler_params=pltpu.CompilerParams(
            dimension_semantics=("arbitrary",), vmem_limit_bytes=VMEM_LIMIT
        ),
        cost_estimate=pl.CostEstimate(
            flops=heads * seq_len * seq_len * 640 // halves,
            bytes_accessed=10 << 20,
            transcendentals=heads * seq_len * seq_len // 3 // halves,
        ),
        name="attend_backward",
    )(lane, *bounds, *qkv, seg_col, seg_row, ctx, grad, lse, *earlier, *before)


def dense_chain(
    marks, place_ref, ratio_ref, ctx_ref, in_ref, teacher_ref, cotangent_ref, valid_ref, vec_ref,
    inner_bias_ref, *refs
):
    pieces = refs[: len(marks)]
    (
        layer_ref, first_grad_ref, ctx_grad_ref, first_ref, branch_grad_ref, attn_grad_ref,
        act_ref, hidden_grad_ref, sums_ref, inner_sums_ref, w_out, w_in, w_up, slope, sems,
    ) = refs[len(marks) :]
    parts, _, head_cols = w_out.shape
    hidden_cols = w_in.shape[2]
    index = place_ref[parts]
    step = pl.program_id(0)
    groups = (
        (2 * hidden_cols, head_cols, w_out),
        (0, hidden_cols, w_in),
        (hidden_cols, hidden_cols, w_up),
    )

    @pl.when(step == 0)
    def _():
        for group, (start, size, target) in enumerate(groups):
            for piece, marked in zip(pieces, marks):
                block = piece.shape[1]
                for at, (slot, turn, relative) in enumerate(marked):
                    offset = pl.multiple_of((index ^ turn) * block, block) if relative else turn * block
                    pltpu.make_async_copy(
                        piece.at[at, :, pl.ds(start, size)],
                        target.at[slot, pl.ds(offset, block), :],
                        sems.at[group, slot],
                    ).start()
        sums_ref[...] = jnp.zeros_like(sums_ref)
        inner_sums_ref[...] = jnp.zeros_like(inner_sums_ref)

    def arrive(group, slot):
        whole = groups[group][2].at[slot]

        @pl.when(step == 0)
        def _():
            pltpu.make_async_copy(whole, whole, sems.at[group, slot]).wait()

    def vec(which):
        return vec_ref[which : which + 1, :]

    attention = jnp.zeros(in_ref.shape, F32)
    for slot in range(parts):
        arrive(0, slot)
        attention = attention + dot(unpack(ctx_ref[place_ref[slot], 0]), w_out[slot, :, : 3 * DH], NT)
    first_exact, normed_one, inverse_one = norm_forward(
        in_ref[...].astype(F32) + attention + vec(0), vec(1), vec(2)
    )
    first = first_exact.astype(BF16)
    first_ref[...] = first

    def up(slot, branch):
        t = place_ref[slot]
        arrive(1, slot)
        hidden = dot(first, w_in[slot]) + inner_bias_ref[t]
        bend = 0.5 * (1.0 + lax.erf(hidden * ROOT_HALF))
        activated = (hidden * bend).astype(BF16)
        act_ref[t] = activated
        slope[slot] = bend + hidden * INV_ROOT_TAU * jnp.exp2(hidden * hidden * (-0.5 * LOG2E))
        arrive(2, slot)
        return branch + dot(activated, w_up[slot], NT)

    branch = lax.fori_loop(0, parts, up, jnp.zeros(in_ref.shape, F32))
    layer_rows, normed_two, inverse_two = norm_forward(first.astype(F32) + branch + vec(3), vec(4), vec(5))
    layer_ref[...] = layer_rows.astype(BF16)
    misfit = layer_rows - teacher_ref[...].astype(F32)
    weighted = valid_ref[...] * misfit
    out_grad = cotangent_ref[...].astype(F32) + weighted * ratio_ref[0]
    second_grad = norm_backward(out_grad, normed_two, inverse_two, vec(4))
    branch_grad = second_grad.astype(BF16)
    branch_grad_ref[...] = branch_grad
    sums_ref[0:1, :] += column_sum(weighted * misfit)
    sums_ref[1:2, :] += column_sum(branch_grad.astype(F32))
    sums_ref[2:3, :] += column_sum(out_grad * normed_two)
    sums_ref[3:4, :] += column_sum(out_grad)

    def down(slot, back):
        t = place_ref[slot]
        hidden_grad = (dot(branch_grad, w_up[slot]) * slope[slot]).astype(BF16)
        hidden_grad_ref[t] = hidden_grad
        inner_sums_ref[t] += column_sum(hidden_grad.astype(F32))
        return back + dot(hidden_grad, w_in[slot], NT)

    upstream = lax.fori_loop(0, parts, down, second_grad)
    first_grad = norm_backward(upstream, normed_one, inverse_one, vec(1))
    first_grad_ref[...] = first_grad
    attn_grad = first_grad.astype(BF16)
    attn_grad_ref[...] = attn_grad
    sums_ref[4:5, :] += column_sum(attn_grad.astype(F32))
    sums_ref[5:6, :] += column_sum(upstream * normed_one)
    sums_ref[6:7, :] += column_sum(upstream)
    middle = BLOCK // 2
    for slot in range(parts):
        back = dot(attn_grad, w_out[slot, :, : 3 * DH]).astype(BF16)
        ctx_grad_ref[place_ref[slot], 0] = pack(
            back[:, : 2 * DH], back[:middle, 2 * DH :], back[middle:, 2 * DH :]
        )


def run_dense(marks, place, ratio, ctx, rows_in, teacher, cotangent, valid, vecs, inner_bias, pieces):
    parts, halves = ctx.shape[:2]
    part_len, width = rows_in.shape
    hidden_cols = inner_bias.shape[2]
    out_cols = pieces[0].shape[2] - 2 * hidden_cols

    def by_rows(columns):
        return pl.BlockSpec((BLOCK, columns), lambda i: (i, 0))

    def by_part(columns):
        return pl.BlockSpec((parts, BLOCK, columns), lambda i: (0, i, 0))

    def fixed(shape):
        return pl.BlockSpec(shape, lambda i: (0,) * len(shape))

    packed = pl.BlockSpec((parts, 1) + ctx.shape[2:], lambda i: (0, i, 0, 0))
    low = jax.ShapeDtypeStruct((part_len, width), BF16)
    wide = jax.ShapeDtypeStruct((parts, part_len, hidden_cols), BF16)
    smem = pl.BlockSpec(memory_space=pltpu.SMEM)
    return pl.pallas_call(
        functools.partial(dense_chain, marks),
        out_shape=(
            low,
            jax.ShapeDtypeStruct((part_len, width), F32),
            jax.ShapeDtypeStruct(ctx.shape, BF16),
            low,
            low,
            low,
            wide,
            wide,
            jax.ShapeDtypeStruct((8, width), F32),
            jax.ShapeDtypeStruct((parts, 1, hidden_cols), F32),
        ),
        grid=(halves,),
        in_specs=[
            smem,
            smem,
            packed,
            by_rows(width),
            by_rows(width),
            by_rows(width),
            by_rows(1),
            fixed(vecs.shape),
            fixed(inner_bias.shape),
        ]
        + [pl.BlockSpec(memory_space=pl.ANY)] * len(pieces),
        out_specs=(
            by_rows(width),
            by_rows(width),
            packed,
            by_rows(width),
            by_rows(width),
            by_rows(width),
            by_part(hidden_cols),
            by_part(hidden_cols),
            fixed((8, width)),
            fixed((parts, 1, hidden_cols)),
        ),
        scratch_shapes=[
            pltpu.VMEM((parts, width, out_cols), BF16),
            pltpu.VMEM((parts, width, hidden_cols), BF16),
            pltpu.VMEM((parts, width, hidden_cols), BF16),
            pltpu.VMEM((parts, BLOCK, hidden_cols), F32),
            pltpu.SemaphoreType.DMA((3, parts)),
        ],
        compiler_params=pltpu.CompilerParams(
            dimension_semantics=("arbitrary",), vmem_limit_bytes=VMEM_LIMIT
        ),
        cost_estimate=pl.CostEstimate(
            flops=part_len * width * (8 * hidden_cols + 4 * out_cols) * parts,
            bytes_accessed=24 << 20,
            transcendentals=2 * part_len * hidden_cols * parts,
        ),
        name="dense_chain",
    )(place, ratio, ctx, rows_in, teacher, cotangent, valid, vecs, inner_bias, *pieces)


def dense_weights(
    plans, place_ref, first_ref, branch_grad_ref, attn_grad_ref, act_ref, hidden_grad_ref, ctx_ref,
    notes_ref, *refs
):
    outs, (turned, whole, sems) = refs[:-3], refs[-3:]
    step = pl.program_id(0)
    slots = whole.shape[0]

    @pl.when(step == 0)
    def _():
        for which, source in enumerate((first_ref, branch_grad_ref, attn_grad_ref)):
            turned[which] = jnp.transpose(source[...])

    hidden_cols = act_ref.shape[2]
    whole[step, :, :hidden_cols] = dot(turned[0], hidden_grad_ref[0]).astype(BF16)
    whole[step, :, hidden_cols : 2 * hidden_cols] = dot(turned[1], act_ref[0]).astype(BF16)
    ctx = jnp.concatenate([unpack(ctx_ref[0, half]) for half in range(ctx_ref.shape[1])], axis=0)
    plain = 2 * hidden_cols + ctx.shape[1]
    whole[step, :, 2 * hidden_cols : plain] = dot(turned[2], ctx).astype(BF16)
    whole[step, :, plain : plain + notes_ref.shape[1]] = notes_ref[...]
    for out, (start, stop, turns) in zip(outs, plans):

        @pl.when((step >= start) & (step < stop))
        def _():
            block = out.shape[1]
            for at, turn in enumerate(turns):
                offset = 0
                if block < whole.shape[1]:
                    offset = pl.multiple_of((place_ref[slots] ^ turn) * block, block)
                pltpu.make_async_copy(
                    whole.at[step, pl.ds(offset, block), :],
                    out.at[at * (stop - start) + step - start],
                    sems.at[step],
                ).start()

    @pl.when(step == slots - 1)
    def _():
        for slot in range(slots):
            pltpu.make_async_copy(whole.at[slot], whole.at[slot], sems.at[slot]).wait()


def run_weights(plans, place, notes, first, branch_grad, attn_grad, act, hidden_grad, ctx):
    parts, part_len, hidden_cols = act.shape
    width = first.shape[1]
    columns = 2 * hidden_cols + 3 * DH + notes.shape[1]
    fixed = pl.BlockSpec((part_len, width), lambda s, place: (0, 0))
    by_slot = pl.BlockSpec((1, part_len, hidden_cols), lambda s, place: (place[s], 0, 0))
    outs = tuple(
        jax.ShapeDtypeStruct((len(turns) * (stop - start), block, columns), BF16)
        for start, stop, block, turns in plans
    )
    inner = tuple((start, stop, turns) for start, stop, _, turns in plans)
    return pl.pallas_call(
        functools.partial(dense_weights, inner),
        out_shape=outs,
        grid_spec=pltpu.PrefetchScalarGridSpec(
            num_scalar_prefetch=1,
            grid=(parts,),
            in_specs=[
                fixed,
                fixed,
                fixed,
                by_slot,
                by_slot,
                pl.BlockSpec((1,) + ctx.shape[1:], lambda s, place: (place[s], 0, 0, 0)),
                pl.BlockSpec(notes.shape, lambda s, place: (0, 0)),
            ],
            out_specs=tuple(pl.BlockSpec(memory_space=pl.ANY) for _ in outs),
            scratch_shapes=[
                pltpu.VMEM((3, width, part_len), BF16),
                pltpu.VMEM((parts, width, columns), BF16),
                pltpu.SemaphoreType.DMA((parts,)),
            ],
        ),
        compiler_params=pltpu.CompilerParams(
            dimension_semantics=("arbitrary",), vmem_limit_bytes=VMEM_LIMIT
        ),
        cost_estimate=pl.CostEstimate(
            flops=2 * part_len * width * columns * parts,
            bytes_accessed=20 << 20,
            transcendentals=0,
        ),
        name="dense_weights",
    )(place, first, branch_grad, attn_grad, act, hidden_grad, ctx, notes)


def finish_dense(packed_ref, inner_ref, outer_ref, output_ref, notes_ref):
    hidden_cols = inner_ref.shape[1]
    summed = packed_ref[...].astype(F32)
    inner_ref[...] = summed[:, :hidden_cols]
    outer_ref[...] = summed[:, hidden_cols : 2 * hidden_cols]
    plain = 2 * hidden_cols + output_ref.shape[0]
    output_ref[...] = jnp.transpose(summed[:, 2 * hidden_cols : plain])
    notes_ref[...] = summed[:, plain:]


def run_finish_dense(packed, hidden_cols, head_cols):
    rows = packed.shape[0]
    return pl.pallas_call(
        finish_dense,
        out_shape=(
            jax.ShapeDtypeStruct((rows, hidden_cols), F32),
            jax.ShapeDtypeStruct((rows, hidden_cols), F32),
            jax.ShapeDtypeStruct((head_cols, rows), F32),
            jax.ShapeDtypeStruct((rows, packed.shape[1] - 2 * hidden_cols - head_cols), F32),
        ),
        name="finish_dense",
    )(packed)


def finish_heads(value_ref, *refs):
    summed = value_ref[...].astype(F32)
    heads = summed.shape[1] // SLAB
    for ref, which in zip(refs, (0, 2, 3, 1)):
        columns = [summed[:, SLAB * h + which * DH : SLAB * h + (which + 1) * DH] for h in range(heads)]
        ref[...] = jnp.concatenate(columns, axis=1)[: ref.shape[0]]


def run_finish_heads(value):
    rows, width = value.shape
    out = jax.ShapeDtypeStruct((rows, width // 4), F32)
    notes = jax.ShapeDtypeStruct((8, width // 4), F32)
    return pl.pallas_call(finish_heads, out_shape=(out, out, out, notes), name="finish_heads")(value)


def interleave(query, key, value, heads):
    rows = query.shape[0]
    parts = [part.reshape(rows, heads, 1, DH) for part in (query, jnp.zeros_like(query), key, value)]
    return jnp.concatenate(parts, axis=2).reshape(rows, heads * SLAB)


def swap(value, axis, bit):
    size = lax.axis_size(axis)
    return lax.ppermute(value, axis, [(i, i ^ bit) for i in range(size)])


def bits_of(axis):
    bit = 1
    while bit < lax.axis_size(axis):
        yield bit
        bit *= 2


def after(value, *others):
    return lax.optimization_barrier((value,) + others)[0]


def merge(held, other, axis, bit):
    mine_first = (lax.axis_index(axis) & bit) == 0
    return jnp.where(
        mine_first, jnp.concatenate([held, other], axis=0), jnp.concatenate([other, held], axis=0)
    )


def add_low(left_side, right_side):
    return (left_side.astype(F32) + right_side.astype(F32)).astype(BF16)


def add_halves(left_side, right_side):
    half = left_side.shape[0] // 2
    return (
        add_low(left_side[:half], right_side[:half]),
        add_low(left_side[half:], right_side[half:]),
    )


def scatter_rows(held):
    index = lax.axis_index("dp")
    for bit in bits_of("dp"):
        held = held.reshape((held.shape[0] // 2, 2) + held.shape[1:])
        own = (index & bit) // bit
        send = lax.dynamic_index_in_dim(held, 1 - own, 1, keepdims=False)
        keep = lax.dynamic_index_in_dim(held, own, 1, keepdims=False)
        held = add_low(keep, swap(send, "dp", bit))
    return held[0]


def local(
    inputs, segment_ids, valid_mask, teacher, cotangent,
    w_query, w_key, w_value, w_output, w_inner, w_outer,
    query_bias, value_bias, output_bias, inner_bias, outer_bias,
    gain_attn, shift_attn, gain_ffn, shift_ffn,
):
    _, part_len, width = inputs.shape
    parts = lax.axis_size("tensor")
    copies = lax.axis_size("dp")
    rank = lax.axis_index("tensor")
    total_tokens = part_len * parts * copies
    seq_len = part_len * parts
    head_cols = w_query.shape[1]
    heads = head_cols // DH
    hidden_cols = w_inner.shape[1]
    shard_rows = w_inner.shape[0]
    halves = part_len // BLOCK

    rows_in = inputs.reshape(part_len, width)
    tokens = lax.all_gather(rows_in, "tensor", axis=0, tiled=True)
    w_heads = interleave(w_query, w_key, w_value, heads)
    paired = shard_rows % 16 == 0 and parts == 4 and copies == 8

    valid_rows = valid_mask.astype(F32).reshape(part_len, 1)
    valid_count = jnp.sum(valid_mask.astype(F32))
    upper = jnp.floor(valid_count / 256.0)
    spot = lax.broadcasted_iota(jnp.int32, (shard_rows, DH), 0) * DH + lax.broadcasted_iota(
        jnp.int32, (shard_rows, DH), 1
    )
    count_row = jnp.where(spot == 0, upper, jnp.where(spot == 1, valid_count - 256.0 * upper, 0.0))
    mine = jnp.concatenate((w_inner, w_outer.T, w_output.T, count_row.astype(BF16)), axis=1)
    if paired:
        place = jnp.stack([rank, rank ^ 1, rank ^ 2, rank ^ 3, lax.axis_index("dp")]).astype(jnp.int32)
        pair = jnp.concatenate([mine[None], swap(mine[None], "tensor", 1)], axis=0)
        far = swap(pair, "tensor", 2)
        near = jnp.concatenate([pair, swap(pair, "dp", 2)], axis=0)
        turns = [0, 2, 4, 6]
        for bit in (1, 2, 4):
            w_heads = merge(w_heads, swap(w_heads, "dp", bit), "dp", bit)
        near, w_heads = lax.optimization_barrier((near, w_heads))
        near_next = swap(near, "dp", 4)
        tokens, far, near_next = lax.optimization_barrier((tokens, far, near_next))
        weights = lax.all_gather(far, "dp", axis=0, tiled=False)
    else:
        place = jnp.asarray(list(range(parts)) + [0], jnp.int32)
        weights = lax.all_gather(mine, ("tensor", "dp"), axis=0, tiled=False)
        for bit in bits_of("dp"):
            w_heads = merge(w_heads, swap(w_heads, "dp", bit), "dp", bit)

    mine_cols = rank * head_cols
    query_shift = lax.dynamic_slice_in_dim(query_bias, mine_cols, head_cols).astype(F32)
    value_shift = lax.dynamic_slice_in_dim(value_bias, mine_cols, head_cols).astype(F32)
    shifts = interleave(query_shift[None], jnp.zeros_like(query_shift)[None], value_shift[None], heads)
    qkv = [(dot(tokens, w_heads) + shifts).astype(BF16)]

    segment_row = segment_ids.reshape(seq_len)
    bounds = document_blocks(segment_row)
    seg_col = segment_row.reshape(seq_len, 1)
    seg_row = segment_row.reshape(1, seq_len)
    lane = rank.astype(jnp.int32).reshape(1)

    def exchange(packed_blocks):
        return lax.all_to_all(packed_blocks.reshape(parts, halves, PACKED, 2 * DH), "tensor", 0, 0)

    context, lse = run_forward((1, 0), lane, bounds, qkv, seg_col, seg_row)
    if paired:
        near_next, context = lax.optimization_barrier((near_next, context))
        near = jnp.concatenate([near, near_next], axis=0)
        near_other = swap(near, "dp", 1)
    arrived = exchange(context)
    if paired:
        weights = weights.reshape((copies * 2,) + mine.shape)
        pieces = [near, near_other, weights]
        marks = [[(slot, turn ^ flip, True) for turn in turns for slot in (0, 1)] for flip in (0, 1)]
        marks.append([(2 + at % 2, at // 2, False) for at in range(2 * copies)])
    else:
        pieces = [weights.reshape(parts, width, -1)]
        marks = [[(t, 0, False) for t in range(parts)]]
    counts = [piece.reshape((-1,) + mine.shape)[:, 0, -DH : 2 - DH].astype(F32) for piece in pieces + [weights]]
    counts = jnp.concatenate(counts[:-1] if paired else counts[-1:], axis=0)
    counted = 256.0 * jnp.sum(counts[:, 0]) + jnp.sum(counts[:, 1])
    ratio = (total_tokens / counted).reshape(1)

    vecs = jnp.stack(
        (output_bias, gain_attn, shift_attn, outer_bias, gain_ffn, shift_ffn, outer_bias, outer_bias)
    ).astype(F32)
    inner_rows = inner_bias.astype(F32).reshape(parts, 1, hidden_cols)
    teacher_rows = teacher.reshape(part_len, width)
    cotangent_rows = cotangent.reshape(part_len, width)
    (
        layer_out, first_grad, context_grad, first, branch_grad, attn_grad, activated, hidden_grad,
        dense_sums, inner_sums,
    ) = run_dense(
        marks, place, ratio, arrived, rows_in, teacher_rows, cotangent_rows, valid_rows, vecs,
        inner_rows, pieces,
    )
    head_grad = exchange(context_grad).reshape(context.shape)
    sources = (first, branch_grad, attn_grad, activated, hidden_grad, arrived)
    notes = jnp.concatenate((dense_sums.reshape(-1), inner_sums.reshape(-1))).astype(BF16)
    room = -(-notes.shape[0] // (shard_rows * 128)) * 128
    notes = jnp.pad(notes, (0, shard_rows * room - notes.shape[0])).reshape(shard_rows, room)
    notes = jnp.tile(notes, (copies, 1))
    if paired:
        keep_turns = (0, 4, 2, 6)
        plans = (
            (0, 2, shard_rows, keep_turns),
            (0, 2, shard_rows, tuple(turn | 1 for turn in keep_turns)),
            (2, 4, width, (0,)),
        )
        keep, send, distant = run_weights(plans, place, notes, *sources)
        keep, send = (value.reshape((4, 2) + value.shape[1:]) for value in (keep, send))
        distant = lax.psum_scatter(distant, "dp", scatter_dimension=1, tiled=True)
        came = swap(send, "dp", 1)
    else:
        (packed,) = run_weights(((0, parts, width, (0,)),), place, notes, *sources)
        packed = lax.psum_scatter(packed, "dp", scatter_dimension=1, tiled=True)

    joined_grad, sums = run_backward(
        (1, 0), lane, bounds, qkv, seg_col, seg_row, context, head_grad, lse, [], []
    )
    joined_grad = joined_grad.reshape(seq_len, -1)
    attn_back = dot(joined_grad, w_heads, NT).astype(BF16)
    if paired:
        came = after(came, attn_back)
    attn_back, sums, joined_grad = lax.optimization_barrier((attn_back, sums, joined_grad))
    attn_back = lax.psum_scatter(attn_back, "tensor", scatter_dimension=0, tiled=True)
    if paired:
        keep, send = add_halves(keep, came)
        keep, send, joined_grad = lax.optimization_barrier((keep, send, joined_grad))
        came = swap(send, "dp", 2)
    head_weights = dot(tokens, joined_grad, TN).reshape((copies, shard_rows, -1))
    if paired:
        came, head_weights = lax.optimization_barrier((came, head_weights))
        keep, send = add_halves(keep, came)
        keep, send, head_weights = lax.optimization_barrier((keep, send, head_weights))
        came = swap(send, "dp", 4)
    sums = sums.reshape(heads, 4, DH)
    sums = jnp.concatenate((sums[:, 0].reshape(1, head_cols), sums[:, 3].reshape(1, head_cols)), axis=1)
    for bit in bits_of("tensor"):
        sums = merge(sums, swap(sums, "tensor", bit), "tensor", bit)
    if paired:
        came, head_weights = lax.optimization_barrier((came, head_weights))
        slots = jnp.concatenate([add_low(keep, came)[0], distant], axis=0)
        packed = jnp.stack(
            [lax.dynamic_index_in_dim(slots, rank ^ t, 0, keepdims=False) for t in range(parts)]
        )
    packed = lax.psum_scatter(packed, "tensor", scatter_dimension=0, tiled=True)[0]
    biases = jnp.concatenate((sums[:, :head_cols].reshape(-1), sums[:, head_cols:].reshape(-1)))
    biases = jnp.pad(
        biases.reshape(8, heads, 1, DH), ((0, shard_rows - 8), (0, 0), (1, 2), (0, 0))
    ).reshape(1, shard_rows, -1)
    query_grad, key_grad, value_grad, biases = run_finish_heads(
        scatter_rows((head_weights + biases).astype(BF16))
    )
    biases = biases.reshape(2, width)
    input_grad = first_grad + attn_back.astype(F32)

    inner_grad, outer_grad, output_grad, notes = run_finish_dense(packed, hidden_cols, head_cols)
    notes = notes.reshape(-1)

    def total(which):
        return notes[which * width : (which + 1) * width]

    mse_loss = jnp.sum(total(0)) / (counted * width)
    return (
        layer_out.reshape(1, part_len, width),
        mse_loss,
        input_grad.reshape(1, part_len, width),
        query_grad,
        key_grad,
        value_grad,
        output_grad,
        inner_grad,
        outer_grad.T,
        biases[0],
        biases[1],
        total(4),
        notes[8 * width : 8 * width + hidden_cols * parts],
        total(1),
        total(5),
        total(6),
        total(2),
        total(3),
    )


def solution(mesh):
    shard = P("dp", "tensor", None)
    by_dp, by_tensor = P("dp", "tensor"), P("tensor", "dp")
    in_specs = (
        (shard, P("dp", None), by_dp, shard, shard)
        + (by_dp,) * 3
        + (by_tensor, by_dp, by_tensor)
        + (P(),) * 9
    )
    out_specs = (shard, P(), shard) + (by_dp,) * 3 + (by_tensor, by_dp, by_tensor) + (P(),) * 9
    return jax.shard_map(local, mesh=mesh, in_specs=in_specs, out_specs=out_specs, check_vma=False)
```

```python
import functools

import jax
import jax.numpy as jnp
from jax import lax
from jax.experimental import pallas as pl
from jax.experimental.pallas import tpu as pltpu
from jax.sharding import PartitionSpec as P

DH = 64
BLOCK = 256
SLAB = 4 * DH
EPSILON = 1e-12
ROOT_HALF = 0.7071067811865476
INV_ROOT_TAU = 0.3989422804014327
LOG2E = 1.4426950408889634
LN2 = 0.6931471805599453
SCALE = DH ** (-0.5)
MASKED = -1e30
VMEM_LIMIT = 60 << 20

BF16 = jnp.bfloat16
F32 = jnp.float32
NN = (((1,), (0,)), ((), ()))
NT = (((1,), (1,)), ((), ()))
TN = (((0,), (0,)), ((), ()))


def dot(left_side, right_side, dims=NN):
    return lax.dot_general(left_side, right_side, dims, preferred_element_type=F32)


def norm_forward(summed, gain_vec, shift_vec):
    average = jnp.mean(summed, axis=-1, keepdims=True)
    centered = summed - average
    variance = jnp.mean(centered * centered, axis=-1, keepdims=True)
    inverse = lax.rsqrt(variance + EPSILON)
    normed = centered * inverse
    return (normed * gain_vec + shift_vec, normed, inverse)


def norm_backward(upstream, normed, inverse, gain_vec):
    scaled = upstream * gain_vec
    first_mean = jnp.mean(scaled, axis=-1, keepdims=True)
    second_mean = jnp.mean(scaled * normed, axis=-1, keepdims=True)
    return inverse * (scaled - first_mean - normed * second_mean)


def column_sum(value):
    return jnp.sum(value, axis=0, keepdims=True)


def lane_is_right(rows):
    return lax.broadcasted_iota(jnp.int32, (rows, 2 * DH), 1) >= DH


def pack(first_two, third_top, third_bottom):
    return jnp.concatenate([first_two, jnp.concatenate([third_top, third_bottom], axis=1)], axis=0)


def unpack(packed):
    third = packed[BLOCK:]
    third = jnp.concatenate([third[:, :DH], third[:, DH:]], axis=0)
    return jnp.concatenate([packed[:BLOCK], third], axis=1)


def fetch_chunks(lane_ref, chunk_refs, target, sems):
    rows = chunk_refs[0].shape[0]
    copies = []
    for at, chunk in enumerate(chunk_refs):
        offset = pl.multiple_of(lax.rem(lane_ref[0] + at, len(chunk_refs)) * rows, rows)
        copies.append(pltpu.make_async_copy(chunk, target.at[pl.ds(offset, rows), :], sems.at[at]))
    return copies


def attend_forward(
    which, lane_ref, low_ref, count_ref, *refs
):
    chunk_refs, (seg_col_ref, seg_row_ref, ctx_ref, lse_ref, held, qkv_ref, sems) = refs[:-7], refs[-7:]
    halves, half = which
    heads = lse_ref.shape[0]

    @pl.when(pl.program_id(0) == 0)
    def _():
        copies = fetch_chunks(lane_ref, chunk_refs, qkv_ref, sems)
        for copy in copies:
            copy.start()
        for copy in copies:
            copy.wait()

    qb = pl.program_id(0) * halves + half
    rows = pl.ds(pl.multiple_of(qb * BLOCK, BLOCK), BLOCK)
    seg_q = seg_col_ref[...]
    queries = [
        qkv_ref[rows, SLAB * h : SLAB * h + 2 * DH] * jnp.asarray(SCALE, BF16) for h in range(heads)
    ]
    low, count = low_ref[qb], count_ref[qb]

    def score(kb, peaks):
        keys = pl.ds(pl.multiple_of(low * STEP + kb * BLOCK, STEP), BLOCK)
        allowed = seg_q == seg_row_ref[:, keys]
        found = []
        for h in range(heads):
            scores = dot(queries[h], qkv_ref[keys, SLAB * h + 2 * DH : SLAB * (h + 1)], NT)
            scores = jnp.where(allowed, scores, MASKED)
            held[h, kb] = scores
            found.append(jnp.maximum(peaks[h], jnp.maximum(scores[:, :128], scores[:, 128:])))
        return tuple(found)

    start = tuple(jnp.full((BLOCK, 128), MASKED, F32) for _ in range(heads))
    peaks = lax.fori_loop(0, count, score, start)
    highest = [jnp.max(peak, axis=-1, keepdims=True) for peak in peaks]

    def weigh(kb, carry):
        keys = pl.ds(pl.multiple_of(low * STEP + kb * BLOCK, STEP), BLOCK)
        found = []
        for h in range(heads):
            total, acc = carry[h]
            raised = jnp.exp2((held[h, kb] - highest[h]) * LOG2E)
            total = total + (raised[:, :128] + raised[:, 128:])
            acc = acc + dot(raised.astype(BF16), qkv_ref[keys, SLAB * h + 2 * DH : SLAB * (h + 1)])
            found.append((total, acc))
        return tuple(found)

    zero = jnp.zeros((BLOCK, 128), F32)
    done = lax.fori_loop(0, count, weigh, tuple((zero, zero) for _ in range(heads)))
    values = []
    for h in range(heads):
        total, acc = done[h]
        summed = jnp.sum(total, axis=-1, keepdims=True)
        values.append((acc / summed).astype(BF16))
        lse_ref[h] = jnp.transpose(highest[h] + jnp.log(summed))
    middle = BLOCK // 2
    ctx_ref[0, :BLOCK, :] = jnp.where(lane_is_right(BLOCK), values[1], pltpu.roll(values[0], DH, 1))
    ctx_ref[0, BLOCK:, :] = jnp.where(
        lane_is_right(middle), values[2][middle:], pltpu.roll(values[2][:middle], DH, 1)
    )


def attend_backward(which, chunks, lane_ref, low_ref, count_ref, *refs):
    halves, half = which
    last = half == halves - 1
    chunk_refs, refs = refs[:chunks], refs[chunks:]
    (seg_col_ref, seg_row_ref, ctx_ref, grad_ref, lse_ref), refs = refs[:5], refs[5:]
    earlier, refs = refs[:half], refs[half:]
    if half > 0:
        before_ref, refs = refs[0], refs[1:]
    if last:
        final_ref, sums_ref, dkv, out_ref, qkv_ref, sems = refs
    else:
        dkv, query_ref, qkv_ref, sems = refs
    heads = dkv.shape[0]
    step_index = pl.program_id(0)
    qb = step_index * halves + half

    @pl.when(step_index == 0)
    def _():
        copies = fetch_chunks(lane_ref, chunk_refs, qkv_ref, sems)
        for copy in copies:
            copy.start()
        dkv[...] = before_ref[...] if half > 0 else jnp.zeros_like(dkv)
        for copy in copies:
            copy.wait()

    rows = pl.ds(pl.multiple_of(qb * BLOCK, BLOCK), BLOCK)
    right = lane_is_right(BLOCK)
    arrived = grad_ref[0]
    product = arrived.astype(F32) * ctx_ref[0].astype(F32)
    upper = product.astype(BF16)
    lower = (product - upper.astype(F32)).astype(BF16)
    pick = (
        lax.broadcasted_iota(jnp.int32, (8, 2 * DH), 1) // DH
        == lax.broadcasted_iota(jnp.int32, (8, 2 * DH), 0)
    ).astype(BF16)
    summed = dot(pick, upper, NT) + dot(pick, lower, NT)
    deltas = [
        summed[0:1, :BLOCK],
        summed[1:2, :BLOCK],
        jnp.concatenate([summed[0:1, BLOCK:], summed[1:2, BLOCK:]], axis=1),
    ]
    two, third = arrived[:BLOCK], arrived[BLOCK:]
    placed = [
        pltpu.roll(two, DH, 1),
        two,
        jnp.concatenate([pltpu.roll(third, DH, 1), third], axis=0),
    ]
    grads = [jnp.where(right, grad, jnp.zeros_like(grad)) for grad in placed]
    queries, pairs = [], []
    for h in range(heads):
        queries.append(qkv_ref[rows, SLAB * h : SLAB * h + 2 * DH] * jnp.asarray(SCALE, BF16))
        pairs.append(jnp.concatenate([queries[h], grads[h]], axis=0))
    seg_q = seg_row_ref[...]
    lses = lse_ref[...]
    low, count = low_ref[qb], count_ref[qb]

    def step(kb, accs):
        keys = pl.ds(pl.multiple_of(low * STEP + kb * BLOCK, STEP), BLOCK)
        allowed = seg_col_ref[keys, :] == seg_q
        found = []
        for h in range(heads):
            pair = qkv_ref[keys, SLAB * h + 2 * DH : SLAB * (h + 1)]
            scores = jnp.where(allowed, dot(pair, queries[h], NT), MASKED)
            probs = jnp.exp2((scores - lses[h]) * LOG2E)
            score_grad = (probs * (dot(pair, grads[h], NT) - deltas[h])).astype(BF16)
            both = jnp.concatenate([score_grad, probs.astype(BF16)], axis=1)
            dkv[h, keys, :] += dot(both, pairs[h])
            found.append(accs[h] + dot(score_grad, pair, TN))
        return tuple(found)

    zero = jnp.zeros((BLOCK, 128), F32)
    accs = lax.fori_loop(0, count, step, tuple(zero for _ in range(heads)))
    for h in range(heads):
        query_grad = jnp.where(right, 0.0, accs[h] * SCALE).astype(BF16)
        if last:
            out_ref[rows, SLAB * h : SLAB * h + 2 * DH] = query_grad
        else:
            query_ref[0, :, 2 * DH * h : 2 * DH * (h + 1)] = query_grad

    if last:

        @pl.when(step_index == pl.num_programs(0) - 1)
        def _():
            for h in range(heads):
                at = SLAB * h
                for other, ref in enumerate(earlier):
                    for block in range(ref.shape[0]):
                        start = (block * halves + other) * BLOCK
                        out_ref[start : start + BLOCK, at : at + 2 * DH] = ref[
                            block, :, 2 * DH * h : 2 * DH * (h + 1)
                        ]
                out_ref[:, at + 2 * DH : at + SLAB] = dkv[h].astype(BF16)
                sums_ref[:, at : at + SLAB] = column_sum(out_ref[:, at : at + SLAB].astype(F32))
            rows_each = final_ref.shape[1]
            copies = []
            for at in range(final_ref.shape[0]):
                offset = pl.multiple_of(lax.rem(lane_ref[0] + at, final_ref.shape[0]) * rows_each, rows_each)
                copies.append(
                    pltpu.make_async_copy(
                        out_ref.at[pl.ds(offset, rows_each), :], final_ref.at[at], sems.at[at]
                    )
                )
            for copy in copies:
                copy.start()
            for copy in copies:
                copy.wait()


STEP = 128


def document_blocks(segment_row):
    starts = segment_row[::BLOCK]
    stops = segment_row[BLOCK - 1 :: BLOCK]
    low = jnp.sum((segment_row[None, :] < starts[:, None]).astype(jnp.int32), axis=1) // STEP
    high = jnp.sum((segment_row[None, :] <= stops[:, None]).astype(jnp.int32), axis=1)
    each = BLOCK // STEP
    count = (high - low * STEP + BLOCK - 1) // BLOCK
    return (jnp.minimum(low, segment_row.shape[0] // STEP - each * count), count)


PACKED = BLOCK + BLOCK // 2


def run_forward(which, lane, bounds, qkv, seg_col, seg_row):
    halves, half = which
    seq_len, width = seg_col.shape[0], qkv[0].shape[1]
    heads = width // SLAB
    blocks = seq_len // BLOCK
    steps = blocks // halves
    return pl.pallas_call(
        functools.partial(attend_forward, which),
        out_shape=(
            jax.ShapeDtypeStruct((steps, PACKED, 2 * DH), BF16),
            jax.ShapeDtypeStruct((heads, 1, steps * BLOCK), F32),
        ),
        grid_spec=pltpu.PrefetchScalarGridSpec(
            num_scalar_prefetch=3,
            grid=(steps,),
            in_specs=[pl.BlockSpec(memory_space=pl.ANY)] * len(qkv)
            + [
                pl.BlockSpec((BLOCK, 1), lambda q, *_: (q * halves + half, 0)),
                pl.BlockSpec((1, seq_len), lambda q, *_: (0, 0)),
            ],
            out_specs=(
                pl.BlockSpec((1, PACKED, 2 * DH), lambda q, *_: (q, 0, 0)),
                pl.BlockSpec((heads, 1, BLOCK), lambda q, *_: (0, 0, q)),
            ),
            scratch_shapes=[
                pltpu.VMEM((heads, blocks, BLOCK, BLOCK), F32),
                pltpu.VMEM((seq_len, width), BF16),
                pltpu.SemaphoreType.DMA((len(qkv),)),
            ],
        ),
        compiler_params=pltpu.CompilerParams(
            dimension_semantics=("arbitrary",), vmem_limit_bytes=VMEM_LIMIT
        ),
        cost_estimate=pl.CostEstimate(
            flops=heads * seq_len * seq_len * 256 // halves,
            bytes_accessed=5 << 20,
            transcendentals=heads * seq_len * seq_len // 3 // halves,
        ),
        name="attend_forward",
    )(lane, *bounds, *qkv, seg_col, seg_row)


def run_backward(which, lane, bounds, qkv, seg_col, seg_row, ctx, grad, lse, earlier, before):
    halves, half = which
    seq_len, width = seg_col.shape[0], qkv[0].shape[1]
    heads = width // SLAB
    steps = seq_len // BLOCK // halves
    packed = pl.BlockSpec((1, PACKED, 2 * DH), lambda q, *_: (q, 0, 0))

    def fixed(shape, **more):
        return pl.BlockSpec(shape, lambda q, *_: (0,) * len(shape), **more)

    once = {"pipeline_mode": pl.Buffered(1)}
    gathered = (heads, seq_len, 2 * DH)
    carried = [fixed(value.shape, **once) for value in earlier]
    carried += [fixed(gathered, **once)] * len(before)
    scratch = [pltpu.VMEM((seq_len, width), BF16), pltpu.SemaphoreType.DMA((len(qkv),))]
    if half == halves - 1:
        out_shape = (
            jax.ShapeDtypeStruct((len(qkv), seq_len // len(qkv), width), BF16),
            jax.ShapeDtypeStruct((1, width), F32),
        )
        out_specs = (pl.BlockSpec(memory_space=pl.ANY), fixed((1, width)))
        scratch = [pltpu.VMEM(gathered, F32), pltpu.VMEM((seq_len, width), BF16)] + scratch
    else:
        out_shape = (
            jax.ShapeDtypeStruct(gathered, F32),
            jax.ShapeDtypeStruct((steps, BLOCK, heads * 2 * DH), BF16),
        )
        out_specs = (
            fixed(gathered),
            pl.BlockSpec((1, BLOCK, heads * 2 * DH), lambda q, *_: (q, 0, 0)),
        )
    return pl.pallas_call(
        functools.partial(attend_backward, which, len(qkv)),
        out_shape=out_shape,
        grid_spec=pltpu.PrefetchScalarGridSpec(
            num_scalar_prefetch=3,
            grid=(steps,),
            in_specs=[pl.BlockSpec(memory_space=pl.ANY)] * len(qkv)
            + [
                fixed((seq_len, 1)),
                pl.BlockSpec((1, BLOCK), lambda q, *_: (0, q * halves + half)),
                packed,
                packed,
                pl.BlockSpec((heads, 1, BLOCK), lambda q, *_: (0, 0, q)),
            ]
            + carried,
            out_specs=out_specs,
            scratch_shapes=scratch,
        ),
        compiler_params=pltpu.CompilerParams(
            dimension_semantics=("arbitrary",), vmem_limit_bytes=VMEM_LIMIT
        ),
        cost_estimate=pl.CostEstimate(
            flops=heads * seq_len * seq_len * 640 // halves,
            bytes_accessed=10 << 20,
            transcendentals=heads * seq_len * seq_len // 3 // halves,
        ),
        name="attend_backward",
    )(lane, *bounds, *qkv, seg_col, seg_row, ctx, grad, lse, *earlier, *before)


def dense_chain(
    marks, place_ref, ratio_ref, ctx_ref, in_ref, teacher_ref, cotangent_ref, valid_ref, vec_ref,
    inner_bias_ref, *refs
):
    pieces = refs[: len(marks)]
    (
        layer_ref, first_grad_ref, ctx_grad_ref, first_ref, branch_grad_ref, attn_grad_ref,
        act_ref, hidden_grad_ref, sums_ref, inner_sums_ref, w_out, w_in, w_up, slope, sems,
    ) = refs[len(marks) :]
    parts, _, head_cols = w_out.shape
    hidden_cols = w_in.shape[2]
    index = place_ref[parts]
    step = pl.program_id(0)
    groups = (
        (2 * hidden_cols, head_cols, w_out),
        (0, hidden_cols, w_in),
        (hidden_cols, hidden_cols, w_up),
    )

    @pl.when(step == 0)
    def _():
        for group, (start, size, target) in enumerate(groups):
            for piece, marked in zip(pieces, marks):
                block = piece.shape[1]
                for at, (slot, turn, relative) in enumerate(marked):
                    offset = pl.multiple_of((index ^ turn) * block, block) if relative else turn * block
                    pltpu.make_async_copy(
                        piece.at[at, :, pl.ds(start, size)],
                        target.at[slot, pl.ds(offset, block), :],
                        sems.at[group, slot],
                    ).start()
        sums_ref[...] = jnp.zeros_like(sums_ref)
        inner_sums_ref[...] = jnp.zeros_like(inner_sums_ref)

    def arrive(group, slot):
        whole = groups[group][2].at[slot]

        @pl.when(step == 0)
        def _():
            pltpu.make_async_copy(whole, whole, sems.at[group, slot]).wait()

    def vec(which):
        return vec_ref[which : which + 1, :]

    attention = jnp.zeros(in_ref.shape, F32)
    for slot in range(parts):
        arrive(0, slot)
        attention = attention + dot(unpack(ctx_ref[place_ref[slot], 0]), w_out[slot, :, : 3 * DH], NT)
    first_exact, normed_one, inverse_one = norm_forward(
        in_ref[...].astype(F32) + attention + vec(0), vec(1), vec(2)
    )
    first = first_exact.astype(BF16)
    first_ref[...] = first

    def up(slot, branch):
        t = place_ref[slot]
        arrive(1, slot)
        hidden = dot(first, w_in[slot]) + inner_bias_ref[t]
        bend = 0.5 * (1.0 + lax.erf(hidden * ROOT_HALF))
        activated = (hidden * bend).astype(BF16)
        act_ref[t] = activated
        slope[slot] = bend + hidden * INV_ROOT_TAU * jnp.exp2(hidden * hidden * (-0.5 * LOG2E))
        arrive(2, slot)
        return branch + dot(activated, w_up[slot], NT)

    branch = jnp.zeros(in_ref.shape, F32)
    for slot in range(parts):
        branch = up(slot, branch)
    layer_rows, normed_two, inverse_two = norm_forward(first.astype(F32) + branch + vec(3), vec(4), vec(5))
    layer_ref[...] = layer_rows.astype(BF16)
    misfit = layer_rows - teacher_ref[...].astype(F32)
    weighted = valid_ref[...] * misfit
    out_grad = cotangent_ref[...].astype(F32) + weighted * ratio_ref[0]
    second_grad = norm_backward(out_grad, normed_two, inverse_two, vec(4))
    branch_grad = second_grad.astype(BF16)
    branch_grad_ref[...] = branch_grad
    sums_ref[0:1, :] += column_sum(weighted * misfit)
    sums_ref[1:2, :] += column_sum(branch_grad.astype(F32))
    sums_ref[2:3, :] += column_sum(out_grad * normed_two)
    sums_ref[3:4, :] += column_sum(out_grad)

    def down(slot, back):
        t = place_ref[slot]
        hidden_grad = (dot(branch_grad, w_up[slot]) * slope[slot]).astype(BF16)
        hidden_grad_ref[t] = hidden_grad
        inner_sums_ref[t] += column_sum(hidden_grad.astype(F32))
        return back + dot(hidden_grad, w_in[slot], NT)

    upstream = second_grad
    for slot in range(parts):
        upstream = down(slot, upstream)
    first_grad = norm_backward(upstream, normed_one, inverse_one, vec(1))
    first_grad_ref[...] = first_grad
    attn_grad = first_grad.astype(BF16)
    attn_grad_ref[...] = attn_grad
    sums_ref[4:5, :] += column_sum(attn_grad.astype(F32))
    sums_ref[5:6, :] += column_sum(upstream * normed_one)
    sums_ref[6:7, :] += column_sum(upstream)
    middle = BLOCK // 2
    for slot in range(parts):
        back = dot(attn_grad, w_out[slot, :, : 3 * DH]).astype(BF16)
        ctx_grad_ref[place_ref[slot], 0] = pack(
            back[:, : 2 * DH], back[:middle, 2 * DH :], back[middle:, 2 * DH :]
        )


def run_dense(marks, place, ratio, ctx, rows_in, teacher, cotangent, valid, vecs, inner_bias, pieces):
    parts, halves = ctx.shape[:2]
    part_len, width = rows_in.shape
    hidden_cols = inner_bias.shape[2]
    out_cols = pieces[0].shape[2] - 2 * hidden_cols

    def by_rows(columns):
        return pl.BlockSpec((BLOCK, columns), lambda i: (i, 0))

    def by_part(columns):
        return pl.BlockSpec((parts, BLOCK, columns), lambda i: (0, i, 0))

    def fixed(shape):
        return pl.BlockSpec(shape, lambda i: (0,) * len(shape))

    packed = pl.BlockSpec((parts, 1) + ctx.shape[2:], lambda i: (0, i, 0, 0))
    low = jax.ShapeDtypeStruct((part_len, width), BF16)
    wide = jax.ShapeDtypeStruct((parts, part_len, hidden_cols), BF16)
    smem = pl.BlockSpec(memory_space=pltpu.SMEM)
    return pl.pallas_call(
        functools.partial(dense_chain, marks),
        out_shape=(
            low,
            jax.ShapeDtypeStruct((part_len, width), F32),
            jax.ShapeDtypeStruct(ctx.shape, BF16),
            low,
            low,
            low,
            wide,
            wide,
            jax.ShapeDtypeStruct((8, width), F32),
            jax.ShapeDtypeStruct((parts, 1, hidden_cols), F32),
        ),
        grid=(halves,),
        in_specs=[
            smem,
            smem,
            packed,
            by_rows(width),
            by_rows(width),
            by_rows(width),
            by_rows(1),
            fixed(vecs.shape),
            fixed(inner_bias.shape),
        ]
        + [pl.BlockSpec(memory_space=pl.ANY)] * len(pieces),
        out_specs=(
            by_rows(width),
            by_rows(width),
            packed,
            by_rows(width),
            by_rows(width),
            by_rows(width),
            by_part(hidden_cols),
            by_part(hidden_cols),
            fixed((8, width)),
            fixed((parts, 1, hidden_cols)),
        ),
        scratch_shapes=[
            pltpu.VMEM((parts, width, out_cols), BF16),
            pltpu.VMEM((parts, width, hidden_cols), BF16),
            pltpu.VMEM((parts, width, hidden_cols), BF16),
            pltpu.VMEM((parts, BLOCK, hidden_cols), F32),
            pltpu.SemaphoreType.DMA((3, parts)),
        ],
        compiler_params=pltpu.CompilerParams(
            dimension_semantics=("arbitrary",), vmem_limit_bytes=VMEM_LIMIT
        ),
        cost_estimate=pl.CostEstimate(
            flops=part_len * width * (8 * hidden_cols + 4 * out_cols) * parts,
            bytes_accessed=24 << 20,
            transcendentals=2 * part_len * hidden_cols * parts,
        ),
        name="dense_chain",
    )(place, ratio, ctx, rows_in, teacher, cotangent, valid, vecs, inner_bias, *pieces)


def dense_weights(
    plans, place_ref, first_ref, branch_grad_ref, attn_grad_ref, act_ref, hidden_grad_ref, ctx_ref,
    notes_ref, *refs
):
    outs, (turned, whole, sems) = refs[:-3], refs[-3:]
    step = pl.program_id(0)
    slots = whole.shape[0]

    @pl.when(step == 0)
    def _():
        for which, source in enumerate((first_ref, branch_grad_ref, attn_grad_ref)):
            turned[which] = jnp.transpose(source[...])

    hidden_cols = act_ref.shape[2]
    whole[step, :, :hidden_cols] = dot(turned[0], hidden_grad_ref[0]).astype(BF16)
    whole[step, :, hidden_cols : 2 * hidden_cols] = dot(turned[1], act_ref[0]).astype(BF16)
    ctx = jnp.concatenate([unpack(ctx_ref[0, half]) for half in range(ctx_ref.shape[1])], axis=0)
    plain = 2 * hidden_cols + ctx.shape[1]
    whole[step, :, 2 * hidden_cols : plain] = dot(turned[2], ctx).astype(BF16)
    whole[step, :, plain : plain + notes_ref.shape[1]] = notes_ref[...]
    for out, turns in zip(outs, plans):
        block = out.shape[1]
        for at, turn in enumerate(turns):
            offset = 0
            if block < whole.shape[1]:
                offset = pl.multiple_of((place_ref[place_ref.shape[0] - 1] ^ turn) * block, block)
            pltpu.make_async_copy(
                whole.at[step, pl.ds(offset, block), :], out.at[at * slots + step], sems.at[step]
            ).start()

    @pl.when(step == slots - 1)
    def _():
        for slot in range(slots):
            pltpu.make_async_copy(whole.at[slot], whole.at[slot], sems.at[slot]).wait()


def run_weights(base, slots, plans, place, notes, first, branch_grad, attn_grad, act, hidden_grad, ctx):
    _, part_len, hidden_cols = act.shape
    width = first.shape[1]
    columns = 2 * hidden_cols + 3 * DH + notes.shape[1]
    fixed = pl.BlockSpec((part_len, width), lambda s, place: (0, 0))
    by_slot = pl.BlockSpec((1, part_len, hidden_cols), lambda s, place: (place[base + s], 0, 0))
    outs = tuple(
        jax.ShapeDtypeStruct((len(turns) * slots, block, columns), BF16) for block, turns in plans
    )
    return pl.pallas_call(
        functools.partial(dense_weights, tuple(turns for _, turns in plans)),
        out_shape=outs,
        grid_spec=pltpu.PrefetchScalarGridSpec(
            num_scalar_prefetch=1,
            grid=(slots,),
            in_specs=[
                fixed,
                fixed,
                fixed,
                by_slot,
                by_slot,
                pl.BlockSpec((1,) + ctx.shape[1:], lambda s, place: (place[base + s], 0, 0, 0)),
                pl.BlockSpec(notes.shape, lambda s, place: (0, 0)),
            ],
            out_specs=tuple(pl.BlockSpec(memory_space=pl.ANY) for _ in outs),
            scratch_shapes=[
                pltpu.VMEM((3, width, part_len), BF16),
                pltpu.VMEM((slots, width, columns), BF16),
                pltpu.SemaphoreType.DMA((slots,)),
            ],
        ),
        compiler_params=pltpu.CompilerParams(
            dimension_semantics=("arbitrary",), vmem_limit_bytes=VMEM_LIMIT
        ),
        cost_estimate=pl.CostEstimate(
            flops=2 * part_len * width * columns * slots,
            bytes_accessed=5 * slots << 20,
            transcendentals=0,
        ),
        name="dense_weights",
    )(place, first, branch_grad, attn_grad, act, hidden_grad, ctx, notes)


def finish_dense(packed_ref, inner_ref, outer_ref, output_ref, notes_ref):
    hidden_cols = inner_ref.shape[1]
    summed = packed_ref[...].astype(F32)
    inner_ref[...] = summed[:, :hidden_cols]
    outer_ref[...] = summed[:, hidden_cols : 2 * hidden_cols]
    plain = 2 * hidden_cols + output_ref.shape[0]
    output_ref[...] = jnp.transpose(summed[:, 2 * hidden_cols : plain])
    notes_ref[...] = summed[:, plain:]


def run_finish_dense(packed, hidden_cols, head_cols):
    rows = packed.shape[0]
    return pl.pallas_call(
        finish_dense,
        out_shape=(
            jax.ShapeDtypeStruct((rows, hidden_cols), F32),
            jax.ShapeDtypeStruct((rows, hidden_cols), F32),
            jax.ShapeDtypeStruct((head_cols, rows), F32),
            jax.ShapeDtypeStruct((rows, packed.shape[1] - 2 * hidden_cols - head_cols), F32),
        ),
        name="finish_dense",
    )(packed)


def finish_heads(value_ref, *refs):
    summed = value_ref[...].astype(F32)
    heads = summed.shape[1] // SLAB
    for ref, which in zip(refs, (0, 2, 3, 1)):
        columns = [summed[:, SLAB * h + which * DH : SLAB * h + (which + 1) * DH] for h in range(heads)]
        ref[...] = jnp.concatenate(columns, axis=1)[: ref.shape[0]]


def run_finish_heads(value):
    rows, width = value.shape
    out = jax.ShapeDtypeStruct((rows, width // 4), F32)
    notes = jax.ShapeDtypeStruct((8, width // 4), F32)
    return pl.pallas_call(finish_heads, out_shape=(out, out, out, notes), name="finish_heads")(value)


def interleave(query, key, value, heads):
    rows = query.shape[0]
    parts = [part.reshape(rows, heads, 1, DH) for part in (query, jnp.zeros_like(query), key, value)]
    return jnp.concatenate(parts, axis=2).reshape(rows, heads * SLAB)


def swap(value, axis, bit):
    size = lax.axis_size(axis)
    return lax.ppermute(value, axis, [(i, i ^ bit) for i in range(size)])


def bits_of(axis):
    bit = 1
    while bit < lax.axis_size(axis):
        yield bit
        bit *= 2


def after(value, *others):
    return lax.optimization_barrier((value,) + others)[0]


def merge(held, other, axis, bit):
    mine_first = (lax.axis_index(axis) & bit) == 0
    return jnp.where(
        mine_first, jnp.concatenate([held, other], axis=0), jnp.concatenate([other, held], axis=0)
    )


def add_low(left_side, right_side):
    return (left_side.astype(F32) + right_side.astype(F32)).astype(BF16)


def add_halves(left_side, right_side):
    half = left_side.shape[0] // 2
    return (
        add_low(left_side[:half], right_side[:half]),
        add_low(left_side[half:], right_side[half:]),
    )


def scatter_rows(held):
    index = lax.axis_index("dp")
    for bit in bits_of("dp"):
        held = held.reshape((held.shape[0] // 2, 2) + held.shape[1:])
        own = (index & bit) // bit
        send = lax.dynamic_index_in_dim(held, 1 - own, 1, keepdims=False)
        keep = lax.dynamic_index_in_dim(held, own, 1, keepdims=False)
        held = add_low(keep, swap(send, "dp", bit))
    return held[0]


def local(
    inputs, segment_ids, valid_mask, teacher, cotangent,
    w_query, w_key, w_value, w_output, w_inner, w_outer,
    query_bias, value_bias, output_bias, inner_bias, outer_bias,
    gain_attn, shift_attn, gain_ffn, shift_ffn,
):
    _, part_len, width = inputs.shape
    parts = lax.axis_size("tensor")
    copies = lax.axis_size("dp")
    rank = lax.axis_index("tensor")
    total_tokens = part_len * parts * copies
    seq_len = part_len * parts
    head_cols = w_query.shape[1]
    heads = head_cols // DH
    hidden_cols = w_inner.shape[1]
    shard_rows = w_inner.shape[0]
    halves = part_len // BLOCK

    rows_in = inputs.reshape(part_len, width)
    tokens = lax.all_gather(rows_in, "tensor", axis=0, tiled=True)
    w_heads = interleave(w_query, w_key, w_value, heads)
    paired = shard_rows % 16 == 0 and parts == 4 and copies == 8

    valid_rows = valid_mask.astype(F32).reshape(part_len, 1)
    valid_count = jnp.sum(valid_mask.astype(F32))
    upper = jnp.floor(valid_count / 256.0)
    spot = lax.broadcasted_iota(jnp.int32, (shard_rows, DH), 0) * DH + lax.broadcasted_iota(
        jnp.int32, (shard_rows, DH), 1
    )
    count_row = jnp.where(spot == 0, upper, jnp.where(spot == 1, valid_count - 256.0 * upper, 0.0))
    mine = jnp.concatenate((w_inner, w_outer.T, w_output.T, count_row.astype(BF16)), axis=1)
    if paired:
        place = jnp.stack([rank, rank ^ 1, rank ^ 2, rank ^ 3, lax.axis_index("dp")]).astype(jnp.int32)
        pair = jnp.concatenate([mine[None], swap(mine[None], "tensor", 1)], axis=0)
        near = jnp.concatenate([pair, swap(pair, "dp", 2)], axis=0)
        turns = [0, 2, 4, 6]
        for bit in (1, 2, 4):
            w_heads = merge(w_heads, swap(w_heads, "dp", bit), "dp", bit)
        near, w_heads = lax.optimization_barrier((near, w_heads))
        near_next = swap(near, "dp", 4)
        tokens, pair, near_next = lax.optimization_barrier((tokens, pair, near_next))
        far = swap(pair, "tensor", 2)
    else:
        place = jnp.asarray(list(range(parts)) + [0], jnp.int32)
        weights = lax.all_gather(mine, ("tensor", "dp"), axis=0, tiled=False)
        for bit in bits_of("dp"):
            w_heads = merge(w_heads, swap(w_heads, "dp", bit), "dp", bit)

    mine_cols = rank * head_cols
    query_shift = lax.dynamic_slice_in_dim(query_bias, mine_cols, head_cols).astype(F32)
    value_shift = lax.dynamic_slice_in_dim(value_bias, mine_cols, head_cols).astype(F32)
    shifts = interleave(query_shift[None], jnp.zeros_like(query_shift)[None], value_shift[None], heads)
    qkv = [(dot(tokens, w_heads) + shifts).astype(BF16)]

    segment_row = segment_ids.reshape(seq_len)
    bounds = document_blocks(segment_row)
    seg_col = segment_row.reshape(seq_len, 1)
    seg_row = segment_row.reshape(1, seq_len)
    lane = rank.astype(jnp.int32).reshape(1)

    def exchange(packed_blocks):
        return lax.all_to_all(packed_blocks.reshape(parts, halves, PACKED, 2 * DH), "tensor", 0, 0)

    context, lse = run_forward((1, 0), lane, bounds, qkv, seg_col, seg_row)
    if paired:
        near_next, far, context = lax.optimization_barrier((near_next, far, context))
        weights = lax.all_gather(far, "dp", axis=0, tiled=False)
        near = jnp.concatenate([near, near_next], axis=0)
        near_other = swap(near, "dp", 1)
    arrived = exchange(context)
    if paired:
        weights = weights.reshape((copies * 2,) + mine.shape)
        pieces = [near, near_other, weights]
        marks = [[(slot, turn ^ flip, True) for turn in turns for slot in (0, 1)] for flip in (0, 1)]
        marks.append([(2 + at % 2, at // 2, False) for at in range(2 * copies)])
    else:
        pieces = [weights.reshape(parts, width, -1)]
        marks = [[(t, 0, False) for t in range(parts)]]
    counts = [piece.reshape((-1,) + mine.shape)[:, 0, -DH : 2 - DH].astype(F32) for piece in pieces + [weights]]
    counts = jnp.concatenate(counts[:-1] if paired else counts[-1:], axis=0)
    counted = 256.0 * jnp.sum(counts[:, 0]) + jnp.sum(counts[:, 1])
    ratio = (total_tokens / counted).reshape(1)

    vecs = jnp.stack(
        (output_bias, gain_attn, shift_attn, outer_bias, gain_ffn, shift_ffn, outer_bias, outer_bias)
    ).astype(F32)
    inner_rows = inner_bias.astype(F32).reshape(parts, 1, hidden_cols)
    teacher_rows = teacher.reshape(part_len, width)
    cotangent_rows = cotangent.reshape(part_len, width)
    (
        layer_out, first_grad, context_grad, first, branch_grad, attn_grad, activated, hidden_grad,
        dense_sums, inner_sums,
    ) = run_dense(
        marks, place, ratio, arrived, rows_in, teacher_rows, cotangent_rows, valid_rows, vecs,
        inner_rows, pieces,
    )
    head_grad = exchange(context_grad).reshape(context.shape)
    sources = (first, branch_grad, attn_grad, activated, hidden_grad, arrived)
    notes = jnp.concatenate((dense_sums.reshape(-1), inner_sums.reshape(-1))).astype(BF16)
    room = -(-notes.shape[0] // (shard_rows * 128)) * 128
    notes = jnp.pad(notes, (0, shard_rows * room - notes.shape[0])).reshape(shard_rows, room)
    notes = jnp.tile(notes, (copies, 1))
    if paired:
        keep_turns = (0, 4, 2, 6)
        (distant,) = run_weights(2, 2, ((width, (0,)),), place, notes, *sources)
        plans = tuple((shard_rows, tuple(turn | flip for turn in keep_turns)) for flip in (0, 1))
        keep, send = run_weights(0, 2, plans, place, notes, *sources)
        keep, send = (value.reshape((4, 2) + value.shape[1:]) for value in (keep, send))
        distant = lax.psum_scatter(distant, "dp", scatter_dimension=1, tiled=True)
        came = swap(send, "dp", 1)
    else:
        (packed,) = run_weights(0, parts, ((width, (0,)),), place, notes, *sources)
        packed = lax.psum_scatter(packed, "dp", scatter_dimension=1, tiled=True)

    joined_grad, sums = run_backward(
        (1, 0), lane, bounds, qkv, seg_col, seg_row, context, head_grad, lse, [], []
    )
    joined_grad = joined_grad.reshape(seq_len, -1)
    attn_back = dot(joined_grad, w_heads, NT).astype(BF16)
    if paired:
        came = after(came, attn_back)
    attn_back, sums, joined_grad = lax.optimization_barrier((attn_back, sums, joined_grad))
    attn_back = lax.psum_scatter(attn_back, "tensor", scatter_dimension=0, tiled=True)
    if paired:
        keep, send = add_halves(keep, came)
        keep, send, joined_grad = lax.optimization_barrier((keep, send, joined_grad))
        came = swap(send, "dp", 2)
    head_weights = dot(tokens, joined_grad, TN).reshape((copies, shard_rows, -1))
    if paired:
        came, head_weights = lax.optimization_barrier((came, head_weights))
        keep, send = add_halves(keep, came)
        keep, send, head_weights = lax.optimization_barrier((keep, send, head_weights))
        came = swap(send, "dp", 4)
    sums = sums.reshape(heads, 4, DH)
    sums = jnp.concatenate((sums[:, 0].reshape(1, head_cols), sums[:, 3].reshape(1, head_cols)), axis=1)
    for bit in bits_of("tensor"):
        sums = merge(sums, swap(sums, "tensor", bit), "tensor", bit)
    if paired:
        came, head_weights = lax.optimization_barrier((came, head_weights))
        slots = jnp.concatenate([add_low(keep, came)[0], distant], axis=0)
        packed = jnp.stack(
            [lax.dynamic_index_in_dim(slots, rank ^ t, 0, keepdims=False) for t in range(parts)]
        )
    packed = lax.psum_scatter(packed, "tensor", scatter_dimension=0, tiled=True)[0]
    biases = jnp.concatenate((sums[:, :head_cols].reshape(-1), sums[:, head_cols:].reshape(-1)))
    biases = jnp.pad(
        biases.reshape(8, heads, 1, DH), ((0, shard_rows - 8), (0, 0), (1, 2), (0, 0))
    ).reshape(1, shard_rows, -1)
    query_grad, key_grad, value_grad, biases = run_finish_heads(
        scatter_rows((head_weights + biases).astype(BF16))
    )
    biases = biases.reshape(2, width)
    input_grad = first_grad + attn_back.astype(F32)

    inner_grad, outer_grad, output_grad, notes = run_finish_dense(packed, hidden_cols, head_cols)
    notes = notes.reshape(-1)

    def total(which):
        return notes[which * width : (which + 1) * width]

    mse_loss = jnp.sum(total(0)) / (counted * width)
    return (
        layer_out.reshape(1, part_len, width),
        mse_loss,
        input_grad.reshape(1, part_len, width),
        query_grad,
        key_grad,
        value_grad,
        output_grad,
        inner_grad,
        outer_grad.T,
        biases[0],
        biases[1],
        total(4),
        notes[8 * width : 8 * width + hidden_cols * parts],
        total(1),
        total(5),
        total(6),
        total(2),
        total(3),
    )


def solution(mesh):
    shard = P("dp", "tensor", None)
    by_dp, by_tensor = P("dp", "tensor"), P("tensor", "dp")
    in_specs = (
        (shard, P("dp", None), by_dp, shard, shard)
        + (by_dp,) * 3
        + (by_tensor, by_dp, by_tensor)
        + (P(),) * 9
    )
    out_specs = (shard, P(), shard) + (by_dp,) * 3 + (by_tensor, by_dp, by_tensor) + (P(),) * 9
    return jax.shard_map(local, mesh=mesh, in_specs=in_specs, out_specs=out_specs, check_vma=False)
```

```python
import functools

import jax
import jax.numpy as jnp
from jax import lax
from jax.experimental import pallas as pl
from jax.experimental.pallas import tpu as pltpu
from jax.sharding import PartitionSpec as P

DH = 64
BLOCK = 256
SLAB = 4 * DH
EPSILON = 1e-12
ROOT_HALF = 0.7071067811865476
INV_ROOT_TAU = 0.3989422804014327
LOG2E = 1.4426950408889634
LN2 = 0.6931471805599453
SCALE = DH ** (-0.5)
MASKED = -1e30
VMEM_LIMIT = 60 << 20

BF16 = jnp.bfloat16
F32 = jnp.float32
NN = (((1,), (0,)), ((), ()))
NT = (((1,), (1,)), ((), ()))
TN = (((0,), (0,)), ((), ()))


def dot(left_side, right_side, dims=NN):
    return lax.dot_general(left_side, right_side, dims, preferred_element_type=F32)


def norm_forward(summed, gain_vec, shift_vec):
    average = jnp.mean(summed, axis=-1, keepdims=True)
    centered = summed - average
    variance = jnp.mean(centered * centered, axis=-1, keepdims=True)
    inverse = lax.rsqrt(variance + EPSILON)
    normed = centered * inverse
    return (normed * gain_vec + shift_vec, normed, inverse)


def norm_backward(upstream, normed, inverse, gain_vec):
    scaled = upstream * gain_vec
    first_mean = jnp.mean(scaled, axis=-1, keepdims=True)
    second_mean = jnp.mean(scaled * normed, axis=-1, keepdims=True)
    return inverse * (scaled - first_mean - normed * second_mean)


def column_sum(value):
    return jnp.sum(value, axis=0, keepdims=True)


def lane_is_right(rows):
    return lax.broadcasted_iota(jnp.int32, (rows, 2 * DH), 1) >= DH


def pack(first_two, third_top, third_bottom):
    return jnp.concatenate([first_two, jnp.concatenate([third_top, third_bottom], axis=1)], axis=0)


def unpack(packed):
    third = packed[BLOCK:]
    third = jnp.concatenate([third[:, :DH], third[:, DH:]], axis=0)
    return jnp.concatenate([packed[:BLOCK], third], axis=1)


def fetch_chunks(lane_ref, chunk_refs, target, sems):
    rows = chunk_refs[0].shape[0]
    copies = []
    for at, chunk in enumerate(chunk_refs):
        offset = pl.multiple_of(lax.rem(lane_ref[0] + at, len(chunk_refs)) * rows, rows)
        copies.append(pltpu.make_async_copy(chunk, target.at[pl.ds(offset, rows), :], sems.at[at]))
    return copies


def attend_forward(
    first_block, lane_ref, low_ref, count_ref, *refs
):
    chunk_refs, (seg_col_ref, seg_row_ref, ctx_ref, lse_ref, held, qkv_ref, sems) = refs[:-7], refs[-7:]
    heads = lse_ref.shape[0]

    @pl.when(pl.program_id(0) == 0)
    def _():
        copies = fetch_chunks(lane_ref, chunk_refs, qkv_ref, sems)
        for copy in copies:
            copy.start()
        for copy in copies:
            copy.wait()

    qb = pl.program_id(0) + first_block
    rows = pl.ds(pl.multiple_of(qb * BLOCK, BLOCK), BLOCK)
    seg_q = seg_col_ref[...]
    queries = [
        qkv_ref[rows, SLAB * h : SLAB * h + 2 * DH] * jnp.asarray(SCALE, BF16) for h in range(heads)
    ]
    low, count = low_ref[qb], count_ref[qb]

    def score(kb, peaks):
        keys = pl.ds(pl.multiple_of(low * STEP + kb * BLOCK, STEP), BLOCK)
        allowed = seg_q == seg_row_ref[:, keys]
        found = []
        for h in range(heads):
            scores = dot(queries[h], qkv_ref[keys, SLAB * h + 2 * DH : SLAB * (h + 1)], NT)
            scores = jnp.where(allowed, scores, MASKED)
            held[h, kb] = scores
            found.append(jnp.maximum(peaks[h], jnp.maximum(scores[:, :128], scores[:, 128:])))
        return tuple(found)

    start = tuple(jnp.full((BLOCK, 128), MASKED, F32) for _ in range(heads))
    peaks = lax.fori_loop(0, count, score, start)
    highest = [jnp.max(peak, axis=-1, keepdims=True) for peak in peaks]

    def weigh(kb, carry):
        keys = pl.ds(pl.multiple_of(low * STEP + kb * BLOCK, STEP), BLOCK)
        found = []
        for h in range(heads):
            total, acc = carry[h]
            raised = jnp.exp2((held[h, kb] - highest[h]) * LOG2E)
            total = total + (raised[:, :128] + raised[:, 128:])
            acc = acc + dot(raised.astype(BF16), qkv_ref[keys, SLAB * h + 2 * DH : SLAB * (h + 1)])
            found.append((total, acc))
        return tuple(found)

    zero = jnp.zeros((BLOCK, 128), F32)
    done = lax.fori_loop(0, count, weigh, tuple((zero, zero) for _ in range(heads)))
    values = []
    for h in range(heads):
        total, acc = done[h]
        summed = jnp.sum(total, axis=-1, keepdims=True)
        values.append((acc / summed).astype(BF16))
        lse_ref[h] = jnp.transpose(highest[h] + jnp.log(summed))
    middle = BLOCK // 2
    ctx_ref[0, :BLOCK, :] = jnp.where(lane_is_right(BLOCK), values[1], pltpu.roll(values[0], DH, 1))
    ctx_ref[0, BLOCK:, :] = jnp.where(
        lane_is_right(middle), values[2][middle:], pltpu.roll(values[2][:middle], DH, 1)
    )


def attend_backward(which, chunks, lane_ref, low_ref, count_ref, *refs):
    halves, half = which
    last = half == halves - 1
    chunk_refs, refs = refs[:chunks], refs[chunks:]
    (seg_col_ref, seg_row_ref, ctx_ref, grad_ref, lse_ref), refs = refs[:5], refs[5:]
    earlier, refs = refs[:half], refs[half:]
    if half > 0:
        before_ref, refs = refs[0], refs[1:]
    if last:
        final_ref, sums_ref, dkv, out_ref, qkv_ref, sems = refs
    else:
        dkv, query_ref, qkv_ref, sems = refs
    heads = dkv.shape[0]
    step_index = pl.program_id(0)
    qb = step_index * halves + half

    @pl.when(step_index == 0)
    def _():
        copies = fetch_chunks(lane_ref, chunk_refs, qkv_ref, sems)
        for copy in copies:
            copy.start()
        dkv[...] = before_ref[...] if half > 0 else jnp.zeros_like(dkv)
        for copy in copies:
            copy.wait()

    rows = pl.ds(pl.multiple_of(qb * BLOCK, BLOCK), BLOCK)
    right = lane_is_right(BLOCK)
    arrived = grad_ref[0]
    product = arrived.astype(F32) * ctx_ref[0].astype(F32)
    upper = product.astype(BF16)
    lower = (product - upper.astype(F32)).astype(BF16)
    pick = (
        lax.broadcasted_iota(jnp.int32, (8, 2 * DH), 1) // DH
        == lax.broadcasted_iota(jnp.int32, (8, 2 * DH), 0)
    ).astype(BF16)
    summed = dot(pick, upper, NT) + dot(pick, lower, NT)
    deltas = [
        summed[0:1, :BLOCK],
        summed[1:2, :BLOCK],
        jnp.concatenate([summed[0:1, BLOCK:], summed[1:2, BLOCK:]], axis=1),
    ]
    two, third = arrived[:BLOCK], arrived[BLOCK:]
    placed = [
        pltpu.roll(two, DH, 1),
        two,
        jnp.concatenate([pltpu.roll(third, DH, 1), third], axis=0),
    ]
    grads = [jnp.where(right, grad, jnp.zeros_like(grad)) for grad in placed]
    queries, pairs = [], []
    for h in range(heads):
        queries.append(qkv_ref[rows, SLAB * h : SLAB * h + 2 * DH] * jnp.asarray(SCALE, BF16))
        pairs.append(jnp.concatenate([queries[h], grads[h]], axis=0))
    seg_q = seg_row_ref[...]
    lses = lse_ref[...]
    low, count = low_ref[qb], count_ref[qb]

    def step(kb, accs):
        keys = pl.ds(pl.multiple_of(low * STEP + kb * BLOCK, STEP), BLOCK)
        allowed = seg_col_ref[keys, :] == seg_q
        found = []
        for h in range(heads):
            pair = qkv_ref[keys, SLAB * h + 2 * DH : SLAB * (h + 1)]
            scores = jnp.where(allowed, dot(pair, queries[h], NT), MASKED)
            probs = jnp.exp2((scores - lses[h]) * LOG2E)
            score_grad = (probs * (dot(pair, grads[h], NT) - deltas[h])).astype(BF16)
            both = jnp.concatenate([score_grad, probs.astype(BF16)], axis=1)
            dkv[h, keys, :] += dot(both, pairs[h])
            found.append(accs[h] + dot(score_grad, pair, TN))
        return tuple(found)

    zero = jnp.zeros((BLOCK, 128), F32)
    accs = lax.fori_loop(0, count, step, tuple(zero for _ in range(heads)))
    for h in range(heads):
        query_grad = jnp.where(right, 0.0, accs[h] * SCALE).astype(BF16)
        if last:
            out_ref[rows, SLAB * h : SLAB * h + 2 * DH] = query_grad
        else:
            query_ref[0, :, 2 * DH * h : 2 * DH * (h + 1)] = query_grad

    if last:

        @pl.when(step_index == pl.num_programs(0) - 1)
        def _():
            for h in range(heads):
                at = SLAB * h
                for other, ref in enumerate(earlier):
                    for block in range(ref.shape[0]):
                        start = (block * halves + other) * BLOCK
                        out_ref[start : start + BLOCK, at : at + 2 * DH] = ref[
                            block, :, 2 * DH * h : 2 * DH * (h + 1)
                        ]
                out_ref[:, at + 2 * DH : at + SLAB] = dkv[h].astype(BF16)
                sums_ref[:, at : at + SLAB] = column_sum(out_ref[:, at : at + SLAB].astype(F32))
            rows_each = final_ref.shape[1]
            copies = []
            for at in range(final_ref.shape[0]):
                offset = pl.multiple_of(lax.rem(lane_ref[0] + at, final_ref.shape[0]) * rows_each, rows_each)
                copies.append(
                    pltpu.make_async_copy(
                        out_ref.at[pl.ds(offset, rows_each), :], final_ref.at[at], sems.at[at]
                    )
                )
            for copy in copies:
                copy.start()
            for copy in copies:
                copy.wait()


STEP = 128


def document_blocks(segment_row):
    starts = segment_row[::BLOCK]
    stops = segment_row[BLOCK - 1 :: BLOCK]
    low = jnp.sum((segment_row[None, :] < starts[:, None]).astype(jnp.int32), axis=1) // STEP
    high = jnp.sum((segment_row[None, :] <= stops[:, None]).astype(jnp.int32), axis=1)
    each = BLOCK // STEP
    count = (high - low * STEP + BLOCK - 1) // BLOCK
    return (jnp.minimum(low, segment_row.shape[0] // STEP - each * count), count)


PACKED = BLOCK + BLOCK // 2


def run_forward(first_block, steps, lane, bounds, qkv, seg_col, seg_row):
    seq_len, width = seg_col.shape[0], qkv[0].shape[1]
    heads = width // SLAB
    blocks = seq_len // BLOCK
    return pl.pallas_call(
        functools.partial(attend_forward, first_block),
        out_shape=(
            jax.ShapeDtypeStruct((steps, PACKED, 2 * DH), BF16),
            jax.ShapeDtypeStruct((heads, 1, steps * BLOCK), F32),
        ),
        grid_spec=pltpu.PrefetchScalarGridSpec(
            num_scalar_prefetch=3,
            grid=(steps,),
            in_specs=[pl.BlockSpec(memory_space=pl.ANY)] * len(qkv)
            + [
                pl.BlockSpec((BLOCK, 1), lambda q, *_: (q + first_block, 0)),
                pl.BlockSpec((1, seq_len), lambda q, *_: (0, 0)),
            ],
            out_specs=(
                pl.BlockSpec((1, PACKED, 2 * DH), lambda q, *_: (q, 0, 0)),
                pl.BlockSpec((heads, 1, BLOCK), lambda q, *_: (0, 0, q)),
            ),
            scratch_shapes=[
                pltpu.VMEM((heads, blocks, BLOCK, BLOCK), F32),
                pltpu.VMEM((seq_len, width), BF16),
                pltpu.SemaphoreType.DMA((len(qkv),)),
            ],
        ),
        compiler_params=pltpu.CompilerParams(
            dimension_semantics=("arbitrary",), vmem_limit_bytes=VMEM_LIMIT
        ),
        cost_estimate=pl.CostEstimate(
            flops=heads * seq_len * seq_len * 2048 * steps // blocks,
            bytes_accessed=5 << 20,
            transcendentals=heads * seq_len * seq_len // 3,
        ),
        name="attend_forward",
    )(lane, *bounds, *qkv, seg_col, seg_row)


def run_backward(which, lane, bounds, qkv, seg_col, seg_row, ctx, grad, lse, earlier, before):
    halves, half = which
    seq_len, width = seg_col.shape[0], qkv[0].shape[1]
    heads = width // SLAB
    steps = seq_len // BLOCK // halves
    packed = pl.BlockSpec((1, PACKED, 2 * DH), lambda q, *_: (q, 0, 0))

    def fixed(shape, **more):
        return pl.BlockSpec(shape, lambda q, *_: (0,) * len(shape), **more)

    once = {"pipeline_mode": pl.Buffered(1)}
    gathered = (heads, seq_len, 2 * DH)
    carried = [fixed(value.shape, **once) for value in earlier]
    carried += [fixed(gathered, **once)] * len(before)
    scratch = [pltpu.VMEM((seq_len, width), BF16), pltpu.SemaphoreType.DMA((len(qkv),))]
    if half == halves - 1:
        out_shape = (
            jax.ShapeDtypeStruct((len(qkv), seq_len // len(qkv), width), BF16),
            jax.ShapeDtypeStruct((1, width), F32),
        )
        out_specs = (pl.BlockSpec(memory_space=pl.ANY), fixed((1, width)))
        scratch = [pltpu.VMEM(gathered, F32), pltpu.VMEM((seq_len, width), BF16)] + scratch
    else:
        out_shape = (
            jax.ShapeDtypeStruct(gathered, F32),
            jax.ShapeDtypeStruct((steps, BLOCK, heads * 2 * DH), BF16),
        )
        out_specs = (
            fixed(gathered),
            pl.BlockSpec((1, BLOCK, heads * 2 * DH), lambda q, *_: (q, 0, 0)),
        )
    return pl.pallas_call(
        functools.partial(attend_backward, which, len(qkv)),
        out_shape=out_shape,
        grid_spec=pltpu.PrefetchScalarGridSpec(
            num_scalar_prefetch=3,
            grid=(steps,),
            in_specs=[pl.BlockSpec(memory_space=pl.ANY)] * len(qkv)
            + [
                fixed((seq_len, 1)),
                pl.BlockSpec((1, BLOCK), lambda q, *_: (0, q * halves + half)),
                packed,
                packed,
                pl.BlockSpec((heads, 1, BLOCK), lambda q, *_: (0, 0, q)),
            ]
            + carried,
            out_specs=out_specs,
            scratch_shapes=scratch,
        ),
        compiler_params=pltpu.CompilerParams(
            dimension_semantics=("arbitrary",), vmem_limit_bytes=VMEM_LIMIT
        ),
        cost_estimate=pl.CostEstimate(
            flops=heads * seq_len * seq_len * 4096,
            bytes_accessed=10 << 20,
            transcendentals=heads * seq_len * seq_len // 3 // halves,
        ),
        name="attend_backward",
    )(lane, *bounds, *qkv, seg_col, seg_row, ctx, grad, lse, *earlier, *before)


def dense_chain(
    marks, total_tokens, place_ref, ctx_ref, in_ref, teacher_ref, cotangent_ref, valid_ref, vec_ref,
    inner_bias_ref, *refs
):
    pieces = refs[: len(marks)]
    (
        layer_ref, first_grad_ref, ctx_grad_ref, first_ref, branch_grad_ref, attn_grad_ref,
        act_ref, hidden_grad_ref, sums_ref, inner_sums_ref, w_out, w_in, w_up, slope, sems,
    ) = refs[len(marks) :]
    parts, _, head_cols = w_out.shape
    hidden_cols = w_in.shape[2]
    index = place_ref[parts]
    step = pl.program_id(0)
    groups = (
        (2 * hidden_cols, head_cols, w_out),
        (0, hidden_cols, w_in),
        (hidden_cols, hidden_cols, w_up),
    )

    @pl.when(step == 0)
    def _():
        for group, (start, size, target) in enumerate(groups):
            for piece, marked in zip(pieces, marks):
                block = piece.shape[1]
                for at, (slot, turn, relative) in enumerate(marked):
                    offset = pl.multiple_of((index ^ turn) * block, block) if relative else turn * block
                    pltpu.make_async_copy(
                        piece.at[at, :, pl.ds(start, size)],
                        target.at[slot, pl.ds(offset, block), :],
                        sems.at[group, slot],
                    ).start()
        sums_ref[...] = jnp.zeros_like(sums_ref)
        inner_sums_ref[...] = jnp.zeros_like(inner_sums_ref)

    def arrive(group, slot):
        whole = groups[group][2].at[slot]

        @pl.when(step == 0)
        def _():
            pltpu.make_async_copy(whole, whole, sems.at[group, slot]).wait()

    def vec(which):
        return vec_ref[which : which + 1, :]

    counts = jnp.zeros((1, 2 * DH), F32)

    attention = jnp.zeros(in_ref.shape, F32)
    for slot in range(parts):
        arrive(0, slot)
        counts = counts + column_sum(w_out[slot, :, 2 * DH :].astype(F32))
        attention = attention + dot(unpack(ctx_ref[place_ref[slot], 0]), w_out[slot, :, : 3 * DH], NT)
    first_exact, normed_one, inverse_one = norm_forward(
        in_ref[...].astype(F32) + attention + vec(0), vec(1), vec(2)
    )
    first = first_exact.astype(BF16)
    first_ref[...] = first

    def up(slot, branch):
        t = place_ref[slot]
        arrive(1, slot)
        hidden = dot(first, w_in[slot]) + inner_bias_ref[t]
        bend = 0.5 * (1.0 + lax.erf(hidden * ROOT_HALF))
        activated = (hidden * bend).astype(BF16)
        act_ref[t] = activated
        slope[slot] = bend + hidden * INV_ROOT_TAU * jnp.exp2(hidden * hidden * (-0.5 * LOG2E))
        arrive(2, slot)
        return branch + dot(activated, w_up[slot], NT)

    branch = jnp.zeros(in_ref.shape, F32)
    for slot in range(parts):
        branch = up(slot, branch)
    lanes = lax.broadcasted_iota(jnp.int32, counts.shape, 1)
    weight = jnp.where(lanes == DH, 256.0, jnp.where(lanes == DH + 1, 1.0, 0.0))
    ratio = total_tokens / jnp.sum(jnp.where(weight > 0.0, counts, 0.0) * weight, axis=-1, keepdims=True)
    layer_rows, normed_two, inverse_two = norm_forward(first.astype(F32) + branch + vec(3), vec(4), vec(5))
    layer_ref[...] = layer_rows.astype(BF16)
    misfit = layer_rows - teacher_ref[...].astype(F32)
    weighted = valid_ref[...] * misfit
    out_grad = cotangent_ref[...].astype(F32) + weighted * ratio
    second_grad = norm_backward(out_grad, normed_two, inverse_two, vec(4))
    branch_grad = second_grad.astype(BF16)
    branch_grad_ref[...] = branch_grad
    sums_ref[0:1, :] += column_sum(weighted * misfit)
    sums_ref[1:2, :] += column_sum(branch_grad.astype(F32))
    sums_ref[2:3, :] += column_sum(out_grad * normed_two)
    sums_ref[3:4, :] += column_sum(out_grad)

    def down(slot, back):
        t = place_ref[slot]
        hidden_grad = (dot(branch_grad, w_up[slot]) * slope[slot]).astype(BF16)
        hidden_grad_ref[t] = hidden_grad
        inner_sums_ref[t] += column_sum(hidden_grad.astype(F32))
        return back + dot(hidden_grad, w_in[slot], NT)

    upstream = second_grad
    for slot in range(parts):
        upstream = down(slot, upstream)
    first_grad = norm_backward(upstream, normed_one, inverse_one, vec(1))
    first_grad_ref[...] = first_grad
    attn_grad = first_grad.astype(BF16)
    attn_grad_ref[...] = attn_grad
    sums_ref[4:5, :] += column_sum(attn_grad.astype(F32))
    sums_ref[5:6, :] += column_sum(upstream * normed_one)
    sums_ref[6:7, :] += column_sum(upstream)
    middle = BLOCK // 2
    for slot in range(parts):
        back = dot(attn_grad, w_out[slot, :, : 3 * DH]).astype(BF16)
        ctx_grad_ref[place_ref[slot], 0] = pack(
            back[:, : 2 * DH], back[:middle, 2 * DH :], back[middle:, 2 * DH :]
        )


def run_dense(marks, total_tokens, place, ctx, rows_in, teacher, cotangent, valid, vecs, inner_bias, pieces):
    parts, halves = ctx.shape[:2]
    part_len, width = rows_in.shape
    hidden_cols = inner_bias.shape[2]
    out_cols = pieces[0].shape[2] - 2 * hidden_cols

    def by_rows(columns):
        return pl.BlockSpec((BLOCK, columns), lambda i: (i, 0))

    def by_part(columns):
        return pl.BlockSpec((parts, BLOCK, columns), lambda i: (0, i, 0))

    def fixed(shape):
        return pl.BlockSpec(shape, lambda i: (0,) * len(shape))

    packed = pl.BlockSpec((parts, 1) + ctx.shape[2:], lambda i: (0, i, 0, 0))
    low = jax.ShapeDtypeStruct((part_len, width), BF16)
    wide = jax.ShapeDtypeStruct((parts, part_len, hidden_cols), BF16)
    smem = pl.BlockSpec(memory_space=pltpu.SMEM)
    return pl.pallas_call(
        functools.partial(dense_chain, marks, total_tokens),
        out_shape=(
            low,
            jax.ShapeDtypeStruct((part_len, width), F32),
            jax.ShapeDtypeStruct(ctx.shape, BF16),
            low,
            low,
            low,
            wide,
            wide,
            jax.ShapeDtypeStruct((8, width), F32),
            jax.ShapeDtypeStruct((parts, 1, hidden_cols), F32),
        ),
        grid=(halves,),
        in_specs=[
            smem,
            packed,
            by_rows(width),
            by_rows(width),
            by_rows(width),
            by_rows(1),
            fixed(vecs.shape),
            fixed(inner_bias.shape),
        ]
        + [pl.BlockSpec(memory_space=pl.ANY)] * len(pieces),
        out_specs=(
            by_rows(width),
            by_rows(width),
            packed,
            by_rows(width),
            by_rows(width),
            by_rows(width),
            by_part(hidden_cols),
            by_part(hidden_cols),
            fixed((8, width)),
            fixed((parts, 1, hidden_cols)),
        ),
        scratch_shapes=[
            pltpu.VMEM((parts, width, out_cols), BF16),
            pltpu.VMEM((parts, width, hidden_cols), BF16),
            pltpu.VMEM((parts, width, hidden_cols), BF16),
            pltpu.VMEM((parts, BLOCK, hidden_cols), F32),
            pltpu.SemaphoreType.DMA((3, parts)),
        ],
        compiler_params=pltpu.CompilerParams(
            dimension_semantics=("arbitrary",), vmem_limit_bytes=VMEM_LIMIT
        ),
        cost_estimate=pl.CostEstimate(
            flops=2 * part_len * width * (8 * hidden_cols + 4 * out_cols) * parts,
            bytes_accessed=24 << 20,
            transcendentals=2 * part_len * hidden_cols * parts,
        ),
        name="dense_chain",
    )(place, ctx, rows_in, teacher, cotangent, valid, vecs, inner_bias, *pieces)


def dense_weights(
    plans, place_ref, first_ref, branch_grad_ref, attn_grad_ref, act_ref, hidden_grad_ref, ctx_ref,
    notes_ref, *refs
):
    outs, (turned, whole, sems) = refs[:-3], refs[-3:]
    step = pl.program_id(0)
    slots = whole.shape[0]

    @pl.when(step == 0)
    def _():
        for which, source in enumerate((first_ref, branch_grad_ref, attn_grad_ref)):
            turned[which] = jnp.transpose(source[...])

    hidden_cols = act_ref.shape[2]
    whole[step, :, :hidden_cols] = dot(turned[0], hidden_grad_ref[0]).astype(BF16)
    whole[step, :, hidden_cols : 2 * hidden_cols] = dot(turned[1], act_ref[0]).astype(BF16)
    ctx = jnp.concatenate([unpack(ctx_ref[0, half]) for half in range(ctx_ref.shape[1])], axis=0)
    plain = 2 * hidden_cols + ctx.shape[1]
    whole[step, :, 2 * hidden_cols : plain] = dot(turned[2], ctx).astype(BF16)
    whole[step, :, plain : plain + notes_ref.shape[1]] = notes_ref[...]
    for out, turns in zip(outs, plans):
        block = out.shape[1]
        for at, turn in enumerate(turns):
            offset = 0
            if block < whole.shape[1]:
                offset = pl.multiple_of((place_ref[place_ref.shape[0] - 1] ^ turn) * block, block)
            pltpu.make_async_copy(
                whole.at[step, pl.ds(offset, block), :], out.at[at * slots + step], sems.at[step]
            ).start()

    @pl.when(step == slots - 1)
    def _():
        for slot in range(slots):
            pltpu.make_async_copy(whole.at[slot], whole.at[slot], sems.at[slot]).wait()


def run_weights(base, slots, plans, place, notes, first, branch_grad, attn_grad, act, hidden_grad, ctx):
    _, part_len, hidden_cols = act.shape
    width = first.shape[1]
    columns = 2 * hidden_cols + 3 * DH + notes.shape[1]
    fixed = pl.BlockSpec((part_len, width), lambda s, place: (0, 0))
    by_slot = pl.BlockSpec((1, part_len, hidden_cols), lambda s, place: (place[base + s], 0, 0))
    outs = tuple(
        jax.ShapeDtypeStruct((len(turns) * slots, block, columns), BF16) for block, turns in plans
    )
    return pl.pallas_call(
        functools.partial(dense_weights, tuple(turns for _, turns in plans)),
        out_shape=outs,
        grid_spec=pltpu.PrefetchScalarGridSpec(
            num_scalar_prefetch=1,
            grid=(slots,),
            in_specs=[
                fixed,
                fixed,
                fixed,
                by_slot,
                by_slot,
                pl.BlockSpec((1,) + ctx.shape[1:], lambda s, place: (place[base + s], 0, 0, 0)),
                pl.BlockSpec(notes.shape, lambda s, place: (0, 0)),
            ],
            out_specs=tuple(pl.BlockSpec(memory_space=pl.ANY) for _ in outs),
            scratch_shapes=[
                pltpu.VMEM((3, width, part_len), BF16),
                pltpu.VMEM((slots, width, columns), BF16),
                pltpu.SemaphoreType.DMA((slots,)),
            ],
        ),
        compiler_params=pltpu.CompilerParams(
            dimension_semantics=("arbitrary",), vmem_limit_bytes=VMEM_LIMIT
        ),
        cost_estimate=pl.CostEstimate(
            flops=2 * part_len * width * columns * slots,
            bytes_accessed=5 * slots << 20,
            transcendentals=0,
        ),
        name="dense_weights",
    )(place, first, branch_grad, attn_grad, act, hidden_grad, ctx, notes)


def finish_dense(packed_ref, inner_ref, outer_ref, output_ref, notes_ref):
    hidden_cols = inner_ref.shape[1]
    summed = packed_ref[...].astype(F32)
    inner_ref[...] = summed[:, :hidden_cols]
    outer_ref[...] = summed[:, hidden_cols : 2 * hidden_cols]
    plain = 2 * hidden_cols + output_ref.shape[0]
    output_ref[...] = jnp.transpose(summed[:, 2 * hidden_cols : plain])
    notes_ref[...] = summed[:, plain:]


def run_finish_dense(packed, hidden_cols, head_cols):
    rows = packed.shape[0]
    return pl.pallas_call(
        finish_dense,
        out_shape=(
            jax.ShapeDtypeStruct((rows, hidden_cols), F32),
            jax.ShapeDtypeStruct((rows, hidden_cols), F32),
            jax.ShapeDtypeStruct((head_cols, rows), F32),
            jax.ShapeDtypeStruct((rows, packed.shape[1] - 2 * hidden_cols - head_cols), F32),
        ),
        name="finish_dense",
    )(packed)


def finish_heads(value_ref, *refs):
    summed = value_ref[...].astype(F32)
    heads = summed.shape[1] // SLAB
    for ref, which in zip(refs, (0, 2, 3, 1)):
        columns = [summed[:, SLAB * h + which * DH : SLAB * h + (which + 1) * DH] for h in range(heads)]
        ref[...] = jnp.concatenate(columns, axis=1)[: ref.shape[0]]


def run_finish_heads(value):
    rows, width = value.shape
    out = jax.ShapeDtypeStruct((rows, width // 4), F32)
    notes = jax.ShapeDtypeStruct((8, width // 4), F32)
    return pl.pallas_call(finish_heads, out_shape=(out, out, out, notes), name="finish_heads")(value)


def interleave(query, key, value, heads):
    rows = query.shape[0]
    parts = [part.reshape(rows, heads, 1, DH) for part in (query, jnp.zeros_like(query), key, value)]
    return jnp.concatenate(parts, axis=2).reshape(rows, heads * SLAB)


def swap(value, axis, bit):
    size = lax.axis_size(axis)
    return lax.ppermute(value, axis, [(i, i ^ bit) for i in range(size)])


def bits_of(axis):
    bit = 1
    while bit < lax.axis_size(axis):
        yield bit
        bit *= 2


def after(value, *others):
    return lax.optimization_barrier((value,) + others)[0]


def merge(held, other, axis, bit):
    mine_first = (lax.axis_index(axis) & bit) == 0
    return jnp.where(
        mine_first, jnp.concatenate([held, other], axis=0), jnp.concatenate([other, held], axis=0)
    )


def add_low(left_side, right_side):
    return (left_side.astype(F32) + right_side.astype(F32)).astype(BF16)


def add_halves(left_side, right_side):
    half = left_side.shape[0] // 2
    return (
        add_low(left_side[:half], right_side[:half]),
        add_low(left_side[half:], right_side[half:]),
    )


def scatter_rows(held):
    index = lax.axis_index("dp")
    for bit in bits_of("dp"):
        held = held.reshape((held.shape[0] // 2, 2) + held.shape[1:])
        own = (index & bit) // bit
        send = lax.dynamic_index_in_dim(held, 1 - own, 1, keepdims=False)
        keep = lax.dynamic_index_in_dim(held, own, 1, keepdims=False)
        held = add_low(keep, swap(send, "dp", bit))
    return held[0]


def local(
    inputs, segment_ids, valid_mask, teacher, cotangent,
    w_query, w_key, w_value, w_output, w_inner, w_outer,
    query_bias, value_bias, output_bias, inner_bias, outer_bias,
    gain_attn, shift_attn, gain_ffn, shift_ffn,
):
    _, part_len, width = inputs.shape
    parts = lax.axis_size("tensor")
    copies = lax.axis_size("dp")
    rank = lax.axis_index("tensor")
    total_tokens = part_len * parts * copies
    seq_len = part_len * parts
    head_cols = w_query.shape[1]
    heads = head_cols // DH
    hidden_cols = w_inner.shape[1]
    shard_rows = w_inner.shape[0]
    halves = part_len // BLOCK

    rows_in = inputs.reshape(part_len, width)
    tokens = lax.all_gather(rows_in, "tensor", axis=0, tiled=True)
    w_heads = interleave(w_query, w_key, w_value, heads)
    paired = shard_rows % 16 == 0 and parts == 4 and copies == 8

    valid_rows = valid_mask.astype(F32).reshape(part_len, 1)
    valid_count = jnp.sum(valid_mask.astype(F32))
    upper = jnp.floor(valid_count / 256.0)
    spot = lax.broadcasted_iota(jnp.int32, (shard_rows, DH), 0) * DH + lax.broadcasted_iota(
        jnp.int32, (shard_rows, DH), 1
    )
    count_row = jnp.where(spot == 0, upper, jnp.where(spot == 1, valid_count - 256.0 * upper, 0.0))
    mine = jnp.concatenate((w_inner, w_outer.T, w_output.T, count_row.astype(BF16)), axis=1)
    if paired:
        place = jnp.stack([rank, rank ^ 1, rank ^ 2, rank ^ 3, lax.axis_index("dp")]).astype(jnp.int32)
        pair = jnp.concatenate([mine[None], swap(mine[None], "tensor", 1)], axis=0)
        near = jnp.concatenate([pair, swap(pair, "dp", 2)], axis=0)
        turns = [0, 2, 4, 6]
        for bit in (1, 2, 4):
            w_heads = merge(w_heads, swap(w_heads, "dp", bit), "dp", bit)
        near, w_heads = lax.optimization_barrier((near, w_heads))
        near_next = swap(near, "dp", 4)
        tokens, pair, near_next = lax.optimization_barrier((tokens, pair, near_next))
        far = swap(pair, "tensor", 2)
    else:
        place = jnp.asarray(list(range(parts)) + [0], jnp.int32)
        weights = lax.all_gather(mine, ("tensor", "dp"), axis=0, tiled=False)
        for bit in bits_of("dp"):
            w_heads = merge(w_heads, swap(w_heads, "dp", bit), "dp", bit)

    mine_cols = rank * head_cols
    query_shift = lax.dynamic_slice_in_dim(query_bias, mine_cols, head_cols).astype(F32)
    value_shift = lax.dynamic_slice_in_dim(value_bias, mine_cols, head_cols).astype(F32)
    shifts = interleave(query_shift[None], jnp.zeros_like(query_shift)[None], value_shift[None], heads)
    qkv = [(dot(tokens, w_heads) + shifts).astype(BF16)]

    segment_row = segment_ids.reshape(seq_len)
    bounds = document_blocks(segment_row)
    seg_col = segment_row.reshape(seq_len, 1)
    seg_row = segment_row.reshape(1, seq_len)
    lane = rank.astype(jnp.int32).reshape(1)

    def exchange(packed_blocks):
        return lax.all_to_all(packed_blocks.reshape(parts, halves, PACKED, 2 * DH), "tensor", 0, 0)

    blocks = seq_len // BLOCK
    early = run_forward(0, blocks // 2, lane, bounds, qkv, seg_col, seg_row)
    if paired:
        far, early, bounds = lax.optimization_barrier((far, early, bounds))
        weights = lax.all_gather(far, "dp", axis=0, tiled=False)
    late = run_forward(blocks // 2, blocks // 2, lane, bounds, qkv, seg_col, seg_row)
    context = jnp.concatenate((early[0], late[0]), axis=0)
    lse = jnp.concatenate((early[1], late[1]), axis=2)
    if paired:
        near_next, context = lax.optimization_barrier((near_next, context))
        near = jnp.concatenate([near, near_next], axis=0)
        near_other = swap(near, "dp", 1)
    arrived = exchange(context)
    if paired:
        weights = weights.reshape((copies * 2,) + mine.shape)
        pieces = [near, near_other, weights]
        marks = [[(slot, turn ^ flip, True) for turn in turns for slot in (0, 1)] for flip in (0, 1)]
        marks.append([(2 + at % 2, at // 2, False) for at in range(2 * copies)])
    else:
        pieces = [weights.reshape(parts, width, -1)]
        marks = [[(t, 0, False) for t in range(parts)]]
    counts = [piece.reshape((-1,) + mine.shape)[:, 0, -DH : 2 - DH].astype(F32) for piece in pieces + [weights]]
    counts = jnp.concatenate(counts[:-1] if paired else counts[-1:], axis=0)
    counted = 256.0 * jnp.sum(counts[:, 0]) + jnp.sum(counts[:, 1])

    vecs = jnp.stack(
        (output_bias, gain_attn, shift_attn, outer_bias, gain_ffn, shift_ffn, outer_bias, outer_bias)
    ).astype(F32)
    inner_rows = inner_bias.astype(F32).reshape(parts, 1, hidden_cols)
    teacher_rows = teacher.reshape(part_len, width)
    cotangent_rows = cotangent.reshape(part_len, width)
    (
        layer_out, first_grad, context_grad, first, branch_grad, attn_grad, activated, hidden_grad,
        dense_sums, inner_sums,
    ) = run_dense(
        marks, float(total_tokens), place, arrived, rows_in, teacher_rows, cotangent_rows, valid_rows, vecs,
        inner_rows, pieces,
    )
    head_grad = exchange(context_grad).reshape(context.shape)
    sources = (first, branch_grad, attn_grad, activated, hidden_grad, arrived)
    notes = jnp.concatenate((dense_sums.reshape(-1), inner_sums.reshape(-1))).astype(BF16)
    room = -(-notes.shape[0] // (shard_rows * 128)) * 128
    notes = jnp.pad(notes, (0, shard_rows * room - notes.shape[0])).reshape(shard_rows, room)
    notes = jnp.tile(notes, (copies, 1))
    if paired:
        keep_turns = (0, 4, 2, 6)
        (distant,) = run_weights(2, 2, ((width, (0,)),), place, notes, *sources)
        plans = tuple((shard_rows, tuple(turn | flip for turn in keep_turns)) for flip in (0, 1))
        keep, send = run_weights(0, 2, plans, place, notes, *sources)
        keep, send = (value.reshape((4, 2) + value.shape[1:]) for value in (keep, send))
        distant = lax.psum_scatter(distant, "dp", scatter_dimension=1, tiled=True)
        came = swap(send, "dp", 1)
    else:
        (packed,) = run_weights(0, parts, ((width, (0,)),), place, notes, *sources)
        packed = lax.psum_scatter(packed, "dp", scatter_dimension=1, tiled=True)

    joined_grad, sums = run_backward(
        (1, 0), lane, bounds, qkv, seg_col, seg_row, context, head_grad, lse, [], []
    )
    joined_grad = joined_grad.reshape(seq_len, -1)
    attn_back = dot(joined_grad, w_heads, NT).astype(BF16)
    if paired:
        came = after(came, attn_back)
    attn_back, sums, joined_grad = lax.optimization_barrier((attn_back, sums, joined_grad))
    attn_back = lax.psum_scatter(attn_back, "tensor", scatter_dimension=0, tiled=True)
    if paired:
        keep, send = add_halves(keep, came)
        keep, send, joined_grad = lax.optimization_barrier((keep, send, joined_grad))
        came = swap(send, "dp", 2)
    head_weights = dot(tokens, joined_grad, TN).reshape((copies, shard_rows, -1))
    if paired:
        came, head_weights = lax.optimization_barrier((came, head_weights))
        keep, send = add_halves(keep, came)
        keep, send, head_weights = lax.optimization_barrier((keep, send, head_weights))
        came = swap(send, "dp", 4)
    sums = sums.reshape(heads, 4, DH)
    sums = jnp.concatenate((sums[:, 0].reshape(1, head_cols), sums[:, 3].reshape(1, head_cols)), axis=1)
    for bit in bits_of("tensor"):
        sums = merge(sums, swap(sums, "tensor", bit), "tensor", bit)
    if paired:
        came, head_weights = lax.optimization_barrier((came, head_weights))
        slots = jnp.concatenate([add_low(keep, came)[0], distant], axis=0)
        packed = jnp.stack(
            [lax.dynamic_index_in_dim(slots, rank ^ t, 0, keepdims=False) for t in range(parts)]
        )
    packed = lax.psum_scatter(packed, "tensor", scatter_dimension=0, tiled=True)[0]
    biases = jnp.concatenate((sums[:, :head_cols].reshape(-1), sums[:, head_cols:].reshape(-1)))
    biases = jnp.pad(
        biases.reshape(8, heads, 1, DH), ((0, shard_rows - 8), (0, 0), (1, 2), (0, 0))
    ).reshape(1, shard_rows, -1)
    query_grad, key_grad, value_grad, biases = run_finish_heads(
        scatter_rows((head_weights + biases).astype(BF16))
    )
    biases = biases.reshape(2, width)
    input_grad = first_grad + attn_back.astype(F32)

    inner_grad, outer_grad, output_grad, notes = run_finish_dense(packed, hidden_cols, head_cols)
    notes = notes.reshape(-1)

    def total(which):
        return notes[which * width : (which + 1) * width]

    mse_loss = jnp.sum(total(0)) / (counted * width)
    return (
        layer_out.reshape(1, part_len, width),
        mse_loss,
        input_grad.reshape(1, part_len, width),
        query_grad,
        key_grad,
        value_grad,
        output_grad,
        inner_grad,
        outer_grad.T,
        biases[0],
        biases[1],
        total(4),
        notes[8 * width : 8 * width + hidden_cols * parts],
        total(1),
        total(5),
        total(6),
        total(2),
        total(3),
    )


def solution(mesh):
    shard = P("dp", "tensor", None)
    by_dp, by_tensor = P("dp", "tensor"), P("tensor", "dp")
    in_specs = (
        (shard, P("dp", None), by_dp, shard, shard)
        + (by_dp,) * 3
        + (by_tensor, by_dp, by_tensor)
        + (P(),) * 9
    )
    out_specs = (shard, P(), shard) + (by_dp,) * 3 + (by_tensor, by_dp, by_tensor) + (P(),) * 9
    return jax.shard_map(local, mesh=mesh, in_specs=in_specs, out_specs=out_specs, check_vma=False)
```

```python
import functools

import jax
import jax.numpy as jnp
from jax import lax
from jax.experimental import pallas as pl
from jax.experimental.pallas import tpu as pltpu
from jax.sharding import PartitionSpec as P

DH = 64
BLOCK = 256
SLAB = 4 * DH
EPSILON = 1e-12
ROOT_HALF = 0.7071067811865476
INV_ROOT_TAU = 0.3989422804014327
LOG2E = 1.4426950408889634
LN2 = 0.6931471805599453
SCALE = DH ** (-0.5)
MASKED = -1e30
VMEM_LIMIT = 60 << 20

BF16 = jnp.bfloat16
F32 = jnp.float32
NN = (((1,), (0,)), ((), ()))
NT = (((1,), (1,)), ((), ()))
TN = (((0,), (0,)), ((), ()))


def dot(left_side, right_side, dims=NN):
    return lax.dot_general(left_side, right_side, dims, preferred_element_type=F32)


def norm_forward(summed, gain_vec, shift_vec):
    average = jnp.mean(summed, axis=-1, keepdims=True)
    centered = summed - average
    variance = jnp.mean(centered * centered, axis=-1, keepdims=True)
    inverse = lax.rsqrt(variance + EPSILON)
    normed = centered * inverse
    return (normed * gain_vec + shift_vec, normed, inverse)


def norm_backward(upstream, normed, inverse, gain_vec):
    scaled = upstream * gain_vec
    first_mean = jnp.mean(scaled, axis=-1, keepdims=True)
    second_mean = jnp.mean(scaled * normed, axis=-1, keepdims=True)
    return inverse * (scaled - first_mean - normed * second_mean)


def column_sum(value):
    return jnp.sum(value, axis=0, keepdims=True)


def lane_is_right(rows):
    return lax.broadcasted_iota(jnp.int32, (rows, 2 * DH), 1) >= DH


def pack(first_two, third_top, third_bottom):
    return jnp.concatenate([first_two, jnp.concatenate([third_top, third_bottom], axis=1)], axis=0)


def unpack(packed):
    third = packed[BLOCK:]
    third = jnp.concatenate([third[:, :DH], third[:, DH:]], axis=0)
    return jnp.concatenate([packed[:BLOCK], third], axis=1)


def fetch_chunks(lane_ref, chunk_refs, target, sems):
    rows = chunk_refs[0].shape[0]
    copies = []
    for at, chunk in enumerate(chunk_refs):
        offset = pl.multiple_of(lax.rem(lane_ref[0] + at, len(chunk_refs)) * rows, rows)
        copies.append(pltpu.make_async_copy(chunk, target.at[pl.ds(offset, rows), :], sems.at[at]))
    return copies


def attend_forward(
    first_block, lane_ref, low_ref, count_ref, *refs
):
    chunk_refs, (seg_col_ref, seg_row_ref, ctx_ref, lse_ref, held, qkv_ref, sems) = refs[:-7], refs[-7:]
    heads = lse_ref.shape[0]

    @pl.when(pl.program_id(0) == 0)
    def _():
        copies = fetch_chunks(lane_ref, chunk_refs, qkv_ref, sems)
        for copy in copies:
            copy.start()
        for copy in copies:
            copy.wait()

    qb = pl.program_id(0) + first_block
    rows = pl.ds(pl.multiple_of(qb * BLOCK, BLOCK), BLOCK)
    seg_q = seg_col_ref[...]
    queries = [
        qkv_ref[rows, SLAB * h : SLAB * h + 2 * DH] * jnp.asarray(SCALE, BF16) for h in range(heads)
    ]
    low, count = low_ref[qb], count_ref[qb]

    def score(kb, peaks):
        keys = pl.ds(pl.multiple_of(low * STEP + kb * BLOCK, STEP), BLOCK)
        allowed = seg_q == seg_row_ref[:, keys]
        found = []
        for h in range(heads):
            scores = dot(queries[h], qkv_ref[keys, SLAB * h + 2 * DH : SLAB * (h + 1)], NT)
            scores = jnp.where(allowed, scores, MASKED)
            held[h, kb] = scores
            found.append(jnp.maximum(peaks[h], jnp.maximum(scores[:, :128], scores[:, 128:])))
        return tuple(found)

    start = tuple(jnp.full((BLOCK, 128), MASKED, F32) for _ in range(heads))
    peaks = lax.fori_loop(0, count, score, start)
    highest = [jnp.max(peak, axis=-1, keepdims=True) for peak in peaks]

    def weigh(kb, carry):
        keys = pl.ds(pl.multiple_of(low * STEP + kb * BLOCK, STEP), BLOCK)
        found = []
        for h in range(heads):
            total, acc = carry[h]
            raised = jnp.exp2((held[h, kb] - highest[h]) * LOG2E)
            total = total + (raised[:, :128] + raised[:, 128:])
            acc = acc + dot(raised.astype(BF16), qkv_ref[keys, SLAB * h + 2 * DH : SLAB * (h + 1)])
            found.append((total, acc))
        return tuple(found)

    zero = jnp.zeros((BLOCK, 128), F32)
    done = lax.fori_loop(0, count, weigh, tuple((zero, zero) for _ in range(heads)))
    values = []
    for h in range(heads):
        total, acc = done[h]
        summed = jnp.sum(total, axis=-1, keepdims=True)
        values.append((acc / summed).astype(BF16))
        lse_ref[h] = jnp.transpose(highest[h] + jnp.log(summed))
    middle = BLOCK // 2
    ctx_ref[0, :BLOCK, :] = jnp.where(lane_is_right(BLOCK), values[1], pltpu.roll(values[0], DH, 1))
    ctx_ref[0, BLOCK:, :] = jnp.where(
        lane_is_right(middle), values[2][middle:], pltpu.roll(values[2][:middle], DH, 1)
    )


def attend_backward(which, chunks, lane_ref, low_ref, count_ref, *refs):
    halves, half = which
    last = half == halves - 1
    chunk_refs, refs = refs[:chunks], refs[chunks:]
    (seg_col_ref, seg_row_ref, ctx_ref, grad_ref, lse_ref), refs = refs[:5], refs[5:]
    earlier, refs = refs[:half], refs[half:]
    if half > 0:
        before_ref, refs = refs[0], refs[1:]
    if last:
        final_ref, sums_ref, dkv, out_ref, qkv_ref, sems = refs
    else:
        dkv, query_ref, qkv_ref, sems = refs
    heads = dkv.shape[0]
    step_index = pl.program_id(0)
    qb = step_index * halves + half

    @pl.when(step_index == 0)
    def _():
        copies = fetch_chunks(lane_ref, chunk_refs, qkv_ref, sems)
        for copy in copies:
            copy.start()
        dkv[...] = before_ref[...] if half > 0 else jnp.zeros_like(dkv)
        for copy in copies:
            copy.wait()

    rows = pl.ds(pl.multiple_of(qb * BLOCK, BLOCK), BLOCK)
    right = lane_is_right(BLOCK)
    arrived = grad_ref[0]
    product = arrived.astype(F32) * ctx_ref[0].astype(F32)
    upper = product.astype(BF16)
    lower = (product - upper.astype(F32)).astype(BF16)
    pick = (
        lax.broadcasted_iota(jnp.int32, (8, 2 * DH), 1) // DH
        == lax.broadcasted_iota(jnp.int32, (8, 2 * DH), 0)
    ).astype(BF16)
    summed = dot(pick, upper, NT) + dot(pick, lower, NT)
    deltas = [
        summed[0:1, :BLOCK],
        summed[1:2, :BLOCK],
        jnp.concatenate([summed[0:1, BLOCK:], summed[1:2, BLOCK:]], axis=1),
    ]
    two, third = arrived[:BLOCK], arrived[BLOCK:]
    placed = [
        pltpu.roll(two, DH, 1),
        two,
        jnp.concatenate([pltpu.roll(third, DH, 1), third], axis=0),
    ]
    grads = [jnp.where(right, grad, jnp.zeros_like(grad)) for grad in placed]
    queries, pairs = [], []
    for h in range(heads):
        queries.append(qkv_ref[rows, SLAB * h : SLAB * h + 2 * DH] * jnp.asarray(SCALE, BF16))
        pairs.append(jnp.concatenate([queries[h], grads[h]], axis=0))
    seg_q = seg_row_ref[...]
    lses = lse_ref[...]
    low, count = low_ref[qb], count_ref[qb]

    def step(kb, accs):
        keys = pl.ds(pl.multiple_of(low * STEP + kb * BLOCK, STEP), BLOCK)
        allowed = seg_col_ref[keys, :] == seg_q
        keyed = [qkv_ref[keys, SLAB * h + 2 * DH : SLAB * (h + 1)] for h in range(heads)]
        raw = [dot(keyed[h], queries[h], NT) for h in range(heads)]
        probs_grads = [dot(keyed[h], grads[h], NT) for h in range(heads)]
        both = []
        for h in range(heads):
            probs = jnp.exp2((jnp.where(allowed, raw[h], MASKED) - lses[h]) * LOG2E)
            score_grad = (probs * (probs_grads[h] - deltas[h])).astype(BF16)
            both.append((score_grad, probs.astype(BF16)))
        found = []
        for h in range(heads):
            dkv[h, keys, :] += dot(jnp.concatenate(both[h], axis=1), pairs[h])
            found.append(accs[h] + dot(both[h][0], keyed[h], TN))
        return tuple(found)

    zero = jnp.zeros((BLOCK, 128), F32)
    accs = lax.fori_loop(0, count, step, tuple(zero for _ in range(heads)))
    for h in range(heads):
        query_grad = jnp.where(right, 0.0, accs[h] * SCALE).astype(BF16)
        if last:
            out_ref[rows, SLAB * h : SLAB * h + 2 * DH] = query_grad
        else:
            query_ref[0, :, 2 * DH * h : 2 * DH * (h + 1)] = query_grad

    if last:

        @pl.when(step_index == pl.num_programs(0) - 1)
        def _():
            for h in range(heads):
                at = SLAB * h
                for other, ref in enumerate(earlier):
                    for block in range(ref.shape[0]):
                        start = (block * halves + other) * BLOCK
                        out_ref[start : start + BLOCK, at : at + 2 * DH] = ref[
                            block, :, 2 * DH * h : 2 * DH * (h + 1)
                        ]
                out_ref[:, at + 2 * DH : at + SLAB] = dkv[h].astype(BF16)
                sums_ref[:, at : at + SLAB] = column_sum(out_ref[:, at : at + SLAB].astype(F32))
            rows_each = final_ref.shape[1]
            copies = []
            for at in range(final_ref.shape[0]):
                offset = pl.multiple_of(lax.rem(lane_ref[0] + at, final_ref.shape[0]) * rows_each, rows_each)
                copies.append(
                    pltpu.make_async_copy(
                        out_ref.at[pl.ds(offset, rows_each), :], final_ref.at[at], sems.at[at]
                    )
                )
            for copy in copies:
                copy.start()
            for copy in copies:
                copy.wait()


STEP = 128


def document_blocks(segment_row):
    starts = segment_row[::BLOCK]
    stops = segment_row[BLOCK - 1 :: BLOCK]
    low = jnp.sum((segment_row[None, :] < starts[:, None]).astype(jnp.int32), axis=1) // STEP
    high = jnp.sum((segment_row[None, :] <= stops[:, None]).astype(jnp.int32), axis=1)
    each = BLOCK // STEP
    count = (high - low * STEP + BLOCK - 1) // BLOCK
    return (jnp.minimum(low, segment_row.shape[0] // STEP - each * count), count)


PACKED = BLOCK + BLOCK // 2


def run_forward(first_block, steps, lane, bounds, qkv, seg_col, seg_row):
    seq_len, width = seg_col.shape[0], qkv[0].shape[1]
    heads = width // SLAB
    blocks = seq_len // BLOCK
    return pl.pallas_call(
        functools.partial(attend_forward, first_block),
        out_shape=(
            jax.ShapeDtypeStruct((steps, PACKED, 2 * DH), BF16),
            jax.ShapeDtypeStruct((heads, 1, steps * BLOCK), F32),
        ),
        grid_spec=pltpu.PrefetchScalarGridSpec(
            num_scalar_prefetch=3,
            grid=(steps,),
            in_specs=[pl.BlockSpec(memory_space=pl.ANY)] * len(qkv)
            + [
                pl.BlockSpec((BLOCK, 1), lambda q, *_: (q + first_block, 0)),
                pl.BlockSpec((1, seq_len), lambda q, *_: (0, 0)),
            ],
            out_specs=(
                pl.BlockSpec((1, PACKED, 2 * DH), lambda q, *_: (q, 0, 0)),
                pl.BlockSpec((heads, 1, BLOCK), lambda q, *_: (0, 0, q)),
            ),
            scratch_shapes=[
                pltpu.VMEM((heads, blocks, BLOCK, BLOCK), F32),
                pltpu.VMEM((seq_len, width), BF16),
                pltpu.SemaphoreType.DMA((len(qkv),)),
            ],
        ),
        compiler_params=pltpu.CompilerParams(
            dimension_semantics=("arbitrary",), vmem_limit_bytes=VMEM_LIMIT
        ),
        cost_estimate=pl.CostEstimate(
            flops=heads * seq_len * seq_len * 2048 * steps // blocks,
            bytes_accessed=5 << 20,
            transcendentals=heads * seq_len * seq_len // 3,
        ),
        name="attend_forward",
    )(lane, *bounds, *qkv, seg_col, seg_row)


def run_backward(which, lane, bounds, qkv, seg_col, seg_row, ctx, grad, lse, earlier, before):
    halves, half = which
    seq_len, width = seg_col.shape[0], qkv[0].shape[1]
    heads = width // SLAB
    steps = seq_len // BLOCK // halves
    packed = pl.BlockSpec((1, PACKED, 2 * DH), lambda q, *_: (q, 0, 0))

    def fixed(shape, **more):
        return pl.BlockSpec(shape, lambda q, *_: (0,) * len(shape), **more)

    once = {"pipeline_mode": pl.Buffered(1)}
    gathered = (heads, seq_len, 2 * DH)
    carried = [fixed(value.shape, **once) for value in earlier]
    carried += [fixed(gathered, **once)] * len(before)
    scratch = [pltpu.VMEM((seq_len, width), BF16), pltpu.SemaphoreType.DMA((len(qkv),))]
    if half == halves - 1:
        out_shape = (
            jax.ShapeDtypeStruct((len(qkv), seq_len // len(qkv), width), BF16),
            jax.ShapeDtypeStruct((1, width), F32),
        )
        out_specs = (pl.BlockSpec(memory_space=pl.ANY), fixed((1, width)))
        scratch = [pltpu.VMEM(gathered, F32), pltpu.VMEM((seq_len, width), BF16)] + scratch
    else:
        out_shape = (
            jax.ShapeDtypeStruct(gathered, F32),
            jax.ShapeDtypeStruct((steps, BLOCK, heads * 2 * DH), BF16),
        )
        out_specs = (
            fixed(gathered),
            pl.BlockSpec((1, BLOCK, heads * 2 * DH), lambda q, *_: (q, 0, 0)),
        )
    return pl.pallas_call(
        functools.partial(attend_backward, which, len(qkv)),
        out_shape=out_shape,
        grid_spec=pltpu.PrefetchScalarGridSpec(
            num_scalar_prefetch=3,
            grid=(steps,),
            in_specs=[pl.BlockSpec(memory_space=pl.ANY)] * len(qkv)
            + [
                fixed((seq_len, 1)),
                pl.BlockSpec((1, BLOCK), lambda q, *_: (0, q * halves + half)),
                packed,
                packed,
                pl.BlockSpec((heads, 1, BLOCK), lambda q, *_: (0, 0, q)),
            ]
            + carried,
            out_specs=out_specs,
            scratch_shapes=scratch,
        ),
        compiler_params=pltpu.CompilerParams(
            dimension_semantics=("arbitrary",), vmem_limit_bytes=VMEM_LIMIT
        ),
        cost_estimate=pl.CostEstimate(
            flops=heads * seq_len * seq_len * 4096,
            bytes_accessed=10 << 20,
            transcendentals=heads * seq_len * seq_len // 3 // halves,
        ),
        name="attend_backward",
    )(lane, *bounds, *qkv, seg_col, seg_row, ctx, grad, lse, *earlier, *before)


def dense_chain(
    marks, total_tokens, place_ref, ctx_ref, in_ref, teacher_ref, cotangent_ref, valid_ref, vec_ref,
    inner_bias_ref, *refs
):
    pieces = refs[: len(marks)]
    (
        layer_ref, first_grad_ref, ctx_grad_ref, first_ref, branch_grad_ref, attn_grad_ref,
        act_ref, hidden_grad_ref, notes_ref, w_out, w_in, w_up, slope, sums_ref, inner_sums_ref,
        gathered, sems,
    ) = refs[len(marks) :]
    parts, _, head_cols = w_out.shape
    hidden_cols = w_in.shape[2]
    index = place_ref[parts]
    step = pl.program_id(0)
    groups = (
        (2 * hidden_cols, head_cols, w_out),
        (0, hidden_cols, w_in),
        (hidden_cols, hidden_cols, w_up),
    )

    @pl.when(step == 0)
    def _():
        for group, (start, size, target) in enumerate(groups):
            for piece, marked in zip(pieces, marks):
                block = piece.shape[1]
                for at, (slot, turn, relative) in enumerate(marked):
                    offset = pl.multiple_of((index ^ turn) * block, block) if relative else turn * block
                    pltpu.make_async_copy(
                        piece.at[at, :, pl.ds(start, size)],
                        target.at[slot, pl.ds(offset, block), :],
                        sems.at[group, slot],
                    ).start()
        sums_ref[...] = jnp.zeros_like(sums_ref)
        inner_sums_ref[...] = jnp.zeros_like(inner_sums_ref)

    def arrive(group, slot):
        whole = groups[group][2].at[slot]

        @pl.when(step == 0)
        def _():
            pltpu.make_async_copy(whole, whole, sems.at[group, slot]).wait()

    def vec(which):
        return vec_ref[which : which + 1, :]

    counts = jnp.zeros((1, 2 * DH), F32)

    attention = jnp.zeros(in_ref.shape, F32)
    for slot in range(parts):
        arrive(0, slot)
        counts = counts + column_sum(w_out[slot, :, 2 * DH :].astype(F32))
        attention = attention + dot(unpack(ctx_ref[place_ref[slot], 0]), w_out[slot, :, : 3 * DH], NT)
    first_exact, normed_one, inverse_one = norm_forward(
        in_ref[...].astype(F32) + attention + vec(0), vec(1), vec(2)
    )
    first = first_exact.astype(BF16)
    first_ref[...] = first

    def up(slot, branch):
        t = place_ref[slot]
        arrive(1, slot)
        hidden = dot(first, w_in[slot]) + inner_bias_ref[t]
        bend = 0.5 * (1.0 + lax.erf(hidden * ROOT_HALF))
        activated = (hidden * bend).astype(BF16)
        act_ref[t] = activated
        slope[slot] = bend + hidden * INV_ROOT_TAU * jnp.exp2(hidden * hidden * (-0.5 * LOG2E))
        arrive(2, slot)
        return branch + dot(activated, w_up[slot], NT)

    branch = jnp.zeros(in_ref.shape, F32)
    for slot in range(parts):
        branch = up(slot, branch)
    lanes = lax.broadcasted_iota(jnp.int32, counts.shape, 1)
    weight = jnp.where(lanes == DH, 256.0, jnp.where(lanes == DH + 1, 1.0, 0.0))
    ratio = total_tokens / jnp.sum(jnp.where(weight > 0.0, counts, 0.0) * weight, axis=-1, keepdims=True)
    layer_rows, normed_two, inverse_two = norm_forward(first.astype(F32) + branch + vec(3), vec(4), vec(5))
    layer_ref[...] = layer_rows.astype(BF16)
    misfit = layer_rows - teacher_ref[...].astype(F32)
    weighted = valid_ref[...] * misfit
    out_grad = cotangent_ref[...].astype(F32) + weighted * ratio
    second_grad = norm_backward(out_grad, normed_two, inverse_two, vec(4))
    branch_grad = second_grad.astype(BF16)
    branch_grad_ref[...] = branch_grad
    sums_ref[0:1, :] += column_sum(weighted * misfit)
    sums_ref[1:2, :] += column_sum(branch_grad.astype(F32))
    sums_ref[2:3, :] += column_sum(out_grad * normed_two)
    sums_ref[3:4, :] += column_sum(out_grad)

    def down(slot, back):
        t = place_ref[slot]
        hidden_grad = (dot(branch_grad, w_up[slot]) * slope[slot]).astype(BF16)
        hidden_grad_ref[t] = hidden_grad
        inner_sums_ref[t] += column_sum(hidden_grad.astype(F32))
        return back + dot(hidden_grad, w_in[slot], NT)

    upstream = second_grad
    for slot in range(parts):
        upstream = down(slot, upstream)
    first_grad = norm_backward(upstream, normed_one, inverse_one, vec(1))
    first_grad_ref[...] = first_grad
    attn_grad = first_grad.astype(BF16)
    attn_grad_ref[...] = attn_grad
    sums_ref[4:5, :] += column_sum(attn_grad.astype(F32))
    sums_ref[5:6, :] += column_sum(upstream * normed_one)
    sums_ref[6:7, :] += column_sum(upstream)
    middle = BLOCK // 2
    for slot in range(parts):
        back = dot(attn_grad, w_out[slot, :, : 3 * DH]).astype(BF16)
        ctx_grad_ref[place_ref[slot], 0] = pack(
            back[:, : 2 * DH], back[:middle, 2 * DH :], back[middle:, 2 * DH :]
        )


    @pl.when(step == pl.num_programs(0) - 1)
    def _():
        lanes = 2 * DH
        gathered[...] = jnp.zeros_like(gathered)
        rows_each, inner_rows = width_of(sums_ref) // lanes, width_of(inner_sums_ref) // lanes
        per_note = gathered.shape[1] // lanes

        def put(at, value):
            gathered[at // per_note : at // per_note + 1, pl.ds(at % per_note * lanes, lanes)] = value

        for row in range(sums_ref.shape[0]):
            for k in range(rows_each):
                put(row * rows_each + k, sums_ref[row : row + 1, k * lanes : (k + 1) * lanes])
        for t in range(parts):
            for k in range(inner_rows):
                put(
                    sums_ref.shape[0] * rows_each + t * inner_rows + k,
                    inner_sums_ref[t, :, k * lanes : (k + 1) * lanes],
                )
        notes_ref[...] = gathered[...].astype(BF16)


def width_of(ref):
    return ref.shape[-1]


def run_dense(note_rows, marks, total_tokens, place, ctx, rows_in, teacher, cotangent, valid, vecs, inner_bias, pieces):
    parts, halves = ctx.shape[:2]
    part_len, width = rows_in.shape
    hidden_cols = inner_bias.shape[2]
    out_cols = pieces[0].shape[2] - 2 * hidden_cols
    room = -(-(8 * width + parts * hidden_cols) // (note_rows * 2 * DH)) * 2 * DH

    def by_rows(columns):
        return pl.BlockSpec((BLOCK, columns), lambda i: (i, 0))

    def by_part(columns):
        return pl.BlockSpec((parts, BLOCK, columns), lambda i: (0, i, 0))

    def fixed(shape):
        return pl.BlockSpec(shape, lambda i: (0,) * len(shape))

    packed = pl.BlockSpec((parts, 1) + ctx.shape[2:], lambda i: (0, i, 0, 0))
    low = jax.ShapeDtypeStruct((part_len, width), BF16)
    wide = jax.ShapeDtypeStruct((parts, part_len, hidden_cols), BF16)
    smem = pl.BlockSpec(memory_space=pltpu.SMEM)
    return pl.pallas_call(
        functools.partial(dense_chain, marks, total_tokens),
        out_shape=(
            low,
            jax.ShapeDtypeStruct((part_len, width), F32),
            jax.ShapeDtypeStruct(ctx.shape, BF16),
            low,
            low,
            low,
            wide,
            wide,
            jax.ShapeDtypeStruct((note_rows, room), BF16),
        ),
        grid=(halves,),
        in_specs=[
            smem,
            packed,
            by_rows(width),
            by_rows(width),
            by_rows(width),
            by_rows(1),
            fixed(vecs.shape),
            fixed(inner_bias.shape),
        ]
        + [pl.BlockSpec(memory_space=pl.ANY)] * len(pieces),
        out_specs=(
            by_rows(width),
            by_rows(width),
            packed,
            by_rows(width),
            by_rows(width),
            by_rows(width),
            by_part(hidden_cols),
            by_part(hidden_cols),
            fixed((note_rows, room)),
        ),
        scratch_shapes=[
            pltpu.VMEM((parts, width, out_cols), BF16),
            pltpu.VMEM((parts, width, hidden_cols), BF16),
            pltpu.VMEM((parts, width, hidden_cols), BF16),
            pltpu.VMEM((parts, BLOCK, hidden_cols), F32),
            pltpu.VMEM((8, width), F32),
            pltpu.VMEM((parts, 1, hidden_cols), F32),
            pltpu.VMEM((note_rows, room), F32),
            pltpu.SemaphoreType.DMA((3, parts)),
        ],
        compiler_params=pltpu.CompilerParams(
            dimension_semantics=("arbitrary",), vmem_limit_bytes=VMEM_LIMIT
        ),
        cost_estimate=pl.CostEstimate(
            flops=2 * part_len * width * (8 * hidden_cols + 4 * out_cols) * parts,
            bytes_accessed=24 << 20,
            transcendentals=2 * part_len * hidden_cols * parts,
        ),
        name="dense_chain",
    )(place, ctx, rows_in, teacher, cotangent, valid, vecs, inner_bias, *pieces)


def dense_weights(
    plans, place_ref, first_ref, branch_grad_ref, attn_grad_ref, act_ref, hidden_grad_ref, ctx_ref,
    notes_ref, *refs
):
    outs, (whole, sems) = refs[:-2], refs[-2:]
    step = pl.program_id(0)
    slots = whole.shape[0]

    hidden_cols = act_ref.shape[2]
    whole[step, :, :hidden_cols] = dot(first_ref[...], hidden_grad_ref[0], TN).astype(BF16)
    whole[step, :, hidden_cols : 2 * hidden_cols] = dot(branch_grad_ref[...], act_ref[0], TN).astype(BF16)
    ctx = jnp.concatenate([unpack(ctx_ref[0, half]) for half in range(ctx_ref.shape[1])], axis=0)
    plain = 2 * hidden_cols + ctx.shape[1]
    whole[step, :, 2 * hidden_cols : plain] = dot(attn_grad_ref[...], ctx, TN).astype(BF16)
    whole[step, :, plain : plain + notes_ref.shape[1]] = notes_ref[...]
    for out, turns in zip(outs, plans):
        block = out.shape[1]
        for at, turn in enumerate(turns):
            offset = 0
            if block < whole.shape[1]:
                offset = pl.multiple_of((place_ref[place_ref.shape[0] - 1] ^ turn) * block, block)
            pltpu.make_async_copy(
                whole.at[step, pl.ds(offset, block), :], out.at[at * slots + step], sems.at[step]
            ).start()

    @pl.when(step == slots - 1)
    def _():
        for slot in range(slots):
            pltpu.make_async_copy(whole.at[slot], whole.at[slot], sems.at[slot]).wait()


def run_weights(base, slots, plans, place, notes, first, branch_grad, attn_grad, act, hidden_grad, ctx):
    _, part_len, hidden_cols = act.shape
    width = first.shape[1]
    columns = 2 * hidden_cols + 3 * DH + notes.shape[1]
    fixed = pl.BlockSpec((part_len, width), lambda s, place: (0, 0))
    by_slot = pl.BlockSpec((1, part_len, hidden_cols), lambda s, place: (place[base + s], 0, 0))
    outs = tuple(
        jax.ShapeDtypeStruct((len(turns) * slots, block, columns), BF16) for block, turns in plans
    )
    return pl.pallas_call(
        functools.partial(dense_weights, tuple(turns for _, turns in plans)),
        out_shape=outs,
        grid_spec=pltpu.PrefetchScalarGridSpec(
            num_scalar_prefetch=1,
            grid=(slots,),
            in_specs=[
                fixed,
                fixed,
                fixed,
                by_slot,
                by_slot,
                pl.BlockSpec((1,) + ctx.shape[1:], lambda s, place: (place[base + s], 0, 0, 0)),
                pl.BlockSpec(notes.shape, lambda s, place: (0, 0)),
            ],
            out_specs=tuple(pl.BlockSpec(memory_space=pl.ANY) for _ in outs),
            scratch_shapes=[
                pltpu.VMEM((slots, width, columns), BF16),
                pltpu.SemaphoreType.DMA((slots,)),
            ],
        ),
        compiler_params=pltpu.CompilerParams(
            dimension_semantics=("arbitrary",), vmem_limit_bytes=VMEM_LIMIT
        ),
        cost_estimate=pl.CostEstimate(
            flops=2 * part_len * width * columns * slots,
            bytes_accessed=5 * slots << 20,
            transcendentals=0,
        ),
        name="dense_weights",
    )(place, first, branch_grad, attn_grad, act, hidden_grad, ctx, notes)


def finish_dense(packed_ref, inner_ref, outer_ref, output_ref, notes_ref):
    hidden_cols = inner_ref.shape[1]
    summed = packed_ref[...].astype(F32)
    inner_ref[...] = summed[:, :hidden_cols]
    outer_ref[...] = summed[:, hidden_cols : 2 * hidden_cols]
    plain = 2 * hidden_cols + output_ref.shape[0]
    output_ref[...] = jnp.transpose(summed[:, 2 * hidden_cols : plain])
    notes_ref[...] = summed[:, plain:]


def run_finish_dense(packed, hidden_cols, head_cols):
    rows = packed.shape[0]
    return pl.pallas_call(
        finish_dense,
        out_shape=(
            jax.ShapeDtypeStruct((rows, hidden_cols), F32),
            jax.ShapeDtypeStruct((rows, hidden_cols), F32),
            jax.ShapeDtypeStruct((head_cols, rows), F32),
            jax.ShapeDtypeStruct((rows, packed.shape[1] - 2 * hidden_cols - head_cols), F32),
        ),
        name="finish_dense",
    )(packed)


def finish_heads(value_ref, *refs):
    summed = value_ref[...].astype(F32)
    heads = summed.shape[1] // SLAB
    for ref, which in zip(refs, (0, 2, 3, 1)):
        columns = [summed[:, SLAB * h + which * DH : SLAB * h + (which + 1) * DH] for h in range(heads)]
        ref[...] = jnp.concatenate(columns, axis=1)[: ref.shape[0]]


def run_finish_heads(value):
    rows, width = value.shape
    out = jax.ShapeDtypeStruct((rows, width // 4), F32)
    notes = jax.ShapeDtypeStruct((8, width // 4), F32)
    return pl.pallas_call(finish_heads, out_shape=(out, out, out, notes), name="finish_heads")(value)


def interleave(query, key, value, heads):
    rows = query.shape[0]
    parts = [part.reshape(rows, heads, 1, DH) for part in (query, jnp.zeros_like(query), key, value)]
    return jnp.concatenate(parts, axis=2).reshape(rows, heads * SLAB)


def swap(value, axis, bit):
    size = lax.axis_size(axis)
    return lax.ppermute(value, axis, [(i, i ^ bit) for i in range(size)])


def bits_of(axis):
    bit = 1
    while bit < lax.axis_size(axis):
        yield bit
        bit *= 2


def after(value, *others):
    return lax.optimization_barrier((value,) + others)[0]


def merge(held, other, axis, bit):
    mine_first = (lax.axis_index(axis) & bit) == 0
    return jnp.where(
        mine_first, jnp.concatenate([held, other], axis=0), jnp.concatenate([other, held], axis=0)
    )


def add_low(left_side, right_side):
    return (left_side.astype(F32) + right_side.astype(F32)).astype(BF16)


def add_halves(left_side, right_side):
    half = left_side.shape[0] // 2
    return (
        add_low(left_side[:half], right_side[:half]),
        add_low(left_side[half:], right_side[half:]),
    )


def scatter_rows(held):
    index = lax.axis_index("dp")
    for bit in bits_of("dp"):
        held = held.reshape((held.shape[0] // 2, 2) + held.shape[1:])
        own = (index & bit) // bit
        send = lax.dynamic_index_in_dim(held, 1 - own, 1, keepdims=False)
        keep = lax.dynamic_index_in_dim(held, own, 1, keepdims=False)
        held = add_low(keep, swap(send, "dp", bit))
    return held[0]


def local(
    inputs, segment_ids, valid_mask, teacher, cotangent,
    w_query, w_key, w_value, w_output, w_inner, w_outer,
    query_bias, value_bias, output_bias, inner_bias, outer_bias,
    gain_attn, shift_attn, gain_ffn, shift_ffn,
):
    _, part_len, width = inputs.shape
    parts = lax.axis_size("tensor")
    copies = lax.axis_size("dp")
    rank = lax.axis_index("tensor")
    total_tokens = part_len * parts * copies
    seq_len = part_len * parts
    head_cols = w_query.shape[1]
    heads = head_cols // DH
    hidden_cols = w_inner.shape[1]
    shard_rows = w_inner.shape[0]
    halves = part_len // BLOCK

    rows_in = inputs.reshape(part_len, width)
    tokens = lax.all_gather(rows_in, "tensor", axis=0, tiled=True)
    w_heads = interleave(w_query, w_key, w_value, heads)
    paired = shard_rows % 16 == 0 and parts == 4 and copies == 8

    valid_rows = valid_mask.astype(F32).reshape(part_len, 1)
    valid_count = jnp.sum(valid_mask.astype(F32))
    upper = jnp.floor(valid_count / 256.0)
    spot = lax.broadcasted_iota(jnp.int32, (shard_rows, DH), 0) * DH + lax.broadcasted_iota(
        jnp.int32, (shard_rows, DH), 1
    )
    count_row = jnp.where(spot == 0, upper, jnp.where(spot == 1, valid_count - 256.0 * upper, 0.0))
    mine = jnp.concatenate((w_inner, w_outer.T, w_output.T, count_row.astype(BF16)), axis=1)
    if paired:
        place = jnp.stack([rank, rank ^ 1, rank ^ 2, rank ^ 3, lax.axis_index("dp")]).astype(jnp.int32)
        pair = jnp.concatenate([mine[None], swap(mine[None], "tensor", 1)], axis=0)
        near = jnp.concatenate([pair, swap(pair, "dp", 2)], axis=0)
        turns = [0, 2, 4, 6]
        for bit in (1, 2, 4):
            w_heads = merge(w_heads, swap(w_heads, "dp", bit), "dp", bit)
        near, w_heads = lax.optimization_barrier((near, w_heads))
        near_next = swap(near, "dp", 4)
        tokens, pair, near_next = lax.optimization_barrier((tokens, pair, near_next))
        far = swap(pair, "tensor", 2)
    else:
        place = jnp.asarray(list(range(parts)) + [0], jnp.int32)
        weights = lax.all_gather(mine, ("tensor", "dp"), axis=0, tiled=False)
        for bit in bits_of("dp"):
            w_heads = merge(w_heads, swap(w_heads, "dp", bit), "dp", bit)

    mine_cols = rank * head_cols
    query_shift = lax.dynamic_slice_in_dim(query_bias, mine_cols, head_cols).astype(F32)
    value_shift = lax.dynamic_slice_in_dim(value_bias, mine_cols, head_cols).astype(F32)
    shifts = interleave(query_shift[None], jnp.zeros_like(query_shift)[None], value_shift[None], heads)
    qkv = [(dot(tokens, w_heads) + shifts).astype(BF16)]

    segment_row = segment_ids.reshape(seq_len)
    bounds = document_blocks(segment_row)
    seg_col = segment_row.reshape(seq_len, 1)
    seg_row = segment_row.reshape(1, seq_len)
    lane = rank.astype(jnp.int32).reshape(1)

    def exchange(packed_blocks):
        return lax.all_to_all(packed_blocks.reshape(parts, halves, PACKED, 2 * DH), "tensor", 0, 0)

    blocks = seq_len // BLOCK
    early = run_forward(0, blocks // 2, lane, bounds, qkv, seg_col, seg_row)
    if paired:
        far, early, bounds = lax.optimization_barrier((far, early, bounds))
        weights = lax.all_gather(far, "dp", axis=0, tiled=False)
    late = run_forward(blocks // 2, blocks // 2, lane, bounds, qkv, seg_col, seg_row)
    context = jnp.concatenate((early[0], late[0]), axis=0)
    lse = jnp.concatenate((early[1], late[1]), axis=2)
    if paired:
        near_next, context = lax.optimization_barrier((near_next, context))
        near = jnp.concatenate([near, near_next], axis=0)
        near_other = swap(near, "dp", 1)
    arrived = exchange(context)
    if paired:
        weights = weights.reshape((copies * 2,) + mine.shape)
        pieces = [near, near_other, weights]
        marks = [[(slot, turn ^ flip, True) for turn in turns for slot in (0, 1)] for flip in (0, 1)]
        marks.append([(2 + at % 2, at // 2, False) for at in range(2 * copies)])
    else:
        pieces = [weights.reshape(parts, width, -1)]
        marks = [[(t, 0, False) for t in range(parts)]]
    counts = [piece.reshape((-1,) + mine.shape)[:, 0, -DH : 2 - DH].astype(F32) for piece in pieces + [weights]]
    counts = jnp.concatenate(counts[:-1] if paired else counts[-1:], axis=0)
    counted = 256.0 * jnp.sum(counts[:, 0]) + jnp.sum(counts[:, 1])

    vecs = jnp.stack(
        (output_bias, gain_attn, shift_attn, outer_bias, gain_ffn, shift_ffn, outer_bias, outer_bias)
    ).astype(F32)
    inner_rows = inner_bias.astype(F32).reshape(parts, 1, hidden_cols)
    teacher_rows = teacher.reshape(part_len, width)
    cotangent_rows = cotangent.reshape(part_len, width)
    (
        layer_out, first_grad, context_grad, first, branch_grad, attn_grad, activated, hidden_grad, notes,
    ) = run_dense(
        shard_rows, marks, float(total_tokens), place, arrived, rows_in, teacher_rows, cotangent_rows, valid_rows, vecs,
        inner_rows, pieces,
    )
    head_grad = exchange(context_grad).reshape(context.shape)
    sources = (first, branch_grad, attn_grad, activated, hidden_grad, arrived)
    notes = jnp.tile(notes, (copies, 1))
    if paired:
        keep_turns = (0, 4, 2, 6)
        (distant,) = run_weights(2, 2, ((width, (0,)),), place, notes, *sources)
        plans = tuple((shard_rows, tuple(turn | flip for turn in keep_turns)) for flip in (0, 1))
        keep, send = run_weights(0, 2, plans, place, notes, *sources)
        keep, send = (value.reshape((4, 2) + value.shape[1:]) for value in (keep, send))
        distant = lax.psum_scatter(distant, "dp", scatter_dimension=1, tiled=True)
        came = swap(send, "dp", 1)
    else:
        (packed,) = run_weights(0, parts, ((width, (0,)),), place, notes, *sources)
        packed = lax.psum_scatter(packed, "dp", scatter_dimension=1, tiled=True)

    joined_grad, sums = run_backward(
        (1, 0), lane, bounds, qkv, seg_col, seg_row, context, head_grad, lse, [], []
    )
    joined_grad = joined_grad.reshape(seq_len, -1)
    attn_back = dot(joined_grad, w_heads, NT).astype(BF16)
    if paired:
        came = after(came, attn_back)
    attn_back, sums, joined_grad = lax.optimization_barrier((attn_back, sums, joined_grad))
    attn_back = lax.psum_scatter(attn_back, "tensor", scatter_dimension=0, tiled=True)
    if paired:
        keep, send = add_halves(keep, came)
        keep, send, joined_grad = lax.optimization_barrier((keep, send, joined_grad))
        came = swap(send, "dp", 2)
    head_weights = dot(tokens, joined_grad, TN).reshape((copies, shard_rows, -1))
    if paired:
        came, head_weights = lax.optimization_barrier((came, head_weights))
        keep, send = add_halves(keep, came)
        keep, send, head_weights = lax.optimization_barrier((keep, send, head_weights))
        came = swap(send, "dp", 4)
    sums = sums.reshape(heads, 4, DH)
    sums = jnp.concatenate((sums[:, 0].reshape(1, head_cols), sums[:, 3].reshape(1, head_cols)), axis=1)
    for bit in bits_of("tensor"):
        sums = merge(sums, swap(sums, "tensor", bit), "tensor", bit)
    if paired:
        came, head_weights = lax.optimization_barrier((came, head_weights))
        slots = jnp.concatenate([add_low(keep, came)[0], distant], axis=0)
        packed = jnp.stack(
            [lax.dynamic_index_in_dim(slots, rank ^ t, 0, keepdims=False) for t in range(parts)]
        )
    packed = lax.psum_scatter(packed, "tensor", scatter_dimension=0, tiled=True)[0]
    biases = jnp.concatenate((sums[:, :head_cols].reshape(-1), sums[:, head_cols:].reshape(-1)))
    biases = jnp.pad(
        biases.reshape(8, heads, 1, DH), ((0, shard_rows - 8), (0, 0), (1, 2), (0, 0))
    ).reshape(1, shard_rows, -1)
    query_grad, key_grad, value_grad, biases = run_finish_heads(
        scatter_rows((head_weights + biases).astype(BF16))
    )
    biases = biases.reshape(2, width)
    input_grad = first_grad + attn_back.astype(F32)

    inner_grad, outer_grad, output_grad, notes = run_finish_dense(packed, hidden_cols, head_cols)
    notes = notes.reshape(-1)

    def total(which):
        return notes[which * width : (which + 1) * width]

    mse_loss = jnp.sum(total(0)) / (counted * width)
    return (
        layer_out.reshape(1, part_len, width),
        mse_loss,
        input_grad.reshape(1, part_len, width),
        query_grad,
        key_grad,
        value_grad,
        output_grad,
        inner_grad,
        outer_grad.T,
        biases[0],
        biases[1],
        total(4),
        notes[8 * width : 8 * width + hidden_cols * parts],
        total(1),
        total(5),
        total(6),
        total(2),
        total(3),
    )


def solution(mesh):
    shard = P("dp", "tensor", None)
    by_dp, by_tensor = P("dp", "tensor"), P("tensor", "dp")
    in_specs = (
        (shard, P("dp", None), by_dp, shard, shard)
        + (by_dp,) * 3
        + (by_tensor, by_dp, by_tensor)
        + (P(),) * 9
    )
    out_specs = (shard, P(), shard) + (by_dp,) * 3 + (by_tensor, by_dp, by_tensor) + (P(),) * 9
    return jax.shard_map(local, mesh=mesh, in_specs=in_specs, out_specs=out_specs, check_vma=False)
```

```python
import functools

import jax
import jax.numpy as jnp
from jax import lax
from jax.experimental import pallas as pl
from jax.experimental.pallas import tpu as pltpu
from jax.sharding import PartitionSpec as P

DH = 64
BLOCK = 256
SLAB = 4 * DH
EPSILON = 1e-12
ROOT_HALF = 0.7071067811865476
INV_ROOT_TAU = 0.3989422804014327
LOG2E = 1.4426950408889634
LN2 = 0.6931471805599453
SCALE = DH ** (-0.5)
MASKED = -1e30
VMEM_LIMIT = 60 << 20

BF16 = jnp.bfloat16
F32 = jnp.float32
NN = (((1,), (0,)), ((), ()))
NT = (((1,), (1,)), ((), ()))
TN = (((0,), (0,)), ((), ()))


def dot(left_side, right_side, dims=NN):
    return lax.dot_general(left_side, right_side, dims, preferred_element_type=F32)


def norm_forward(summed, gain_vec, shift_vec):
    average = jnp.mean(summed, axis=-1, keepdims=True)
    centered = summed - average
    variance = jnp.mean(centered * centered, axis=-1, keepdims=True)
    inverse = lax.rsqrt(variance + EPSILON)
    normed = centered * inverse
    return (normed * gain_vec + shift_vec, normed, inverse)


def norm_backward(upstream, normed, inverse, gain_vec):
    scaled = upstream * gain_vec
    first_mean = jnp.mean(scaled, axis=-1, keepdims=True)
    second_mean = jnp.mean(scaled * normed, axis=-1, keepdims=True)
    return inverse * (scaled - first_mean - normed * second_mean)


def column_sum(value):
    return jnp.sum(value, axis=0, keepdims=True)


def lane_is_right(rows):
    return lax.broadcasted_iota(jnp.int32, (rows, 2 * DH), 1) >= DH


def pack(first_two, third_top, third_bottom):
    return jnp.concatenate([first_two, jnp.concatenate([third_top, third_bottom], axis=1)], axis=0)


def unpack(packed):
    third = packed[BLOCK:]
    third = jnp.concatenate([third[:, :DH], third[:, DH:]], axis=0)
    return jnp.concatenate([packed[:BLOCK], third], axis=1)


def fetch_chunks(lane_ref, chunk_refs, target, sems):
    rows = chunk_refs[0].shape[0]
    copies = []
    for at, chunk in enumerate(chunk_refs):
        offset = pl.multiple_of(lax.rem(lane_ref[0] + at, len(chunk_refs)) * rows, rows)
        copies.append(pltpu.make_async_copy(chunk, target.at[pl.ds(offset, rows), :], sems.at[at]))
    return copies


def attend_forward(
    which, lane_ref, low_ref, count_ref, *refs
):
    chunk_refs, (seg_col_ref, seg_row_ref, ctx_ref, lse_ref, held, qkv_ref, sems) = refs[:-7], refs[-7:]
    heads = lse_ref.shape[0]

    @pl.when(pl.program_id(0) == 0)
    def _():
        copies = fetch_chunks(lane_ref, chunk_refs, qkv_ref, sems)
        for copy in copies:
            copy.start()
        for copy in copies:
            copy.wait()

    halves, half = which
    qb = pl.program_id(0) * halves + half
    rows = pl.ds(pl.multiple_of(qb * BLOCK, BLOCK), BLOCK)
    seg_q = seg_col_ref[...]
    queries = [
        qkv_ref[rows, SLAB * h : SLAB * h + 2 * DH] * jnp.asarray(SCALE, BF16) for h in range(heads)
    ]
    low, count = low_ref[qb], count_ref[qb]

    def score(kb, peaks):
        keys = pl.ds(pl.multiple_of(low * STEP + kb * BLOCK, STEP), BLOCK)
        allowed = seg_q == seg_row_ref[:, keys]
        found = []
        for h in range(heads):
            scores = dot(queries[h], qkv_ref[keys, SLAB * h + 2 * DH : SLAB * (h + 1)], NT)
            scores = jnp.where(allowed, scores, MASKED)
            held[h, kb] = scores
            found.append(jnp.maximum(peaks[h], jnp.maximum(scores[:, :128], scores[:, 128:])))
        return tuple(found)

    start = tuple(jnp.full((BLOCK, 128), MASKED, F32) for _ in range(heads))
    peaks = lax.fori_loop(0, count, score, start)
    highest = [jnp.max(peak, axis=-1, keepdims=True) for peak in peaks]

    def weigh(kb, carry):
        keys = pl.ds(pl.multiple_of(low * STEP + kb * BLOCK, STEP), BLOCK)
        found = []
        for h in range(heads):
            total, acc = carry[h]
            raised = jnp.exp2((held[h, kb] - highest[h]) * LOG2E)
            total = total + (raised[:, :128] + raised[:, 128:])
            acc = acc + dot(raised.astype(BF16), qkv_ref[keys, SLAB * h + 2 * DH : SLAB * (h + 1)])
            found.append((total, acc))
        return tuple(found)

    zero = jnp.zeros((BLOCK, 128), F32)
    done = lax.fori_loop(0, count, weigh, tuple((zero, zero) for _ in range(heads)))
    values = []
    for h in range(heads):
        total, acc = done[h]
        summed = jnp.sum(total, axis=-1, keepdims=True)
        values.append((acc / summed).astype(BF16))
        lse_ref[h] = jnp.transpose(highest[h] + jnp.log(summed))
    middle = BLOCK // 2
    ctx_ref[0, :BLOCK, :] = jnp.where(lane_is_right(BLOCK), values[1], pltpu.roll(values[0], DH, 1))
    ctx_ref[0, BLOCK:, :] = jnp.where(
        lane_is_right(middle), values[2][middle:], pltpu.roll(values[2][:middle], DH, 1)
    )


def attend_backward(halves, chunks, lane_ref, low_ref, count_ref, *refs):
    chunk_refs, refs = refs[:chunks], refs[chunks:]
    (seg_col_ref, seg_row_ref, grad_ref), refs = refs[:3], refs[3:]
    ctx_refs, lse_refs, refs = refs[:halves], refs[halves : 2 * halves], refs[2 * halves :]
    final_ref, sums_ref, dkv, out_ref, qkv_ref, sems = refs
    heads = dkv.shape[0]
    qb = pl.program_id(0)
    half = lax.rem(qb, halves)

    def choose(options):
        value = options[0][...]
        for other in range(1, halves):
            value = jnp.where(half == other, options[other][...], value)
        return value

    @pl.when(qb == 0)
    def _():
        copies = fetch_chunks(lane_ref, chunk_refs, qkv_ref, sems)
        for copy in copies:
            copy.start()
        dkv[...] = jnp.zeros_like(dkv)
        for copy in copies:
            copy.wait()

    rows = pl.ds(pl.multiple_of(qb * BLOCK, BLOCK), BLOCK)
    right = lane_is_right(BLOCK)
    arrived = grad_ref[0]
    product = arrived.astype(F32) * choose(ctx_refs)[0].astype(F32)
    upper = product.astype(BF16)
    lower = (product - upper.astype(F32)).astype(BF16)
    pick = (
        lax.broadcasted_iota(jnp.int32, (8, 2 * DH), 1) // DH
        == lax.broadcasted_iota(jnp.int32, (8, 2 * DH), 0)
    ).astype(BF16)
    summed = dot(pick, upper, NT) + dot(pick, lower, NT)
    deltas = [
        summed[0:1, :BLOCK],
        summed[1:2, :BLOCK],
        jnp.concatenate([summed[0:1, BLOCK:], summed[1:2, BLOCK:]], axis=1),
    ]
    two, third = arrived[:BLOCK], arrived[BLOCK:]
    placed = [
        pltpu.roll(two, DH, 1),
        two,
        jnp.concatenate([pltpu.roll(third, DH, 1), third], axis=0),
    ]
    grads = [jnp.where(right, grad, jnp.zeros_like(grad)) for grad in placed]
    queries, pairs = [], []
    for h in range(heads):
        queries.append(qkv_ref[rows, SLAB * h : SLAB * h + 2 * DH] * jnp.asarray(SCALE, BF16))
        pairs.append(jnp.concatenate([queries[h], grads[h]], axis=0))
    seg_q = seg_row_ref[...]
    lses = choose(lse_refs)
    low, count = low_ref[qb], count_ref[qb]

    def step(kb, accs):
        keys = pl.ds(pl.multiple_of(low * STEP + kb * BLOCK, STEP), BLOCK)
        allowed = seg_col_ref[keys, :] == seg_q
        keyed = [qkv_ref[keys, SLAB * h + 2 * DH : SLAB * (h + 1)] for h in range(heads)]
        raw = [dot(keyed[h], queries[h], NT) for h in range(heads)]
        probs_grads = [dot(keyed[h], grads[h], NT) for h in range(heads)]
        both = []
        for h in range(heads):
            probs = jnp.exp2((jnp.where(allowed, raw[h], MASKED) - lses[h]) * LOG2E)
            score_grad = (probs * (probs_grads[h] - deltas[h])).astype(BF16)
            both.append((score_grad, probs.astype(BF16)))
        found = []
        for h in range(heads):
            dkv[h, keys, :] += dot(jnp.concatenate(both[h], axis=1), pairs[h])
            found.append(accs[h] + dot(both[h][0], keyed[h], TN))
        return tuple(found)

    zero = jnp.zeros((BLOCK, 128), F32)
    accs = lax.fori_loop(0, count, step, tuple(zero for _ in range(heads)))
    for h in range(heads):
        query_grad = jnp.where(right, 0.0, accs[h] * SCALE).astype(BF16)
        out_ref[rows, SLAB * h : SLAB * h + 2 * DH] = query_grad

    @pl.when(qb == pl.num_programs(0) - 1)
    def _():
        for h in range(heads):
            at = SLAB * h
            out_ref[:, at + 2 * DH : at + SLAB] = dkv[h].astype(BF16)
            sums_ref[:, at : at + SLAB] = column_sum(out_ref[:, at : at + SLAB].astype(F32))
        rows_each = final_ref.shape[1]
        copies = []
        for at in range(final_ref.shape[0]):
            offset = pl.multiple_of(lax.rem(lane_ref[0] + at, final_ref.shape[0]) * rows_each, rows_each)
            copies.append(
                pltpu.make_async_copy(out_ref.at[pl.ds(offset, rows_each), :], final_ref.at[at], sems.at[at])
            )
        for copy in copies:
            copy.start()
        for copy in copies:
            copy.wait()


STEP = 128


def document_blocks(segment_row):
    starts = segment_row[::BLOCK]
    stops = segment_row[BLOCK - 1 :: BLOCK]
    low = jnp.sum((segment_row[None, :] < starts[:, None]).astype(jnp.int32), axis=1) // STEP
    high = jnp.sum((segment_row[None, :] <= stops[:, None]).astype(jnp.int32), axis=1)
    each = BLOCK // STEP
    count = (high - low * STEP + BLOCK - 1) // BLOCK
    return (jnp.minimum(low, segment_row.shape[0] // STEP - each * count), count)


PACKED = BLOCK + BLOCK // 2


def run_forward(which, lane, bounds, qkv, seg_col, seg_row):
    halves, half = which
    seq_len, width = seg_col.shape[0], qkv[0].shape[1]
    heads = width // SLAB
    blocks = seq_len // BLOCK
    steps = blocks // halves
    return pl.pallas_call(
        functools.partial(attend_forward, which),
        out_shape=(
            jax.ShapeDtypeStruct((steps, PACKED, 2 * DH), BF16),
            jax.ShapeDtypeStruct((heads, 1, steps * BLOCK), F32),
        ),
        grid_spec=pltpu.PrefetchScalarGridSpec(
            num_scalar_prefetch=3,
            grid=(steps,),
            in_specs=[pl.BlockSpec(memory_space=pl.ANY)] * len(qkv)
            + [
                pl.BlockSpec((BLOCK, 1), lambda q, *_: (q * halves + half, 0)),
                pl.BlockSpec((1, seq_len), lambda q, *_: (0, 0)),
            ],
            out_specs=(
                pl.BlockSpec((1, PACKED, 2 * DH), lambda q, *_: (q, 0, 0)),
                pl.BlockSpec((heads, 1, BLOCK), lambda q, *_: (0, 0, q)),
            ),
            scratch_shapes=[
                pltpu.VMEM((heads, blocks, BLOCK, BLOCK), F32),
                pltpu.VMEM((seq_len, width), BF16),
                pltpu.SemaphoreType.DMA((len(qkv),)),
            ],
        ),
        compiler_params=pltpu.CompilerParams(
            dimension_semantics=("arbitrary",), vmem_limit_bytes=VMEM_LIMIT
        ),
        cost_estimate=pl.CostEstimate(
            flops=heads * seq_len * seq_len * 2048 * steps // blocks,
            bytes_accessed=5 << 20,
            transcendentals=heads * seq_len * seq_len // 3,
        ),
        name="attend_forward",
    )(lane, *bounds, *qkv, seg_col, seg_row)


def run_backward(lane, bounds, qkv, seg_col, seg_row, grad, ctxs, lses):
    seq_len, width = seg_col.shape[0], qkv[0].shape[1]
    heads = width // SLAB
    halves = len(ctxs)

    def fixed(shape):
        return pl.BlockSpec(shape, lambda q, *_: (0,) * len(shape))

    return pl.pallas_call(
        functools.partial(attend_backward, halves, len(qkv)),
        out_shape=(
            jax.ShapeDtypeStruct((len(qkv), seq_len // len(qkv), width), BF16),
            jax.ShapeDtypeStruct((1, width), F32),
        ),
        grid_spec=pltpu.PrefetchScalarGridSpec(
            num_scalar_prefetch=3,
            grid=(seq_len // BLOCK,),
            in_specs=[pl.BlockSpec(memory_space=pl.ANY)] * len(qkv)
            + [
                fixed((seq_len, 1)),
                pl.BlockSpec((1, BLOCK), lambda q, *_: (0, q)),
                pl.BlockSpec((1, PACKED, 2 * DH), lambda q, *_: (q, 0, 0)),
            ]
            + [pl.BlockSpec((1, PACKED, 2 * DH), lambda q, *_: (q // halves, 0, 0))] * halves
            + [pl.BlockSpec((heads, 1, BLOCK), lambda q, *_: (0, 0, q // halves))] * halves,
            out_specs=(pl.BlockSpec(memory_space=pl.ANY), fixed((1, width))),
            scratch_shapes=[
                pltpu.VMEM((heads, seq_len, 2 * DH), F32),
                pltpu.VMEM((seq_len, width), BF16),
                pltpu.VMEM((seq_len, width), BF16),
                pltpu.SemaphoreType.DMA((len(qkv),)),
            ],
        ),
        compiler_params=pltpu.CompilerParams(
            dimension_semantics=("arbitrary",), vmem_limit_bytes=VMEM_LIMIT
        ),
        cost_estimate=pl.CostEstimate(
            flops=heads * seq_len * seq_len * 4096,
            bytes_accessed=10 << 20,
            transcendentals=heads * seq_len * seq_len // 3,
        ),
        name="attend_backward",
    )(lane, *bounds, *qkv, seg_col, seg_row, grad, *ctxs, *lses)


def dense_chain(
    marks, halves, total_tokens, place_ref, in_ref, teacher_ref, cotangent_ref, valid_ref, vec_ref,
    inner_bias_ref, *refs
):
    ctx_refs, refs = refs[:halves], refs[halves:]
    pieces = refs[: len(marks)]
    (
        layer_ref, first_grad_ref, ctx_grad_ref, first_ref, branch_grad_ref, attn_grad_ref,
        act_out, hidden_grad_out, notes_ref, w_out, w_in, w_up, slope, act_ref, hidden_grad_ref,
        sums_ref, inner_sums_ref, gathered, sems, out_sems,
    ) = refs[len(marks) :]
    parts, _, head_cols = w_out.shape
    hidden_cols = w_in.shape[2]
    index = place_ref[parts]
    step = pl.program_id(0)
    groups = (
        (2 * hidden_cols, head_cols, w_out),
        (0, hidden_cols, w_in),
        (hidden_cols, hidden_cols, w_up),
    )

    def leave(which, slot):
        source, target = ((act_ref, act_out), (hidden_grad_ref, hidden_grad_out))[which]
        return pltpu.make_async_copy(
            source.at[slot], target.at[place_ref[slot]], out_sems.at[which, slot]
        )

    @pl.when(step == 0)
    def _():
        for group, (start, size, target) in enumerate(groups):
            for piece, marked in zip(pieces, marks):
                block = piece.shape[1]
                for at, (slot, turn, relative) in enumerate(marked):
                    offset = pl.multiple_of((index ^ turn) * block, block) if relative else turn * block
                    pltpu.make_async_copy(
                        piece.at[at, :, pl.ds(start, size)],
                        target.at[slot, pl.ds(offset, block), :],
                        sems.at[group, slot],
                    ).start()
        sums_ref[...] = jnp.zeros_like(sums_ref)
        inner_sums_ref[...] = jnp.zeros_like(inner_sums_ref)

    def arrive(group, slot):
        whole = groups[group][2].at[slot]

        @pl.when(step == 0)
        def _():
            pltpu.make_async_copy(whole, whole, sems.at[group, slot]).wait()

    def vec(which):
        return vec_ref[which : which + 1, :]

    counts = jnp.zeros((1, 2 * DH), F32)

    attention = jnp.zeros(in_ref.shape, F32)
    for slot in range(parts):
        arrive(0, slot)
        counts = counts + column_sum(w_out[slot, :, 2 * DH :].astype(F32))
        attention = attention + dot(jnp.concatenate([unpack(ref[place_ref[slot]]) for ref in ctx_refs], axis=0), w_out[slot, :, : 3 * DH], NT)
    first_exact, normed_one, inverse_one = norm_forward(
        in_ref[...].astype(F32) + attention + vec(0), vec(1), vec(2)
    )
    first = first_exact.astype(BF16)
    first_ref[...] = first

    def up(slot, branch):
        t = place_ref[slot]
        arrive(1, slot)
        hidden = dot(first, w_in[slot]) + inner_bias_ref[t]
        bend = 0.5 * (1.0 + lax.erf(hidden * ROOT_HALF))
        activated = (hidden * bend).astype(BF16)
        act_ref[slot] = activated
        leave(0, slot).start()
        slope[slot] = bend + hidden * INV_ROOT_TAU * jnp.exp2(hidden * hidden * (-0.5 * LOG2E))
        arrive(2, slot)
        return branch + dot(activated, w_up[slot], NT)

    branch = jnp.zeros(in_ref.shape, F32)
    for slot in range(parts):
        branch = up(slot, branch)
    lanes = lax.broadcasted_iota(jnp.int32, counts.shape, 1)
    weight = jnp.where(lanes == DH, 256.0, jnp.where(lanes == DH + 1, 1.0, 0.0))
    ratio = total_tokens / jnp.sum(jnp.where(weight > 0.0, counts, 0.0) * weight, axis=-1, keepdims=True)
    layer_rows, normed_two, inverse_two = norm_forward(first.astype(F32) + branch + vec(3), vec(4), vec(5))
    layer_ref[...] = layer_rows.astype(BF16)
    misfit = layer_rows - teacher_ref[...].astype(F32)
    weighted = valid_ref[...] * misfit
    out_grad = cotangent_ref[...].astype(F32) + weighted * ratio
    second_grad = norm_backward(out_grad, normed_two, inverse_two, vec(4))
    branch_grad = second_grad.astype(BF16)
    branch_grad_ref[...] = branch_grad
    sums_ref[0:1, :] += column_sum(weighted * misfit)
    sums_ref[1:2, :] += column_sum(branch_grad.astype(F32))
    sums_ref[2:3, :] += column_sum(out_grad * normed_two)
    sums_ref[3:4, :] += column_sum(out_grad)

    def down(slot, back):
        t = place_ref[slot]
        hidden_grad = (dot(branch_grad, w_up[slot]) * slope[slot]).astype(BF16)
        hidden_grad_ref[slot] = hidden_grad
        leave(1, slot).start()
        inner_sums_ref[t] += column_sum(hidden_grad.astype(F32))
        return back + dot(hidden_grad, w_in[slot], NT)

    upstream = second_grad
    for slot in range(parts):
        upstream = down(slot, upstream)
    first_grad = norm_backward(upstream, normed_one, inverse_one, vec(1))
    first_grad_ref[...] = first_grad
    attn_grad = first_grad.astype(BF16)
    attn_grad_ref[...] = attn_grad
    sums_ref[4:5, :] += column_sum(attn_grad.astype(F32))
    sums_ref[5:6, :] += column_sum(upstream * normed_one)
    sums_ref[6:7, :] += column_sum(upstream)
    middle = BLOCK // 2
    for slot in range(parts):
        back = dot(attn_grad, w_out[slot, :, : 3 * DH]).astype(BF16)
        for half in range(halves):
            part = back[half * BLOCK : (half + 1) * BLOCK]
            ctx_grad_ref[place_ref[slot], half] = pack(
                part[:, : 2 * DH], part[:middle, 2 * DH :], part[middle:, 2 * DH :]
            )


    @pl.when(step == pl.num_programs(0) - 1)
    def _():
        lanes = 2 * DH
        gathered[...] = jnp.zeros_like(gathered)
        rows_each, inner_rows = width_of(sums_ref) // lanes, width_of(inner_sums_ref) // lanes
        per_note = gathered.shape[1] // lanes

        def put(at, value):
            gathered[at // per_note : at // per_note + 1, pl.ds(at % per_note * lanes, lanes)] = value

        for row in range(sums_ref.shape[0]):
            for k in range(rows_each):
                put(row * rows_each + k, sums_ref[row : row + 1, k * lanes : (k + 1) * lanes])
        for t in range(parts):
            for k in range(inner_rows):
                put(
                    sums_ref.shape[0] * rows_each + t * inner_rows + k,
                    inner_sums_ref[t, :, k * lanes : (k + 1) * lanes],
                )
        notes_ref[...] = gathered[...].astype(BF16)

    for which in range(2):
        for slot in range(parts):
            leave(which, slot).wait()


def width_of(ref):
    return ref.shape[-1]


def run_dense(note_rows, marks, total_tokens, place, ctxs, rows_in, teacher, cotangent, valid, vecs, inner_bias, pieces):
    halves, parts = len(ctxs), ctxs[0].shape[0]
    part_len, width = rows_in.shape
    hidden_cols = inner_bias.shape[2]
    out_cols = pieces[0].shape[2] - 2 * hidden_cols
    room = -(-(8 * width + parts * hidden_cols) // (note_rows * 2 * DH)) * 2 * DH

    def fixed(shape):
        return pl.BlockSpec(shape, lambda i: (0,) * len(shape))

    anywhere = pl.BlockSpec(memory_space=pl.ANY)
    low = jax.ShapeDtypeStruct((part_len, width), BF16)
    wide = jax.ShapeDtypeStruct((parts, part_len, hidden_cols), BF16)
    packed = (parts, halves) + ctxs[0].shape[1:]
    given = (rows_in, teacher, cotangent, valid, vecs, inner_bias) + tuple(ctxs)
    return pl.pallas_call(
        functools.partial(dense_chain, marks, halves, total_tokens),
        out_shape=(
            low,
            jax.ShapeDtypeStruct((part_len, width), F32),
            jax.ShapeDtypeStruct(packed, BF16),
            low,
            low,
            low,
            wide,
            wide,
            jax.ShapeDtypeStruct((note_rows, room), BF16),
        ),
        grid=(1,),
        in_specs=[pl.BlockSpec(memory_space=pltpu.SMEM)]
        + [fixed(value.shape) for value in given]
        + [anywhere] * len(pieces),
        out_specs=(
            fixed(low.shape),
            fixed(low.shape),
            fixed(packed),
            fixed(low.shape),
            fixed(low.shape),
            fixed(low.shape),
            anywhere,
            anywhere,
            fixed((note_rows, room)),
        ),
        scratch_shapes=[
            pltpu.VMEM((parts, width, out_cols), BF16),
            pltpu.VMEM((parts, width, hidden_cols), BF16),
            pltpu.VMEM((parts, width, hidden_cols), BF16),
            pltpu.VMEM((parts, part_len, hidden_cols), F32),
            pltpu.VMEM((parts, part_len, hidden_cols), BF16),
            pltpu.VMEM((parts, part_len, hidden_cols), BF16),
            pltpu.VMEM((8, width), F32),
            pltpu.VMEM((parts, 1, hidden_cols), F32),
            pltpu.VMEM((note_rows, room), F32),
            pltpu.SemaphoreType.DMA((3, parts)),
            pltpu.SemaphoreType.DMA((2, parts)),
        ],
        compiler_params=pltpu.CompilerParams(
            dimension_semantics=("arbitrary",), vmem_limit_bytes=VMEM_LIMIT
        ),
        cost_estimate=pl.CostEstimate(
            flops=2 * part_len * width * (8 * hidden_cols + 4 * out_cols) * parts,
            bytes_accessed=24 << 20,
            transcendentals=2 * part_len * hidden_cols * parts,
        ),
        name="dense_chain",
    )(place, *given, *pieces)


def dense_weights(
    plans, halves, place_ref, first_ref, branch_grad_ref, attn_grad_ref, act_ref, hidden_grad_ref, notes_ref,
    *refs
):
    ctx_refs, outs, (whole, sems) = refs[:halves], refs[halves:-2], refs[-2:]
    step = pl.program_id(0)
    slots = whole.shape[0]

    hidden_cols = act_ref.shape[2]
    whole[step, :, :hidden_cols] = dot(first_ref[...], hidden_grad_ref[0], TN).astype(BF16)
    whole[step, :, hidden_cols : 2 * hidden_cols] = dot(branch_grad_ref[...], act_ref[0], TN).astype(BF16)
    ctx = jnp.concatenate([unpack(ref[0]) for ref in ctx_refs], axis=0)
    plain = 2 * hidden_cols + ctx.shape[1]
    whole[step, :, 2 * hidden_cols : plain] = dot(attn_grad_ref[...], ctx, TN).astype(BF16)
    note_rows, room = notes_ref.shape
    for at in range(whole.shape[1] // note_rows):
        whole[step, at * note_rows : (at + 1) * note_rows, plain : plain + room] = notes_ref[...]
    for out, turns in zip(outs, plans):
        block = out.shape[1]
        for at, turn in enumerate(turns):
            offset = 0
            if block < whole.shape[1]:
                offset = pl.multiple_of((place_ref[place_ref.shape[0] - 1] ^ turn) * block, block)
            pltpu.make_async_copy(
                whole.at[step, pl.ds(offset, block), :], out.at[at * slots + step], sems.at[step]
            ).start()

    @pl.when(step == slots - 1)
    def _():
        for slot in range(slots):
            pltpu.make_async_copy(whole.at[slot], whole.at[slot], sems.at[slot]).wait()


def run_weights(base, slots, plans, place, notes, first, branch_grad, attn_grad, act, hidden_grad, ctxs):
    _, part_len, hidden_cols = act.shape
    width = first.shape[1]
    columns = 2 * hidden_cols + 3 * DH + notes.shape[1]
    fixed = pl.BlockSpec((part_len, width), lambda s, place: (0, 0))
    by_slot = pl.BlockSpec((1, part_len, hidden_cols), lambda s, place: (place[base + s], 0, 0))
    outs = tuple(
        jax.ShapeDtypeStruct((len(turns) * slots, block, columns), BF16) for block, turns in plans
    )
    return pl.pallas_call(
        functools.partial(dense_weights, tuple(turns for _, turns in plans), len(ctxs)),
        out_shape=outs,
        grid_spec=pltpu.PrefetchScalarGridSpec(
            num_scalar_prefetch=1,
            grid=(slots,),
            in_specs=[
                fixed,
                fixed,
                fixed,
                by_slot,
                by_slot,
                pl.BlockSpec(notes.shape, lambda s, place: (0, 0)),
            ]
            + [
                pl.BlockSpec((1,) + ctx.shape[1:], lambda s, place: (place[base + s], 0, 0)) for ctx in ctxs
            ],
            out_specs=tuple(pl.BlockSpec(memory_space=pl.ANY) for _ in outs),
            scratch_shapes=[
                pltpu.VMEM((slots, width, columns), BF16),
                pltpu.SemaphoreType.DMA((slots,)),
            ],
        ),
        compiler_params=pltpu.CompilerParams(
            dimension_semantics=("arbitrary",), vmem_limit_bytes=VMEM_LIMIT
        ),
        cost_estimate=pl.CostEstimate(
            flops=2 * part_len * width * columns * slots,
            bytes_accessed=5 * slots << 20,
            transcendentals=0,
        ),
        name="dense_weights",
    )(place, first, branch_grad, attn_grad, act, hidden_grad, notes, *ctxs)


def finish_dense(packed_ref, inner_ref, outer_ref, output_ref, notes_ref):
    hidden_cols = inner_ref.shape[1]
    summed = packed_ref[...].astype(F32)
    inner_ref[...] = summed[:, :hidden_cols]
    outer_ref[...] = summed[:, hidden_cols : 2 * hidden_cols]
    plain = 2 * hidden_cols + output_ref.shape[0]
    output_ref[...] = jnp.transpose(summed[:, 2 * hidden_cols : plain])
    notes_ref[...] = summed[:, plain:]


def run_finish_dense(packed, hidden_cols, head_cols):
    rows = packed.shape[0]
    return pl.pallas_call(
        finish_dense,
        out_shape=(
            jax.ShapeDtypeStruct((rows, hidden_cols), F32),
            jax.ShapeDtypeStruct((rows, hidden_cols), F32),
            jax.ShapeDtypeStruct((head_cols, rows), F32),
            jax.ShapeDtypeStruct((rows, packed.shape[1] - 2 * hidden_cols - head_cols), F32),
        ),
        name="finish_dense",
    )(packed)


def finish_heads(value_ref, *refs):
    summed = value_ref[...].astype(F32)
    heads = summed.shape[1] // SLAB
    for ref, which in zip(refs, (0, 2, 3, 1)):
        columns = [summed[:, SLAB * h + which * DH : SLAB * h + (which + 1) * DH] for h in range(heads)]
        ref[...] = jnp.concatenate(columns, axis=1)[: ref.shape[0]]


def run_finish_heads(value):
    rows, width = value.shape
    out = jax.ShapeDtypeStruct((rows, width // 4), F32)
    notes = jax.ShapeDtypeStruct((8, width // 4), F32)
    return pl.pallas_call(finish_heads, out_shape=(out, out, out, notes), name="finish_heads")(value)


def interleave(query, key, value, heads):
    rows = query.shape[0]
    parts = [part.reshape(rows, heads, 1, DH) for part in (query, jnp.zeros_like(query), key, value)]
    return jnp.concatenate(parts, axis=2).reshape(rows, heads * SLAB)


def swap(value, axis, bit):
    size = lax.axis_size(axis)
    return lax.ppermute(value, axis, [(i, i ^ bit) for i in range(size)])


def bits_of(axis):
    bit = 1
    while bit < lax.axis_size(axis):
        yield bit
        bit *= 2


def after(value, *others):
    return lax.optimization_barrier((value,) + others)[0]


def merge(held, other, axis, bit):
    mine_first = (lax.axis_index(axis) & bit) == 0
    return jnp.where(
        mine_first, jnp.concatenate([held, other], axis=0), jnp.concatenate([other, held], axis=0)
    )


def add_low(left_side, right_side):
    return (left_side.astype(F32) + right_side.astype(F32)).astype(BF16)


def add_halves(left_side, right_side):
    half = left_side.shape[0] // 2
    return (
        add_low(left_side[:half], right_side[:half]),
        add_low(left_side[half:], right_side[half:]),
    )


def scatter_rows(held):
    index = lax.axis_index("dp")
    for bit in bits_of("dp"):
        held = held.reshape((held.shape[0] // 2, 2) + held.shape[1:])
        own = (index & bit) // bit
        send = lax.dynamic_index_in_dim(held, 1 - own, 1, keepdims=False)
        keep = lax.dynamic_index_in_dim(held, own, 1, keepdims=False)
        held = add_low(keep, swap(send, "dp", bit))
    return held[0]


def local(
    inputs, segment_ids, valid_mask, teacher, cotangent,
    w_query, w_key, w_value, w_output, w_inner, w_outer,
    query_bias, value_bias, output_bias, inner_bias, outer_bias,
    gain_attn, shift_attn, gain_ffn, shift_ffn,
):
    _, part_len, width = inputs.shape
    parts = lax.axis_size("tensor")
    copies = lax.axis_size("dp")
    rank = lax.axis_index("tensor")
    total_tokens = part_len * parts * copies
    seq_len = part_len * parts
    head_cols = w_query.shape[1]
    heads = head_cols // DH
    hidden_cols = w_inner.shape[1]
    shard_rows = w_inner.shape[0]
    halves = part_len // BLOCK

    rows_in = inputs.reshape(part_len, width)
    tokens = lax.all_gather(rows_in, "tensor", axis=0, tiled=True)
    w_heads = interleave(w_query, w_key, w_value, heads)
    paired = shard_rows % 16 == 0 and parts == 4 and copies == 8

    valid_rows = valid_mask.astype(F32).reshape(part_len, 1)
    valid_count = jnp.sum(valid_mask.astype(F32))
    upper = jnp.floor(valid_count / 256.0)
    spot = lax.broadcasted_iota(jnp.int32, (shard_rows, DH), 0) * DH + lax.broadcasted_iota(
        jnp.int32, (shard_rows, DH), 1
    )
    count_row = jnp.where(spot == 0, upper, jnp.where(spot == 1, valid_count - 256.0 * upper, 0.0))
    mine = jnp.concatenate((w_inner, w_outer.T, w_output.T, count_row.astype(BF16)), axis=1)
    if paired:
        place = jnp.stack([rank, rank ^ 1, rank ^ 2, rank ^ 3, lax.axis_index("dp")]).astype(jnp.int32)
        pair = jnp.concatenate([mine[None], swap(mine[None], "tensor", 1)], axis=0)
        near = jnp.concatenate([pair, swap(pair, "dp", 2)], axis=0)
        turns = [0, 2, 4, 6]
        for bit in (1, 2, 4):
            w_heads = merge(w_heads, swap(w_heads, "dp", bit), "dp", bit)
        near, w_heads = lax.optimization_barrier((near, w_heads))
        near_next = swap(near, "dp", 4)
        tokens, pair, near_next = lax.optimization_barrier((tokens, pair, near_next))
        far = swap(pair, "tensor", 2)
    else:
        place = jnp.asarray(list(range(parts)) + [0], jnp.int32)
        weights = lax.all_gather(mine, ("tensor", "dp"), axis=0, tiled=False)
        for bit in bits_of("dp"):
            w_heads = merge(w_heads, swap(w_heads, "dp", bit), "dp", bit)

    mine_cols = rank * head_cols
    query_shift = lax.dynamic_slice_in_dim(query_bias, mine_cols, head_cols).astype(F32)
    value_shift = lax.dynamic_slice_in_dim(value_bias, mine_cols, head_cols).astype(F32)
    shifts = interleave(query_shift[None], jnp.zeros_like(query_shift)[None], value_shift[None], heads)
    qkv = [(dot(tokens, w_heads) + shifts).astype(BF16)]

    segment_row = segment_ids.reshape(seq_len)
    bounds = document_blocks(segment_row)
    seg_col = segment_row.reshape(seq_len, 1)
    seg_row = segment_row.reshape(1, seq_len)
    lane = rank.astype(jnp.int32).reshape(1)

    def exchange(packed_blocks):
        return lax.all_to_all(packed_blocks, "tensor", 0, 0)

    contexts, lses, arrived = [], [], []
    for half in range(halves):
        if paired and half == 1:
            far, contexts[0], bounds = lax.optimization_barrier((far, contexts[0], bounds))
            weights = lax.all_gather(far, "dp", axis=0, tiled=False)
        context, lse = run_forward((halves, half), lane, bounds, qkv, seg_col, seg_row)
        contexts.append(context)
        lses.append(lse)
        arrived.append(exchange(context))
    if paired:
        near_next, context = lax.optimization_barrier((near_next, contexts[-1]))
        near = jnp.concatenate([near, near_next], axis=0)
        near_other = swap(near, "dp", 1)
    if paired:
        weights = weights.reshape((copies * 2,) + mine.shape)
        pieces = [near, near_other, weights]
        marks = [[(slot, turn ^ flip, True) for turn in turns for slot in (0, 1)] for flip in (0, 1)]
        marks.append([(2 + at % 2, at // 2, False) for at in range(2 * copies)])
    else:
        pieces = [weights.reshape(parts, width, -1)]
        marks = [[(t, 0, False) for t in range(parts)]]
    counts = [piece.reshape((-1,) + mine.shape)[:, 0, -DH : 2 - DH].astype(F32) for piece in pieces + [weights]]
    counts = jnp.concatenate(counts[:-1] if paired else counts[-1:], axis=0)
    counted = 256.0 * jnp.sum(counts[:, 0]) + jnp.sum(counts[:, 1])

    vecs = jnp.stack(
        (output_bias, gain_attn, shift_attn, outer_bias, gain_ffn, shift_ffn, outer_bias, outer_bias)
    ).astype(F32)
    inner_rows = inner_bias.astype(F32).reshape(parts, 1, hidden_cols)
    teacher_rows = teacher.reshape(part_len, width)
    cotangent_rows = cotangent.reshape(part_len, width)
    (
        layer_out, first_grad, context_grad, first, branch_grad, attn_grad, activated, hidden_grad, notes,
    ) = run_dense(
        shard_rows, marks, float(total_tokens), place, arrived, rows_in, teacher_rows, cotangent_rows, valid_rows, vecs,
        inner_rows, pieces,
    )
    head_grad = exchange(context_grad).reshape((parts * halves, PACKED, 2 * DH))
    sources = (first, branch_grad, attn_grad, activated, hidden_grad, arrived)
    if shard_rows % 16:
        notes = jnp.tile(notes, (copies, 1))
    if paired:
        keep_turns = (0, 4, 2, 6)
        (distant,) = run_weights(2, 2, ((width, (0,)),), place, notes, *sources)
        plans = tuple((shard_rows, tuple(turn | flip for turn in keep_turns)) for flip in (0, 1))
        keep, send = run_weights(0, 2, plans, place, notes, *sources)
        keep, send = (value.reshape((4, 2) + value.shape[1:]) for value in (keep, send))
        distant = lax.psum_scatter(distant, "dp", scatter_dimension=1, tiled=True)
        came = swap(send, "dp", 1)
    else:
        (packed,) = run_weights(0, parts, ((width, (0,)),), place, notes, *sources)
        packed = lax.psum_scatter(packed, "dp", scatter_dimension=1, tiled=True)

    joined_grad, sums = run_backward(lane, bounds, qkv, seg_col, seg_row, head_grad, contexts, lses)
    joined_grad = joined_grad.reshape(seq_len, -1)
    attn_back = dot(joined_grad, w_heads, NT).astype(BF16)
    if paired:
        came = after(came, attn_back)
    attn_back, sums, joined_grad = lax.optimization_barrier((attn_back, sums, joined_grad))
    attn_back = lax.psum_scatter(attn_back, "tensor", scatter_dimension=0, tiled=True)
    if paired:
        keep, send = add_halves(keep, came)
        keep, send, joined_grad = lax.optimization_barrier((keep, send, joined_grad))
        came = swap(send, "dp", 2)
    head_weights = dot(tokens, joined_grad, TN).reshape((copies, shard_rows, -1))
    if paired:
        came, head_weights = lax.optimization_barrier((came, head_weights))
        keep, send = add_halves(keep, came)
        keep, send, head_weights = lax.optimization_barrier((keep, send, head_weights))
        came = swap(send, "dp", 4)
    sums = sums.reshape(heads, 4, DH)
    sums = jnp.concatenate((sums[:, 0].reshape(1, head_cols), sums[:, 3].reshape(1, head_cols)), axis=1)
    for bit in bits_of("tensor"):
        sums = merge(sums, swap(sums, "tensor", bit), "tensor", bit)
    if paired:
        came, head_weights = lax.optimization_barrier((came, head_weights))
        slots = jnp.concatenate([add_low(keep, came)[0], distant], axis=0)
        packed = jnp.stack(
            [lax.dynamic_index_in_dim(slots, rank ^ t, 0, keepdims=False) for t in range(parts)]
        )
    packed = lax.psum_scatter(packed, "tensor", scatter_dimension=0, tiled=True)[0]
    biases = jnp.concatenate((sums[:, :head_cols].reshape(-1), sums[:, head_cols:].reshape(-1)))
    biases = jnp.pad(
        biases.reshape(8, heads, 1, DH), ((0, shard_rows - 8), (0, 0), (1, 2), (0, 0))
    ).reshape(1, shard_rows, -1)
    query_grad, key_grad, value_grad, biases = run_finish_heads(
        scatter_rows((head_weights + biases).astype(BF16))
    )
    biases = biases.reshape(2, width)
    input_grad = first_grad + attn_back.astype(F32)

    inner_grad, outer_grad, output_grad, notes = run_finish_dense(packed, hidden_cols, head_cols)
    notes = notes.reshape(-1)

    def total(which):
        return notes[which * width : (which + 1) * width]

    mse_loss = jnp.sum(total(0)) / (counted * width)
    return (
        layer_out.reshape(1, part_len, width),
        mse_loss,
        input_grad.reshape(1, part_len, width),
        query_grad,
        key_grad,
        value_grad,
        output_grad,
        inner_grad,
        outer_grad.T,
        biases[0],
        biases[1],
        total(4),
        notes[8 * width : 8 * width + hidden_cols * parts],
        total(1),
        total(5),
        total(6),
        total(2),
        total(3),
    )


def solution(mesh):
    shard = P("dp", "tensor", None)
    by_dp, by_tensor = P("dp", "tensor"), P("tensor", "dp")
    in_specs = (
        (shard, P("dp", None), by_dp, shard, shard)
        + (by_dp,) * 3
        + (by_tensor, by_dp, by_tensor)
        + (P(),) * 9
    )
    out_specs = (shard, P(), shard) + (by_dp,) * 3 + (by_tensor, by_dp, by_tensor) + (P(),) * 9
    return jax.shard_map(local, mesh=mesh, in_specs=in_specs, out_specs=out_specs, check_vma=False)
```

```python
import functools

import jax
import jax.numpy as jnp
from jax import lax
from jax.experimental import pallas as pl
from jax.experimental.pallas import tpu as pltpu
from jax.sharding import PartitionSpec as P

DH = 64
BLOCK = 256
SLAB = 4 * DH
EPSILON = 1e-12
ROOT_HALF = 0.7071067811865476
INV_ROOT_TAU = 0.3989422804014327
LOG2E = 1.4426950408889634
LN2 = 0.6931471805599453
SCALE = DH ** (-0.5)
MASKED = -1e30
VMEM_LIMIT = 60 << 20

BF16 = jnp.bfloat16
F32 = jnp.float32
NN = (((1,), (0,)), ((), ()))
NT = (((1,), (1,)), ((), ()))
TN = (((0,), (0,)), ((), ()))


def dot(left_side, right_side, dims=NN):
    return lax.dot_general(left_side, right_side, dims, preferred_element_type=F32)


def norm_forward(summed, gain_vec, shift_vec):
    average = jnp.mean(summed, axis=-1, keepdims=True)
    centered = summed - average
    variance = jnp.mean(centered * centered, axis=-1, keepdims=True)
    inverse = lax.rsqrt(variance + EPSILON)
    normed = centered * inverse
    return (normed * gain_vec + shift_vec, normed, inverse)


def norm_backward(upstream, normed, inverse, gain_vec):
    scaled = upstream * gain_vec
    first_mean = jnp.mean(scaled, axis=-1, keepdims=True)
    second_mean = jnp.mean(scaled * normed, axis=-1, keepdims=True)
    return inverse * (scaled - first_mean - normed * second_mean)


def column_sum(value):
    return jnp.sum(value, axis=0, keepdims=True)


def lane_is_right(rows):
    return lax.broadcasted_iota(jnp.int32, (rows, 2 * DH), 1) >= DH


def pack(first_two, third_top, third_bottom):
    return jnp.concatenate([first_two, jnp.concatenate([third_top, third_bottom], axis=1)], axis=0)


def unpack(packed):
    third = packed[BLOCK:]
    third = jnp.concatenate([third[:, :DH], third[:, DH:]], axis=0)
    return jnp.concatenate([packed[:BLOCK], third], axis=1)


def fetch_chunks(lane_ref, chunk_refs, target, sems):
    rows = chunk_refs[0].shape[0]
    copies = []
    for at, chunk in enumerate(chunk_refs):
        offset = pl.multiple_of(lax.rem(lane_ref[0] + at, len(chunk_refs)) * rows, rows)
        copies.append(pltpu.make_async_copy(chunk, target.at[pl.ds(offset, rows), :], sems.at[at]))
    return copies


def attend_forward(
    which, lane_ref, low_ref, count_ref, *refs
):
    chunk_refs, (seg_col_ref, seg_row_ref, ctx_ref, lse_ref, held, qkv_ref, sems) = refs[:-7], refs[-7:]
    heads = lse_ref.shape[0]

    @pl.when(pl.program_id(0) == 0)
    def _():
        copies = fetch_chunks(lane_ref, chunk_refs, qkv_ref, sems)
        for copy in copies:
            copy.start()
        for copy in copies:
            copy.wait()

    halves, half = which
    qb = pl.program_id(0) * halves + half
    rows = pl.ds(pl.multiple_of(qb * BLOCK, BLOCK), BLOCK)
    seg_q = seg_col_ref[...]
    queries = [
        qkv_ref[rows, SLAB * h : SLAB * h + 2 * DH] * jnp.asarray(SCALE, BF16) for h in range(heads)
    ]
    low, count = low_ref[qb], count_ref[qb]

    def score(kb, peaks):
        keys = pl.ds(pl.multiple_of(low * STEP + kb * BLOCK, STEP), BLOCK)
        allowed = seg_q == seg_row_ref[:, keys]
        found = []
        for h in range(heads):
            scores = dot(queries[h], qkv_ref[keys, SLAB * h + 2 * DH : SLAB * (h + 1)], NT)
            scores = jnp.where(allowed, scores, MASKED)
            held[h, kb] = scores
            found.append(jnp.maximum(peaks[h], jnp.maximum(scores[:, :128], scores[:, 128:])))
        return tuple(found)

    start = tuple(jnp.full((BLOCK, 128), MASKED, F32) for _ in range(heads))
    peaks = lax.fori_loop(0, count, score, start)
    highest = [jnp.max(peak, axis=-1, keepdims=True) for peak in peaks]

    def weigh(kb, carry):
        keys = pl.ds(pl.multiple_of(low * STEP + kb * BLOCK, STEP), BLOCK)
        found = []
        for h in range(heads):
            total, acc = carry[h]
            raised = jnp.exp2((held[h, kb] - highest[h]) * LOG2E)
            total = total + (raised[:, :128] + raised[:, 128:])
            acc = acc + dot(raised.astype(BF16), qkv_ref[keys, SLAB * h + 2 * DH : SLAB * (h + 1)])
            found.append((total, acc))
        return tuple(found)

    zero = jnp.zeros((BLOCK, 128), F32)
    done = lax.fori_loop(0, count, weigh, tuple((zero, zero) for _ in range(heads)))
    values = []
    for h in range(heads):
        total, acc = done[h]
        summed = jnp.sum(total, axis=-1, keepdims=True)
        values.append((acc / summed).astype(BF16))
        lse_ref[h] = jnp.transpose(highest[h] + jnp.log(summed))
    middle = BLOCK // 2
    ctx_ref[0, :BLOCK, :] = jnp.where(lane_is_right(BLOCK), values[1], pltpu.roll(values[0], DH, 1))
    ctx_ref[0, BLOCK:, :] = jnp.where(
        lane_is_right(middle), values[2][middle:], pltpu.roll(values[2][:middle], DH, 1)
    )


def attend_backward(halves, chunks, lane_ref, low_ref, count_ref, *refs):
    chunk_refs, refs = refs[:chunks], refs[chunks:]
    (seg_col_ref, seg_row_ref, grad_ref), refs = refs[:3], refs[3:]
    ctx_refs, lse_refs, refs = refs[:halves], refs[halves : 2 * halves], refs[2 * halves :]
    final_ref, sums_ref, dkv, out_ref, qkv_ref, sems = refs
    heads = dkv.shape[0]
    qb = pl.program_id(0)
    half = lax.rem(qb, halves)

    def choose(options):
        value = options[0][...]
        for other in range(1, halves):
            value = jnp.where(half == other, options[other][...], value)
        return value

    @pl.when(qb == 0)
    def _():
        copies = fetch_chunks(lane_ref, chunk_refs, qkv_ref, sems)
        for copy in copies:
            copy.start()
        dkv[...] = jnp.zeros_like(dkv)
        for copy in copies:
            copy.wait()

    rows = pl.ds(pl.multiple_of(qb * BLOCK, BLOCK), BLOCK)
    right = lane_is_right(BLOCK)
    arrived = grad_ref[0]
    product = arrived.astype(F32) * choose(ctx_refs)[0].astype(F32)
    upper = product.astype(BF16)
    lower = (product - upper.astype(F32)).astype(BF16)
    pick = (
        lax.broadcasted_iota(jnp.int32, (8, 2 * DH), 1) // DH
        == lax.broadcasted_iota(jnp.int32, (8, 2 * DH), 0)
    ).astype(BF16)
    summed = dot(pick, upper, NT) + dot(pick, lower, NT)
    deltas = [
        summed[0:1, :BLOCK],
        summed[1:2, :BLOCK],
        jnp.concatenate([summed[0:1, BLOCK:], summed[1:2, BLOCK:]], axis=1),
    ]
    two, third = arrived[:BLOCK], arrived[BLOCK:]
    placed = [
        pltpu.roll(two, DH, 1),
        two,
        jnp.concatenate([pltpu.roll(third, DH, 1), third], axis=0),
    ]
    grads = [jnp.where(right, grad, jnp.zeros_like(grad)) for grad in placed]
    queries, pairs = [], []
    for h in range(heads):
        queries.append(qkv_ref[rows, SLAB * h : SLAB * h + 2 * DH] * jnp.asarray(SCALE, BF16))
        pairs.append(jnp.concatenate([queries[h], grads[h]], axis=0))
    seg_q = seg_row_ref[...]
    lses = choose(lse_refs)
    low, count = low_ref[qb], count_ref[qb]

    def step(kb, accs):
        keys = pl.ds(pl.multiple_of(low * STEP + kb * BLOCK, STEP), BLOCK)
        allowed = seg_col_ref[keys, :] == seg_q
        keyed = [qkv_ref[keys, SLAB * h + 2 * DH : SLAB * (h + 1)] for h in range(heads)]
        raw = [dot(keyed[h], queries[h], NT) for h in range(heads)]
        probs_grads = [dot(keyed[h], grads[h], NT) for h in range(heads)]
        both = []
        for h in range(heads):
            probs = jnp.exp2((jnp.where(allowed, raw[h], MASKED) - lses[h]) * LOG2E)
            score_grad = (probs * (probs_grads[h] - deltas[h])).astype(BF16)
            both.append((score_grad, probs.astype(BF16)))
        found = []
        for h in range(heads):
            dkv[h, keys, :] += dot(jnp.concatenate(both[h], axis=1), pairs[h])
            found.append(accs[h] + dot(both[h][0], keyed[h], TN))
        return tuple(found)

    zero = jnp.zeros((BLOCK, 128), F32)
    accs = lax.fori_loop(0, count, step, tuple(zero for _ in range(heads)))
    for h in range(heads):
        query_grad = jnp.where(right, 0.0, accs[h] * SCALE).astype(BF16)
        out_ref[rows, SLAB * h : SLAB * h + 2 * DH] = query_grad

    @pl.when(qb == pl.num_programs(0) - 1)
    def _():
        for h in range(heads):
            at = SLAB * h
            out_ref[:, at + 2 * DH : at + SLAB] = dkv[h].astype(BF16)
            sums_ref[:, at : at + SLAB] = column_sum(out_ref[:, at : at + SLAB].astype(F32))
        rows_each = final_ref.shape[1]
        copies = []
        for at in range(final_ref.shape[0]):
            offset = pl.multiple_of(lax.rem(lane_ref[0] + at, final_ref.shape[0]) * rows_each, rows_each)
            copies.append(
                pltpu.make_async_copy(out_ref.at[pl.ds(offset, rows_each), :], final_ref.at[at], sems.at[at])
            )
        for copy in copies:
            copy.start()
        for copy in copies:
            copy.wait()


STEP = 128


def document_blocks(segment_row):
    starts = segment_row[::BLOCK]
    stops = segment_row[BLOCK - 1 :: BLOCK]
    low = jnp.sum((segment_row[None, :] < starts[:, None]).astype(jnp.int32), axis=1) // STEP
    high = jnp.sum((segment_row[None, :] <= stops[:, None]).astype(jnp.int32), axis=1)
    each = BLOCK // STEP
    count = (high - low * STEP + BLOCK - 1) // BLOCK
    return (jnp.minimum(low, segment_row.shape[0] // STEP - each * count), count)


PACKED = BLOCK + BLOCK // 2


def run_forward(which, lane, bounds, qkv, seg_col, seg_row):
    halves, half = which
    seq_len, width = seg_col.shape[0], qkv[0].shape[1]
    heads = width // SLAB
    blocks = seq_len // BLOCK
    steps = blocks // halves
    return pl.pallas_call(
        functools.partial(attend_forward, which),
        out_shape=(
            jax.ShapeDtypeStruct((steps, PACKED, 2 * DH), BF16),
            jax.ShapeDtypeStruct((heads, 1, steps * BLOCK), F32),
        ),
        grid_spec=pltpu.PrefetchScalarGridSpec(
            num_scalar_prefetch=3,
            grid=(steps,),
            in_specs=[pl.BlockSpec(memory_space=pl.ANY)] * len(qkv)
            + [
                pl.BlockSpec((BLOCK, 1), lambda q, *_: (q * halves + half, 0)),
                pl.BlockSpec((1, seq_len), lambda q, *_: (0, 0)),
            ],
            out_specs=(
                pl.BlockSpec((1, PACKED, 2 * DH), lambda q, *_: (q, 0, 0)),
                pl.BlockSpec((heads, 1, BLOCK), lambda q, *_: (0, 0, q)),
            ),
            scratch_shapes=[
                pltpu.VMEM((heads, blocks, BLOCK, BLOCK), F32),
                pltpu.VMEM((seq_len, width), BF16),
                pltpu.SemaphoreType.DMA((len(qkv),)),
            ],
        ),
        compiler_params=pltpu.CompilerParams(
            dimension_semantics=("arbitrary",), vmem_limit_bytes=VMEM_LIMIT
        ),
        cost_estimate=pl.CostEstimate(
            flops=heads * seq_len * seq_len * 2048 * steps // blocks,
            bytes_accessed=5 << 20,
            transcendentals=heads * seq_len * seq_len // 3,
        ),
        name="attend_forward",
    )(lane, *bounds, *qkv, seg_col, seg_row)


def run_backward(lane, bounds, qkv, seg_col, seg_row, grad, ctxs, lses):
    seq_len, width = seg_col.shape[0], qkv[0].shape[1]
    heads = width // SLAB
    halves = len(ctxs)

    def fixed(shape):
        return pl.BlockSpec(shape, lambda q, *_: (0,) * len(shape))

    return pl.pallas_call(
        functools.partial(attend_backward, halves, len(qkv)),
        out_shape=(
            jax.ShapeDtypeStruct((len(qkv), seq_len // len(qkv), width), BF16),
            jax.ShapeDtypeStruct((1, width), F32),
        ),
        grid_spec=pltpu.PrefetchScalarGridSpec(
            num_scalar_prefetch=3,
            grid=(seq_len // BLOCK,),
            in_specs=[pl.BlockSpec(memory_space=pl.ANY)] * len(qkv)
            + [
                fixed((seq_len, 1)),
                pl.BlockSpec((1, BLOCK), lambda q, *_: (0, q)),
                pl.BlockSpec((1, PACKED, 2 * DH), lambda q, *_: (q, 0, 0)),
            ]
            + [pl.BlockSpec((1, PACKED, 2 * DH), lambda q, *_: (q // halves, 0, 0))] * halves
            + [pl.BlockSpec((heads, 1, BLOCK), lambda q, *_: (0, 0, q // halves))] * halves,
            out_specs=(pl.BlockSpec(memory_space=pl.ANY), fixed((1, width))),
            scratch_shapes=[
                pltpu.VMEM((heads, seq_len, 2 * DH), F32),
                pltpu.VMEM((seq_len, width), BF16),
                pltpu.VMEM((seq_len, width), BF16),
                pltpu.SemaphoreType.DMA((len(qkv),)),
            ],
        ),
        compiler_params=pltpu.CompilerParams(
            dimension_semantics=("arbitrary",), vmem_limit_bytes=VMEM_LIMIT
        ),
        cost_estimate=pl.CostEstimate(
            flops=heads * seq_len * seq_len * 4096,
            bytes_accessed=10 << 20,
            transcendentals=heads * seq_len * seq_len // 3,
        ),
        name="attend_backward",
    )(lane, *bounds, *qkv, seg_col, seg_row, grad, *ctxs, *lses)


def dense_chain(
    marks, halves, total_tokens, place_ref, in_ref, teacher_ref, cotangent_ref, valid_ref, vec_ref,
    inner_bias_ref, *refs
):
    ctx_refs, refs = refs[:halves], refs[halves:]
    pieces = refs[: len(marks)]
    (
        layer_ref, first_grad_ref, ctx_grad_ref, first_ref, branch_grad_ref, attn_grad_ref,
        act_ref, hidden_grad_ref, notes_ref, w_out, w_in, w_up, slope, sums_ref, inner_sums_ref,
        gathered, sems,
    ) = refs[len(marks) :]
    parts, _, head_cols = w_out.shape
    hidden_cols = w_in.shape[2]
    index = place_ref[parts]
    step = pl.program_id(0)
    groups = (
        (2 * hidden_cols, head_cols, w_out),
        (0, hidden_cols, w_in),
        (hidden_cols, hidden_cols, w_up),
    )

    @pl.when(step == 0)
    def _():
        for group, (start, size, target) in enumerate(groups):
            for piece, marked in zip(pieces, marks):
                block = piece.shape[1]
                for at, (slot, turn, relative) in enumerate(marked):
                    offset = pl.multiple_of((index ^ turn) * block, block) if relative else turn * block
                    pltpu.make_async_copy(
                        piece.at[at, :, pl.ds(start, size)],
                        target.at[slot, pl.ds(offset, block), :],
                        sems.at[group, slot],
                    ).start()
        sums_ref[...] = jnp.zeros_like(sums_ref)
        inner_sums_ref[...] = jnp.zeros_like(inner_sums_ref)

    def context(t):
        value = ctx_refs[0][t]
        for half in range(1, halves):
            value = jnp.where(step == half, ctx_refs[half][t], value)
        return value

    def arrive(group, slot):
        whole = groups[group][2].at[slot]

        @pl.when(step == 0)
        def _():
            pltpu.make_async_copy(whole, whole, sems.at[group, slot]).wait()

    def vec(which):
        return vec_ref[which : which + 1, :]

    counts = jnp.zeros((1, 2 * DH), F32)

    attention = jnp.zeros(in_ref.shape, F32)
    for slot in range(parts):
        arrive(0, slot)
        counts = counts + column_sum(w_out[slot, :, 2 * DH :].astype(F32))
        attention = attention + dot(unpack(context(place_ref[slot])), w_out[slot, :, : 3 * DH], NT)
    first_exact, normed_one, inverse_one = norm_forward(
        in_ref[...].astype(F32) + attention + vec(0), vec(1), vec(2)
    )
    first = first_exact.astype(BF16)
    first_ref[...] = first

    def up(slot, branch):
        t = place_ref[slot]
        arrive(1, slot)
        hidden = dot(first, w_in[slot]) + inner_bias_ref[t]
        bend = 0.5 * (1.0 + lax.erf(hidden * ROOT_HALF))
        activated = (hidden * bend).astype(BF16)
        act_ref[t] = activated
        slope[slot] = bend + hidden * INV_ROOT_TAU * jnp.exp2(hidden * hidden * (-0.5 * LOG2E))
        arrive(2, slot)
        return branch + dot(activated, w_up[slot], NT)

    branch = jnp.zeros(in_ref.shape, F32)
    for slot in range(parts):
        branch = up(slot, branch)
    lanes = lax.broadcasted_iota(jnp.int32, counts.shape, 1)
    weight = jnp.where(lanes == DH, 256.0, jnp.where(lanes == DH + 1, 1.0, 0.0))
    ratio = total_tokens / jnp.sum(jnp.where(weight > 0.0, counts, 0.0) * weight, axis=-1, keepdims=True)
    layer_rows, normed_two, inverse_two = norm_forward(first.astype(F32) + branch + vec(3), vec(4), vec(5))
    layer_ref[...] = layer_rows.astype(BF16)
    misfit = layer_rows - teacher_ref[...].astype(F32)
    weighted = valid_ref[...] * misfit
    out_grad = cotangent_ref[...].astype(F32) + weighted * ratio
    second_grad = norm_backward(out_grad, normed_two, inverse_two, vec(4))
    branch_grad = second_grad.astype(BF16)
    branch_grad_ref[...] = branch_grad
    sums_ref[0:1, :] += column_sum(weighted * misfit)
    sums_ref[1:2, :] += column_sum(branch_grad.astype(F32))
    sums_ref[2:3, :] += column_sum(out_grad * normed_two)
    sums_ref[3:4, :] += column_sum(out_grad)

    def down(slot, back):
        t = place_ref[slot]
        hidden_grad = (dot(branch_grad, w_up[slot]) * slope[slot]).astype(BF16)
        hidden_grad_ref[t] = hidden_grad
        inner_sums_ref[t] += column_sum(hidden_grad.astype(F32))
        return back + dot(hidden_grad, w_in[slot], NT)

    upstream = second_grad
    for slot in range(parts):
        upstream = down(slot, upstream)
    first_grad = norm_backward(upstream, normed_one, inverse_one, vec(1))
    first_grad_ref[...] = first_grad
    attn_grad = first_grad.astype(BF16)
    attn_grad_ref[...] = attn_grad
    sums_ref[4:5, :] += column_sum(attn_grad.astype(F32))
    sums_ref[5:6, :] += column_sum(upstream * normed_one)
    sums_ref[6:7, :] += column_sum(upstream)
    middle = BLOCK // 2
    for slot in range(parts):
        back = dot(attn_grad, w_out[slot, :, : 3 * DH]).astype(BF16)
        ctx_grad_ref[place_ref[slot], 0] = pack(
            back[:, : 2 * DH], back[:middle, 2 * DH :], back[middle:, 2 * DH :]
        )


    @pl.when(step == pl.num_programs(0) - 1)
    def _():
        lanes = 2 * DH
        gathered[...] = jnp.zeros_like(gathered)
        rows_each, inner_rows = width_of(sums_ref) // lanes, width_of(inner_sums_ref) // lanes
        per_note = gathered.shape[1] // lanes

        def put(at, value):
            gathered[at // per_note : at // per_note + 1, pl.ds(at % per_note * lanes, lanes)] = value

        for row in range(sums_ref.shape[0]):
            for k in range(rows_each):
                put(row * rows_each + k, sums_ref[row : row + 1, k * lanes : (k + 1) * lanes])
        for t in range(parts):
            for k in range(inner_rows):
                put(
                    sums_ref.shape[0] * rows_each + t * inner_rows + k,
                    inner_sums_ref[t, :, k * lanes : (k + 1) * lanes],
                )
        notes_ref[...] = gathered[...].astype(BF16)


def width_of(ref):
    return ref.shape[-1]


def run_dense(note_rows, marks, total_tokens, place, ctxs, rows_in, teacher, cotangent, valid, vecs, inner_bias, pieces):
    halves, parts = len(ctxs), ctxs[0].shape[0]
    part_len, width = rows_in.shape
    hidden_cols = inner_bias.shape[2]
    out_cols = pieces[0].shape[2] - 2 * hidden_cols
    room = -(-(8 * width + parts * hidden_cols) // (note_rows * 2 * DH)) * 2 * DH

    def by_rows(columns):
        return pl.BlockSpec((BLOCK, columns), lambda i: (i, 0))

    def by_part(columns):
        return pl.BlockSpec((parts, BLOCK, columns), lambda i: (0, i, 0))

    def fixed(shape):
        return pl.BlockSpec(shape, lambda i: (0,) * len(shape))

    packed_shape = (parts, halves) + ctxs[0].shape[1:]
    packed = pl.BlockSpec((parts, 1) + packed_shape[2:], lambda i: (0, i, 0, 0))
    low = jax.ShapeDtypeStruct((part_len, width), BF16)
    wide = jax.ShapeDtypeStruct((parts, part_len, hidden_cols), BF16)
    smem = pl.BlockSpec(memory_space=pltpu.SMEM)
    return pl.pallas_call(
        functools.partial(dense_chain, marks, halves, total_tokens),
        out_shape=(
            low,
            jax.ShapeDtypeStruct((part_len, width), F32),
            jax.ShapeDtypeStruct(packed_shape, BF16),
            low,
            low,
            low,
            wide,
            wide,
            jax.ShapeDtypeStruct((note_rows, room), BF16),
        ),
        grid=(halves,),
        in_specs=[
            smem,
            by_rows(width),
            by_rows(width),
            by_rows(width),
            by_rows(1),
            fixed(vecs.shape),
            fixed(inner_bias.shape),
        ]
        + [fixed(ctx.shape) for ctx in ctxs]
        + [pl.BlockSpec(memory_space=pl.ANY)] * len(pieces),
        out_specs=(
            by_rows(width),
            by_rows(width),
            packed,
            by_rows(width),
            by_rows(width),
            by_rows(width),
            by_part(hidden_cols),
            by_part(hidden_cols),
            fixed((note_rows, room)),
        ),
        scratch_shapes=[
            pltpu.VMEM((parts, width, out_cols), BF16),
            pltpu.VMEM((parts, width, hidden_cols), BF16),
            pltpu.VMEM((parts, width, hidden_cols), BF16),
            pltpu.VMEM((parts, BLOCK, hidden_cols), F32),
            pltpu.VMEM((8, width), F32),
            pltpu.VMEM((parts, 1, hidden_cols), F32),
            pltpu.VMEM((note_rows, room), F32),
            pltpu.SemaphoreType.DMA((3, parts)),
        ],
        compiler_params=pltpu.CompilerParams(
            dimension_semantics=("arbitrary",), vmem_limit_bytes=VMEM_LIMIT
        ),
        cost_estimate=pl.CostEstimate(
            flops=2 * part_len * width * (8 * hidden_cols + 4 * out_cols) * parts,
            bytes_accessed=24 << 20,
            transcendentals=2 * part_len * hidden_cols * parts,
        ),
        name="dense_chain",
    )(place, rows_in, teacher, cotangent, valid, vecs, inner_bias, *ctxs, *pieces)


def dense_weights(
    plans, halves, place_ref, first_ref, branch_grad_ref, attn_grad_ref, act_ref, hidden_grad_ref, notes_ref,
    *refs
):
    ctx_refs, outs, (whole, sems) = refs[:halves], refs[halves:-2], refs[-2:]
    step = pl.program_id(0)
    slots = whole.shape[0]

    hidden_cols = act_ref.shape[2]
    whole[step, :, :hidden_cols] = dot(first_ref[...], hidden_grad_ref[0], TN).astype(BF16)
    whole[step, :, hidden_cols : 2 * hidden_cols] = dot(branch_grad_ref[...], act_ref[0], TN).astype(BF16)
    ctx = jnp.concatenate([unpack(ref[0]) for ref in ctx_refs], axis=0)
    plain = 2 * hidden_cols + ctx.shape[1]
    whole[step, :, 2 * hidden_cols : plain] = dot(attn_grad_ref[...], ctx, TN).astype(BF16)
    note_rows, room = notes_ref.shape
    for at in range(whole.shape[1] // note_rows):
        whole[step, at * note_rows : (at + 1) * note_rows, plain : plain + room] = notes_ref[...]
    for out, turns in zip(outs, plans):
        block = out.shape[1]
        for at, turn in enumerate(turns):
            offset = 0
            if block < whole.shape[1]:
                offset = pl.multiple_of((place_ref[place_ref.shape[0] - 1] ^ turn) * block, block)
            pltpu.make_async_copy(
                whole.at[step, pl.ds(offset, block), :], out.at[at * slots + step], sems.at[step]
            ).start()

    @pl.when(step == slots - 1)
    def _():
        for slot in range(slots):
            pltpu.make_async_copy(whole.at[slot], whole.at[slot], sems.at[slot]).wait()


def run_weights(base, slots, plans, place, notes, first, branch_grad, attn_grad, act, hidden_grad, ctxs):
    _, part_len, hidden_cols = act.shape
    width = first.shape[1]
    columns = 2 * hidden_cols + 3 * DH + notes.shape[1]
    fixed = pl.BlockSpec((part_len, width), lambda s, place: (0, 0))
    by_slot = pl.BlockSpec((1, part_len, hidden_cols), lambda s, place: (place[base + s], 0, 0))
    outs = tuple(
        jax.ShapeDtypeStruct((len(turns) * slots, block, columns), BF16) for block, turns in plans
    )
    return pl.pallas_call(
        functools.partial(dense_weights, tuple(turns for _, turns in plans), len(ctxs)),
        out_shape=outs,
        grid_spec=pltpu.PrefetchScalarGridSpec(
            num_scalar_prefetch=1,
            grid=(slots,),
            in_specs=[
                fixed,
                fixed,
                fixed,
                by_slot,
                by_slot,
                pl.BlockSpec(notes.shape, lambda s, place: (0, 0)),
            ]
            + [
                pl.BlockSpec((1,) + ctx.shape[1:], lambda s, place: (place[base + s], 0, 0)) for ctx in ctxs
            ],
            out_specs=tuple(pl.BlockSpec(memory_space=pl.ANY) for _ in outs),
            scratch_shapes=[
                pltpu.VMEM((slots, width, columns), BF16),
                pltpu.SemaphoreType.DMA((slots,)),
            ],
        ),
        compiler_params=pltpu.CompilerParams(
            dimension_semantics=("arbitrary",), vmem_limit_bytes=VMEM_LIMIT
        ),
        cost_estimate=pl.CostEstimate(
            flops=2 * part_len * width * columns * slots,
            bytes_accessed=5 * slots << 20,
            transcendentals=0,
        ),
        name="dense_weights",
    )(place, first, branch_grad, attn_grad, act, hidden_grad, notes, *ctxs)


def finish_dense(packed_ref, inner_ref, outer_ref, output_ref, notes_ref):
    hidden_cols = inner_ref.shape[1]
    summed = packed_ref[...].astype(F32)
    inner_ref[...] = summed[:, :hidden_cols]
    outer_ref[...] = summed[:, hidden_cols : 2 * hidden_cols]
    plain = 2 * hidden_cols + output_ref.shape[0]
    output_ref[...] = jnp.transpose(summed[:, 2 * hidden_cols : plain])
    notes_ref[...] = summed[:, plain:]


def run_finish_dense(packed, hidden_cols, head_cols):
    rows = packed.shape[0]
    return pl.pallas_call(
        finish_dense,
        out_shape=(
            jax.ShapeDtypeStruct((rows, hidden_cols), F32),
            jax.ShapeDtypeStruct((rows, hidden_cols), F32),
            jax.ShapeDtypeStruct((head_cols, rows), F32),
            jax.ShapeDtypeStruct((rows, packed.shape[1] - 2 * hidden_cols - head_cols), F32),
        ),
        name="finish_dense",
    )(packed)


def finish_heads(value_ref, *refs):
    summed = value_ref[...].astype(F32)
    heads = summed.shape[1] // SLAB
    for ref, which in zip(refs, (0, 2, 3, 1)):
        columns = [summed[:, SLAB * h + which * DH : SLAB * h + (which + 1) * DH] for h in range(heads)]
        ref[...] = jnp.concatenate(columns, axis=1)[: ref.shape[0]]


def run_finish_heads(value):
    rows, width = value.shape
    out = jax.ShapeDtypeStruct((rows, width // 4), F32)
    notes = jax.ShapeDtypeStruct((8, width // 4), F32)
    return pl.pallas_call(finish_heads, out_shape=(out, out, out, notes), name="finish_heads")(value)


def interleave(query, key, value, heads):
    rows = query.shape[0]
    parts = [part.reshape(rows, heads, 1, DH) for part in (query, jnp.zeros_like(query), key, value)]
    return jnp.concatenate(parts, axis=2).reshape(rows, heads * SLAB)


def swap(value, axis, bit):
    size = lax.axis_size(axis)
    return lax.ppermute(value, axis, [(i, i ^ bit) for i in range(size)])


def bits_of(axis):
    bit = 1
    while bit < lax.axis_size(axis):
        yield bit
        bit *= 2


def after(value, *others):
    return lax.optimization_barrier((value,) + others)[0]


def merge(held, other, axis, bit):
    mine_first = (lax.axis_index(axis) & bit) == 0
    return jnp.where(
        mine_first, jnp.concatenate([held, other], axis=0), jnp.concatenate([other, held], axis=0)
    )


def add_low(left_side, right_side):
    return (left_side.astype(F32) + right_side.astype(F32)).astype(BF16)


def add_halves(left_side, right_side):
    half = left_side.shape[0] // 2
    return (
        add_low(left_side[:half], right_side[:half]),
        add_low(left_side[half:], right_side[half:]),
    )


def scatter_rows(held):
    index = lax.axis_index("dp")
    for bit in bits_of("dp"):
        held = held.reshape((held.shape[0] // 2, 2) + held.shape[1:])
        own = (index & bit) // bit
        send = lax.dynamic_index_in_dim(held, 1 - own, 1, keepdims=False)
        keep = lax.dynamic_index_in_dim(held, own, 1, keepdims=False)
        held = add_low(keep, swap(send, "dp", bit))
    return held[0]


def local(
    inputs, segment_ids, valid_mask, teacher, cotangent,
    w_query, w_key, w_value, w_output, w_inner, w_outer,
    query_bias, value_bias, output_bias, inner_bias, outer_bias,
    gain_attn, shift_attn, gain_ffn, shift_ffn,
):
    _, part_len, width = inputs.shape
    parts = lax.axis_size("tensor")
    copies = lax.axis_size("dp")
    rank = lax.axis_index("tensor")
    total_tokens = part_len * parts * copies
    seq_len = part_len * parts
    head_cols = w_query.shape[1]
    heads = head_cols // DH
    hidden_cols = w_inner.shape[1]
    shard_rows = w_inner.shape[0]
    halves = part_len // BLOCK

    rows_in = inputs.reshape(part_len, width)
    tokens = lax.all_gather(rows_in, "tensor", axis=0, tiled=True)
    w_heads = interleave(w_query, w_key, w_value, heads)
    paired = shard_rows % 16 == 0 and parts == 4 and copies == 8

    valid_rows = valid_mask.astype(F32).reshape(part_len, 1)
    valid_count = jnp.sum(valid_mask.astype(F32))
    upper = jnp.floor(valid_count / 256.0)
    spot = lax.broadcasted_iota(jnp.int32, (shard_rows, DH), 0) * DH + lax.broadcasted_iota(
        jnp.int32, (shard_rows, DH), 1
    )
    count_row = jnp.where(spot == 0, upper, jnp.where(spot == 1, valid_count - 256.0 * upper, 0.0))
    mine = jnp.concatenate((w_inner, w_outer.T, w_output.T, count_row.astype(BF16)), axis=1)
    if paired:
        place = jnp.stack([rank, rank ^ 1, rank ^ 2, rank ^ 3, lax.axis_index("dp")]).astype(jnp.int32)
        pair = jnp.concatenate([mine[None], swap(mine[None], "tensor", 1)], axis=0)
        near = jnp.concatenate([pair, swap(pair, "dp", 2)], axis=0)
        turns = [0, 2, 4, 6]
        for bit in (1, 2, 4):
            w_heads = merge(w_heads, swap(w_heads, "dp", bit), "dp", bit)
        near, w_heads = lax.optimization_barrier((near, w_heads))
        near_next = swap(near, "dp", 4)
        tokens, pair, near_next = lax.optimization_barrier((tokens, pair, near_next))
        far = swap(pair, "tensor", 2)
    else:
        place = jnp.asarray(list(range(parts)) + [0], jnp.int32)
        weights = lax.all_gather(mine, ("tensor", "dp"), axis=0, tiled=False)
        for bit in bits_of("dp"):
            w_heads = merge(w_heads, swap(w_heads, "dp", bit), "dp", bit)

    mine_cols = rank * head_cols
    query_shift = lax.dynamic_slice_in_dim(query_bias, mine_cols, head_cols).astype(F32)
    value_shift = lax.dynamic_slice_in_dim(value_bias, mine_cols, head_cols).astype(F32)
    shifts = interleave(query_shift[None], jnp.zeros_like(query_shift)[None], value_shift[None], heads)
    qkv = [(dot(tokens, w_heads) + shifts).astype(BF16)]

    segment_row = segment_ids.reshape(seq_len)
    bounds = document_blocks(segment_row)
    seg_col = segment_row.reshape(seq_len, 1)
    seg_row = segment_row.reshape(1, seq_len)
    lane = rank.astype(jnp.int32).reshape(1)

    def exchange(packed_blocks):
        return lax.all_to_all(packed_blocks, "tensor", 0, 0)

    contexts, lses, arrived = [], [], []
    for half in range(halves):
        if paired and half == 1:
            far, contexts[0], bounds = lax.optimization_barrier((far, contexts[0], bounds))
            weights = lax.all_gather(far, "dp", axis=0, tiled=False)
        context, lse = run_forward((halves, half), lane, bounds, qkv, seg_col, seg_row)
        if half > 0:
            context, arrived[0] = lax.optimization_barrier((context, arrived[0]))
        contexts.append(context)
        lses.append(lse)
        arrived.append(exchange(context))
    if paired:
        near_next, context = lax.optimization_barrier((near_next, contexts[-1]))
        near = jnp.concatenate([near, near_next], axis=0)
        near_other = swap(near, "dp", 1)
    if paired:
        weights = weights.reshape((copies * 2,) + mine.shape)
        pieces = [near, near_other, weights]
        marks = [[(slot, turn ^ flip, True) for turn in turns for slot in (0, 1)] for flip in (0, 1)]
        marks.append([(2 + at % 2, at // 2, False) for at in range(2 * copies)])
    else:
        pieces = [weights.reshape(parts, width, -1)]
        marks = [[(t, 0, False) for t in range(parts)]]
    counts = [piece.reshape((-1,) + mine.shape)[:, 0, -DH : 2 - DH].astype(F32) for piece in pieces + [weights]]
    counts = jnp.concatenate(counts[:-1] if paired else counts[-1:], axis=0)
    counted = 256.0 * jnp.sum(counts[:, 0]) + jnp.sum(counts[:, 1])

    vecs = jnp.stack(
        (output_bias, gain_attn, shift_attn, outer_bias, gain_ffn, shift_ffn, outer_bias, outer_bias)
    ).astype(F32)
    inner_rows = inner_bias.astype(F32).reshape(parts, 1, hidden_cols)
    teacher_rows = teacher.reshape(part_len, width)
    cotangent_rows = cotangent.reshape(part_len, width)
    (
        layer_out, first_grad, context_grad, first, branch_grad, attn_grad, activated, hidden_grad, notes,
    ) = run_dense(
        shard_rows, marks, float(total_tokens), place, arrived, rows_in, teacher_rows, cotangent_rows, valid_rows, vecs,
        inner_rows, pieces,
    )
    head_grad = exchange(context_grad).reshape((parts * halves, PACKED, 2 * DH))
    sources = (first, branch_grad, attn_grad, activated, hidden_grad, arrived)
    if shard_rows % 16:
        notes = jnp.tile(notes, (copies, 1))
    if paired:
        keep_turns = (0, 4, 2, 6)
        (distant,) = run_weights(2, 2, ((width, (0,)),), place, notes, *sources)
        plans = tuple((shard_rows, tuple(turn | flip for turn in keep_turns)) for flip in (0, 1))
        keep, send = run_weights(0, 2, plans, place, notes, *sources)
        keep, send = (value.reshape((4, 2) + value.shape[1:]) for value in (keep, send))
        distant = lax.psum_scatter(distant, "dp", scatter_dimension=1, tiled=True)
        came = swap(send, "dp", 1)
    else:
        (packed,) = run_weights(0, parts, ((width, (0,)),), place, notes, *sources)
        packed = lax.psum_scatter(packed, "dp", scatter_dimension=1, tiled=True)

    joined_grad, sums = run_backward(lane, bounds, qkv, seg_col, seg_row, head_grad, contexts, lses)
    joined_grad = joined_grad.reshape(seq_len, -1)
    attn_back = dot(joined_grad, w_heads, NT).astype(BF16)
    if paired:
        came = after(came, attn_back)
    attn_back, sums, joined_grad = lax.optimization_barrier((attn_back, sums, joined_grad))
    attn_back = lax.psum_scatter(attn_back, "tensor", scatter_dimension=0, tiled=True)
    if paired:
        keep, send = add_halves(keep, came)
        keep, send, joined_grad = lax.optimization_barrier((keep, send, joined_grad))
        came = swap(send, "dp", 2)
    head_weights = dot(tokens, joined_grad, TN).reshape((copies, shard_rows, -1))
    if paired:
        came, head_weights = lax.optimization_barrier((came, head_weights))
        keep, send = add_halves(keep, came)
        keep, send, head_weights = lax.optimization_barrier((keep, send, head_weights))
        came = swap(send, "dp", 4)
    sums = sums.reshape(heads, 4, DH)
    sums = jnp.concatenate((sums[:, 0].reshape(1, head_cols), sums[:, 3].reshape(1, head_cols)), axis=1)
    for bit in bits_of("tensor"):
        sums = merge(sums, swap(sums, "tensor", bit), "tensor", bit)
    if paired:
        came, head_weights = lax.optimization_barrier((came, head_weights))
        slots = jnp.concatenate([add_low(keep, came)[0], distant], axis=0)
        packed = jnp.stack(
            [lax.dynamic_index_in_dim(slots, rank ^ t, 0, keepdims=False) for t in range(parts)]
        )
    packed = lax.psum_scatter(packed, "tensor", scatter_dimension=0, tiled=True)[0]
    biases = jnp.concatenate((sums[:, :head_cols].reshape(-1), sums[:, head_cols:].reshape(-1)))
    biases = jnp.pad(
        biases.reshape(8, heads, 1, DH), ((0, shard_rows - 8), (0, 0), (1, 2), (0, 0))
    ).reshape(1, shard_rows, -1)
    query_grad, key_grad, value_grad, biases = run_finish_heads(
        scatter_rows((head_weights + biases).astype(BF16))
    )
    biases = biases.reshape(2, width)
    input_grad = first_grad + attn_back.astype(F32)

    inner_grad, outer_grad, output_grad, notes = run_finish_dense(packed, hidden_cols, head_cols)
    notes = notes.reshape(-1)

    def total(which):
        return notes[which * width : (which + 1) * width]

    mse_loss = jnp.sum(total(0)) / (counted * width)
    return (
        layer_out.reshape(1, part_len, width),
        mse_loss,
        input_grad.reshape(1, part_len, width),
        query_grad,
        key_grad,
        value_grad,
        output_grad,
        inner_grad,
        outer_grad.T,
        biases[0],
        biases[1],
        total(4),
        notes[8 * width : 8 * width + hidden_cols * parts],
        total(1),
        total(5),
        total(6),
        total(2),
        total(3),
    )


def solution(mesh):
    shard = P("dp", "tensor", None)
    by_dp, by_tensor = P("dp", "tensor"), P("tensor", "dp")
    in_specs = (
        (shard, P("dp", None), by_dp, shard, shard)
        + (by_dp,) * 3
        + (by_tensor, by_dp, by_tensor)
        + (P(),) * 9
    )
    out_specs = (shard, P(), shard) + (by_dp,) * 3 + (by_tensor, by_dp, by_tensor) + (P(),) * 9
    return jax.shard_map(local, mesh=mesh, in_specs=in_specs, out_specs=out_specs, check_vma=False)
```

```python
import functools

import jax
import jax.numpy as jnp
from jax import lax
from jax.experimental import pallas as pl
from jax.experimental.pallas import tpu as pltpu
from jax.sharding import PartitionSpec as P

DH = 64
BLOCK = 256
SLAB = 4 * DH
EPSILON = 1e-12
ROOT_HALF = 0.7071067811865476
INV_ROOT_TAU = 0.3989422804014327
LOG2E = 1.4426950408889634
LN2 = 0.6931471805599453
SCALE = DH ** (-0.5)
MASKED = -1e30
VMEM_LIMIT = 60 << 20

BF16 = jnp.bfloat16
F32 = jnp.float32
NN = (((1,), (0,)), ((), ()))
NT = (((1,), (1,)), ((), ()))
TN = (((0,), (0,)), ((), ()))


def dot(left_side, right_side, dims=NN):
    return lax.dot_general(left_side, right_side, dims, preferred_element_type=F32)


def norm_forward(summed, gain_vec, shift_vec):
    average = jnp.mean(summed, axis=-1, keepdims=True)
    centered = summed - average
    variance = jnp.mean(centered * centered, axis=-1, keepdims=True)
    inverse = lax.rsqrt(variance + EPSILON)
    normed = centered * inverse
    return (normed * gain_vec + shift_vec, normed, inverse)


def norm_backward(upstream, normed, inverse, gain_vec):
    scaled = upstream * gain_vec
    first_mean = jnp.mean(scaled, axis=-1, keepdims=True)
    second_mean = jnp.mean(scaled * normed, axis=-1, keepdims=True)
    return inverse * (scaled - first_mean - normed * second_mean)


def column_sum(value):
    return jnp.sum(value, axis=0, keepdims=True)


def lane_is_right(rows):
    return lax.broadcasted_iota(jnp.int32, (rows, 2 * DH), 1) >= DH


def pack(first_two, third_top, third_bottom):
    return jnp.concatenate([first_two, jnp.concatenate([third_top, third_bottom], axis=1)], axis=0)


def unpack(packed):
    third = packed[BLOCK:]
    third = jnp.concatenate([third[:, :DH], third[:, DH:]], axis=0)
    return jnp.concatenate([packed[:BLOCK], third], axis=1)


def fetch_chunks(lane_ref, chunk_refs, target, sems):
    rows = chunk_refs[0].shape[0]
    copies = []
    for at, chunk in enumerate(chunk_refs):
        offset = pl.multiple_of(lax.rem(lane_ref[0] + at, len(chunk_refs)) * rows, rows)
        copies.append(pltpu.make_async_copy(chunk, target.at[pl.ds(offset, rows), :], sems.at[at]))
    return copies


def attend_forward(
    which, lane_ref, low_ref, count_ref, *refs
):
    chunk_refs, (seg_col_ref, seg_row_ref, ctx_ref, lse_ref, held, qkv_ref, sems) = refs[:-7], refs[-7:]
    heads = lse_ref.shape[0]

    @pl.when(pl.program_id(0) == 0)
    def _():
        copies = fetch_chunks(lane_ref, chunk_refs, qkv_ref, sems)
        for copy in copies:
            copy.start()
        for copy in copies:
            copy.wait()

    halves, half = which
    qb = pl.program_id(0) * halves + half
    rows = pl.ds(pl.multiple_of(qb * BLOCK, BLOCK), BLOCK)
    seg_q = seg_col_ref[...]
    queries = [
        qkv_ref[rows, SLAB * h : SLAB * h + 2 * DH] * jnp.asarray(SCALE, BF16) for h in range(heads)
    ]
    low, count = low_ref[qb], count_ref[qb]

    def score(kb, peaks):
        keys = pl.ds(pl.multiple_of(low * STEP + kb * BLOCK, STEP), BLOCK)
        allowed = seg_q == seg_row_ref[:, keys]
        found = []
        for h in range(heads):
            scores = dot(queries[h], qkv_ref[keys, SLAB * h + 2 * DH : SLAB * (h + 1)], NT)
            scores = jnp.where(allowed, scores, MASKED)
            held[h, kb] = scores
            found.append(jnp.maximum(peaks[h], jnp.maximum(scores[:, :128], scores[:, 128:])))
        return tuple(found)

    start = tuple(jnp.full((BLOCK, 128), MASKED, F32) for _ in range(heads))
    peaks = lax.fori_loop(0, count, score, start)
    highest = [jnp.max(peak, axis=-1, keepdims=True) for peak in peaks]

    def weigh(kb, carry):
        keys = pl.ds(pl.multiple_of(low * STEP + kb * BLOCK, STEP), BLOCK)
        found = []
        for h in range(heads):
            total, acc = carry[h]
            raised = jnp.exp2((held[h, kb] - highest[h]) * LOG2E)
            total = total + (raised[:, :128] + raised[:, 128:])
            acc = acc + dot(raised.astype(BF16), qkv_ref[keys, SLAB * h + 2 * DH : SLAB * (h + 1)])
            found.append((total, acc))
        return tuple(found)

    zero = jnp.zeros((BLOCK, 128), F32)
    done = lax.fori_loop(0, count, weigh, tuple((zero, zero) for _ in range(heads)))
    values = []
    for h in range(heads):
        total, acc = done[h]
        summed = jnp.sum(total, axis=-1, keepdims=True)
        values.append((acc / summed).astype(BF16))
        lse_ref[h] = jnp.transpose(highest[h] + jnp.log(summed))
    middle = BLOCK // 2
    ctx_ref[0, :BLOCK, :] = jnp.where(lane_is_right(BLOCK), values[1], pltpu.roll(values[0], DH, 1))
    ctx_ref[0, BLOCK:, :] = jnp.where(
        lane_is_right(middle), values[2][middle:], pltpu.roll(values[2][:middle], DH, 1)
    )


def attend_backward(halves, chunks, lane_ref, low_ref, count_ref, *refs):
    chunk_refs, refs = refs[:chunks], refs[chunks:]
    (seg_col_ref, seg_row_ref, grad_ref), refs = refs[:3], refs[3:]
    ctx_refs, lse_refs, refs = refs[:halves], refs[halves : 2 * halves], refs[2 * halves :]
    final_ref, sums_ref, dkv, out_ref, qkv_ref, sems = refs
    heads = dkv.shape[0]
    qb = pl.program_id(0)
    half = lax.rem(qb, halves)

    def choose(options):
        value = options[0][...]
        for other in range(1, halves):
            value = jnp.where(half == other, options[other][...], value)
        return value

    @pl.when(qb == 0)
    def _():
        copies = fetch_chunks(lane_ref, chunk_refs, qkv_ref, sems)
        for copy in copies:
            copy.start()
        dkv[...] = jnp.zeros_like(dkv)
        for copy in copies:
            copy.wait()

    rows = pl.ds(pl.multiple_of(qb * BLOCK, BLOCK), BLOCK)
    right = lane_is_right(BLOCK)
    arrived = grad_ref[0]
    product = arrived.astype(F32) * choose(ctx_refs)[0].astype(F32)
    upper = product.astype(BF16)
    lower = (product - upper.astype(F32)).astype(BF16)
    pick = (
        lax.broadcasted_iota(jnp.int32, (8, 2 * DH), 1) // DH
        == lax.broadcasted_iota(jnp.int32, (8, 2 * DH), 0)
    ).astype(BF16)
    summed = dot(pick, upper, NT) + dot(pick, lower, NT)
    deltas = [
        summed[0:1, :BLOCK],
        summed[1:2, :BLOCK],
        jnp.concatenate([summed[0:1, BLOCK:], summed[1:2, BLOCK:]], axis=1),
    ]
    two, third = arrived[:BLOCK], arrived[BLOCK:]
    placed = [
        pltpu.roll(two, DH, 1),
        two,
        jnp.concatenate([pltpu.roll(third, DH, 1), third], axis=0),
    ]
    grads = [jnp.where(right, grad, jnp.zeros_like(grad)) for grad in placed]
    queries, pairs = [], []
    for h in range(heads):
        queries.append(qkv_ref[rows, SLAB * h : SLAB * h + 2 * DH] * jnp.asarray(SCALE, BF16))
        pairs.append(jnp.concatenate([queries[h], grads[h]], axis=0))
    seg_q = seg_row_ref[...]
    lses = choose(lse_refs)
    low, count = low_ref[qb], count_ref[qb]

    def step(kb, accs):
        keys = pl.ds(pl.multiple_of(low * STEP + kb * BLOCK, STEP), BLOCK)
        allowed = seg_col_ref[keys, :] == seg_q
        keyed = [qkv_ref[keys, SLAB * h + 2 * DH : SLAB * (h + 1)] for h in range(heads)]
        raw = [dot(keyed[h], queries[h], NT) for h in range(heads)]
        probs_grads = [dot(keyed[h], grads[h], NT) for h in range(heads)]
        both = []
        for h in range(heads):
            probs = jnp.exp2((jnp.where(allowed, raw[h], MASKED) - lses[h]) * LOG2E)
            score_grad = (probs * (probs_grads[h] - deltas[h])).astype(BF16)
            both.append((score_grad, probs.astype(BF16)))
        found = []
        for h in range(heads):
            dkv[h, keys, :] += dot(jnp.concatenate(both[h], axis=1), pairs[h])
            found.append(accs[h] + dot(both[h][0], keyed[h], TN))
        return tuple(found)

    zero = jnp.zeros((BLOCK, 128), F32)
    accs = lax.fori_loop(0, count, step, tuple(zero for _ in range(heads)))
    for h in range(heads):
        query_grad = jnp.where(right, 0.0, accs[h] * SCALE).astype(BF16)
        out_ref[rows, SLAB * h : SLAB * h + 2 * DH] = query_grad

    @pl.when(qb == pl.num_programs(0) - 1)
    def _():
        for h in range(heads):
            at = SLAB * h
            out_ref[:, at + 2 * DH : at + SLAB] = dkv[h].astype(BF16)
            sums_ref[:, at : at + SLAB] = column_sum(out_ref[:, at : at + SLAB].astype(F32))
        rows_each = final_ref.shape[1]
        copies = []
        for at in range(final_ref.shape[0]):
            offset = pl.multiple_of(lax.rem(lane_ref[0] + at, final_ref.shape[0]) * rows_each, rows_each)
            copies.append(
                pltpu.make_async_copy(out_ref.at[pl.ds(offset, rows_each), :], final_ref.at[at], sems.at[at])
            )
        for copy in copies:
            copy.start()
        for copy in copies:
            copy.wait()


STEP = 128


def document_blocks(segment_row):
    starts = segment_row[::BLOCK]
    stops = segment_row[BLOCK - 1 :: BLOCK]
    low = jnp.sum((segment_row[None, :] < starts[:, None]).astype(jnp.int32), axis=1) // STEP
    high = jnp.sum((segment_row[None, :] <= stops[:, None]).astype(jnp.int32), axis=1)
    each = BLOCK // STEP
    count = (high - low * STEP + BLOCK - 1) // BLOCK
    return (jnp.minimum(low, segment_row.shape[0] // STEP - each * count), count)


PACKED = BLOCK + BLOCK // 2


def run_forward(which, lane, bounds, qkv, seg_col, seg_row):
    halves, half = which
    seq_len, width = seg_col.shape[0], qkv[0].shape[1]
    heads = width // SLAB
    blocks = seq_len // BLOCK
    steps = blocks // halves
    return pl.pallas_call(
        functools.partial(attend_forward, which),
        out_shape=(
            jax.ShapeDtypeStruct((steps, PACKED, 2 * DH), BF16),
            jax.ShapeDtypeStruct((heads, 1, steps * BLOCK), F32),
        ),
        grid_spec=pltpu.PrefetchScalarGridSpec(
            num_scalar_prefetch=3,
            grid=(steps,),
            in_specs=[pl.BlockSpec(memory_space=pl.ANY)] * len(qkv)
            + [
                pl.BlockSpec((BLOCK, 1), lambda q, *_: (q * halves + half, 0)),
                pl.BlockSpec((1, seq_len), lambda q, *_: (0, 0)),
            ],
            out_specs=(
                pl.BlockSpec((1, PACKED, 2 * DH), lambda q, *_: (q, 0, 0)),
                pl.BlockSpec((heads, 1, BLOCK), lambda q, *_: (0, 0, q)),
            ),
            scratch_shapes=[
                pltpu.VMEM((heads, blocks, BLOCK, BLOCK), F32),
                pltpu.VMEM((seq_len, width), BF16),
                pltpu.SemaphoreType.DMA((len(qkv),)),
            ],
        ),
        compiler_params=pltpu.CompilerParams(
            dimension_semantics=("arbitrary",), vmem_limit_bytes=28 << 20
        ),
        cost_estimate=pl.CostEstimate(
            flops=heads * seq_len * seq_len * 2048 * steps // blocks,
            bytes_accessed=5 << 20,
            transcendentals=heads * seq_len * seq_len // 3,
        ),
        name="attend_forward",
    )(lane, *bounds, *qkv, seg_col, seg_row)


def run_backward(lane, bounds, qkv, seg_col, seg_row, grad, ctxs, lses):
    seq_len, width = seg_col.shape[0], qkv[0].shape[1]
    heads = width // SLAB
    halves = len(ctxs)

    def fixed(shape):
        return pl.BlockSpec(shape, lambda q, *_: (0,) * len(shape))

    return pl.pallas_call(
        functools.partial(attend_backward, halves, len(qkv)),
        out_shape=(
            jax.ShapeDtypeStruct((len(qkv), seq_len // len(qkv), width), BF16),
            jax.ShapeDtypeStruct((1, width), F32),
        ),
        grid_spec=pltpu.PrefetchScalarGridSpec(
            num_scalar_prefetch=3,
            grid=(seq_len // BLOCK,),
            in_specs=[pl.BlockSpec(memory_space=pl.ANY)] * len(qkv)
            + [
                fixed((seq_len, 1)),
                pl.BlockSpec((1, BLOCK), lambda q, *_: (0, q)),
                pl.BlockSpec((1, PACKED, 2 * DH), lambda q, *_: (q, 0, 0)),
            ]
            + [pl.BlockSpec((1, PACKED, 2 * DH), lambda q, *_: (q // halves, 0, 0))] * halves
            + [pl.BlockSpec((heads, 1, BLOCK), lambda q, *_: (0, 0, q // halves))] * halves,
            out_specs=(pl.BlockSpec(memory_space=pl.ANY), fixed((1, width))),
            scratch_shapes=[
                pltpu.VMEM((heads, seq_len, 2 * DH), F32),
                pltpu.VMEM((seq_len, width), BF16),
                pltpu.VMEM((seq_len, width), BF16),
                pltpu.SemaphoreType.DMA((len(qkv),)),
            ],
        ),
        compiler_params=pltpu.CompilerParams(
            dimension_semantics=("arbitrary",), vmem_limit_bytes=28 << 20
        ),
        cost_estimate=pl.CostEstimate(
            flops=heads * seq_len * seq_len * 4096,
            bytes_accessed=10 << 20,
            transcendentals=heads * seq_len * seq_len // 3,
        ),
        name="attend_backward",
    )(lane, *bounds, *qkv, seg_col, seg_row, grad, *ctxs, *lses)


def dense_chain(
    marks, halves, total_tokens, place_ref, in_ref, teacher_ref, cotangent_ref, valid_ref, vec_ref,
    inner_bias_ref, *refs
):
    ctx_refs, refs = refs[:halves], refs[halves:]
    pieces = refs[: len(marks)]
    (
        layer_ref, first_grad_ref, ctx_grad_ref, first_ref, branch_grad_ref, attn_grad_ref,
        act_ref, hidden_grad_ref, notes_ref, w_out, w_in, w_up, slope, sums_ref, inner_sums_ref,
        gathered, sems,
    ) = refs[len(marks) :]
    parts, _, head_cols = w_out.shape
    hidden_cols = w_in.shape[2]
    index = place_ref[parts]
    step = pl.program_id(0)
    groups = (
        (2 * hidden_cols, head_cols, w_out),
        (0, hidden_cols, w_in),
        (hidden_cols, hidden_cols, w_up),
    )

    @pl.when(step == 0)
    def _():
        for group, (start, size, target) in enumerate(groups):
            for piece, marked in zip(pieces, marks):
                block = piece.shape[1]
                for at, (slot, turn, relative) in enumerate(marked):
                    offset = pl.multiple_of((index ^ turn) * block, block) if relative else turn * block
                    pltpu.make_async_copy(
                        piece.at[at, :, pl.ds(start, size)],
                        target.at[slot, pl.ds(offset, block), :],
                        sems.at[group, slot],
                    ).start()
        sums_ref[...] = jnp.zeros_like(sums_ref)
        inner_sums_ref[...] = jnp.zeros_like(inner_sums_ref)

    def context(t):
        value = ctx_refs[0][t]
        for half in range(1, halves):
            value = jnp.where(step == half, ctx_refs[half][t], value)
        return value

    def arrive(group, slot):
        whole = groups[group][2].at[slot]

        @pl.when(step == 0)
        def _():
            pltpu.make_async_copy(whole, whole, sems.at[group, slot]).wait()

    def vec(which):
        return vec_ref[which : which + 1, :]

    counts = jnp.zeros((1, 2 * DH), F32)

    attention = jnp.zeros(in_ref.shape, F32)
    for slot in range(parts):
        arrive(0, slot)
        counts = counts + column_sum(w_out[slot, :, 2 * DH :].astype(F32))
        attention = attention + dot(unpack(context(place_ref[slot])), w_out[slot, :, : 3 * DH], NT)
    first_exact, normed_one, inverse_one = norm_forward(
        in_ref[...].astype(F32) + attention + vec(0), vec(1), vec(2)
    )
    first = first_exact.astype(BF16)
    first_ref[...] = first

    def up(slot, branch):
        t = place_ref[slot]
        arrive(1, slot)
        hidden = dot(first, w_in[slot]) + inner_bias_ref[t]
        bend = 0.5 * (1.0 + lax.erf(hidden * ROOT_HALF))
        activated = (hidden * bend).astype(BF16)
        act_ref[t] = activated
        slope[slot] = bend + hidden * INV_ROOT_TAU * jnp.exp2(hidden * hidden * (-0.5 * LOG2E))
        arrive(2, slot)
        return branch + dot(activated, w_up[slot], NT)

    branch = jnp.zeros(in_ref.shape, F32)
    for slot in range(parts):
        branch = up(slot, branch)
    lanes = lax.broadcasted_iota(jnp.int32, counts.shape, 1)
    weight = jnp.where(lanes == DH, 256.0, jnp.where(lanes == DH + 1, 1.0, 0.0))
    ratio = total_tokens / jnp.sum(jnp.where(weight > 0.0, counts, 0.0) * weight, axis=-1, keepdims=True)
    layer_rows, normed_two, inverse_two = norm_forward(first.astype(F32) + branch + vec(3), vec(4), vec(5))
    layer_ref[...] = layer_rows.astype(BF16)
    misfit = layer_rows - teacher_ref[...].astype(F32)
    weighted = valid_ref[...] * misfit
    out_grad = cotangent_ref[...].astype(F32) + weighted * ratio
    second_grad = norm_backward(out_grad, normed_two, inverse_two, vec(4))
    branch_grad = second_grad.astype(BF16)
    branch_grad_ref[...] = branch_grad
    sums_ref[0:1, :] += column_sum(weighted * misfit)
    sums_ref[1:2, :] += column_sum(branch_grad.astype(F32))
    sums_ref[2:3, :] += column_sum(out_grad * normed_two)
    sums_ref[3:4, :] += column_sum(out_grad)

    def down(slot, back):
        t = place_ref[slot]
        hidden_grad = (dot(branch_grad, w_up[slot]) * slope[slot]).astype(BF16)
        hidden_grad_ref[t] = hidden_grad
        inner_sums_ref[t] += column_sum(hidden_grad.astype(F32))
        return back + dot(hidden_grad, w_in[slot], NT)

    upstream = second_grad
    for slot in range(parts):
        upstream = down(slot, upstream)
    first_grad = norm_backward(upstream, normed_one, inverse_one, vec(1))
    first_grad_ref[...] = first_grad
    attn_grad = first_grad.astype(BF16)
    attn_grad_ref[...] = attn_grad
    sums_ref[4:5, :] += column_sum(attn_grad.astype(F32))
    sums_ref[5:6, :] += column_sum(upstream * normed_one)
    sums_ref[6:7, :] += column_sum(upstream)
    middle = BLOCK // 2
    for slot in range(parts):
        back = dot(attn_grad, w_out[slot, :, : 3 * DH]).astype(BF16)
        ctx_grad_ref[place_ref[slot], 0] = pack(
            back[:, : 2 * DH], back[:middle, 2 * DH :], back[middle:, 2 * DH :]
        )


    @pl.when(step == pl.num_programs(0) - 1)
    def _():
        lanes = 2 * DH
        gathered[...] = jnp.zeros_like(gathered)
        rows_each, inner_rows = width_of(sums_ref) // lanes, width_of(inner_sums_ref) // lanes
        per_note = gathered.shape[1] // lanes

        def put(at, value):
            gathered[at // per_note : at // per_note + 1, pl.ds(at % per_note * lanes, lanes)] = value

        for row in range(sums_ref.shape[0]):
            for k in range(rows_each):
                put(row * rows_each + k, sums_ref[row : row + 1, k * lanes : (k + 1) * lanes])
        for t in range(parts):
            for k in range(inner_rows):
                put(
                    sums_ref.shape[0] * rows_each + t * inner_rows + k,
                    inner_sums_ref[t, :, k * lanes : (k + 1) * lanes],
                )
        notes_ref[...] = gathered[...].astype(BF16)


def width_of(ref):
    return ref.shape[-1]


def run_dense(note_rows, marks, total_tokens, place, ctxs, rows_in, teacher, cotangent, valid, vecs, inner_bias, pieces):
    halves, parts = len(ctxs), ctxs[0].shape[0]
    part_len, width = rows_in.shape
    hidden_cols = inner_bias.shape[2]
    out_cols = pieces[0].shape[2] - 2 * hidden_cols
    room = -(-(8 * width + parts * hidden_cols) // (note_rows * 2 * DH)) * 2 * DH

    def by_rows(columns):
        return pl.BlockSpec((BLOCK, columns), lambda i: (i, 0))

    def by_part(columns):
        return pl.BlockSpec((parts, BLOCK, columns), lambda i: (0, i, 0))

    def fixed(shape):
        return pl.BlockSpec(shape, lambda i: (0,) * len(shape))

    packed_shape = (parts, halves) + ctxs[0].shape[1:]
    packed = pl.BlockSpec((parts, 1) + packed_shape[2:], lambda i: (0, i, 0, 0))
    low = jax.ShapeDtypeStruct((part_len, width), BF16)
    wide = jax.ShapeDtypeStruct((parts, part_len, hidden_cols), BF16)
    smem = pl.BlockSpec(memory_space=pltpu.SMEM)
    return pl.pallas_call(
        functools.partial(dense_chain, marks, halves, total_tokens),
        out_shape=(
            low,
            jax.ShapeDtypeStruct((part_len, width), F32),
            jax.ShapeDtypeStruct(packed_shape, BF16),
            low,
            low,
            low,
            wide,
            wide,
            jax.ShapeDtypeStruct((note_rows, room), BF16),
        ),
        grid=(halves,),
        in_specs=[
            smem,
            by_rows(width),
            by_rows(width),
            by_rows(width),
            by_rows(1),
            fixed(vecs.shape),
            fixed(inner_bias.shape),
        ]
        + [fixed(ctx.shape) for ctx in ctxs]
        + [pl.BlockSpec(memory_space=pl.ANY)] * len(pieces),
        out_specs=(
            by_rows(width),
            by_rows(width),
            packed,
            by_rows(width),
            by_rows(width),
            by_rows(width),
            by_part(hidden_cols),
            by_part(hidden_cols),
            fixed((note_rows, room)),
        ),
        scratch_shapes=[
            pltpu.VMEM((parts, width, out_cols), BF16),
            pltpu.VMEM((parts, width, hidden_cols), BF16),
            pltpu.VMEM((parts, width, hidden_cols), BF16),
            pltpu.VMEM((parts, BLOCK, hidden_cols), F32),
            pltpu.VMEM((8, width), F32),
            pltpu.VMEM((parts, 1, hidden_cols), F32),
            pltpu.VMEM((note_rows, room), F32),
            pltpu.SemaphoreType.DMA((3, parts)),
        ],
        compiler_params=pltpu.CompilerParams(
            dimension_semantics=("arbitrary",), vmem_limit_bytes=VMEM_LIMIT
        ),
        cost_estimate=pl.CostEstimate(
            flops=2 * part_len * width * (8 * hidden_cols + 4 * out_cols) * parts,
            bytes_accessed=24 << 20,
            transcendentals=2 * part_len * hidden_cols * parts,
        ),
        name="dense_chain",
    )(place, rows_in, teacher, cotangent, valid, vecs, inner_bias, *ctxs, *pieces)


def dense_weights(
    plans, halves, place_ref, first_ref, branch_grad_ref, attn_grad_ref, act_ref, hidden_grad_ref, notes_ref,
    *refs
):
    ctx_refs, outs, (whole, sems) = refs[:halves], refs[halves:-2], refs[-2:]
    step = pl.program_id(0)
    slots = whole.shape[0]

    hidden_cols = act_ref.shape[2]
    whole[step, :, :hidden_cols] = dot(first_ref[...], hidden_grad_ref[0], TN).astype(BF16)
    whole[step, :, hidden_cols : 2 * hidden_cols] = dot(branch_grad_ref[...], act_ref[0], TN).astype(BF16)
    ctx = jnp.concatenate([unpack(ref[0]) for ref in ctx_refs], axis=0)
    plain = 2 * hidden_cols + ctx.shape[1]
    whole[step, :, 2 * hidden_cols : plain] = dot(attn_grad_ref[...], ctx, TN).astype(BF16)
    note_rows, room = notes_ref.shape
    for at in range(whole.shape[1] // note_rows):
        whole[step, at * note_rows : (at + 1) * note_rows, plain : plain + room] = notes_ref[...]
    for out, turns in zip(outs, plans):
        block = out.shape[1]
        for at, turn in enumerate(turns):
            offset = 0
            if block < whole.shape[1]:
                offset = pl.multiple_of((place_ref[place_ref.shape[0] - 1] ^ turn) * block, block)
            pltpu.make_async_copy(
                whole.at[step, pl.ds(offset, block), :], out.at[at * slots + step], sems.at[step]
            ).start()

    @pl.when(step == slots - 1)
    def _():
        for slot in range(slots):
            pltpu.make_async_copy(whole.at[slot], whole.at[slot], sems.at[slot]).wait()


def run_weights(base, slots, plans, place, notes, first, branch_grad, attn_grad, act, hidden_grad, ctxs):
    _, part_len, hidden_cols = act.shape
    width = first.shape[1]
    columns = 2 * hidden_cols + 3 * DH + notes.shape[1]
    fixed = pl.BlockSpec((part_len, width), lambda s, place: (0, 0))
    by_slot = pl.BlockSpec((1, part_len, hidden_cols), lambda s, place: (place[base + s], 0, 0))
    outs = tuple(
        jax.ShapeDtypeStruct((len(turns) * slots, block, columns), BF16) for block, turns in plans
    )
    return pl.pallas_call(
        functools.partial(dense_weights, tuple(turns for _, turns in plans), len(ctxs)),
        out_shape=outs,
        grid_spec=pltpu.PrefetchScalarGridSpec(
            num_scalar_prefetch=1,
            grid=(slots,),
            in_specs=[
                fixed,
                fixed,
                fixed,
                by_slot,
                by_slot,
                pl.BlockSpec(notes.shape, lambda s, place: (0, 0)),
            ]
            + [
                pl.BlockSpec((1,) + ctx.shape[1:], lambda s, place: (place[base + s], 0, 0)) for ctx in ctxs
            ],
            out_specs=tuple(pl.BlockSpec(memory_space=pl.ANY) for _ in outs),
            scratch_shapes=[
                pltpu.VMEM((slots, width, columns), BF16),
                pltpu.SemaphoreType.DMA((slots,)),
            ],
        ),
        compiler_params=pltpu.CompilerParams(
            dimension_semantics=("arbitrary",), vmem_limit_bytes=VMEM_LIMIT
        ),
        cost_estimate=pl.CostEstimate(
            flops=2 * part_len * width * columns * slots,
            bytes_accessed=5 * slots << 20,
            transcendentals=0,
        ),
        name="dense_weights",
    )(place, first, branch_grad, attn_grad, act, hidden_grad, notes, *ctxs)


def finish_dense(packed_ref, inner_ref, outer_ref, output_ref, notes_ref):
    hidden_cols = inner_ref.shape[1]
    summed = packed_ref[...].astype(F32)
    inner_ref[...] = summed[:, :hidden_cols]
    outer_ref[...] = summed[:, hidden_cols : 2 * hidden_cols]
    plain = 2 * hidden_cols + output_ref.shape[0]
    output_ref[...] = jnp.transpose(summed[:, 2 * hidden_cols : plain])
    notes_ref[...] = summed[:, plain:]


def run_finish_dense(packed, hidden_cols, head_cols):
    rows = packed.shape[0]
    return pl.pallas_call(
        finish_dense,
        out_shape=(
            jax.ShapeDtypeStruct((rows, hidden_cols), F32),
            jax.ShapeDtypeStruct((rows, hidden_cols), F32),
            jax.ShapeDtypeStruct((head_cols, rows), F32),
            jax.ShapeDtypeStruct((rows, packed.shape[1] - 2 * hidden_cols - head_cols), F32),
        ),
        name="finish_dense",
    )(packed)


def finish_heads(value_ref, *refs):
    summed = value_ref[...].astype(F32)
    heads = summed.shape[1] // SLAB
    for ref, which in zip(refs, (0, 2, 3, 1)):
        columns = [summed[:, SLAB * h + which * DH : SLAB * h + (which + 1) * DH] for h in range(heads)]
        ref[...] = jnp.concatenate(columns, axis=1)[: ref.shape[0]]


def run_finish_heads(value):
    rows, width = value.shape
    out = jax.ShapeDtypeStruct((rows, width // 4), F32)
    notes = jax.ShapeDtypeStruct((8, width // 4), F32)
    return pl.pallas_call(finish_heads, out_shape=(out, out, out, notes), name="finish_heads")(value)


def interleave(query, key, value, heads):
    rows = query.shape[0]
    parts = [part.reshape(rows, heads, 1, DH) for part in (query, jnp.zeros_like(query), key, value)]
    return jnp.concatenate(parts, axis=2).reshape(rows, heads * SLAB)


def swap(value, axis, bit):
    size = lax.axis_size(axis)
    return lax.ppermute(value, axis, [(i, i ^ bit) for i in range(size)])


def bits_of(axis):
    bit = 1
    while bit < lax.axis_size(axis):
        yield bit
        bit *= 2


def after(value, *others):
    return lax.optimization_barrier((value,) + others)[0]


def merge(held, other, axis, bit):
    mine_first = (lax.axis_index(axis) & bit) == 0
    return jnp.where(
        mine_first, jnp.concatenate([held, other], axis=0), jnp.concatenate([other, held], axis=0)
    )


def add_low(left_side, right_side):
    return (left_side.astype(F32) + right_side.astype(F32)).astype(BF16)


def add_halves(left_side, right_side):
    half = left_side.shape[0] // 2
    return (
        add_low(left_side[:half], right_side[:half]),
        add_low(left_side[half:], right_side[half:]),
    )


def scatter_rows(held):
    index = lax.axis_index("dp")
    for bit in bits_of("dp"):
        held = held.reshape((held.shape[0] // 2, 2) + held.shape[1:])
        own = (index & bit) // bit
        send = lax.dynamic_index_in_dim(held, 1 - own, 1, keepdims=False)
        keep = lax.dynamic_index_in_dim(held, own, 1, keepdims=False)
        held = add_low(keep, swap(send, "dp", bit))
    return held[0]


def local(
    inputs, segment_ids, valid_mask, teacher, cotangent,
    w_query, w_key, w_value, w_output, w_inner, w_outer,
    query_bias, value_bias, output_bias, inner_bias, outer_bias,
    gain_attn, shift_attn, gain_ffn, shift_ffn,
):
    _, part_len, width = inputs.shape
    parts = lax.axis_size("tensor")
    copies = lax.axis_size("dp")
    rank = lax.axis_index("tensor")
    total_tokens = part_len * parts * copies
    seq_len = part_len * parts
    head_cols = w_query.shape[1]
    heads = head_cols // DH
    hidden_cols = w_inner.shape[1]
    shard_rows = w_inner.shape[0]
    halves = part_len // BLOCK

    rows_in = inputs.reshape(part_len, width)
    tokens = lax.all_gather(rows_in, "tensor", axis=0, tiled=True)
    w_heads = interleave(w_query, w_key, w_value, heads)
    paired = shard_rows % 16 == 0 and parts == 4 and copies == 8

    valid_rows = valid_mask.astype(F32).reshape(part_len, 1)
    valid_count = jnp.sum(valid_mask.astype(F32))
    upper = jnp.floor(valid_count / 256.0)
    spot = lax.broadcasted_iota(jnp.int32, (shard_rows, DH), 0) * DH + lax.broadcasted_iota(
        jnp.int32, (shard_rows, DH), 1
    )
    count_row = jnp.where(spot == 0, upper, jnp.where(spot == 1, valid_count - 256.0 * upper, 0.0))
    mine = jnp.concatenate((w_inner, w_outer.T, w_output.T, count_row.astype(BF16)), axis=1)
    if paired:
        place = jnp.stack([rank, rank ^ 1, rank ^ 2, rank ^ 3, lax.axis_index("dp")]).astype(jnp.int32)
        pair = jnp.concatenate([mine[None], swap(mine[None], "tensor", 1)], axis=0)
        near = jnp.concatenate([pair, swap(pair, "dp", 2)], axis=0)
        turns = [0, 2, 4, 6]
        for bit in (1, 2, 4):
            w_heads = merge(w_heads, swap(w_heads, "dp", bit), "dp", bit)
        near, w_heads = lax.optimization_barrier((near, w_heads))
        near_next = swap(near, "dp", 4)
        tokens, pair, near_next = lax.optimization_barrier((tokens, pair, near_next))
        far = swap(pair, "tensor", 2)
    else:
        place = jnp.asarray(list(range(parts)) + [0], jnp.int32)
        weights = lax.all_gather(mine, ("tensor", "dp"), axis=0, tiled=False)
        for bit in bits_of("dp"):
            w_heads = merge(w_heads, swap(w_heads, "dp", bit), "dp", bit)

    mine_cols = rank * head_cols
    query_shift = lax.dynamic_slice_in_dim(query_bias, mine_cols, head_cols).astype(F32)
    value_shift = lax.dynamic_slice_in_dim(value_bias, mine_cols, head_cols).astype(F32)
    shifts = interleave(query_shift[None], jnp.zeros_like(query_shift)[None], value_shift[None], heads)
    qkv = [(dot(tokens, w_heads) + shifts).astype(BF16)]

    segment_row = segment_ids.reshape(seq_len)
    bounds = document_blocks(segment_row)
    seg_col = segment_row.reshape(seq_len, 1)
    seg_row = segment_row.reshape(1, seq_len)
    lane = rank.astype(jnp.int32).reshape(1)

    def exchange(packed_blocks):
        return lax.all_to_all(packed_blocks, "tensor", 0, 0)

    contexts, lses, arrived = [], [], []
    for half in range(halves):
        if paired and half == 1:
            far, contexts[0], bounds = lax.optimization_barrier((far, contexts[0], bounds))
            weights = lax.all_gather(far, "dp", axis=0, tiled=False)
        context, lse = run_forward((halves, half), lane, bounds, qkv, seg_col, seg_row)
        if half > 0:
            context, arrived[0] = lax.optimization_barrier((context, arrived[0]))
        contexts.append(context)
        lses.append(lse)
        arrived.append(exchange(context))
    if paired:
        near_next, context = lax.optimization_barrier((near_next, contexts[-1]))
        near = jnp.concatenate([near, near_next], axis=0)
        near_other = swap(near, "dp", 1)
    if paired:
        weights = weights.reshape((copies * 2,) + mine.shape)
        pieces = [near, near_other, weights]
        marks = [[(slot, turn ^ flip, True) for turn in turns for slot in (0, 1)] for flip in (0, 1)]
        marks.append([(2 + at % 2, at // 2, False) for at in range(2 * copies)])
    else:
        pieces = [weights.reshape(parts, width, -1)]
        marks = [[(t, 0, False) for t in range(parts)]]
    counts = [piece.reshape((-1,) + mine.shape)[:, 0, -DH : 2 - DH].astype(F32) for piece in pieces + [weights]]
    counts = jnp.concatenate(counts[:-1] if paired else counts[-1:], axis=0)
    counted = 256.0 * jnp.sum(counts[:, 0]) + jnp.sum(counts[:, 1])

    vecs = jnp.stack(
        (output_bias, gain_attn, shift_attn, outer_bias, gain_ffn, shift_ffn, outer_bias, outer_bias)
    ).astype(F32)
    inner_rows = inner_bias.astype(F32).reshape(parts, 1, hidden_cols)
    teacher_rows = teacher.reshape(part_len, width)
    cotangent_rows = cotangent.reshape(part_len, width)
    (
        layer_out, first_grad, context_grad, first, branch_grad, attn_grad, activated, hidden_grad, notes,
    ) = run_dense(
        shard_rows, marks, float(total_tokens), place, arrived, rows_in, teacher_rows, cotangent_rows, valid_rows, vecs,
        inner_rows, pieces,
    )
    head_grad = exchange(context_grad).reshape((parts * halves, PACKED, 2 * DH))
    sources = (first, branch_grad, attn_grad, activated, hidden_grad, arrived)
    if shard_rows % 16:
        notes = jnp.tile(notes, (copies, 1))
    if paired:
        keep_turns = (0, 4, 2, 6)
        (distant,) = run_weights(2, 2, ((width, (0,)),), place, notes, *sources)
        plans = tuple((shard_rows, tuple(turn | flip for turn in keep_turns)) for flip in (0, 1))
        keep, send = run_weights(0, 2, plans, place, notes, *sources)
        keep, send = (value.reshape((4, 2) + value.shape[1:]) for value in (keep, send))
        distant = lax.psum_scatter(distant, "dp", scatter_dimension=1, tiled=True)
        came = swap(send, "dp", 1)
    else:
        (packed,) = run_weights(0, parts, ((width, (0,)),), place, notes, *sources)
        packed = lax.psum_scatter(packed, "dp", scatter_dimension=1, tiled=True)

    joined_grad, sums = run_backward(lane, bounds, qkv, seg_col, seg_row, head_grad, contexts, lses)
    joined_grad = joined_grad.reshape(seq_len, -1)
    attn_back = dot(joined_grad, w_heads, NT).astype(BF16)
    if paired:
        came = after(came, attn_back)
    attn_back, sums, joined_grad = lax.optimization_barrier((attn_back, sums, joined_grad))
    attn_back = lax.psum_scatter(attn_back, "tensor", scatter_dimension=0, tiled=True)
    if paired:
        keep, send = add_halves(keep, came)
        keep, send, joined_grad = lax.optimization_barrier((keep, send, joined_grad))
        came = swap(send, "dp", 2)
    head_weights = dot(tokens, joined_grad, TN).reshape((copies, shard_rows, -1))
    if paired:
        came, head_weights = lax.optimization_barrier((came, head_weights))
        keep, send = add_halves(keep, came)
        keep, send, head_weights = lax.optimization_barrier((keep, send, head_weights))
        came = swap(send, "dp", 4)
    sums = sums.reshape(heads, 4, DH)
    sums = jnp.concatenate((sums[:, 0].reshape(1, head_cols), sums[:, 3].reshape(1, head_cols)), axis=1)
    for bit in bits_of("tensor"):
        sums = merge(sums, swap(sums, "tensor", bit), "tensor", bit)
    if paired:
        came, head_weights = lax.optimization_barrier((came, head_weights))
        slots = jnp.concatenate([add_low(keep, came)[0], distant], axis=0)
        packed = jnp.stack(
            [lax.dynamic_index_in_dim(slots, rank ^ t, 0, keepdims=False) for t in range(parts)]
        )
    packed = lax.psum_scatter(packed, "tensor", scatter_dimension=0, tiled=True)[0]
    biases = jnp.concatenate((sums[:, :head_cols].reshape(-1), sums[:, head_cols:].reshape(-1)))
    biases = jnp.pad(
        biases.reshape(8, heads, 1, DH), ((0, shard_rows - 8), (0, 0), (1, 2), (0, 0))
    ).reshape(1, shard_rows, -1)
    query_grad, key_grad, value_grad, biases = run_finish_heads(
        scatter_rows((head_weights + biases).astype(BF16))
    )
    biases = biases.reshape(2, width)
    input_grad = first_grad + attn_back.astype(F32)

    inner_grad, outer_grad, output_grad, notes = run_finish_dense(packed, hidden_cols, head_cols)
    notes = notes.reshape(-1)

    def total(which):
        return notes[which * width : (which + 1) * width]

    mse_loss = jnp.sum(total(0)) / (counted * width)
    return (
        layer_out.reshape(1, part_len, width),
        mse_loss,
        input_grad.reshape(1, part_len, width),
        query_grad,
        key_grad,
        value_grad,
        output_grad,
        inner_grad,
        outer_grad.T,
        biases[0],
        biases[1],
        total(4),
        notes[8 * width : 8 * width + hidden_cols * parts],
        total(1),
        total(5),
        total(6),
        total(2),
        total(3),
    )


def solution(mesh):
    shard = P("dp", "tensor", None)
    by_dp, by_tensor = P("dp", "tensor"), P("tensor", "dp")
    in_specs = (
        (shard, P("dp", None), by_dp, shard, shard)
        + (by_dp,) * 3
        + (by_tensor, by_dp, by_tensor)
        + (P(),) * 9
    )
    out_specs = (shard, P(), shard) + (by_dp,) * 3 + (by_tensor, by_dp, by_tensor) + (P(),) * 9
    return jax.shard_map(local, mesh=mesh, in_specs=in_specs, out_specs=out_specs, check_vma=False)
```

```python
import functools

import jax
import jax.numpy as jnp
from jax import lax
from jax.experimental import pallas as pl
from jax.experimental.pallas import tpu as pltpu
from jax.sharding import PartitionSpec as P

DH = 64
BLOCK = 256
SLAB = 4 * DH
EPSILON = 1e-12
ROOT_HALF = 0.7071067811865476
INV_ROOT_TAU = 0.3989422804014327
LOG2E = 1.4426950408889634
LN2 = 0.6931471805599453
SCALE = DH ** (-0.5)
MASKED = -1e30
VMEM_LIMIT = 60 << 20

BF16 = jnp.bfloat16
F32 = jnp.float32
NN = (((1,), (0,)), ((), ()))
NT = (((1,), (1,)), ((), ()))
TN = (((0,), (0,)), ((), ()))


def dot(left_side, right_side, dims=NN):
    return lax.dot_general(left_side, right_side, dims, preferred_element_type=F32)


def norm_forward(summed, gain_vec, shift_vec):
    average = jnp.mean(summed, axis=-1, keepdims=True)
    centered = summed - average
    variance = jnp.mean(centered * centered, axis=-1, keepdims=True)
    inverse = lax.rsqrt(variance + EPSILON)
    normed = centered * inverse
    return (normed * gain_vec + shift_vec, normed, inverse)


def norm_backward(upstream, normed, inverse, gain_vec):
    scaled = upstream * gain_vec
    first_mean = jnp.mean(scaled, axis=-1, keepdims=True)
    second_mean = jnp.mean(scaled * normed, axis=-1, keepdims=True)
    return inverse * (scaled - first_mean - normed * second_mean)


def column_sum(value):
    return jnp.sum(value, axis=0, keepdims=True)


def lane_is_right(rows):
    return lax.broadcasted_iota(jnp.int32, (rows, 2 * DH), 1) >= DH


def pack(first_two, third_top, third_bottom):
    return jnp.concatenate([first_two, jnp.concatenate([third_top, third_bottom], axis=1)], axis=0)


def unpack(packed):
    third = packed[BLOCK:]
    third = jnp.concatenate([third[:, :DH], third[:, DH:]], axis=0)
    return jnp.concatenate([packed[:BLOCK], third], axis=1)


def fetch_chunks(lane_ref, chunk_refs, target, sems):
    rows = chunk_refs[0].shape[0]
    copies = []
    for at, chunk in enumerate(chunk_refs):
        offset = pl.multiple_of(lax.rem(lane_ref[0] + at, len(chunk_refs)) * rows, rows)
        copies.append(pltpu.make_async_copy(chunk, target.at[pl.ds(offset, rows), :], sems.at[at]))
    return copies


def attend_forward(
    which, lane_ref, low_ref, count_ref, *refs
):
    chunk_refs, (seg_col_ref, seg_row_ref, ctx_ref, lse_ref, held, qkv_ref, sems) = refs[:-7], refs[-7:]
    heads = lse_ref.shape[0]

    @pl.when(pl.program_id(0) == 0)
    def _():
        copies = fetch_chunks(lane_ref, chunk_refs, qkv_ref, sems)
        for copy in copies:
            copy.start()
        for copy in copies:
            copy.wait()

    halves, half = which
    qb = pl.program_id(0) * halves + half
    rows = pl.ds(pl.multiple_of(qb * BLOCK, BLOCK), BLOCK)
    seg_q = seg_col_ref[...]
    queries = [
        qkv_ref[rows, SLAB * h : SLAB * h + 2 * DH] * jnp.asarray(SCALE, BF16) for h in range(heads)
    ]
    low, count = low_ref[qb], count_ref[qb]

    def score(kb, peaks):
        keys = pl.ds(pl.multiple_of(low * STEP + kb * BLOCK, STEP), BLOCK)
        allowed = seg_q == seg_row_ref[:, keys]
        found = []
        for h in range(heads):
            scores = dot(queries[h], qkv_ref[keys, SLAB * h + 2 * DH : SLAB * (h + 1)], NT)
            scores = jnp.where(allowed, scores, MASKED)
            held[h, kb] = scores
            found.append(jnp.maximum(peaks[h], jnp.maximum(scores[:, :128], scores[:, 128:])))
        return tuple(found)

    start = tuple(jnp.full((BLOCK, 128), MASKED, F32) for _ in range(heads))
    peaks = lax.fori_loop(0, count, score, start)
    highest = [jnp.max(peak, axis=-1, keepdims=True) for peak in peaks]

    def weigh(kb, carry):
        keys = pl.ds(pl.multiple_of(low * STEP + kb * BLOCK, STEP), BLOCK)
        found = []
        for h in range(heads):
            total, acc = carry[h]
            raised = jnp.exp2((held[h, kb] - highest[h]) * LOG2E)
            total = total + (raised[:, :128] + raised[:, 128:])
            acc = acc + dot(raised.astype(BF16), qkv_ref[keys, SLAB * h + 2 * DH : SLAB * (h + 1)])
            found.append((total, acc))
        return tuple(found)

    zero = jnp.zeros((BLOCK, 128), F32)
    done = lax.fori_loop(0, count, weigh, tuple((zero, zero) for _ in range(heads)))
    values = []
    for h in range(heads):
        total, acc = done[h]
        summed = jnp.sum(total, axis=-1, keepdims=True)
        values.append((acc / summed).astype(BF16))
        lse_ref[h] = jnp.transpose(highest[h] + jnp.log(summed))
    middle = BLOCK // 2
    ctx_ref[0, :BLOCK, :] = jnp.where(lane_is_right(BLOCK), values[1], pltpu.roll(values[0], DH, 1))
    ctx_ref[0, BLOCK:, :] = jnp.where(
        lane_is_right(middle), values[2][middle:], pltpu.roll(values[2][:middle], DH, 1)
    )


def attend_backward(halves, chunks, lane_ref, low_ref, count_ref, *refs):
    chunk_refs, refs = refs[:chunks], refs[chunks:]
    (seg_col_ref, seg_row_ref, grad_ref), refs = refs[:3], refs[3:]
    ctx_refs, lse_refs, refs = refs[:halves], refs[halves : 2 * halves], refs[2 * halves :]
    final_ref, sums_ref, dkv, out_ref, qkv_ref, sems = refs
    heads = dkv.shape[0]
    qb = pl.program_id(0)
    half = lax.rem(qb, halves)

    def choose(options):
        value = options[0][...]
        for other in range(1, halves):
            value = jnp.where(half == other, options[other][...], value)
        return value

    @pl.when(qb == 0)
    def _():
        copies = fetch_chunks(lane_ref, chunk_refs, qkv_ref, sems)
        for copy in copies:
            copy.start()
        dkv[...] = jnp.zeros_like(dkv)
        for copy in copies:
            copy.wait()

    rows = pl.ds(pl.multiple_of(qb * BLOCK, BLOCK), BLOCK)
    right = lane_is_right(BLOCK)
    arrived = grad_ref[0]
    product = arrived.astype(F32) * choose(ctx_refs)[0].astype(F32)
    upper = product.astype(BF16)
    lower = (product - upper.astype(F32)).astype(BF16)
    pick = (
        lax.broadcasted_iota(jnp.int32, (8, 2 * DH), 1) // DH
        == lax.broadcasted_iota(jnp.int32, (8, 2 * DH), 0)
    ).astype(BF16)
    summed = dot(pick, upper, NT) + dot(pick, lower, NT)
    deltas = [
        summed[0:1, :BLOCK],
        summed[1:2, :BLOCK],
        jnp.concatenate([summed[0:1, BLOCK:], summed[1:2, BLOCK:]], axis=1),
    ]
    two, third = arrived[:BLOCK], arrived[BLOCK:]
    placed = [
        pltpu.roll(two, DH, 1),
        two,
        jnp.concatenate([pltpu.roll(third, DH, 1), third], axis=0),
    ]
    grads = [jnp.where(right, grad, jnp.zeros_like(grad)) for grad in placed]
    queries, pairs = [], []
    for h in range(heads):
        queries.append(qkv_ref[rows, SLAB * h : SLAB * h + 2 * DH] * jnp.asarray(SCALE, BF16))
        pairs.append(jnp.concatenate([queries[h], grads[h]], axis=0))
    seg_q = seg_row_ref[...]
    lses = choose(lse_refs)
    low, count = low_ref[qb], count_ref[qb]

    def step(kb, accs):
        keys = pl.ds(pl.multiple_of(low * STEP + kb * BLOCK, STEP), BLOCK)
        allowed = seg_col_ref[keys, :] == seg_q
        keyed = [qkv_ref[keys, SLAB * h + 2 * DH : SLAB * (h + 1)] for h in range(heads)]
        raw = [dot(keyed[h], queries[h], NT) for h in range(heads)]
        probs_grads = [dot(keyed[h], grads[h], NT) for h in range(heads)]
        both = []
        for h in range(heads):
            probs = jnp.exp2((jnp.where(allowed, raw[h], MASKED) - lses[h]) * LOG2E)
            score_grad = (probs * (probs_grads[h] - deltas[h])).astype(BF16)
            both.append((score_grad, probs.astype(BF16)))
        found = []
        for h in range(heads):
            dkv[h, keys, :] += dot(jnp.concatenate(both[h], axis=1), pairs[h])
            found.append(accs[h] + dot(both[h][0], keyed[h], TN))
        return tuple(found)

    zero = jnp.zeros((BLOCK, 128), F32)
    accs = lax.fori_loop(0, count, step, tuple(zero for _ in range(heads)))
    for h in range(heads):
        query_grad = jnp.where(right, 0.0, accs[h] * SCALE).astype(BF16)
        out_ref[rows, SLAB * h : SLAB * h + 2 * DH] = query_grad

    @pl.when(qb == pl.num_programs(0) - 1)
    def _():
        for h in range(heads):
            at = SLAB * h
            out_ref[:, at + 2 * DH : at + SLAB] = dkv[h].astype(BF16)
            sums_ref[:, at : at + SLAB] = column_sum(out_ref[:, at : at + SLAB].astype(F32))
        rows_each = final_ref.shape[1]
        copies = []
        for at in range(final_ref.shape[0]):
            offset = pl.multiple_of(lax.rem(lane_ref[0] + at, final_ref.shape[0]) * rows_each, rows_each)
            copies.append(
                pltpu.make_async_copy(out_ref.at[pl.ds(offset, rows_each), :], final_ref.at[at], sems.at[at])
            )
        for copy in copies:
            copy.start()
        for copy in copies:
            copy.wait()


STEP = 128


def document_blocks(segment_row):
    starts = segment_row[::BLOCK]
    stops = segment_row[BLOCK - 1 :: BLOCK]
    low = jnp.sum((segment_row[None, :] < starts[:, None]).astype(jnp.int32), axis=1) // STEP
    high = jnp.sum((segment_row[None, :] <= stops[:, None]).astype(jnp.int32), axis=1)
    each = BLOCK // STEP
    count = (high - low * STEP + BLOCK - 1) // BLOCK
    return (jnp.minimum(low, segment_row.shape[0] // STEP - each * count), count)


PACKED = BLOCK + BLOCK // 2


def run_forward(which, lane, bounds, qkv, seg_col, seg_row):
    halves, half = which
    seq_len, width = seg_col.shape[0], qkv[0].shape[1]
    heads = width // SLAB
    blocks = seq_len // BLOCK
    steps = blocks // halves
    return pl.pallas_call(
        functools.partial(attend_forward, which),
        out_shape=(
            jax.ShapeDtypeStruct((steps, PACKED, 2 * DH), BF16),
            jax.ShapeDtypeStruct((heads, 1, steps * BLOCK), F32),
        ),
        grid_spec=pltpu.PrefetchScalarGridSpec(
            num_scalar_prefetch=3,
            grid=(steps,),
            in_specs=[pl.BlockSpec(memory_space=pl.ANY)] * len(qkv)
            + [
                pl.BlockSpec((BLOCK, 1), lambda q, *_: (q * halves + half, 0)),
                pl.BlockSpec((1, seq_len), lambda q, *_: (0, 0)),
            ],
            out_specs=(
                pl.BlockSpec((1, PACKED, 2 * DH), lambda q, *_: (q, 0, 0)),
                pl.BlockSpec((heads, 1, BLOCK), lambda q, *_: (0, 0, q)),
            ),
            scratch_shapes=[
                pltpu.VMEM((heads, blocks, BLOCK, BLOCK), F32),
                pltpu.VMEM((seq_len, width), BF16),
                pltpu.SemaphoreType.DMA((len(qkv),)),
            ],
        ),
        compiler_params=pltpu.CompilerParams(
            dimension_semantics=("arbitrary",), vmem_limit_bytes=28 << 20
        ),
        cost_estimate=pl.CostEstimate(
            flops=heads * seq_len * seq_len * 2048 * steps // blocks,
            bytes_accessed=5 << 20,
            transcendentals=heads * seq_len * seq_len // 3,
        ),
        name="attend_forward",
    )(lane, *bounds, *qkv, seg_col, seg_row)


def run_backward(lane, bounds, qkv, seg_col, seg_row, grad, ctxs, lses):
    seq_len, width = seg_col.shape[0], qkv[0].shape[1]
    heads = width // SLAB
    halves = len(ctxs)

    def fixed(shape):
        return pl.BlockSpec(shape, lambda q, *_: (0,) * len(shape))

    return pl.pallas_call(
        functools.partial(attend_backward, halves, len(qkv)),
        out_shape=(
            jax.ShapeDtypeStruct((len(qkv), seq_len // len(qkv), width), BF16),
            jax.ShapeDtypeStruct((1, width), F32),
        ),
        grid_spec=pltpu.PrefetchScalarGridSpec(
            num_scalar_prefetch=3,
            grid=(seq_len // BLOCK,),
            in_specs=[pl.BlockSpec(memory_space=pl.ANY)] * len(qkv)
            + [
                fixed((seq_len, 1)),
                pl.BlockSpec((1, BLOCK), lambda q, *_: (0, q)),
                pl.BlockSpec((1, PACKED, 2 * DH), lambda q, *_: (q, 0, 0)),
            ]
            + [pl.BlockSpec((1, PACKED, 2 * DH), lambda q, *_: (q // halves, 0, 0))] * halves
            + [pl.BlockSpec((heads, 1, BLOCK), lambda q, *_: (0, 0, q // halves))] * halves,
            out_specs=(pl.BlockSpec(memory_space=pl.ANY), fixed((1, width))),
            scratch_shapes=[
                pltpu.VMEM((heads, seq_len, 2 * DH), F32),
                pltpu.VMEM((seq_len, width), BF16),
                pltpu.VMEM((seq_len, width), BF16),
                pltpu.SemaphoreType.DMA((len(qkv),)),
            ],
        ),
        compiler_params=pltpu.CompilerParams(
            dimension_semantics=("arbitrary",), vmem_limit_bytes=28 << 20
        ),
        cost_estimate=pl.CostEstimate(
            flops=heads * seq_len * seq_len * 4096,
            bytes_accessed=10 << 20,
            transcendentals=heads * seq_len * seq_len // 3,
        ),
        name="attend_backward",
    )(lane, *bounds, *qkv, seg_col, seg_row, grad, *ctxs, *lses)


def dense_chain(
    marks, halves, total_tokens, place_ref, in_ref, teacher_ref, cotangent_ref, valid_ref, vec_ref,
    inner_bias_ref, *refs
):
    ctx_refs, refs = refs[:halves], refs[halves:]
    pieces = refs[: len(marks)]
    (
        layer_ref, first_grad_ref, ctx_grad_ref, first_ref, branch_grad_ref, attn_grad_ref,
        act_ref, hidden_grad_ref, notes_ref, w_out, w_in, w_up, slope, sums_ref, inner_sums_ref,
        gathered, sems,
    ) = refs[len(marks) :]
    parts, _, head_cols = w_out.shape
    hidden_cols = w_in.shape[2]
    index = place_ref[parts]
    step = pl.program_id(0)
    groups = (
        (2 * hidden_cols, head_cols, w_out),
        (0, hidden_cols, w_in),
        (hidden_cols, hidden_cols, w_up),
    )

    @pl.when(step == 0)
    def _():
        order = [(0, slot) for slot in range(parts)]
        order += [(group, slot) for slot in range(parts) for group in (1, 2)]
        for group, wanted in order:
            start, size, target = groups[group]
            for piece, marked in zip(pieces, marks):
                block = piece.shape[1]
                for at, (slot, turn, relative) in enumerate(marked):
                    if slot != wanted:
                        continue
                    offset = pl.multiple_of((index ^ turn) * block, block) if relative else turn * block
                    pltpu.make_async_copy(
                        piece.at[at, :, pl.ds(start, size)],
                        target.at[slot, pl.ds(offset, block), :],
                        sems.at[group, slot],
                    ).start()
        sums_ref[...] = jnp.zeros_like(sums_ref)
        inner_sums_ref[...] = jnp.zeros_like(inner_sums_ref)

    def context(t):
        value = ctx_refs[0][t]
        for half in range(1, halves):
            value = jnp.where(step == half, ctx_refs[half][t], value)
        return value

    def arrive(group, slot):
        whole = groups[group][2].at[slot]

        @pl.when(step == 0)
        def _():
            pltpu.make_async_copy(whole, whole, sems.at[group, slot]).wait()

    def vec(which):
        return vec_ref[which : which + 1, :]

    counts = jnp.zeros((1, 2 * DH), F32)

    attention = jnp.zeros(in_ref.shape, F32)
    for slot in range(parts):
        arrive(0, slot)
        counts = counts + column_sum(w_out[slot, :, 2 * DH :].astype(F32))
        attention = attention + dot(unpack(context(place_ref[slot])), w_out[slot, :, : 3 * DH], NT)
    first_exact, normed_one, inverse_one = norm_forward(
        in_ref[...].astype(F32) + attention + vec(0), vec(1), vec(2)
    )
    first = first_exact.astype(BF16)
    first_ref[...] = first

    def up(slot, branch):
        t = place_ref[slot]
        arrive(1, slot)
        hidden = dot(first, w_in[slot]) + inner_bias_ref[t]
        bend = 0.5 * (1.0 + lax.erf(hidden * ROOT_HALF))
        activated = (hidden * bend).astype(BF16)
        act_ref[t] = activated
        slope[slot] = bend + hidden * INV_ROOT_TAU * jnp.exp2(hidden * hidden * (-0.5 * LOG2E))
        arrive(2, slot)
        return branch + dot(activated, w_up[slot], NT)

    branch = jnp.zeros(in_ref.shape, F32)
    for slot in range(parts):
        branch = up(slot, branch)
    lanes = lax.broadcasted_iota(jnp.int32, counts.shape, 1)
    weight = jnp.where(lanes == DH, 256.0, jnp.where(lanes == DH + 1, 1.0, 0.0))
    ratio = total_tokens / jnp.sum(jnp.where(weight > 0.0, counts, 0.0) * weight, axis=-1, keepdims=True)
    layer_rows, normed_two, inverse_two = norm_forward(first.astype(F32) + branch + vec(3), vec(4), vec(5))
    layer_ref[...] = layer_rows.astype(BF16)
    misfit = layer_rows - teacher_ref[...].astype(F32)
    weighted = valid_ref[...] * misfit
    out_grad = cotangent_ref[...].astype(F32) + weighted * ratio
    second_grad = norm_backward(out_grad, normed_two, inverse_two, vec(4))
    branch_grad = second_grad.astype(BF16)
    branch_grad_ref[...] = branch_grad
    sums_ref[0:1, :] += column_sum(weighted * misfit)
    sums_ref[1:2, :] += column_sum(branch_grad.astype(F32))
    sums_ref[2:3, :] += column_sum(out_grad * normed_two)
    sums_ref[3:4, :] += column_sum(out_grad)

    def down(slot, back):
        t = place_ref[slot]
        hidden_grad = (dot(branch_grad, w_up[slot]) * slope[slot]).astype(BF16)
        hidden_grad_ref[t] = hidden_grad
        inner_sums_ref[t] += column_sum(hidden_grad.astype(F32))
        return back + dot(hidden_grad, w_in[slot], NT)

    upstream = second_grad
    for slot in range(parts):
        upstream = down(slot, upstream)
    first_grad = norm_backward(upstream, normed_one, inverse_one, vec(1))
    first_grad_ref[...] = first_grad
    attn_grad = first_grad.astype(BF16)
    attn_grad_ref[...] = attn_grad
    sums_ref[4:5, :] += column_sum(attn_grad.astype(F32))
    sums_ref[5:6, :] += column_sum(upstream * normed_one)
    sums_ref[6:7, :] += column_sum(upstream)
    middle = BLOCK // 2
    for slot in range(parts):
        back = dot(attn_grad, w_out[slot, :, : 3 * DH]).astype(BF16)
        ctx_grad_ref[place_ref[slot], 0] = pack(
            back[:, : 2 * DH], back[:middle, 2 * DH :], back[middle:, 2 * DH :]
        )


    @pl.when(step == pl.num_programs(0) - 1)
    def _():
        lanes = 2 * DH
        gathered[...] = jnp.zeros_like(gathered)
        rows_each, inner_rows = width_of(sums_ref) // lanes, width_of(inner_sums_ref) // lanes
        per_note = gathered.shape[1] // lanes

        def put(at, value):
            gathered[at // per_note : at // per_note + 1, pl.ds(at % per_note * lanes, lanes)] = value

        for row in range(sums_ref.shape[0]):
            for k in range(rows_each):
                put(row * rows_each + k, sums_ref[row : row + 1, k * lanes : (k + 1) * lanes])
        for t in range(parts):
            for k in range(inner_rows):
                put(
                    sums_ref.shape[0] * rows_each + t * inner_rows + k,
                    inner_sums_ref[t, :, k * lanes : (k + 1) * lanes],
                )
        notes_ref[...] = gathered[...].astype(BF16)


def width_of(ref):
    return ref.shape[-1]


def run_dense(note_rows, marks, total_tokens, place, ctxs, rows_in, teacher, cotangent, valid, vecs, inner_bias, pieces):
    halves, parts = len(ctxs), ctxs[0].shape[0]
    part_len, width = rows_in.shape
    hidden_cols = inner_bias.shape[2]
    out_cols = pieces[0].shape[2] - 2 * hidden_cols
    room = -(-(8 * width + parts * hidden_cols) // (note_rows * 2 * DH)) * 2 * DH

    def by_rows(columns):
        return pl.BlockSpec((BLOCK, columns), lambda i: (i, 0))

    def by_part(columns):
        return pl.BlockSpec((parts, BLOCK, columns), lambda i: (0, i, 0))

    def fixed(shape):
        return pl.BlockSpec(shape, lambda i: (0,) * len(shape))

    packed_shape = (parts, halves) + ctxs[0].shape[1:]
    packed = pl.BlockSpec((parts, 1) + packed_shape[2:], lambda i: (0, i, 0, 0))
    low = jax.ShapeDtypeStruct((part_len, width), BF16)
    wide = jax.ShapeDtypeStruct((parts, part_len, hidden_cols), BF16)
    smem = pl.BlockSpec(memory_space=pltpu.SMEM)
    return pl.pallas_call(
        functools.partial(dense_chain, marks, halves, total_tokens),
        out_shape=(
            low,
            jax.ShapeDtypeStruct((part_len, width), F32),
            jax.ShapeDtypeStruct(packed_shape, BF16),
            low,
            low,
            low,
            wide,
            wide,
            jax.ShapeDtypeStruct((note_rows, room), BF16),
        ),
        grid=(halves,),
        in_specs=[
            smem,
            by_rows(width),
            by_rows(width),
            by_rows(width),
            by_rows(1),
            fixed(vecs.shape),
            fixed(inner_bias.shape),
        ]
        + [fixed(ctx.shape) for ctx in ctxs]
        + [pl.BlockSpec(memory_space=pl.ANY)] * len(pieces),
        out_specs=(
            by_rows(width),
            by_rows(width),
            packed,
            by_rows(width),
            by_rows(width),
            by_rows(width),
            by_part(hidden_cols),
            by_part(hidden_cols),
            fixed((note_rows, room)),
        ),
        scratch_shapes=[
            pltpu.VMEM((parts, width, out_cols), BF16),
            pltpu.VMEM((parts, width, hidden_cols), BF16),
            pltpu.VMEM((parts, width, hidden_cols), BF16),
            pltpu.VMEM((parts, BLOCK, hidden_cols), F32),
            pltpu.VMEM((8, width), F32),
            pltpu.VMEM((parts, 1, hidden_cols), F32),
            pltpu.VMEM((note_rows, room), F32),
            pltpu.SemaphoreType.DMA((3, parts)),
        ],
        compiler_params=pltpu.CompilerParams(
            dimension_semantics=("arbitrary",), vmem_limit_bytes=VMEM_LIMIT
        ),
        cost_estimate=pl.CostEstimate(
            flops=2 * part_len * width * (8 * hidden_cols + 4 * out_cols) * parts,
            bytes_accessed=24 << 20,
            transcendentals=2 * part_len * hidden_cols * parts,
        ),
        name="dense_chain",
    )(place, rows_in, teacher, cotangent, valid, vecs, inner_bias, *ctxs, *pieces)


def dense_weights(
    plans, halves, place_ref, first_ref, branch_grad_ref, attn_grad_ref, act_ref, hidden_grad_ref, notes_ref,
    *refs
):
    ctx_refs, outs, (whole, sems) = refs[:halves], refs[halves:-2], refs[-2:]
    step = pl.program_id(0)
    slots = whole.shape[0]

    def leave(start, stop):
        for out, turns in zip(outs, plans):
            block = out.shape[1]
            for at, turn in enumerate(turns):
                offset = 0
                if block < whole.shape[1]:
                    offset = pl.multiple_of((place_ref[place_ref.shape[0] - 1] ^ turn) * block, block)
                pltpu.make_async_copy(
                    whole.at[step, pl.ds(offset, block), pl.ds(start, stop - start)],
                    out.at[at * slots + step, :, pl.ds(start, stop - start)],
                    sems.at[step],
                ).start()

    hidden_cols = act_ref.shape[2]
    columns = whole.shape[2]
    in_parts = len(plans) == 1 and outs[0].shape[1] == whole.shape[1]
    whole[step, :, :hidden_cols] = dot(first_ref[...], hidden_grad_ref[0], TN).astype(BF16)
    if in_parts:
        leave(0, hidden_cols)
    whole[step, :, hidden_cols : 2 * hidden_cols] = dot(branch_grad_ref[...], act_ref[0], TN).astype(BF16)
    if in_parts:
        leave(hidden_cols, 2 * hidden_cols)
    ctx = jnp.concatenate([unpack(ref[0]) for ref in ctx_refs], axis=0)
    plain = 2 * hidden_cols + ctx.shape[1]
    whole[step, :, 2 * hidden_cols : plain] = dot(attn_grad_ref[...], ctx, TN).astype(BF16)
    note_rows, room = notes_ref.shape
    for at in range(whole.shape[1] // note_rows):
        whole[step, at * note_rows : (at + 1) * note_rows, plain : plain + room] = notes_ref[...]
    leave(2 * hidden_cols if in_parts else 0, columns)

    @pl.when(step == slots - 1)
    def _():
        for slot in range(slots):
            pltpu.make_async_copy(whole.at[slot], whole.at[slot], sems.at[slot]).wait()


def run_weights(base, slots, plans, place, notes, first, branch_grad, attn_grad, act, hidden_grad, ctxs):
    _, part_len, hidden_cols = act.shape
    width = first.shape[1]
    columns = 2 * hidden_cols + 3 * DH + notes.shape[1]
    fixed = pl.BlockSpec((part_len, width), lambda s, place: (0, 0))
    by_slot = pl.BlockSpec((1, part_len, hidden_cols), lambda s, place: (place[base + s], 0, 0))
    outs = tuple(
        jax.ShapeDtypeStruct((len(turns) * slots, block, columns), BF16) for block, turns in plans
    )
    return pl.pallas_call(
        functools.partial(dense_weights, tuple(turns for _, turns in plans), len(ctxs)),
        out_shape=outs,
        grid_spec=pltpu.PrefetchScalarGridSpec(
            num_scalar_prefetch=1,
            grid=(slots,),
            in_specs=[
                fixed,
                fixed,
                fixed,
                by_slot,
                by_slot,
                pl.BlockSpec(notes.shape, lambda s, place: (0, 0)),
            ]
            + [
                pl.BlockSpec((1,) + ctx.shape[1:], lambda s, place: (place[base + s], 0, 0)) for ctx in ctxs
            ],
            out_specs=tuple(pl.BlockSpec(memory_space=pl.ANY) for _ in outs),
            scratch_shapes=[
                pltpu.VMEM((slots, width, columns), BF16),
                pltpu.SemaphoreType.DMA((slots,)),
            ],
        ),
        compiler_params=pltpu.CompilerParams(
            dimension_semantics=("arbitrary",), vmem_limit_bytes=VMEM_LIMIT
        ),
        cost_estimate=pl.CostEstimate(
            flops=2 * part_len * width * columns * slots,
            bytes_accessed=5 * slots << 20,
            transcendentals=0,
        ),
        name="dense_weights",
    )(place, first, branch_grad, attn_grad, act, hidden_grad, notes, *ctxs)


def finish_dense(packed_ref, inner_ref, outer_ref, output_ref, notes_ref):
    hidden_cols = inner_ref.shape[1]
    summed = packed_ref[...].astype(F32)
    inner_ref[...] = summed[:, :hidden_cols]
    outer_ref[...] = summed[:, hidden_cols : 2 * hidden_cols]
    plain = 2 * hidden_cols + output_ref.shape[0]
    output_ref[...] = jnp.transpose(summed[:, 2 * hidden_cols : plain])
    notes_ref[...] = summed[:, plain:]


def run_finish_dense(packed, hidden_cols, head_cols):
    rows = packed.shape[0]
    return pl.pallas_call(
        finish_dense,
        out_shape=(
            jax.ShapeDtypeStruct((rows, hidden_cols), F32),
            jax.ShapeDtypeStruct((rows, hidden_cols), F32),
            jax.ShapeDtypeStruct((head_cols, rows), F32),
            jax.ShapeDtypeStruct((rows, packed.shape[1] - 2 * hidden_cols - head_cols), F32),
        ),
        name="finish_dense",
    )(packed)


def finish_heads(value_ref, *refs):
    summed = value_ref[...].astype(F32)
    heads = summed.shape[1] // SLAB
    for ref, which in zip(refs, (0, 2, 3, 1)):
        columns = [summed[:, SLAB * h + which * DH : SLAB * h + (which + 1) * DH] for h in range(heads)]
        ref[...] = jnp.concatenate(columns, axis=1)[: ref.shape[0]]


def run_finish_heads(value):
    rows, width = value.shape
    out = jax.ShapeDtypeStruct((rows, width // 4), F32)
    notes = jax.ShapeDtypeStruct((8, width // 4), F32)
    return pl.pallas_call(finish_heads, out_shape=(out, out, out, notes), name="finish_heads")(value)


def interleave(query, key, value, heads):
    rows = query.shape[0]
    parts = [part.reshape(rows, heads, 1, DH) for part in (query, jnp.zeros_like(query), key, value)]
    return jnp.concatenate(parts, axis=2).reshape(rows, heads * SLAB)


def swap(value, axis, bit):
    size = lax.axis_size(axis)
    return lax.ppermute(value, axis, [(i, i ^ bit) for i in range(size)])


def bits_of(axis):
    bit = 1
    while bit < lax.axis_size(axis):
        yield bit
        bit *= 2


def after(value, *others):
    return lax.optimization_barrier((value,) + others)[0]


def merge(held, other, axis, bit):
    mine_first = (lax.axis_index(axis) & bit) == 0
    return jnp.where(
        mine_first, jnp.concatenate([held, other], axis=0), jnp.concatenate([other, held], axis=0)
    )


def add_low(left_side, right_side):
    return (left_side.astype(F32) + right_side.astype(F32)).astype(BF16)


def add_halves(left_side, right_side):
    half = left_side.shape[0] // 2
    return (
        add_low(left_side[:half], right_side[:half]),
        add_low(left_side[half:], right_side[half:]),
    )


def scatter_rows(held):
    index = lax.axis_index("dp")
    for bit in bits_of("dp"):
        held = held.reshape((held.shape[0] // 2, 2) + held.shape[1:])
        own = (index & bit) // bit
        send = lax.dynamic_index_in_dim(held, 1 - own, 1, keepdims=False)
        keep = lax.dynamic_index_in_dim(held, own, 1, keepdims=False)
        held = add_low(keep, swap(send, "dp", bit))
    return held[0]


def local(
    inputs, segment_ids, valid_mask, teacher, cotangent,
    w_query, w_key, w_value, w_output, w_inner, w_outer,
    query_bias, value_bias, output_bias, inner_bias, outer_bias,
    gain_attn, shift_attn, gain_ffn, shift_ffn,
):
    _, part_len, width = inputs.shape
    parts = lax.axis_size("tensor")
    copies = lax.axis_size("dp")
    rank = lax.axis_index("tensor")
    total_tokens = part_len * parts * copies
    seq_len = part_len * parts
    head_cols = w_query.shape[1]
    heads = head_cols // DH
    hidden_cols = w_inner.shape[1]
    shard_rows = w_inner.shape[0]
    halves = part_len // BLOCK

    rows_in = inputs.reshape(part_len, width)
    tokens = lax.all_gather(rows_in, "tensor", axis=0, tiled=True)
    w_heads = interleave(w_query, w_key, w_value, heads)
    paired = shard_rows % 16 == 0 and parts == 4 and copies == 8

    valid_rows = valid_mask.astype(F32).reshape(part_len, 1)
    valid_count = jnp.sum(valid_mask.astype(F32))
    upper = jnp.floor(valid_count / 256.0)
    spot = lax.broadcasted_iota(jnp.int32, (shard_rows, DH), 0) * DH + lax.broadcasted_iota(
        jnp.int32, (shard_rows, DH), 1
    )
    count_row = jnp.where(spot == 0, upper, jnp.where(spot == 1, valid_count - 256.0 * upper, 0.0))
    mine = jnp.concatenate((w_inner, w_outer.T, w_output.T, count_row.astype(BF16)), axis=1)
    if paired:
        place = jnp.stack([rank, rank ^ 1, rank ^ 2, rank ^ 3, lax.axis_index("dp")]).astype(jnp.int32)
        pair = jnp.concatenate([mine[None], swap(mine[None], "tensor", 1)], axis=0)
        near = jnp.concatenate([pair, swap(pair, "dp", 2)], axis=0)
        turns = [0, 2, 4, 6]
        for bit in (1, 2, 4):
            w_heads = merge(w_heads, swap(w_heads, "dp", bit), "dp", bit)
        near, w_heads = lax.optimization_barrier((near, w_heads))
        near_next = swap(near, "dp", 4)
        tokens, pair, near_next = lax.optimization_barrier((tokens, pair, near_next))
        far = swap(pair, "tensor", 2)
    else:
        place = jnp.asarray(list(range(parts)) + [0], jnp.int32)
        weights = lax.all_gather(mine, ("tensor", "dp"), axis=0, tiled=False)
        for bit in bits_of("dp"):
            w_heads = merge(w_heads, swap(w_heads, "dp", bit), "dp", bit)

    mine_cols = rank * head_cols
    query_shift = lax.dynamic_slice_in_dim(query_bias, mine_cols, head_cols).astype(F32)
    value_shift = lax.dynamic_slice_in_dim(value_bias, mine_cols, head_cols).astype(F32)
    shifts = interleave(query_shift[None], jnp.zeros_like(query_shift)[None], value_shift[None], heads)
    qkv = [(dot(tokens, w_heads) + shifts).astype(BF16)]

    segment_row = segment_ids.reshape(seq_len)
    bounds = document_blocks(segment_row)
    seg_col = segment_row.reshape(seq_len, 1)
    seg_row = segment_row.reshape(1, seq_len)
    lane = rank.astype(jnp.int32).reshape(1)

    def exchange(packed_blocks):
        return lax.all_to_all(packed_blocks, "tensor", 0, 0)

    contexts, lses, arrived = [], [], []
    for half in range(halves):
        if paired and half == 1:
            far, contexts[0], bounds = lax.optimization_barrier((far, contexts[0], bounds))
            weights = lax.all_gather(far, "dp", axis=0, tiled=False)
        context, lse = run_forward((halves, half), lane, bounds, qkv, seg_col, seg_row)
        if half > 0:
            context, arrived[0] = lax.optimization_barrier((context, arrived[0]))
        contexts.append(context)
        lses.append(lse)
        arrived.append(exchange(context))
    if paired:
        near_next, context = lax.optimization_barrier((near_next, contexts[-1]))
        near = jnp.concatenate([near, near_next], axis=0)
        near_other = swap(near, "dp", 1)
    if paired:
        weights = weights.reshape((copies * 2,) + mine.shape)
        pieces = [near, near_other, weights]
        marks = [[(slot, turn ^ flip, True) for turn in turns for slot in (0, 1)] for flip in (0, 1)]
        marks.append([(2 + at % 2, at // 2, False) for at in range(2 * copies)])
    else:
        pieces = [weights.reshape(parts, width, -1)]
        marks = [[(t, 0, False) for t in range(parts)]]
    counts = [piece.reshape((-1,) + mine.shape)[:, 0, -DH : 2 - DH].astype(F32) for piece in pieces + [weights]]
    counts = jnp.concatenate(counts[:-1] if paired else counts[-1:], axis=0)
    counted = 256.0 * jnp.sum(counts[:, 0]) + jnp.sum(counts[:, 1])

    vecs = jnp.stack(
        (output_bias, gain_attn, shift_attn, outer_bias, gain_ffn, shift_ffn, outer_bias, outer_bias)
    ).astype(F32)
    inner_rows = inner_bias.astype(F32).reshape(parts, 1, hidden_cols)
    teacher_rows = teacher.reshape(part_len, width)
    cotangent_rows = cotangent.reshape(part_len, width)
    (
        layer_out, first_grad, context_grad, first, branch_grad, attn_grad, activated, hidden_grad, notes,
    ) = run_dense(
        shard_rows, marks, float(total_tokens), place, arrived, rows_in, teacher_rows, cotangent_rows, valid_rows, vecs,
        inner_rows, pieces,
    )
    head_grad = exchange(context_grad).reshape((parts * halves, PACKED, 2 * DH))
    sources = (first, branch_grad, attn_grad, activated, hidden_grad, arrived)
    if shard_rows % 16:
        notes = jnp.tile(notes, (copies, 1))
    if paired:
        keep_turns = (0, 4, 2, 6)
        (distant,) = run_weights(2, 2, ((width, (0,)),), place, notes, *sources)
        plans = tuple((shard_rows, tuple(turn | flip for turn in keep_turns)) for flip in (0, 1))
        keep, send = run_weights(0, 2, plans, place, notes, *sources)
        keep, send = (value.reshape((4, 2) + value.shape[1:]) for value in (keep, send))
        distant = lax.psum_scatter(distant, "dp", scatter_dimension=1, tiled=True)
        came = swap(send, "dp", 1)
    else:
        (packed,) = run_weights(0, parts, ((width, (0,)),), place, notes, *sources)
        packed = lax.psum_scatter(packed, "dp", scatter_dimension=1, tiled=True)

    joined_grad, sums = run_backward(lane, bounds, qkv, seg_col, seg_row, head_grad, contexts, lses)
    joined_grad = joined_grad.reshape(seq_len, -1)
    attn_back = dot(joined_grad, w_heads, NT).astype(BF16)
    if paired:
        came = after(came, attn_back)
    attn_back, sums, joined_grad = lax.optimization_barrier((attn_back, sums, joined_grad))
    attn_back = lax.psum_scatter(attn_back, "tensor", scatter_dimension=0, tiled=True)
    if paired:
        keep, send = add_halves(keep, came)
        keep, send, joined_grad = lax.optimization_barrier((keep, send, joined_grad))
        came = swap(send, "dp", 2)
    head_weights = dot(tokens, joined_grad, TN).reshape((copies, shard_rows, -1))
    if paired:
        came, head_weights = lax.optimization_barrier((came, head_weights))
        keep, send = add_halves(keep, came)
        keep, send, head_weights = lax.optimization_barrier((keep, send, head_weights))
        came = swap(send, "dp", 4)
    sums = sums.reshape(heads, 4, DH)
    sums = jnp.concatenate((sums[:, 0].reshape(1, head_cols), sums[:, 3].reshape(1, head_cols)), axis=1)
    for bit in bits_of("tensor"):
        sums = merge(sums, swap(sums, "tensor", bit), "tensor", bit)
    if paired:
        came, head_weights = lax.optimization_barrier((came, head_weights))
        slots = jnp.concatenate([add_low(keep, came)[0], distant], axis=0)
        packed = jnp.stack(
            [lax.dynamic_index_in_dim(slots, rank ^ t, 0, keepdims=False) for t in range(parts)]
        )
    packed = lax.psum_scatter(packed, "tensor", scatter_dimension=0, tiled=True)[0]
    biases = jnp.concatenate((sums[:, :head_cols].reshape(-1), sums[:, head_cols:].reshape(-1)))
    biases = jnp.pad(
        biases.reshape(8, heads, 1, DH), ((0, shard_rows - 8), (0, 0), (1, 2), (0, 0))
    ).reshape(1, shard_rows, -1)
    query_grad, key_grad, value_grad, biases = run_finish_heads(
        scatter_rows((head_weights + biases).astype(BF16))
    )
    biases = biases.reshape(2, width)
    input_grad = first_grad + attn_back.astype(F32)

    inner_grad, outer_grad, output_grad, notes = run_finish_dense(packed, hidden_cols, head_cols)
    notes = notes.reshape(-1)

    def total(which):
        return notes[which * width : (which + 1) * width]

    mse_loss = jnp.sum(total(0)) / (counted * width)
    return (
        layer_out.reshape(1, part_len, width),
        mse_loss,
        input_grad.reshape(1, part_len, width),
        query_grad,
        key_grad,
        value_grad,
        output_grad,
        inner_grad,
        outer_grad.T,
        biases[0],
        biases[1],
        total(4),
        notes[8 * width : 8 * width + hidden_cols * parts],
        total(1),
        total(5),
        total(6),
        total(2),
        total(3),
    )


def solution(mesh):
    shard = P("dp", "tensor", None)
    by_dp, by_tensor = P("dp", "tensor"), P("tensor", "dp")
    in_specs = (
        (shard, P("dp", None), by_dp, shard, shard)
        + (by_dp,) * 3
        + (by_tensor, by_dp, by_tensor)
        + (P(),) * 9
    )
    out_specs = (shard, P(), shard) + (by_dp,) * 3 + (by_tensor, by_dp, by_tensor) + (P(),) * 9
    return jax.shard_map(local, mesh=mesh, in_specs=in_specs, out_specs=out_specs, check_vma=False)
```

```python
import functools

import jax
import jax.numpy as jnp
from jax import lax
from jax.experimental import pallas as pl
from jax.experimental.pallas import tpu as pltpu
from jax.sharding import PartitionSpec as P

DH = 64
BLOCK = 256
SLAB = 4 * DH
EPSILON = 1e-12
ROOT_HALF = 0.7071067811865476
INV_ROOT_TAU = 0.3989422804014327
LOG2E = 1.4426950408889634
LN2 = 0.6931471805599453
SCALE = DH ** (-0.5)
MASKED = -1e30
VMEM_LIMIT = 60 << 20

BF16 = jnp.bfloat16
F32 = jnp.float32
NN = (((1,), (0,)), ((), ()))
NT = (((1,), (1,)), ((), ()))
TN = (((0,), (0,)), ((), ()))


def dot(left_side, right_side, dims=NN):
    return lax.dot_general(left_side, right_side, dims, preferred_element_type=F32)


def norm_forward(summed, gain_vec, shift_vec):
    average = jnp.mean(summed, axis=-1, keepdims=True)
    centered = summed - average
    variance = jnp.mean(centered * centered, axis=-1, keepdims=True)
    inverse = lax.rsqrt(variance + EPSILON)
    normed = centered * inverse
    return (normed * gain_vec + shift_vec, normed, inverse)


def norm_backward(upstream, normed, inverse, gain_vec):
    scaled = upstream * gain_vec
    first_mean = jnp.mean(scaled, axis=-1, keepdims=True)
    second_mean = jnp.mean(scaled * normed, axis=-1, keepdims=True)
    return inverse * (scaled - first_mean - normed * second_mean)


def column_sum(value):
    return jnp.sum(value, axis=0, keepdims=True)


def lane_is_right(rows):
    return lax.broadcasted_iota(jnp.int32, (rows, 2 * DH), 1) >= DH


def pack(first_two, third_top, third_bottom):
    return jnp.concatenate([first_two, jnp.concatenate([third_top, third_bottom], axis=1)], axis=0)


def unpack(packed):
    third = packed[BLOCK:]
    third = jnp.concatenate([third[:, :DH], third[:, DH:]], axis=0)
    return jnp.concatenate([packed[:BLOCK], third], axis=1)


def fetch_chunks(lane_ref, chunk_refs, target, sems):
    rows = chunk_refs[0].shape[0]
    copies = []
    for at, chunk in enumerate(chunk_refs):
        offset = pl.multiple_of(lax.rem(lane_ref[0] + at, len(chunk_refs)) * rows, rows)
        copies.append(pltpu.make_async_copy(chunk, target.at[pl.ds(offset, rows), :], sems.at[at]))
    return copies


def attend_forward(
    which, lane_ref, low_ref, count_ref, *refs
):
    chunk_refs, (seg_col_ref, seg_row_ref, ctx_ref, lse_ref, held, qkv_ref, sems) = refs[:-7], refs[-7:]
    heads = lse_ref.shape[0]

    @pl.when(pl.program_id(0) == 0)
    def _():
        copies = fetch_chunks(lane_ref, chunk_refs, qkv_ref, sems)
        for copy in copies:
            copy.start()
        for copy in copies:
            copy.wait()

    halves, half = which
    qb = pl.program_id(0) * halves + half
    rows = pl.ds(pl.multiple_of(qb * BLOCK, BLOCK), BLOCK)
    seg_q = seg_col_ref[...]
    queries = [
        qkv_ref[rows, SLAB * h : SLAB * h + 2 * DH] * jnp.asarray(SCALE, BF16) for h in range(heads)
    ]
    low, count = low_ref[qb], count_ref[qb]

    def score(kb, peaks):
        keys = pl.ds(pl.multiple_of(low * STEP + kb * BLOCK, STEP), BLOCK)
        allowed = seg_q == seg_row_ref[:, keys]
        found = []
        for h in range(heads):
            scores = dot(queries[h], qkv_ref[keys, SLAB * h + 2 * DH : SLAB * (h + 1)], NT)
            scores = jnp.where(allowed, scores, MASKED)
            held[h, kb] = scores
            found.append(jnp.maximum(peaks[h], jnp.maximum(scores[:, :128], scores[:, 128:])))
        return tuple(found)

    start = tuple(jnp.full((BLOCK, 128), MASKED, F32) for _ in range(heads))
    peaks = lax.fori_loop(0, count, score, start)
    highest = [jnp.max(peak, axis=-1, keepdims=True) for peak in peaks]

    def weigh(kb, carry):
        keys = pl.ds(pl.multiple_of(low * STEP + kb * BLOCK, STEP), BLOCK)
        found = []
        for h in range(heads):
            total, acc = carry[h]
            raised = jnp.exp2((held[h, kb] - highest[h]) * LOG2E)
            total = total + (raised[:, :128] + raised[:, 128:])
            acc = acc + dot(raised.astype(BF16), qkv_ref[keys, SLAB * h + 2 * DH : SLAB * (h + 1)])
            found.append((total, acc))
        return tuple(found)

    zero = jnp.zeros((BLOCK, 128), F32)
    done = lax.fori_loop(0, count, weigh, tuple((zero, zero) for _ in range(heads)))
    values = []
    for h in range(heads):
        total, acc = done[h]
        summed = jnp.sum(total, axis=-1, keepdims=True)
        values.append((acc / summed).astype(BF16))
        lse_ref[h] = jnp.transpose(highest[h] + jnp.log(summed))
    middle = BLOCK // 2
    ctx_ref[0, :BLOCK, :] = jnp.where(lane_is_right(BLOCK), values[1], pltpu.roll(values[0], DH, 1))
    ctx_ref[0, BLOCK:, :] = jnp.where(
        lane_is_right(middle), values[2][middle:], pltpu.roll(values[2][:middle], DH, 1)
    )


def attend_backward(halves, chunks, lane_ref, low_ref, count_ref, *refs):
    chunk_refs, refs = refs[:chunks], refs[chunks:]
    (seg_col_ref, seg_row_ref, grad_ref), refs = refs[:3], refs[3:]
    ctx_refs, lse_refs, refs = refs[:halves], refs[halves : 2 * halves], refs[2 * halves :]
    final_ref, sums_ref, dkv, out_ref, qkv_ref, sems = refs
    heads = dkv.shape[0]
    qb = pl.program_id(0)
    half = lax.rem(qb, halves)

    def choose(options):
        value = options[0][...]
        for other in range(1, halves):
            value = jnp.where(half == other, options[other][...], value)
        return value

    @pl.when(qb == 0)
    def _():
        copies = fetch_chunks(lane_ref, chunk_refs, qkv_ref, sems)
        for copy in copies:
            copy.start()
        dkv[...] = jnp.zeros_like(dkv)
        for copy in copies:
            copy.wait()

    rows = pl.ds(pl.multiple_of(qb * BLOCK, BLOCK), BLOCK)
    right = lane_is_right(BLOCK)
    arrived = grad_ref[0]
    product = arrived.astype(F32) * choose(ctx_refs)[0].astype(F32)
    upper = product.astype(BF16)
    lower = (product - upper.astype(F32)).astype(BF16)
    pick = (
        lax.broadcasted_iota(jnp.int32, (8, 2 * DH), 1) // DH
        == lax.broadcasted_iota(jnp.int32, (8, 2 * DH), 0)
    ).astype(BF16)
    summed = dot(pick, upper, NT) + dot(pick, lower, NT)
    deltas = [
        summed[0:1, :BLOCK],
        summed[1:2, :BLOCK],
        jnp.concatenate([summed[0:1, BLOCK:], summed[1:2, BLOCK:]], axis=1),
    ]
    two, third = arrived[:BLOCK], arrived[BLOCK:]
    placed = [
        pltpu.roll(two, DH, 1),
        two,
        jnp.concatenate([pltpu.roll(third, DH, 1), third], axis=0),
    ]
    grads = [jnp.where(right, grad, jnp.zeros_like(grad)) for grad in placed]
    queries, pairs = [], []
    for h in range(heads):
        queries.append(qkv_ref[rows, SLAB * h : SLAB * h + 2 * DH] * jnp.asarray(SCALE, BF16))
        pairs.append(jnp.concatenate([queries[h], grads[h]], axis=0))
    seg_q = seg_row_ref[...]
    lses = choose(lse_refs)
    low, count = low_ref[qb], count_ref[qb]

    def step(kb, accs):
        keys = pl.ds(pl.multiple_of(low * STEP + kb * BLOCK, STEP), BLOCK)
        allowed = seg_col_ref[keys, :] == seg_q
        keyed = [qkv_ref[keys, SLAB * h + 2 * DH : SLAB * (h + 1)] for h in range(heads)]
        raw = [dot(keyed[h], queries[h], NT) for h in range(heads)]
        probs_grads = [dot(keyed[h], grads[h], NT) for h in range(heads)]
        both = []
        for h in range(heads):
            probs = jnp.exp2((jnp.where(allowed, raw[h], MASKED) - lses[h]) * LOG2E)
            score_grad = (probs * (probs_grads[h] - deltas[h])).astype(BF16)
            both.append((score_grad, probs.astype(BF16)))
        found = []
        for h in range(heads):
            dkv[h, keys, :] += dot(jnp.concatenate(both[h], axis=1), pairs[h])
            found.append(accs[h] + dot(both[h][0], keyed[h], TN))
        return tuple(found)

    zero = jnp.zeros((BLOCK, 128), F32)
    accs = lax.fori_loop(0, count, step, tuple(zero for _ in range(heads)))
    for h in range(heads):
        query_grad = jnp.where(right, 0.0, accs[h] * SCALE).astype(BF16)
        out_ref[rows, SLAB * h : SLAB * h + 2 * DH] = query_grad

    @pl.when(qb == pl.num_programs(0) - 1)
    def _():
        for h in range(heads):
            at = SLAB * h
            out_ref[:, at + 2 * DH : at + SLAB] = dkv[h].astype(BF16)
            sums_ref[:, at : at + SLAB] = column_sum(out_ref[:, at : at + SLAB].astype(F32))
        rows_each = final_ref.shape[1]
        copies = []
        for at in range(final_ref.shape[0]):
            offset = pl.multiple_of(lax.rem(lane_ref[0] + at, final_ref.shape[0]) * rows_each, rows_each)
            copies.append(
                pltpu.make_async_copy(out_ref.at[pl.ds(offset, rows_each), :], final_ref.at[at], sems.at[at])
            )
        for copy in copies:
            copy.start()
        for copy in copies:
            copy.wait()


STEP = 128


def document_blocks(segment_row):
    starts = segment_row[::BLOCK]
    stops = segment_row[BLOCK - 1 :: BLOCK]
    low = jnp.sum((segment_row[None, :] < starts[:, None]).astype(jnp.int32), axis=1) // STEP
    high = jnp.sum((segment_row[None, :] <= stops[:, None]).astype(jnp.int32), axis=1)
    each = BLOCK // STEP
    count = (high - low * STEP + BLOCK - 1) // BLOCK
    return (jnp.minimum(low, segment_row.shape[0] // STEP - each * count), count)


PACKED = BLOCK + BLOCK // 2


def run_forward(which, lane, bounds, qkv, seg_col, seg_row):
    halves, half = which
    seq_len, width = seg_col.shape[0], qkv[0].shape[1]
    heads = width // SLAB
    blocks = seq_len // BLOCK
    steps = blocks // halves
    return pl.pallas_call(
        functools.partial(attend_forward, which),
        out_shape=(
            jax.ShapeDtypeStruct((steps, PACKED, 2 * DH), BF16),
            jax.ShapeDtypeStruct((heads, 1, steps * BLOCK), F32),
        ),
        grid_spec=pltpu.PrefetchScalarGridSpec(
            num_scalar_prefetch=3,
            grid=(steps,),
            in_specs=[pl.BlockSpec(memory_space=pl.ANY)] * len(qkv)
            + [
                pl.BlockSpec((BLOCK, 1), lambda q, *_: (q * halves + half, 0)),
                pl.BlockSpec((1, seq_len), lambda q, *_: (0, 0)),
            ],
            out_specs=(
                pl.BlockSpec((1, PACKED, 2 * DH), lambda q, *_: (q, 0, 0)),
                pl.BlockSpec((heads, 1, BLOCK), lambda q, *_: (0, 0, q)),
            ),
            scratch_shapes=[
                pltpu.VMEM((heads, blocks, BLOCK, BLOCK), F32),
                pltpu.VMEM((seq_len, width), BF16),
                pltpu.SemaphoreType.DMA((len(qkv),)),
            ],
        ),
        compiler_params=pltpu.CompilerParams(
            dimension_semantics=("arbitrary",), vmem_limit_bytes=VMEM_LIMIT if half else 28 << 20
        ),
        cost_estimate=pl.CostEstimate(
            flops=heads * seq_len * seq_len * 2048 * steps // blocks,
            bytes_accessed=5 << 20,
            transcendentals=heads * seq_len * seq_len // 3,
        ),
        name="attend_forward",
    )(lane, *bounds, *qkv, seg_col, seg_row)


def run_backward(lane, bounds, qkv, seg_col, seg_row, grad, ctxs, lses):
    seq_len, width = seg_col.shape[0], qkv[0].shape[1]
    heads = width // SLAB
    halves = len(ctxs)

    def fixed(shape):
        return pl.BlockSpec(shape, lambda q, *_: (0,) * len(shape))

    return pl.pallas_call(
        functools.partial(attend_backward, halves, len(qkv)),
        out_shape=(
            jax.ShapeDtypeStruct((len(qkv), seq_len // len(qkv), width), BF16),
            jax.ShapeDtypeStruct((1, width), F32),
        ),
        grid_spec=pltpu.PrefetchScalarGridSpec(
            num_scalar_prefetch=3,
            grid=(seq_len // BLOCK,),
            in_specs=[pl.BlockSpec(memory_space=pl.ANY)] * len(qkv)
            + [
                fixed((seq_len, 1)),
                pl.BlockSpec((1, BLOCK), lambda q, *_: (0, q)),
                pl.BlockSpec((1, PACKED, 2 * DH), lambda q, *_: (q, 0, 0)),
            ]
            + [pl.BlockSpec((1, PACKED, 2 * DH), lambda q, *_: (q // halves, 0, 0))] * halves
            + [pl.BlockSpec((heads, 1, BLOCK), lambda q, *_: (0, 0, q // halves))] * halves,
            out_specs=(pl.BlockSpec(memory_space=pl.ANY), fixed((1, width))),
            scratch_shapes=[
                pltpu.VMEM((heads, seq_len, 2 * DH), F32),
                pltpu.VMEM((seq_len, width), BF16),
                pltpu.VMEM((seq_len, width), BF16),
                pltpu.SemaphoreType.DMA((len(qkv),)),
            ],
        ),
        compiler_params=pltpu.CompilerParams(
            dimension_semantics=("arbitrary",), vmem_limit_bytes=VMEM_LIMIT
        ),
        cost_estimate=pl.CostEstimate(
            flops=heads * seq_len * seq_len * 4096,
            bytes_accessed=10 << 20,
            transcendentals=heads * seq_len * seq_len // 3,
        ),
        name="attend_backward",
    )(lane, *bounds, *qkv, seg_col, seg_row, grad, *ctxs, *lses)


def dense_chain(
    marks, halves, total_tokens, place_ref, in_ref, teacher_ref, cotangent_ref, valid_ref, vec_ref,
    inner_bias_ref, *refs
):
    ctx_refs, refs = refs[:halves], refs[halves:]
    pieces = refs[: len(marks)]
    (
        layer_ref, first_grad_ref, ctx_grad_ref, first_ref, branch_grad_ref, attn_grad_ref,
        act_ref, hidden_grad_ref, notes_ref, w_out, w_in, w_up, slope, sums_ref, inner_sums_ref,
        gathered, sems,
    ) = refs[len(marks) :]
    parts, _, head_cols = w_out.shape
    hidden_cols = w_in.shape[2]
    index = place_ref[parts]
    step = pl.program_id(0)
    groups = (
        (2 * hidden_cols, head_cols, w_out),
        (0, hidden_cols, w_in),
        (hidden_cols, hidden_cols, w_up),
    )

    @pl.when(step == 0)
    def _():
        order = [(0, slot) for slot in range(parts)]
        order += [(group, slot) for slot in range(parts) for group in (1, 2)]
        for group, wanted in order:
            start, size, target = groups[group]
            for piece, marked in zip(pieces, marks):
                block = piece.shape[1]
                for at, (slot, turn, relative) in enumerate(marked):
                    if slot != wanted:
                        continue
                    offset = pl.multiple_of((index ^ turn) * block, block) if relative else turn * block
                    pltpu.make_async_copy(
                        piece.at[at, :, pl.ds(start, size)],
                        target.at[slot, pl.ds(offset, block), :],
                        sems.at[group, slot],
                    ).start()
        sums_ref[...] = jnp.zeros_like(sums_ref)
        inner_sums_ref[...] = jnp.zeros_like(inner_sums_ref)

    def context(t):
        value = ctx_refs[0][t]
        for half in range(1, halves):
            value = jnp.where(step == half, ctx_refs[half][t], value)
        return value

    def arrive(group, slot):
        whole = groups[group][2].at[slot]

        @pl.when(step == 0)
        def _():
            pltpu.make_async_copy(whole, whole, sems.at[group, slot]).wait()

    def vec(which):
        return vec_ref[which : which + 1, :]

    counts = jnp.zeros((1, 2 * DH), F32)

    attention = jnp.zeros(in_ref.shape, F32)
    for slot in range(parts):
        arrive(0, slot)
        counts = counts + column_sum(w_out[slot, :, 2 * DH :].astype(F32))
        attention = attention + dot(unpack(context(place_ref[slot])), w_out[slot, :, : 3 * DH], NT)
    first_exact, normed_one, inverse_one = norm_forward(
        in_ref[...].astype(F32) + attention + vec(0), vec(1), vec(2)
    )
    first = first_exact.astype(BF16)
    first_ref[...] = first

    def up(slot, branch):
        t = place_ref[slot]
        arrive(1, slot)
        hidden = dot(first, w_in[slot]) + inner_bias_ref[t]
        bend = 0.5 * (1.0 + lax.erf(hidden * ROOT_HALF))
        activated = (hidden * bend).astype(BF16)
        act_ref[t] = activated
        slope[slot] = bend + hidden * INV_ROOT_TAU * jnp.exp2(hidden * hidden * (-0.5 * LOG2E))
        arrive(2, slot)
        return branch + dot(activated, w_up[slot], NT)

    branch = jnp.zeros(in_ref.shape, F32)
    for slot in range(parts):
        branch = up(slot, branch)
    lanes = lax.broadcasted_iota(jnp.int32, counts.shape, 1)
    weight = jnp.where(lanes == DH, 256.0, jnp.where(lanes == DH + 1, 1.0, 0.0))
    ratio = total_tokens / jnp.sum(jnp.where(weight > 0.0, counts, 0.0) * weight, axis=-1, keepdims=True)
    layer_rows, normed_two, inverse_two = norm_forward(first.astype(F32) + branch + vec(3), vec(4), vec(5))
    layer_ref[...] = layer_rows.astype(BF16)
    misfit = layer_rows - teacher_ref[...].astype(F32)
    weighted = valid_ref[...] * misfit
    out_grad = cotangent_ref[...].astype(F32) + weighted * ratio
    second_grad = norm_backward(out_grad, normed_two, inverse_two, vec(4))
    branch_grad = second_grad.astype(BF16)
    branch_grad_ref[...] = branch_grad
    sums_ref[0:1, :] += column_sum(weighted * misfit)
    sums_ref[1:2, :] += column_sum(branch_grad.astype(F32))
    sums_ref[2:3, :] += column_sum(out_grad * normed_two)
    sums_ref[3:4, :] += column_sum(out_grad)

    def down(slot, back):
        t = place_ref[slot]
        hidden_grad = (dot(branch_grad, w_up[slot]) * slope[slot]).astype(BF16)
        hidden_grad_ref[t] = hidden_grad
        inner_sums_ref[t] += column_sum(hidden_grad.astype(F32))
        return back + dot(hidden_grad, w_in[slot], NT)

    upstream = second_grad
    for slot in range(parts):
        upstream = down(slot, upstream)
    first_grad = norm_backward(upstream, normed_one, inverse_one, vec(1))
    first_grad_ref[...] = first_grad
    attn_grad = first_grad.astype(BF16)
    attn_grad_ref[...] = attn_grad
    sums_ref[4:5, :] += column_sum(attn_grad.astype(F32))
    sums_ref[5:6, :] += column_sum(upstream * normed_one)
    sums_ref[6:7, :] += column_sum(upstream)
    middle = BLOCK // 2
    for slot in range(parts):
        back = dot(attn_grad, w_out[slot, :, : 3 * DH]).astype(BF16)
        ctx_grad_ref[place_ref[slot], 0] = pack(
            back[:, : 2 * DH], back[:middle, 2 * DH :], back[middle:, 2 * DH :]
        )


    @pl.when(step == pl.num_programs(0) - 1)
    def _():
        lanes = 2 * DH
        gathered[...] = jnp.zeros_like(gathered)
        rows_each, inner_rows = width_of(sums_ref) // lanes, width_of(inner_sums_ref) // lanes
        per_note = gathered.shape[1] // lanes

        def put(at, value):
            gathered[at // per_note : at // per_note + 1, pl.ds(at % per_note * lanes, lanes)] = value

        for row in range(sums_ref.shape[0]):
            for k in range(rows_each):
                put(row * rows_each + k, sums_ref[row : row + 1, k * lanes : (k + 1) * lanes])
        for t in range(parts):
            for k in range(inner_rows):
                put(
                    sums_ref.shape[0] * rows_each + t * inner_rows + k,
                    inner_sums_ref[t, :, k * lanes : (k + 1) * lanes],
                )
        notes_ref[...] = gathered[...].astype(BF16)


def width_of(ref):
    return ref.shape[-1]


def run_dense(note_rows, marks, total_tokens, place, ctxs, rows_in, teacher, cotangent, valid, vecs, inner_bias, pieces):
    halves, parts = len(ctxs), ctxs[0].shape[0]
    part_len, width = rows_in.shape
    hidden_cols = inner_bias.shape[2]
    out_cols = pieces[0].shape[2] - 2 * hidden_cols
    room = -(-(8 * width + parts * hidden_cols) // (note_rows * 2 * DH)) * 2 * DH

    def by_rows(columns):
        return pl.BlockSpec((BLOCK, columns), lambda i: (i, 0))

    def by_part(columns):
        return pl.BlockSpec((parts, BLOCK, columns), lambda i: (0, i, 0))

    def fixed(shape):
        return pl.BlockSpec(shape, lambda i: (0,) * len(shape))

    packed_shape = (parts, halves) + ctxs[0].shape[1:]
    packed = pl.BlockSpec((parts, 1) + packed_shape[2:], lambda i: (0, i, 0, 0))
    low = jax.ShapeDtypeStruct((part_len, width), BF16)
    wide = jax.ShapeDtypeStruct((parts, part_len, hidden_cols), BF16)
    smem = pl.BlockSpec(memory_space=pltpu.SMEM)
    return pl.pallas_call(
        functools.partial(dense_chain, marks, halves, total_tokens),
        out_shape=(
            low,
            jax.ShapeDtypeStruct((part_len, width), F32),
            jax.ShapeDtypeStruct(packed_shape, BF16),
            low,
            low,
            low,
            wide,
            wide,
            jax.ShapeDtypeStruct((note_rows, room), BF16),
        ),
        grid=(halves,),
        in_specs=[
            smem,
            by_rows(width),
            by_rows(width),
            by_rows(width),
            by_rows(1),
            fixed(vecs.shape),
            fixed(inner_bias.shape),
        ]
        + [fixed(ctx.shape) for ctx in ctxs]
        + [pl.BlockSpec(memory_space=pl.ANY)] * len(pieces),
        out_specs=(
            by_rows(width),
            by_rows(width),
            packed,
            by_rows(width),
            by_rows(width),
            by_rows(width),
            by_part(hidden_cols),
            by_part(hidden_cols),
            fixed((note_rows, room)),
        ),
        scratch_shapes=[
            pltpu.VMEM((parts, width, out_cols), BF16),
            pltpu.VMEM((parts, width, hidden_cols), BF16),
            pltpu.VMEM((parts, width, hidden_cols), BF16),
            pltpu.VMEM((parts, BLOCK, hidden_cols), F32),
            pltpu.VMEM((8, width), F32),
            pltpu.VMEM((parts, 1, hidden_cols), F32),
            pltpu.VMEM((note_rows, room), F32),
            pltpu.SemaphoreType.DMA((3, parts)),
        ],
        compiler_params=pltpu.CompilerParams(
            dimension_semantics=("arbitrary",), vmem_limit_bytes=VMEM_LIMIT
        ),
        cost_estimate=pl.CostEstimate(
            flops=2 * part_len * width * (8 * hidden_cols + 4 * out_cols) * parts,
            bytes_accessed=24 << 20,
            transcendentals=2 * part_len * hidden_cols * parts,
        ),
        name="dense_chain",
    )(place, rows_in, teacher, cotangent, valid, vecs, inner_bias, *ctxs, *pieces)


def dense_weights(
    plans, halves, place_ref, first_ref, branch_grad_ref, attn_grad_ref, act_ref, hidden_grad_ref, notes_ref,
    *refs
):
    ctx_refs, outs, (whole, sems) = refs[:halves], refs[halves:-2], refs[-2:]
    step = pl.program_id(0)
    slots = whole.shape[0]

    def leave(start, stop):
        for out, turns in zip(outs, plans):
            block = out.shape[1]
            for at, turn in enumerate(turns):
                offset = 0
                if block < whole.shape[1]:
                    offset = pl.multiple_of((place_ref[place_ref.shape[0] - 1] ^ turn) * block, block)
                pltpu.make_async_copy(
                    whole.at[step, pl.ds(offset, block), pl.ds(start, stop - start)],
                    out.at[at * slots + step, :, pl.ds(start, stop - start)],
                    sems.at[step],
                ).start()

    hidden_cols = act_ref.shape[2]
    columns = whole.shape[2]
    in_parts = len(plans) == 1 and outs[0].shape[1] == whole.shape[1]
    whole[step, :, :hidden_cols] = dot(first_ref[...], hidden_grad_ref[0], TN).astype(BF16)
    if in_parts:
        leave(0, hidden_cols)
    whole[step, :, hidden_cols : 2 * hidden_cols] = dot(branch_grad_ref[...], act_ref[0], TN).astype(BF16)
    if in_parts:
        leave(hidden_cols, 2 * hidden_cols)
    ctx = jnp.concatenate([unpack(ref[0]) for ref in ctx_refs], axis=0)
    plain = 2 * hidden_cols + ctx.shape[1]
    whole[step, :, 2 * hidden_cols : plain] = dot(attn_grad_ref[...], ctx, TN).astype(BF16)
    note_rows, room = notes_ref.shape
    for at in range(whole.shape[1] // note_rows):
        whole[step, at * note_rows : (at + 1) * note_rows, plain : plain + room] = notes_ref[...]
    leave(2 * hidden_cols if in_parts else 0, columns)

    @pl.when(step == slots - 1)
    def _():
        for slot in range(slots):
            pltpu.make_async_copy(whole.at[slot], whole.at[slot], sems.at[slot]).wait()


def run_weights(base, slots, plans, place, notes, first, branch_grad, attn_grad, act, hidden_grad, ctxs):
    _, part_len, hidden_cols = act.shape
    width = first.shape[1]
    columns = 2 * hidden_cols + 3 * DH + notes.shape[1]
    fixed = pl.BlockSpec((part_len, width), lambda s, place: (0, 0))
    by_slot = pl.BlockSpec((1, part_len, hidden_cols), lambda s, place: (place[base + s], 0, 0))
    outs = tuple(
        jax.ShapeDtypeStruct((len(turns) * slots, block, columns), BF16) for block, turns in plans
    )
    return pl.pallas_call(
        functools.partial(dense_weights, tuple(turns for _, turns in plans), len(ctxs)),
        out_shape=outs,
        grid_spec=pltpu.PrefetchScalarGridSpec(
            num_scalar_prefetch=1,
            grid=(slots,),
            in_specs=[
                fixed,
                fixed,
                fixed,
                by_slot,
                by_slot,
                pl.BlockSpec(notes.shape, lambda s, place: (0, 0)),
            ]
            + [
                pl.BlockSpec((1,) + ctx.shape[1:], lambda s, place: (place[base + s], 0, 0)) for ctx in ctxs
            ],
            out_specs=tuple(pl.BlockSpec(memory_space=pl.ANY) for _ in outs),
            scratch_shapes=[
                pltpu.VMEM((slots, width, columns), BF16),
                pltpu.SemaphoreType.DMA((slots,)),
            ],
        ),
        compiler_params=pltpu.CompilerParams(
            dimension_semantics=("arbitrary",), vmem_limit_bytes=VMEM_LIMIT
        ),
        cost_estimate=pl.CostEstimate(
            flops=2 * part_len * width * columns * slots,
            bytes_accessed=5 * slots << 20,
            transcendentals=0,
        ),
        name="dense_weights",
    )(place, first, branch_grad, attn_grad, act, hidden_grad, notes, *ctxs)


def finish_dense(packed_ref, inner_ref, outer_ref, output_ref, notes_ref):
    hidden_cols = inner_ref.shape[1]
    summed = packed_ref[...].astype(F32)
    inner_ref[...] = summed[:, :hidden_cols]
    outer_ref[...] = summed[:, hidden_cols : 2 * hidden_cols]
    plain = 2 * hidden_cols + output_ref.shape[0]
    output_ref[...] = jnp.transpose(summed[:, 2 * hidden_cols : plain])
    notes_ref[...] = summed[:, plain:]


def run_finish_dense(packed, hidden_cols, head_cols):
    rows = packed.shape[0]
    return pl.pallas_call(
        finish_dense,
        out_shape=(
            jax.ShapeDtypeStruct((rows, hidden_cols), F32),
            jax.ShapeDtypeStruct((rows, hidden_cols), F32),
            jax.ShapeDtypeStruct((head_cols, rows), F32),
            jax.ShapeDtypeStruct((rows, packed.shape[1] - 2 * hidden_cols - head_cols), F32),
        ),
        name="finish_dense",
    )(packed)


def finish_heads(value_ref, *refs):
    summed = value_ref[...].astype(F32)
    heads = summed.shape[1] // SLAB
    for ref, which in zip(refs, (0, 2, 3, 1)):
        columns = [summed[:, SLAB * h + which * DH : SLAB * h + (which + 1) * DH] for h in range(heads)]
        ref[...] = jnp.concatenate(columns, axis=1)[: ref.shape[0]]


def run_finish_heads(value):
    rows, width = value.shape
    out = jax.ShapeDtypeStruct((rows, width // 4), F32)
    notes = jax.ShapeDtypeStruct((8, width // 4), F32)
    return pl.pallas_call(finish_heads, out_shape=(out, out, out, notes), name="finish_heads")(value)


def interleave(query, key, value, heads):
    rows = query.shape[0]
    parts = [part.reshape(rows, heads, 1, DH) for part in (query, jnp.zeros_like(query), key, value)]
    return jnp.concatenate(parts, axis=2).reshape(rows, heads * SLAB)


def swap(value, axis, bit):
    size = lax.axis_size(axis)
    return lax.ppermute(value, axis, [(i, i ^ bit) for i in range(size)])


def bits_of(axis):
    bit = 1
    while bit < lax.axis_size(axis):
        yield bit
        bit *= 2


def after(value, *others):
    return lax.optimization_barrier((value,) + others)[0]


def merge(held, other, axis, bit):
    mine_first = (lax.axis_index(axis) & bit) == 0
    return jnp.where(
        mine_first, jnp.concatenate([held, other], axis=0), jnp.concatenate([other, held], axis=0)
    )


def add_low(left_side, right_side):
    return (left_side.astype(F32) + right_side.astype(F32)).astype(BF16)


def add_halves(left_side, right_side):
    half = left_side.shape[0] // 2
    return (
        add_low(left_side[:half], right_side[:half]),
        add_low(left_side[half:], right_side[half:]),
    )


def scatter_rows(held):
    index = lax.axis_index("dp")
    for bit in bits_of("dp"):
        held = held.reshape((held.shape[0] // 2, 2) + held.shape[1:])
        own = (index & bit) // bit
        send = lax.dynamic_index_in_dim(held, 1 - own, 1, keepdims=False)
        keep = lax.dynamic_index_in_dim(held, own, 1, keepdims=False)
        held = add_low(keep, swap(send, "dp", bit))
    return held[0]


def local(
    inputs, segment_ids, valid_mask, teacher, cotangent,
    w_query, w_key, w_value, w_output, w_inner, w_outer,
    query_bias, value_bias, output_bias, inner_bias, outer_bias,
    gain_attn, shift_attn, gain_ffn, shift_ffn,
):
    _, part_len, width = inputs.shape
    parts = lax.axis_size("tensor")
    copies = lax.axis_size("dp")
    rank = lax.axis_index("tensor")
    total_tokens = part_len * parts * copies
    seq_len = part_len * parts
    head_cols = w_query.shape[1]
    heads = head_cols // DH
    hidden_cols = w_inner.shape[1]
    shard_rows = w_inner.shape[0]
    halves = part_len // BLOCK

    rows_in = inputs.reshape(part_len, width)
    tokens = lax.all_gather(rows_in, "tensor", axis=0, tiled=True)
    w_heads = interleave(w_query, w_key, w_value, heads)
    paired = shard_rows % 16 == 0 and parts == 4 and copies == 8

    valid_rows = valid_mask.astype(F32).reshape(part_len, 1)
    valid_count = jnp.sum(valid_mask.astype(F32))
    upper = jnp.floor(valid_count / 256.0)
    spot = lax.broadcasted_iota(jnp.int32, (shard_rows, DH), 0) * DH + lax.broadcasted_iota(
        jnp.int32, (shard_rows, DH), 1
    )
    count_row = jnp.where(spot == 0, upper, jnp.where(spot == 1, valid_count - 256.0 * upper, 0.0))
    mine = jnp.concatenate((w_inner, w_outer.T, w_output.T, count_row.astype(BF16)), axis=1)
    if paired:
        place = jnp.stack([rank, rank ^ 1, rank ^ 2, rank ^ 3, lax.axis_index("dp")]).astype(jnp.int32)
        pair = jnp.concatenate([mine[None], swap(mine[None], "tensor", 1)], axis=0)
        near = jnp.concatenate([pair, swap(pair, "dp", 2)], axis=0)
        turns = [0, 2, 4, 6]
        for bit in (1, 2, 4):
            w_heads = merge(w_heads, swap(w_heads, "dp", bit), "dp", bit)
        near, w_heads = lax.optimization_barrier((near, w_heads))
        near_next = swap(near, "dp", 4)
        tokens, pair, near_next = lax.optimization_barrier((tokens, pair, near_next))
        far = swap(pair, "tensor", 2)
    else:
        place = jnp.asarray(list(range(parts)) + [0], jnp.int32)
        weights = lax.all_gather(mine, ("tensor", "dp"), axis=0, tiled=False)
        for bit in bits_of("dp"):
            w_heads = merge(w_heads, swap(w_heads, "dp", bit), "dp", bit)

    mine_cols = rank * head_cols
    query_shift = lax.dynamic_slice_in_dim(query_bias, mine_cols, head_cols).astype(F32)
    value_shift = lax.dynamic_slice_in_dim(value_bias, mine_cols, head_cols).astype(F32)
    shifts = interleave(query_shift[None], jnp.zeros_like(query_shift)[None], value_shift[None], heads)
    qkv = [(dot(tokens, w_heads) + shifts).astype(BF16)]

    segment_row = segment_ids.reshape(seq_len)
    bounds = document_blocks(segment_row)
    seg_col = segment_row.reshape(seq_len, 1)
    seg_row = segment_row.reshape(1, seq_len)
    lane = rank.astype(jnp.int32).reshape(1)

    def exchange(packed_blocks):
        return lax.all_to_all(packed_blocks, "tensor", 0, 0)

    contexts, lses, arrived = [], [], []
    for half in range(halves):
        if paired and half == 1:
            far, contexts[0], bounds = lax.optimization_barrier((far, contexts[0], bounds))
            weights = lax.all_gather(far, "dp", axis=0, tiled=False)
        context, lse = run_forward((halves, half), lane, bounds, qkv, seg_col, seg_row)
        if half > 0:
            context, arrived[0] = lax.optimization_barrier((context, arrived[0]))
        contexts.append(context)
        lses.append(lse)
        arrived.append(exchange(context))
    if paired:
        near_next, context = lax.optimization_barrier((near_next, contexts[-1]))
        near = jnp.concatenate([near, near_next], axis=0)
        near_other = swap(near, "dp", 1)
    if paired:
        weights = weights.reshape((copies * 2,) + mine.shape)
        pieces = [near, near_other, weights]
        marks = [[(slot, turn ^ flip, True) for turn in turns for slot in (0, 1)] for flip in (0, 1)]
        marks.append([(2 + at % 2, at // 2, False) for at in range(2 * copies)])
    else:
        pieces = [weights.reshape(parts, width, -1)]
        marks = [[(t, 0, False) for t in range(parts)]]
    counts = [piece.reshape((-1,) + mine.shape)[:, 0, -DH : 2 - DH].astype(F32) for piece in pieces + [weights]]
    counts = jnp.concatenate(counts[:-1] if paired else counts[-1:], axis=0)
    counted = 256.0 * jnp.sum(counts[:, 0]) + jnp.sum(counts[:, 1])

    vecs = jnp.stack(
        (output_bias, gain_attn, shift_attn, outer_bias, gain_ffn, shift_ffn, outer_bias, outer_bias)
    ).astype(F32)
    inner_rows = inner_bias.astype(F32).reshape(parts, 1, hidden_cols)
    teacher_rows = teacher.reshape(part_len, width)
    cotangent_rows = cotangent.reshape(part_len, width)
    (
        layer_out, first_grad, context_grad, first, branch_grad, attn_grad, activated, hidden_grad, notes,
    ) = run_dense(
        shard_rows, marks, float(total_tokens), place, arrived, rows_in, teacher_rows, cotangent_rows, valid_rows, vecs,
        inner_rows, pieces,
    )
    head_grad = exchange(context_grad).reshape((parts * halves, PACKED, 2 * DH))
    sources = (first, branch_grad, attn_grad, activated, hidden_grad, arrived)
    if shard_rows % 16:
        notes = jnp.tile(notes, (copies, 1))
    if paired:
        keep_turns = (0, 4, 2, 6)
        (distant,) = run_weights(2, 2, ((width, (0,)),), place, notes, *sources)
        plans = tuple((shard_rows, tuple(turn | flip for turn in keep_turns)) for flip in (0, 1))
        keep, send = run_weights(0, 2, plans, place, notes, *sources)
        keep, send = (value.reshape((4, 2) + value.shape[1:]) for value in (keep, send))
        distant = lax.psum_scatter(distant, "dp", scatter_dimension=1, tiled=True)
        came = swap(send, "dp", 1)
    else:
        (packed,) = run_weights(0, parts, ((width, (0,)),), place, notes, *sources)
        packed = lax.psum_scatter(packed, "dp", scatter_dimension=1, tiled=True)

    joined_grad, sums = run_backward(lane, bounds, qkv, seg_col, seg_row, head_grad, contexts, lses)
    joined_grad = joined_grad.reshape(seq_len, -1)
    attn_back = dot(joined_grad, w_heads, NT).astype(BF16)
    if paired:
        came = after(came, attn_back)
    attn_back, sums, joined_grad = lax.optimization_barrier((attn_back, sums, joined_grad))
    attn_back = lax.psum_scatter(attn_back, "tensor", scatter_dimension=0, tiled=True)
    if paired:
        keep, send = add_halves(keep, came)
        keep, send, joined_grad = lax.optimization_barrier((keep, send, joined_grad))
        came = swap(send, "dp", 2)
    head_weights = dot(tokens, joined_grad, TN).reshape((copies, shard_rows, -1))
    if paired:
        came, head_weights = lax.optimization_barrier((came, head_weights))
        keep, send = add_halves(keep, came)
        keep, send, head_weights = lax.optimization_barrier((keep, send, head_weights))
        came = swap(send, "dp", 4)
    sums = sums.reshape(heads, 4, DH)
    sums = jnp.concatenate((sums[:, 0].reshape(1, head_cols), sums[:, 3].reshape(1, head_cols)), axis=1)
    for bit in bits_of("tensor"):
        sums = merge(sums, swap(sums, "tensor", bit), "tensor", bit)
    if paired:
        came, head_weights = lax.optimization_barrier((came, head_weights))
        slots = jnp.concatenate([add_low(keep, came)[0], distant], axis=0)
        packed = jnp.stack(
            [lax.dynamic_index_in_dim(slots, rank ^ t, 0, keepdims=False) for t in range(parts)]
        )
    packed = lax.psum_scatter(packed, "tensor", scatter_dimension=0, tiled=True)[0]
    biases = jnp.concatenate((sums[:, :head_cols].reshape(-1), sums[:, head_cols:].reshape(-1)))
    biases = jnp.pad(
        biases.reshape(8, heads, 1, DH), ((0, shard_rows - 8), (0, 0), (1, 2), (0, 0))
    ).reshape(1, shard_rows, -1)
    query_grad, key_grad, value_grad, biases = run_finish_heads(
        scatter_rows((head_weights + biases).astype(BF16))
    )
    biases = biases.reshape(2, width)
    input_grad = first_grad + attn_back.astype(F32)

    inner_grad, outer_grad, output_grad, notes = run_finish_dense(packed, hidden_cols, head_cols)
    notes = notes.reshape(-1)

    def total(which):
        return notes[which * width : (which + 1) * width]

    mse_loss = jnp.sum(total(0)) / (counted * width)
    return (
        layer_out.reshape(1, part_len, width),
        mse_loss,
        input_grad.reshape(1, part_len, width),
        query_grad,
        key_grad,
        value_grad,
        output_grad,
        inner_grad,
        outer_grad.T,
        biases[0],
        biases[1],
        total(4),
        notes[8 * width : 8 * width + hidden_cols * parts],
        total(1),
        total(5),
        total(6),
        total(2),
        total(3),
    )


def solution(mesh):
    shard = P("dp", "tensor", None)
    by_dp, by_tensor = P("dp", "tensor"), P("tensor", "dp")
    in_specs = (
        (shard, P("dp", None), by_dp, shard, shard)
        + (by_dp,) * 3
        + (by_tensor, by_dp, by_tensor)
        + (P(),) * 9
    )
    out_specs = (shard, P(), shard) + (by_dp,) * 3 + (by_tensor, by_dp, by_tensor) + (P(),) * 9
    return jax.shard_map(local, mesh=mesh, in_specs=in_specs, out_specs=out_specs, check_vma=False)
```

```python
import functools

import jax
import jax.numpy as jnp
from jax import lax
from jax.experimental import pallas as pl
from jax.experimental.pallas import tpu as pltpu
from jax.sharding import PartitionSpec as P

DH = 64
BLOCK = 256
SLAB = 4 * DH
EPSILON = 1e-12
ROOT_HALF = 0.7071067811865476
INV_ROOT_TAU = 0.3989422804014327
LOG2E = 1.4426950408889634
LN2 = 0.6931471805599453
SCALE = DH ** (-0.5)
MASKED = -1e30
VMEM_LIMIT = 60 << 20

BF16 = jnp.bfloat16
F32 = jnp.float32
NN = (((1,), (0,)), ((), ()))
NT = (((1,), (1,)), ((), ()))
TN = (((0,), (0,)), ((), ()))


def dot(left_side, right_side, dims=NN):
    return lax.dot_general(left_side, right_side, dims, preferred_element_type=F32)


def norm_forward(summed, gain_vec, shift_vec):
    average = jnp.mean(summed, axis=-1, keepdims=True)
    centered = summed - average
    variance = jnp.mean(centered * centered, axis=-1, keepdims=True)
    inverse = lax.rsqrt(variance + EPSILON)
    normed = centered * inverse
    return (normed * gain_vec + shift_vec, normed, inverse)


def norm_backward(upstream, normed, inverse, gain_vec):
    scaled = upstream * gain_vec
    first_mean = jnp.mean(scaled, axis=-1, keepdims=True)
    second_mean = jnp.mean(scaled * normed, axis=-1, keepdims=True)
    return inverse * (scaled - first_mean - normed * second_mean)


def column_sum(value):
    return jnp.sum(value, axis=0, keepdims=True)


def lane_is_right(rows):
    return lax.broadcasted_iota(jnp.int32, (rows, 2 * DH), 1) >= DH


def pack(first_two, third_top, third_bottom):
    return jnp.concatenate([first_two, jnp.concatenate([third_top, third_bottom], axis=1)], axis=0)


def unpack(packed):
    third = packed[BLOCK:]
    third = jnp.concatenate([third[:, :DH], third[:, DH:]], axis=0)
    return jnp.concatenate([packed[:BLOCK], third], axis=1)


def fetch_chunks(lane_ref, chunk_refs, target, sems):
    rows = chunk_refs[0].shape[0]
    copies = []
    for at, chunk in enumerate(chunk_refs):
        offset = pl.multiple_of(lax.rem(lane_ref[0] + at, len(chunk_refs)) * rows, rows)
        copies.append(pltpu.make_async_copy(chunk, target.at[pl.ds(offset, rows), :], sems.at[at]))
    return copies


def attend_forward(
    which, lane_ref, low_ref, count_ref, *refs
):
    chunk_refs, (seg_col_ref, seg_row_ref, ctx_ref, lse_ref, held, qkv_ref, sems) = refs[:-7], refs[-7:]
    heads = lse_ref.shape[0]

    @pl.when(pl.program_id(0) == 0)
    def _():
        copies = fetch_chunks(lane_ref, chunk_refs, qkv_ref, sems)
        for copy in copies:
            copy.start()
        for copy in copies:
            copy.wait()

    halves, half = which
    qb = pl.program_id(0) * halves + half
    rows = pl.ds(pl.multiple_of(qb * BLOCK, BLOCK), BLOCK)
    seg_q = seg_col_ref[...]
    queries = [
        qkv_ref[rows, SLAB * h : SLAB * h + 2 * DH] * jnp.asarray(SCALE, BF16) for h in range(heads)
    ]
    low, count = low_ref[qb], count_ref[qb]

    def score(kb, peaks):
        keys = pl.ds(pl.multiple_of(low * STEP + kb * BLOCK, STEP), BLOCK)
        allowed = seg_q == seg_row_ref[:, keys]
        found = []
        for h in range(heads):
            scores = dot(queries[h], qkv_ref[keys, SLAB * h + 2 * DH : SLAB * (h + 1)], NT)
            scores = jnp.where(allowed, scores, MASKED)
            held[h, kb] = scores
            found.append(jnp.maximum(peaks[h], jnp.maximum(scores[:, :128], scores[:, 128:])))
        return tuple(found)

    start = tuple(jnp.full((BLOCK, 128), MASKED, F32) for _ in range(heads))
    peaks = lax.fori_loop(0, count, score, start)
    highest = [jnp.max(peak, axis=-1, keepdims=True) for peak in peaks]

    def weigh(kb, carry):
        keys = pl.ds(pl.multiple_of(low * STEP + kb * BLOCK, STEP), BLOCK)
        found = []
        for h in range(heads):
            total, acc = carry[h]
            raised = jnp.exp2((held[h, kb] - highest[h]) * LOG2E)
            total = total + (raised[:, :128] + raised[:, 128:])
            acc = acc + dot(raised.astype(BF16), qkv_ref[keys, SLAB * h + 2 * DH : SLAB * (h + 1)])
            found.append((total, acc))
        return tuple(found)

    zero = jnp.zeros((BLOCK, 128), F32)
    done = lax.fori_loop(0, count, weigh, tuple((zero, zero) for _ in range(heads)))
    values = []
    for h in range(heads):
        total, acc = done[h]
        summed = jnp.sum(total, axis=-1, keepdims=True)
        values.append((acc / summed).astype(BF16))
        lse_ref[h] = jnp.transpose(highest[h] + jnp.log(summed))
    middle = BLOCK // 2
    ctx_ref[0, :BLOCK, :] = jnp.where(lane_is_right(BLOCK), values[1], pltpu.roll(values[0], DH, 1))
    ctx_ref[0, BLOCK:, :] = jnp.where(
        lane_is_right(middle), values[2][middle:], pltpu.roll(values[2][:middle], DH, 1)
    )


def attend_backward(halves, chunks, lane_ref, low_ref, count_ref, *refs):
    chunk_refs, refs = refs[:chunks], refs[chunks:]
    (seg_col_ref, seg_row_ref, grad_ref), refs = refs[:3], refs[3:]
    ctx_refs, lse_refs, refs = refs[:halves], refs[halves : 2 * halves], refs[2 * halves :]
    final_ref, sums_ref, dkv, out_ref, qkv_ref, sems = refs
    heads = dkv.shape[0]
    qb = pl.program_id(0)
    half = lax.rem(qb, halves)

    def choose(options):
        value = options[0][...]
        for other in range(1, halves):
            value = jnp.where(half == other, options[other][...], value)
        return value

    @pl.when(qb == 0)
    def _():
        copies = fetch_chunks(lane_ref, chunk_refs, qkv_ref, sems)
        for copy in copies:
            copy.start()
        dkv[...] = jnp.zeros_like(dkv)
        for copy in copies:
            copy.wait()

    rows = pl.ds(pl.multiple_of(qb * BLOCK, BLOCK), BLOCK)
    right = lane_is_right(BLOCK)
    arrived = grad_ref[0]
    product = arrived.astype(F32) * choose(ctx_refs)[0].astype(F32)
    upper = product.astype(BF16)
    lower = (product - upper.astype(F32)).astype(BF16)
    pick = (
        lax.broadcasted_iota(jnp.int32, (8, 2 * DH), 1) // DH
        == lax.broadcasted_iota(jnp.int32, (8, 2 * DH), 0)
    ).astype(BF16)
    summed = dot(pick, upper, NT) + dot(pick, lower, NT)
    deltas = [
        summed[0:1, :BLOCK],
        summed[1:2, :BLOCK],
        jnp.concatenate([summed[0:1, BLOCK:], summed[1:2, BLOCK:]], axis=1),
    ]
    two, third = arrived[:BLOCK], arrived[BLOCK:]
    placed = [
        pltpu.roll(two, DH, 1),
        two,
        jnp.concatenate([pltpu.roll(third, DH, 1), third], axis=0),
    ]
    grads = [jnp.where(right, grad, jnp.zeros_like(grad)) for grad in placed]
    queries, pairs = [], []
    for h in range(heads):
        queries.append(qkv_ref[rows, SLAB * h : SLAB * h + 2 * DH] * jnp.asarray(SCALE, BF16))
        pairs.append(jnp.concatenate([queries[h], grads[h]], axis=0))
    seg_q = seg_row_ref[...]
    lses = choose(lse_refs)
    low, count = low_ref[qb], count_ref[qb]

    def step(kb, accs):
        keys = pl.ds(pl.multiple_of(low * STEP + kb * BLOCK, STEP), BLOCK)
        allowed = seg_col_ref[keys, :] == seg_q
        keyed = [qkv_ref[keys, SLAB * h + 2 * DH : SLAB * (h + 1)] for h in range(heads)]
        raw = [dot(keyed[h], queries[h], NT) for h in range(heads)]
        probs_grads = [dot(keyed[h], grads[h], NT) for h in range(heads)]
        both = []
        for h in range(heads):
            probs = jnp.exp2((jnp.where(allowed, raw[h], MASKED) - lses[h]) * LOG2E)
            score_grad = (probs * (probs_grads[h] - deltas[h])).astype(BF16)
            both.append((score_grad, probs.astype(BF16)))
        found = []
        for h in range(heads):
            dkv[h, keys, :] += dot(jnp.concatenate(both[h], axis=1), pairs[h])
            found.append(accs[h] + dot(both[h][0], keyed[h], TN))
        return tuple(found)

    zero = jnp.zeros((BLOCK, 128), F32)
    accs = lax.fori_loop(0, count, step, tuple(zero for _ in range(heads)))
    for h in range(heads):
        query_grad = jnp.where(right, 0.0, accs[h] * SCALE).astype(BF16)
        out_ref[rows, SLAB * h : SLAB * h + 2 * DH] = query_grad

    @pl.when(qb == pl.num_programs(0) - 1)
    def _():
        for h in range(heads):
            at = SLAB * h
            out_ref[:, at + 2 * DH : at + SLAB] = dkv[h].astype(BF16)
            sums_ref[:, at : at + SLAB] = column_sum(out_ref[:, at : at + SLAB].astype(F32))
        rows_each = final_ref.shape[1]
        copies = []
        for at in range(final_ref.shape[0]):
            offset = pl.multiple_of(lax.rem(lane_ref[0] + at, final_ref.shape[0]) * rows_each, rows_each)
            copies.append(
                pltpu.make_async_copy(out_ref.at[pl.ds(offset, rows_each), :], final_ref.at[at], sems.at[at])
            )
        for copy in copies:
            copy.start()
        for copy in copies:
            copy.wait()


STEP = 128


def document_blocks(segment_row):
    starts = segment_row[::BLOCK]
    stops = segment_row[BLOCK - 1 :: BLOCK]
    low = jnp.sum((segment_row[None, :] < starts[:, None]).astype(jnp.int32), axis=1) // STEP
    high = jnp.sum((segment_row[None, :] <= stops[:, None]).astype(jnp.int32), axis=1)
    each = BLOCK // STEP
    count = (high - low * STEP + BLOCK - 1) // BLOCK
    return (jnp.minimum(low, segment_row.shape[0] // STEP - each * count), count)


PACKED = BLOCK + BLOCK // 2


def run_forward(which, lane, bounds, qkv, seg_col, seg_row):
    halves, half = which
    seq_len, width = seg_col.shape[0], qkv[0].shape[1]
    heads = width // SLAB
    blocks = seq_len // BLOCK
    steps = blocks // halves
    return pl.pallas_call(
        functools.partial(attend_forward, which),
        out_shape=(
            jax.ShapeDtypeStruct((steps, PACKED, 2 * DH), BF16),
            jax.ShapeDtypeStruct((heads, 1, steps * BLOCK), F32),
        ),
        grid_spec=pltpu.PrefetchScalarGridSpec(
            num_scalar_prefetch=3,
            grid=(steps,),
            in_specs=[pl.BlockSpec(memory_space=pl.ANY)] * len(qkv)
            + [
                pl.BlockSpec((BLOCK, 1), lambda q, *_: (q * halves + half, 0)),
                pl.BlockSpec((1, seq_len), lambda q, *_: (0, 0)),
            ],
            out_specs=(
                pl.BlockSpec((1, PACKED, 2 * DH), lambda q, *_: (q, 0, 0)),
                pl.BlockSpec((heads, 1, BLOCK), lambda q, *_: (0, 0, q)),
            ),
            scratch_shapes=[
                pltpu.VMEM((heads, blocks, BLOCK, BLOCK), F32),
                pltpu.VMEM((seq_len, width), BF16),
                pltpu.SemaphoreType.DMA((len(qkv),)),
            ],
        ),
        compiler_params=pltpu.CompilerParams(
            dimension_semantics=("arbitrary",), vmem_limit_bytes=VMEM_LIMIT if half else 28 << 20
        ),
        cost_estimate=pl.CostEstimate(
            flops=heads * seq_len * seq_len * 2048 * steps // blocks,
            bytes_accessed=5 << 20,
            transcendentals=heads * seq_len * seq_len // 3,
        ),
        name="attend_forward",
    )(lane, *bounds, *qkv, seg_col, seg_row)


def run_backward(lane, bounds, qkv, seg_col, seg_row, grad, ctxs, lses):
    seq_len, width = seg_col.shape[0], qkv[0].shape[1]
    heads = width // SLAB
    halves = len(ctxs)

    def fixed(shape):
        return pl.BlockSpec(shape, lambda q, *_: (0,) * len(shape))

    return pl.pallas_call(
        functools.partial(attend_backward, halves, len(qkv)),
        out_shape=(
            jax.ShapeDtypeStruct((len(qkv), seq_len // len(qkv), width), BF16),
            jax.ShapeDtypeStruct((1, width), F32),
        ),
        grid_spec=pltpu.PrefetchScalarGridSpec(
            num_scalar_prefetch=3,
            grid=(seq_len // BLOCK,),
            in_specs=[pl.BlockSpec(memory_space=pl.ANY)] * len(qkv)
            + [
                fixed((seq_len, 1)),
                pl.BlockSpec((1, BLOCK), lambda q, *_: (0, q)),
                pl.BlockSpec((1, PACKED, 2 * DH), lambda q, *_: (q, 0, 0)),
            ]
            + [pl.BlockSpec((1, PACKED, 2 * DH), lambda q, *_: (q // halves, 0, 0))] * halves
            + [pl.BlockSpec((heads, 1, BLOCK), lambda q, *_: (0, 0, q // halves))] * halves,
            out_specs=(pl.BlockSpec(memory_space=pl.ANY), fixed((1, width))),
            scratch_shapes=[
                pltpu.VMEM((heads, seq_len, 2 * DH), F32),
                pltpu.VMEM((seq_len, width), BF16),
                pltpu.VMEM((seq_len, width), BF16),
                pltpu.SemaphoreType.DMA((len(qkv),)),
            ],
        ),
        compiler_params=pltpu.CompilerParams(
            dimension_semantics=("arbitrary",), vmem_limit_bytes=28 << 20
        ),
        cost_estimate=pl.CostEstimate(
            flops=heads * seq_len * seq_len * 4096,
            bytes_accessed=10 << 20,
            transcendentals=heads * seq_len * seq_len // 3,
        ),
        name="attend_backward",
    )(lane, *bounds, *qkv, seg_col, seg_row, grad, *ctxs, *lses)


def dense_chain(
    marks, halves, total_tokens, place_ref, in_ref, teacher_ref, cotangent_ref, valid_ref, vec_ref,
    inner_bias_ref, *refs
):
    ctx_refs, refs = refs[:halves], refs[halves:]
    pieces = refs[: len(marks)]
    (
        layer_ref, first_grad_ref, ctx_grad_ref, first_ref, branch_grad_ref, attn_grad_ref,
        act_ref, hidden_grad_ref, notes_ref, w_out, w_in, w_up, slope, sums_ref, inner_sums_ref,
        gathered, sems,
    ) = refs[len(marks) :]
    parts, _, head_cols = w_out.shape
    hidden_cols = w_in.shape[2]
    index = place_ref[parts]
    step = pl.program_id(0)
    groups = (
        (2 * hidden_cols, head_cols, w_out),
        (0, hidden_cols, w_in),
        (hidden_cols, hidden_cols, w_up),
    )

    @pl.when(step == 0)
    def _():
        order = [(0, slot) for slot in range(parts)]
        order += [(group, slot) for slot in range(parts) for group in (1, 2)]
        for group, wanted in order:
            start, size, target = groups[group]
            for piece, marked in zip(pieces, marks):
                block = piece.shape[1]
                for at, (slot, turn, relative) in enumerate(marked):
                    if slot != wanted:
                        continue
                    offset = pl.multiple_of((index ^ turn) * block, block) if relative else turn * block
                    pltpu.make_async_copy(
                        piece.at[at, :, pl.ds(start, size)],
                        target.at[slot, pl.ds(offset, block), :],
                        sems.at[group, slot],
                    ).start()
        sums_ref[...] = jnp.zeros_like(sums_ref)
        inner_sums_ref[...] = jnp.zeros_like(inner_sums_ref)

    def context(t):
        value = ctx_refs[0][t]
        for half in range(1, halves):
            value = jnp.where(step == half, ctx_refs[half][t], value)
        return value

    def arrive(group, slot):
        whole = groups[group][2].at[slot]

        @pl.when(step == 0)
        def _():
            pltpu.make_async_copy(whole, whole, sems.at[group, slot]).wait()

    def vec(which):
        return vec_ref[which : which + 1, :]

    counts = jnp.zeros((1, 2 * DH), F32)

    attention = jnp.zeros(in_ref.shape, F32)
    for slot in range(parts):
        arrive(0, slot)
        counts = counts + column_sum(w_out[slot, :, 2 * DH :].astype(F32))
        attention = attention + dot(unpack(context(place_ref[slot])), w_out[slot, :, : 3 * DH], NT)
    first_exact, normed_one, inverse_one = norm_forward(
        in_ref[...].astype(F32) + attention + vec(0), vec(1), vec(2)
    )
    first = first_exact.astype(BF16)
    first_ref[...] = first

    def up(slot, branch):
        t = place_ref[slot]
        arrive(1, slot)
        hidden = dot(first, w_in[slot]) + inner_bias_ref[t]
        bend = 0.5 * (1.0 + lax.erf(hidden * ROOT_HALF))
        activated = (hidden * bend).astype(BF16)
        act_ref[t] = activated
        slope[slot] = bend + hidden * INV_ROOT_TAU * jnp.exp2(hidden * hidden * (-0.5 * LOG2E))
        arrive(2, slot)
        return branch + dot(activated, w_up[slot], NT)

    branch = jnp.zeros(in_ref.shape, F32)
    for slot in range(parts):
        branch = up(slot, branch)
    lanes = lax.broadcasted_iota(jnp.int32, counts.shape, 1)
    weight = jnp.where(lanes == DH, 256.0, jnp.where(lanes == DH + 1, 1.0, 0.0))
    ratio = total_tokens / jnp.sum(jnp.where(weight > 0.0, counts, 0.0) * weight, axis=-1, keepdims=True)
    layer_rows, normed_two, inverse_two = norm_forward(first.astype(F32) + branch + vec(3), vec(4), vec(5))
    layer_ref[...] = layer_rows.astype(BF16)
    misfit = layer_rows - teacher_ref[...].astype(F32)
    weighted = valid_ref[...] * misfit
    out_grad = cotangent_ref[...].astype(F32) + weighted * ratio
    second_grad = norm_backward(out_grad, normed_two, inverse_two, vec(4))
    branch_grad = second_grad.astype(BF16)
    branch_grad_ref[...] = branch_grad
    sums_ref[0:1, :] += column_sum(weighted * misfit)
    sums_ref[1:2, :] += column_sum(branch_grad.astype(F32))
    sums_ref[2:3, :] += column_sum(out_grad * normed_two)
    sums_ref[3:4, :] += column_sum(out_grad)

    def down(slot, back):
        t = place_ref[slot]
        hidden_grad = (dot(branch_grad, w_up[slot]) * slope[slot]).astype(BF16)
        hidden_grad_ref[t] = hidden_grad
        inner_sums_ref[t] += column_sum(hidden_grad.astype(F32))
        return back + dot(hidden_grad, w_in[slot], NT)

    upstream = second_grad
    for slot in range(parts):
        upstream = down(slot, upstream)
    first_grad = norm_backward(upstream, normed_one, inverse_one, vec(1))
    first_grad_ref[...] = first_grad
    attn_grad = first_grad.astype(BF16)
    attn_grad_ref[...] = attn_grad
    sums_ref[4:5, :] += column_sum(attn_grad.astype(F32))
    sums_ref[5:6, :] += column_sum(upstream * normed_one)
    sums_ref[6:7, :] += column_sum(upstream)
    middle = BLOCK // 2
    for slot in range(parts):
        back = dot(attn_grad, w_out[slot, :, : 3 * DH]).astype(BF16)
        ctx_grad_ref[place_ref[slot], 0] = pack(
            back[:, : 2 * DH], back[:middle, 2 * DH :], back[middle:, 2 * DH :]
        )


    @pl.when(step == pl.num_programs(0) - 1)
    def _():
        lanes = 2 * DH
        gathered[...] = jnp.zeros_like(gathered)
        rows_each, inner_rows = width_of(sums_ref) // lanes, width_of(inner_sums_ref) // lanes
        per_note = gathered.shape[1] // lanes

        def put(at, value):
            gathered[at // per_note : at // per_note + 1, pl.ds(at % per_note * lanes, lanes)] = value

        for row in range(sums_ref.shape[0]):
            for k in range(rows_each):
                put(row * rows_each + k, sums_ref[row : row + 1, k * lanes : (k + 1) * lanes])
        for t in range(parts):
            for k in range(inner_rows):
                put(
                    sums_ref.shape[0] * rows_each + t * inner_rows + k,
                    inner_sums_ref[t, :, k * lanes : (k + 1) * lanes],
                )
        notes_ref[...] = gathered[...].astype(BF16)


def width_of(ref):
    return ref.shape[-1]


def run_dense(note_rows, marks, total_tokens, place, ctxs, rows_in, teacher, cotangent, valid, vecs, inner_bias, pieces):
    halves, parts = len(ctxs), ctxs[0].shape[0]
    part_len, width = rows_in.shape
    hidden_cols = inner_bias.shape[2]
    out_cols = pieces[0].shape[2] - 2 * hidden_cols
    room = -(-(8 * width + parts * hidden_cols) // (note_rows * 2 * DH)) * 2 * DH

    def by_rows(columns):
        return pl.BlockSpec((BLOCK, columns), lambda i: (i, 0))

    def by_part(columns):
        return pl.BlockSpec((parts, BLOCK, columns), lambda i: (0, i, 0))

    def fixed(shape):
        return pl.BlockSpec(shape, lambda i: (0,) * len(shape))

    packed_shape = (parts, halves) + ctxs[0].shape[1:]
    packed = pl.BlockSpec((parts, 1) + packed_shape[2:], lambda i: (0, i, 0, 0))
    low = jax.ShapeDtypeStruct((part_len, width), BF16)
    wide = jax.ShapeDtypeStruct((parts, part_len, hidden_cols), BF16)
    smem = pl.BlockSpec(memory_space=pltpu.SMEM)
    return pl.pallas_call(
        functools.partial(dense_chain, marks, halves, total_tokens),
        out_shape=(
            low,
            jax.ShapeDtypeStruct((part_len, width), F32),
            jax.ShapeDtypeStruct(packed_shape, BF16),
            low,
            low,
            low,
            wide,
            wide,
            jax.ShapeDtypeStruct((note_rows, room), BF16),
        ),
        grid=(halves,),
        in_specs=[
            smem,
            by_rows(width),
            by_rows(width),
            by_rows(width),
            by_rows(1),
            fixed(vecs.shape),
            fixed(inner_bias.shape),
        ]
        + [fixed(ctx.shape) for ctx in ctxs]
        + [pl.BlockSpec(memory_space=pl.ANY)] * len(pieces),
        out_specs=(
            by_rows(width),
            by_rows(width),
            packed,
            by_rows(width),
            by_rows(width),
            by_rows(width),
            by_part(hidden_cols),
            by_part(hidden_cols),
            fixed((note_rows, room)),
        ),
        scratch_shapes=[
            pltpu.VMEM((parts, width, out_cols), BF16),
            pltpu.VMEM((parts, width, hidden_cols), BF16),
            pltpu.VMEM((parts, width, hidden_cols), BF16),
            pltpu.VMEM((parts, BLOCK, hidden_cols), F32),
            pltpu.VMEM((8, width), F32),
            pltpu.VMEM((parts, 1, hidden_cols), F32),
            pltpu.VMEM((note_rows, room), F32),
            pltpu.SemaphoreType.DMA((3, parts)),
        ],
        compiler_params=pltpu.CompilerParams(
            dimension_semantics=("arbitrary",), vmem_limit_bytes=VMEM_LIMIT
        ),
        cost_estimate=pl.CostEstimate(
            flops=2 * part_len * width * (8 * hidden_cols + 4 * out_cols) * parts,
            bytes_accessed=24 << 20,
            transcendentals=2 * part_len * hidden_cols * parts,
        ),
        name="dense_chain",
    )(place, rows_in, teacher, cotangent, valid, vecs, inner_bias, *ctxs, *pieces)


def dense_weights(
    plans, halves, place_ref, first_ref, branch_grad_ref, attn_grad_ref, act_ref, hidden_grad_ref, notes_ref,
    *refs
):
    ctx_refs, outs, (whole, sems) = refs[:halves], refs[halves:-2], refs[-2:]
    step = pl.program_id(0)
    slots = whole.shape[0]

    def leave(start, stop):
        for out, turns in zip(outs, plans):
            block = out.shape[1]
            for at, turn in enumerate(turns):
                offset = 0
                if block < whole.shape[1]:
                    offset = pl.multiple_of((place_ref[place_ref.shape[0] - 1] ^ turn) * block, block)
                pltpu.make_async_copy(
                    whole.at[step, pl.ds(offset, block), pl.ds(start, stop - start)],
                    out.at[at * slots + step, :, pl.ds(start, stop - start)],
                    sems.at[step],
                ).start()

    hidden_cols = act_ref.shape[2]
    columns = whole.shape[2]
    in_parts = len(plans) == 1 and outs[0].shape[1] == whole.shape[1]
    whole[step, :, :hidden_cols] = dot(first_ref[...], hidden_grad_ref[0], TN).astype(BF16)
    if in_parts:
        leave(0, hidden_cols)
    whole[step, :, hidden_cols : 2 * hidden_cols] = dot(branch_grad_ref[...], act_ref[0], TN).astype(BF16)
    if in_parts:
        leave(hidden_cols, 2 * hidden_cols)
    ctx = jnp.concatenate([unpack(ref[0]) for ref in ctx_refs], axis=0)
    plain = 2 * hidden_cols + ctx.shape[1]
    whole[step, :, 2 * hidden_cols : plain] = dot(attn_grad_ref[...], ctx, TN).astype(BF16)
    note_rows, room = notes_ref.shape
    for at in range(whole.shape[1] // note_rows):
        whole[step, at * note_rows : (at + 1) * note_rows, plain : plain + room] = notes_ref[...]
    leave(2 * hidden_cols if in_parts else 0, columns)

    @pl.when(step == slots - 1)
    def _():
        for slot in range(slots):
            pltpu.make_async_copy(whole.at[slot], whole.at[slot], sems.at[slot]).wait()


def run_weights(base, slots, plans, place, notes, first, branch_grad, attn_grad, act, hidden_grad, ctxs):
    _, part_len, hidden_cols = act.shape
    width = first.shape[1]
    columns = 2 * hidden_cols + 3 * DH + notes.shape[1]
    fixed = pl.BlockSpec((part_len, width), lambda s, place: (0, 0))
    by_slot = pl.BlockSpec((1, part_len, hidden_cols), lambda s, place: (place[base + s], 0, 0))
    outs = tuple(
        jax.ShapeDtypeStruct((len(turns) * slots, block, columns), BF16) for block, turns in plans
    )
    return pl.pallas_call(
        functools.partial(dense_weights, tuple(turns for _, turns in plans), len(ctxs)),
        out_shape=outs,
        grid_spec=pltpu.PrefetchScalarGridSpec(
            num_scalar_prefetch=1,
            grid=(slots,),
            in_specs=[
                fixed,
                fixed,
                fixed,
                by_slot,
                by_slot,
                pl.BlockSpec(notes.shape, lambda s, place: (0, 0)),
            ]
            + [
                pl.BlockSpec((1,) + ctx.shape[1:], lambda s, place: (place[base + s], 0, 0)) for ctx in ctxs
            ],
            out_specs=tuple(pl.BlockSpec(memory_space=pl.ANY) for _ in outs),
            scratch_shapes=[
                pltpu.VMEM((slots, width, columns), BF16),
                pltpu.SemaphoreType.DMA((slots,)),
            ],
        ),
        compiler_params=pltpu.CompilerParams(
            dimension_semantics=("arbitrary",), vmem_limit_bytes=VMEM_LIMIT
        ),
        cost_estimate=pl.CostEstimate(
            flops=2 * part_len * width * columns * slots,
            bytes_accessed=5 * slots << 20,
            transcendentals=0,
        ),
        name="dense_weights",
    )(place, first, branch_grad, attn_grad, act, hidden_grad, notes, *ctxs)


def finish_dense(packed_ref, inner_ref, outer_ref, output_ref, notes_ref):
    hidden_cols = inner_ref.shape[1]
    summed = packed_ref[...].astype(F32)
    inner_ref[...] = summed[:, :hidden_cols]
    outer_ref[...] = summed[:, hidden_cols : 2 * hidden_cols]
    plain = 2 * hidden_cols + output_ref.shape[0]
    output_ref[...] = jnp.transpose(summed[:, 2 * hidden_cols : plain])
    notes_ref[...] = summed[:, plain:]


def run_finish_dense(packed, hidden_cols, head_cols):
    rows = packed.shape[0]
    return pl.pallas_call(
        finish_dense,
        out_shape=(
            jax.ShapeDtypeStruct((rows, hidden_cols), F32),
            jax.ShapeDtypeStruct((rows, hidden_cols), F32),
            jax.ShapeDtypeStruct((head_cols, rows), F32),
            jax.ShapeDtypeStruct((rows, packed.shape[1] - 2 * hidden_cols - head_cols), F32),
        ),
        name="finish_dense",
    )(packed)


def finish_heads(value_ref, *refs):
    summed = value_ref[...].astype(F32)
    heads = summed.shape[1] // SLAB
    for ref, which in zip(refs, (0, 2, 3, 1)):
        columns = [summed[:, SLAB * h + which * DH : SLAB * h + (which + 1) * DH] for h in range(heads)]
        ref[...] = jnp.concatenate(columns, axis=1)[: ref.shape[0]]


def run_finish_heads(value):
    rows, width = value.shape
    out = jax.ShapeDtypeStruct((rows, width // 4), F32)
    notes = jax.ShapeDtypeStruct((8, width // 4), F32)
    return pl.pallas_call(finish_heads, out_shape=(out, out, out, notes), name="finish_heads")(value)


def interleave(query, key, value, heads):
    rows = query.shape[0]
    parts = [part.reshape(rows, heads, 1, DH) for part in (query, jnp.zeros_like(query), key, value)]
    return jnp.concatenate(parts, axis=2).reshape(rows, heads * SLAB)


def swap(value, axis, bit):
    size = lax.axis_size(axis)
    return lax.ppermute(value, axis, [(i, i ^ bit) for i in range(size)])


def bits_of(axis):
    bit = 1
    while bit < lax.axis_size(axis):
        yield bit
        bit *= 2


def after(value, *others):
    return lax.optimization_barrier((value,) + others)[0]


def merge(held, other, axis, bit):
    mine_first = (lax.axis_index(axis) & bit) == 0
    return jnp.where(
        mine_first, jnp.concatenate([held, other], axis=0), jnp.concatenate([other, held], axis=0)
    )


def add_low(left_side, right_side):
    return (left_side.astype(F32) + right_side.astype(F32)).astype(BF16)


def add_halves(left_side, right_side):
    half = left_side.shape[0] // 2
    return (
        add_low(left_side[:half], right_side[:half]),
        add_low(left_side[half:], right_side[half:]),
    )


def scatter_rows(held):
    index = lax.axis_index("dp")
    for bit in bits_of("dp"):
        held = held.reshape((held.shape[0] // 2, 2) + held.shape[1:])
        own = (index & bit) // bit
        send = lax.dynamic_index_in_dim(held, 1 - own, 1, keepdims=False)
        keep = lax.dynamic_index_in_dim(held, own, 1, keepdims=False)
        held = add_low(keep, swap(send, "dp", bit))
    return held[0]


def local(
    inputs, segment_ids, valid_mask, teacher, cotangent,
    w_query, w_key, w_value, w_output, w_inner, w_outer,
    query_bias, value_bias, output_bias, inner_bias, outer_bias,
    gain_attn, shift_attn, gain_ffn, shift_ffn,
):
    _, part_len, width = inputs.shape
    parts = lax.axis_size("tensor")
    copies = lax.axis_size("dp")
    rank = lax.axis_index("tensor")
    total_tokens = part_len * parts * copies
    seq_len = part_len * parts
    head_cols = w_query.shape[1]
    heads = head_cols // DH
    hidden_cols = w_inner.shape[1]
    shard_rows = w_inner.shape[0]
    halves = part_len // BLOCK

    rows_in = inputs.reshape(part_len, width)
    tokens = lax.all_gather(rows_in, "tensor", axis=0, tiled=True)
    w_heads = interleave(w_query, w_key, w_value, heads)
    paired = shard_rows % 16 == 0 and parts == 4 and copies == 8

    valid_rows = valid_mask.astype(F32).reshape(part_len, 1)
    valid_count = jnp.sum(valid_mask.astype(F32))
    upper = jnp.floor(valid_count / 256.0)
    spot = lax.broadcasted_iota(jnp.int32, (shard_rows, DH), 0) * DH + lax.broadcasted_iota(
        jnp.int32, (shard_rows, DH), 1
    )
    count_row = jnp.where(spot == 0, upper, jnp.where(spot == 1, valid_count - 256.0 * upper, 0.0))
    mine = jnp.concatenate((w_inner, w_outer.T, w_output.T, count_row.astype(BF16)), axis=1)
    if paired:
        place = jnp.stack([rank, rank ^ 1, rank ^ 2, rank ^ 3, lax.axis_index("dp")]).astype(jnp.int32)
        pair = jnp.concatenate([mine[None], swap(mine[None], "tensor", 1)], axis=0)
        near = jnp.concatenate([pair, swap(pair, "dp", 2)], axis=0)
        turns = [0, 2, 4, 6]
        for bit in (1, 2, 4):
            w_heads = merge(w_heads, swap(w_heads, "dp", bit), "dp", bit)
        near, w_heads = lax.optimization_barrier((near, w_heads))
        near_next = swap(near, "dp", 4)
        tokens, pair, near_next = lax.optimization_barrier((tokens, pair, near_next))
        far = swap(pair, "tensor", 2)
    else:
        place = jnp.asarray(list(range(parts)) + [0], jnp.int32)
        weights = lax.all_gather(mine, ("tensor", "dp"), axis=0, tiled=False)
        for bit in bits_of("dp"):
            w_heads = merge(w_heads, swap(w_heads, "dp", bit), "dp", bit)

    mine_cols = rank * head_cols
    query_shift = lax.dynamic_slice_in_dim(query_bias, mine_cols, head_cols).astype(F32)
    value_shift = lax.dynamic_slice_in_dim(value_bias, mine_cols, head_cols).astype(F32)
    shifts = interleave(query_shift[None], jnp.zeros_like(query_shift)[None], value_shift[None], heads)
    qkv = [(dot(tokens, w_heads) + shifts).astype(BF16)]

    segment_row = segment_ids.reshape(seq_len)
    bounds = document_blocks(segment_row)
    seg_col = segment_row.reshape(seq_len, 1)
    seg_row = segment_row.reshape(1, seq_len)
    lane = rank.astype(jnp.int32).reshape(1)

    def exchange(packed_blocks):
        return lax.all_to_all(packed_blocks, "tensor", 0, 0)

    contexts, lses, arrived = [], [], []
    for half in range(halves):
        if paired and half == 1:
            far, contexts[0], bounds = lax.optimization_barrier((far, contexts[0], bounds))
            weights = lax.all_gather(far, "dp", axis=0, tiled=False)
        context, lse = run_forward((halves, half), lane, bounds, qkv, seg_col, seg_row)
        if half > 0:
            context, arrived[0] = lax.optimization_barrier((context, arrived[0]))
        contexts.append(context)
        lses.append(lse)
        arrived.append(exchange(context))
    if paired:
        near_next, context = lax.optimization_barrier((near_next, contexts[-1]))
        near = jnp.concatenate([near, near_next], axis=0)
        near_other = swap(near, "dp", 1)
    if paired:
        weights = weights.reshape((copies * 2,) + mine.shape)
        pieces = [near, near_other, weights]
        marks = [[(slot, turn ^ flip, True) for turn in turns for slot in (0, 1)] for flip in (0, 1)]
        marks.append([(2 + at % 2, at // 2, False) for at in range(2 * copies)])
    else:
        pieces = [weights.reshape(parts, width, -1)]
        marks = [[(t, 0, False) for t in range(parts)]]
    counts = [piece.reshape((-1,) + mine.shape)[:, 0, -DH : 2 - DH].astype(F32) for piece in pieces + [weights]]
    counts = jnp.concatenate(counts[:-1] if paired else counts[-1:], axis=0)
    counted = 256.0 * jnp.sum(counts[:, 0]) + jnp.sum(counts[:, 1])

    vecs = jnp.stack(
        (output_bias, gain_attn, shift_attn, outer_bias, gain_ffn, shift_ffn, outer_bias, outer_bias)
    ).astype(F32)
    inner_rows = inner_bias.astype(F32).reshape(parts, 1, hidden_cols)
    teacher_rows = teacher.reshape(part_len, width)
    cotangent_rows = cotangent.reshape(part_len, width)
    (
        layer_out, first_grad, context_grad, first, branch_grad, attn_grad, activated, hidden_grad, notes,
    ) = run_dense(
        shard_rows, marks, float(total_tokens), place, arrived, rows_in, teacher_rows, cotangent_rows, valid_rows, vecs,
        inner_rows, pieces,
    )
    head_grad = exchange(context_grad).reshape((parts * halves, PACKED, 2 * DH))
    sources = (first, branch_grad, attn_grad, activated, hidden_grad, arrived)
    if shard_rows % 16:
        notes = jnp.tile(notes, (copies, 1))
    if paired:
        keep_turns = (0, 4, 2, 6)
        (distant,) = run_weights(2, 2, ((width, (0,)),), place, notes, *sources)
        plans = tuple((shard_rows, tuple(turn | flip for turn in keep_turns)) for flip in (0, 1))
        keep, send = run_weights(0, 2, plans, place, notes, *sources)
        keep, send = (value.reshape((4, 2) + value.shape[1:]) for value in (keep, send))
        distant = lax.psum_scatter(distant, "dp", scatter_dimension=1, tiled=True)
        came = swap(send, "dp", 1)
    else:
        (packed,) = run_weights(0, parts, ((width, (0,)),), place, notes, *sources)
        packed = lax.psum_scatter(packed, "dp", scatter_dimension=1, tiled=True)

    joined_grad, sums = run_backward(lane, bounds, qkv, seg_col, seg_row, head_grad, contexts, lses)
    joined_grad = joined_grad.reshape(seq_len, -1)
    attn_back = dot(joined_grad, w_heads, NT).astype(BF16)
    if paired:
        came = after(came, attn_back)
    attn_back, sums, joined_grad = lax.optimization_barrier((attn_back, sums, joined_grad))
    attn_back = lax.psum_scatter(attn_back, "tensor", scatter_dimension=0, tiled=True)
    if paired:
        keep, send = add_halves(keep, came)
        keep, send, joined_grad = lax.optimization_barrier((keep, send, joined_grad))
        came = swap(send, "dp", 2)
    head_weights = dot(tokens, joined_grad, TN).reshape((copies, shard_rows, -1))
    if paired:
        came, head_weights = lax.optimization_barrier((came, head_weights))
        keep, send = add_halves(keep, came)
        keep, send, head_weights = lax.optimization_barrier((keep, send, head_weights))
        came = swap(send, "dp", 4)
    sums = sums.reshape(heads, 4, DH)
    sums = jnp.concatenate((sums[:, 0].reshape(1, head_cols), sums[:, 3].reshape(1, head_cols)), axis=1)
    for bit in bits_of("tensor"):
        sums = merge(sums, swap(sums, "tensor", bit), "tensor", bit)
    if paired:
        came, head_weights = lax.optimization_barrier((came, head_weights))
        slots = jnp.concatenate([add_low(keep, came)[0], distant], axis=0)
        packed = jnp.stack(
            [lax.dynamic_index_in_dim(slots, rank ^ t, 0, keepdims=False) for t in range(parts)]
        )
    packed = lax.psum_scatter(packed, "tensor", scatter_dimension=0, tiled=True)[0]
    biases = jnp.concatenate((sums[:, :head_cols].reshape(-1), sums[:, head_cols:].reshape(-1)))
    biases = jnp.pad(
        biases.reshape(8, heads, 1, DH), ((0, shard_rows - 8), (0, 0), (1, 2), (0, 0))
    ).reshape(1, shard_rows, -1)
    query_grad, key_grad, value_grad, biases = run_finish_heads(
        scatter_rows((head_weights + biases).astype(BF16))
    )
    biases = biases.reshape(2, width)
    input_grad = first_grad + attn_back.astype(F32)

    inner_grad, outer_grad, output_grad, notes = run_finish_dense(packed, hidden_cols, head_cols)
    notes = notes.reshape(-1)

    def total(which):
        return notes[which * width : (which + 1) * width]

    mse_loss = jnp.sum(total(0)) / (counted * width)
    return (
        layer_out.reshape(1, part_len, width),
        mse_loss,
        input_grad.reshape(1, part_len, width),
        query_grad,
        key_grad,
        value_grad,
        output_grad,
        inner_grad,
        outer_grad.T,
        biases[0],
        biases[1],
        total(4),
        notes[8 * width : 8 * width + hidden_cols * parts],
        total(1),
        total(5),
        total(6),
        total(2),
        total(3),
    )


def solution(mesh):
    shard = P("dp", "tensor", None)
    by_dp, by_tensor = P("dp", "tensor"), P("tensor", "dp")
    in_specs = (
        (shard, P("dp", None), by_dp, shard, shard)
        + (by_dp,) * 3
        + (by_tensor, by_dp, by_tensor)
        + (P(),) * 9
    )
    out_specs = (shard, P(), shard) + (by_dp,) * 3 + (by_tensor, by_dp, by_tensor) + (P(),) * 9
    return jax.shard_map(local, mesh=mesh, in_specs=in_specs, out_specs=out_specs, check_vma=False)
```
